512 devices in a mesh: river: 16 (over y_hi, x, core), hours: 32 (over y_lo, z).
Axes of the slice: x: 4, y: 8 (y_hi: 2, y_lo: 4; y = y_hi * 4 + y_lo), z: 8, core: 2. Of those that a mesh axis runs over, the one named last changes fastest.
Arguments:
- release: float32 [160, 512, 512], P('river', 'hours'), may hold values from 0 to 1
- storage_dual: float32 [160, 512, 512], P('river', 'hours'), may hold values from -3 to 3
- demand_dual: float32 [512, 512], P('hours'), may hold values from -1 to 0
- cost: float32 [160, 512, 512], P('river', 'hours'), may hold values from -1.8 to 1.8
- inflow: float32 [160, 512, 512], P('river', 'hours'), may hold values from 0 to 1.2
- demand: float32 [512, 512], P('hours'), may hold values from 4.427189 to 8.221922
- storage_start: float32 [160], P('river'), may hold values from -0.5 to 0.5
- storage_low: float32 [160], P('river'), may hold values from -2 to -0.5
- storage_high: float32 [160], P('river'), may hold values from 0.5 to 2
- release_cap: float32 [160], P('river'), may hold values from 0.5 to 1.5
- efficiency: float32 [160], P('river'), may hold values from 0.5 to 1.5
- downstream: int32 [160], P('river'), may hold values from -1 to 159, as said below
- travel_delay: int32 [160], P('river'), may hold values from 1 to 6
Outputs:
- release_new: float32 [160, 512, 512], P('river', 'hours')
- storage_dual_new: float32 [160, 512, 512], P('river', 'hours')
- demand_dual_new: float32 [512, 512], P('hours')
- storage_excess: float32 [160, 512, 512], P('river', 'hours')
The draws below stay inside these ranges and needn't reach their ends.
Inputs may be any that keep to these rules, and one draw needn't show every extreme that they name: Each reservoir's downstream index is -1 or lies 1 to 10 positions after its own index.
All inputs are finite; a program needn't handle non-finite values.
Results may differ from the reference program's by a relative error of at most 0.00013.
Values sent between devices are 32-bit elements; how exact they have to be, the bound alone decides.
A program may use at most 64 MiB of HBM per device.

```python
import math
import jax
import jax.numpy as jnp
from jax import lax

RES_DEV = 10
DMAX = 6
SC = 512
RES = 160
HOURS = 512


def draw_downstream(key, part):
    position = jnp.arange(RES, dtype=jnp.int32)
    offset = jax.random.randint(key, (RES,), 1, RES_DEV + 1, dtype=jnp.int32)
    offset = jnp.where(position % RES_DEV >= RES_DEV - 2, 1, offset)
    target = position + offset
    return jnp.where(target < RES, target, -1).astype(jnp.int32)


def plant(drawn, own_key, least, largest):
    extent = drawn.shape
    spot = [jax.random.randint(jax.random.fold_in(own_key, axis), (), 0, extent[axis]) for axis in range(len(extent))]
    drawn = drawn.at[tuple(spot)].set(least)
    longest = extent.index(max(extent))
    spot[longest] = (spot[longest] + 1) % extent[longest]
    return drawn.at[tuple(spot)].set(largest)


def steps_of(own_key, dims, cuts, low, high):
    loudness, own = 1.0, jax.random.fold_in(own_key, 6)
    for dim, shards_of in cuts:
        heights = jnp.exp(jax.random.uniform(jax.random.fold_in(own, dim), (shards_of,), jnp.float32, low / len(cuts), high / len(cuts)))
        loudness = loudness * jnp.repeat(heights, dims[dim] // shards_of).reshape([-1 if axis == dim else 1 for axis in range(len(dims))])
    return loudness


def normal_values(stream_key, extent, width, most, pieces=(), held_as=jnp.bfloat16):
    array = jax.random.normal(stream_key, extent, jnp.float32) * width
    if len(pieces) > 0:
        array = steps_of(stream_key, extent, pieces, -0.22, 0.18) * array
    return jnp.clip(array, min=-most, max=most).astype(held_as)


def setup_inputs(seed: int = 0) -> dict:
    splits = jax.random.split(jax.random.key(seed), 14)
    return {
        "release": jnp.clip(1.0 * jax.random.uniform(splits[0], (RES, HOURS, SC), jnp.float32) ** steps_of(splits[0], (RES, HOURS, SC), ((0, 16), (1, 32)), -0.2, 0.2), 0.0, 1.0),
        "storage_dual": normal_values(splits[1], (RES, HOURS, SC), 0.5, 3.0, ((0, 16), (1, 32)), jnp.float32),
        "demand_dual": jnp.clip(-1.0 + 1.0 * jax.random.uniform(splits[2], (HOURS, SC), jnp.float32) ** steps_of(splits[2], (HOURS, SC), ((0, 32),), -0.2, 0.2), -1.0, 0.0),
        "cost": normal_values(splits[3], (RES, HOURS, SC), 0.3, 1.8, ((0, 16), (1, 32)), jnp.float32),
        "inflow": jnp.clip(1.2 * jax.random.uniform(splits[4], (RES, HOURS, SC), jnp.float32) ** steps_of(splits[4], (RES, HOURS, SC), ((0, 16), (1, 32)), -0.2, 0.2), 0.0, 1.2),
        "demand": jnp.clip(4.427189 + 3.794733 * jax.random.uniform(splits[5], (HOURS, SC), jnp.float32) ** steps_of(splits[5], (HOURS, SC), ((0, 32),), -0.2, 0.2), 4.427189, 8.221922),
        "storage_start": jnp.clip(jax.random.uniform(splits[6], (RES,), jnp.float32, -0.5, 0.5) * steps_of(splits[6], (RES,), ((0, 16),), -0.4, 0.0), -0.5, 0.5),
        "storage_low": jnp.clip(-2.0 + 1.5 * jax.random.uniform(splits[7], (RES,), jnp.float32) ** steps_of(splits[7], (RES,), ((0, 16),), -0.2, 0.2), -2.0, -0.5),
        "storage_high": jnp.clip(0.5 + 1.5 * jax.random.uniform(splits[8], (RES,), jnp.float32) ** steps_of(splits[8], (RES,), ((0, 16),), -0.2, 0.2), 0.5, 2.0),
        "release_cap": jnp.clip(0.5 + 1.0 * jax.random.uniform(splits[9], (RES,), jnp.float32) ** steps_of(splits[9], (RES,), ((0, 16),), -0.2, 0.2), 0.5, 1.5),
        "efficiency": jnp.clip(0.5 + 1.0 * jax.random.uniform(splits[10], (RES,), jnp.float32) ** steps_of(splits[10], (RES,), ((0, 16),), -0.2, 0.2), 0.5, 1.5),
        "downstream": draw_downstream(jax.random.fold_in(splits[13], 71), 0),
        "travel_delay": plant(jax.random.randint(splits[12], (RES,), 1, DMAX + 1), jax.random.fold_in(splits[12], 1), 1, DMAX).astype(jnp.int32),
    }


primal_step = 1.0
dual_step = 0.1

def reference(release, storage_dual, demand_dual, cost, inflow, demand, storage_start, storage_low, storage_high, release_cap, efficiency, downstream, travel_delay):
    scale_time = 1.0 / HOURS
    scale_sum = 1.0 / math.sqrt(RES)
    sink_index = jnp.where(downstream < 0, RES, downstream).astype(jnp.int32)
    suffix = jnp.flip(jnp.cumsum(jnp.flip(storage_dual, 1), 1), 1)
    padded = jnp.concatenate([suffix, jnp.zeros((1, HOURS, SC), jnp.float32)], 0)
    at_sink = padded[sink_index]
    later_duals = jnp.zeros((RES, HOURS, SC), jnp.float32)
    for lag_hours in range(1, DMAX + 1):
        shifted = jnp.concatenate([at_sink[:, lag_hours:], jnp.zeros((RES, lag_hours, SC), jnp.float32)], 1)
        later_duals = later_duals + jnp.where((travel_delay == lag_hours)[:, None, None], shifted, 0.0)
    gradient = cost + scale_time * (later_duals - suffix) + scale_sum * efficiency[:, None, None] * demand_dual[None]
    release_new = jnp.clip(release - primal_step * gradient, 0.0, release_cap[:, None, None])
    extrapolated = 2.0 * release_new - release
    delayed = jnp.zeros((RES, HOURS, SC), jnp.float32)
    for lag_hours in range(1, DMAX + 1):
        shifted = jnp.concatenate([jnp.zeros((RES, lag_hours, SC), jnp.float32), extrapolated[:, :HOURS - lag_hours]], 1)
        delayed = delayed + jnp.where((travel_delay == lag_hours)[:, None, None], shifted, 0.0)
    routed = jax.ops.segment_sum(delayed, sink_index, num_segments=RES + 1)[:RES]
    storage = storage_start[:, None, None] + scale_time * jnp.cumsum(inflow + routed - extrapolated, 1)
    lower_bound = storage_low[:, None, None]
    upper_bound = storage_high[:, None, None]
    storage_dual_new = storage_dual + dual_step * storage - dual_step * jnp.clip(storage_dual / dual_step + storage, lower_bound, upper_bound)
    storage_excess = storage - jnp.clip(storage, lower_bound, upper_bound)
    supplied = lax.optimization_barrier(jnp.sum(scale_sum * efficiency[:, None, None] * extrapolated, 0))
    demand_dual_new = jnp.minimum(demand_dual + dual_step * (supplied - demand), 0.0)
    return (release_new, storage_dual_new, demand_dual_new, storage_excess)
```

```python
import functools
import math

import jax
import jax.numpy as jnp
from jax import lax
from jax.experimental import pallas as pl
from jax.experimental.pallas import tpu as pltpu
from jax.sharding import PartitionSpec as P

DMAX = 6


primal_step = 1.0
dual_step = 0.1


def passed_along(block, axis, distance):
    devices = range(lax.axis_size(axis))
    route = [(i - distance, i) for i in devices if i - distance in devices]
    return lax.ppermute(block, axis, route)


def exchange_kernel(n, axis, other, mode, x_ref, out_ref, slots, send_sem, recv_sem):
    me = lax.axis_index(axis)
    fixed = lax.axis_index(other)

    def device(p):
        return (fixed, p) if axis == "hours" else (p, fixed)

    def wanted(src, dst):
        if mode == "prefix":
            return src < dst
        if mode == "suffix":
            return src > dst
        return src != dst

    barrier = pltpu.get_barrier_semaphore()

    def greet(i, carry):
        p = lax.rem(me + 1 + i, n)
        pl.semaphore_signal(barrier, 1, device_id=device(p), device_id_type=pl.DeviceIdType.MESH)
        return carry

    lax.fori_loop(0, n - 1, greet, 0)
    pl.semaphore_wait(barrier, n - 1)

    def outgoing(p):
        return pltpu.make_async_remote_copy(
            src_ref=x_ref,
            dst_ref=slots.at[me],
            send_sem=send_sem.at[p],
            recv_sem=recv_sem.at[me],
            device_id=device(p),
            device_id_type=pl.DeviceIdType.MESH,
        )

    def incoming(p):
        return pltpu.make_async_remote_copy(
            src_ref=x_ref,
            dst_ref=slots.at[p],
            send_sem=send_sem.at[p],
            recv_sem=recv_sem.at[p],
            device_id=device(p),
            device_id_type=pl.DeviceIdType.MESH,
        )

    def send(i, carry):
        p = lax.rem(me + 1 + i, n)

        @pl.when(wanted(me, p))
        def _():
            outgoing(p).start()

        return carry

    lax.fori_loop(0, n - 1, send, 0)

    def settle(i, carry):
        p = lax.rem(me + 1 + i, n)

        @pl.when(wanted(me, p))
        def _():
            outgoing(p).wait_send()

        @pl.when(wanted(p, me))
        def _():
            incoming(p).wait_recv()

        return carry

    lax.fori_loop(0, n - 1, settle, 0)
    start = x_ref[...] if mode == "sum" else jnp.zeros_like(x_ref[...])

    def total(i, acc):
        p = lax.rem(me + 1 + i, n)
        return acc + jnp.where(wanted(p, me), slots[p], 0.0)

    out_ref[...] = lax.fori_loop(0, n - 1, total, start)


IDS = {"prefix": 0, "suffix": 1, "sum": 2}


def exchange(part, axis, mode):
    n = lax.axis_size(axis)
    other = "river" if axis == "hours" else "hours"
    return pl.pallas_call(
        functools.partial(exchange_kernel, n, axis, other, mode),
        out_shape=jax.ShapeDtypeStruct(part.shape, part.dtype),
        in_specs=[pl.BlockSpec(memory_space=pltpu.VMEM)],
        out_specs=pl.BlockSpec(memory_space=pltpu.VMEM),
        scratch_shapes=[
            pltpu.VMEM((n,) + part.shape, part.dtype),
            pltpu.SemaphoreType.DMA((n,)),
            pltpu.SemaphoreType.DMA((n,)),
        ],
        compiler_params=pltpu.CompilerParams(collective_id=IDS[mode], has_side_effects=True),
    )(part)


def add_pair(earlier_part, later_part):
    return earlier_part + later_part


def hold_back(field, travel_delay, earlier_rim):
    length = field.shape[1]
    extended = jnp.concatenate([earlier_rim, field], 1)
    result = jnp.zeros_like(field)
    for lag_hours in range(1, DMAX + 1):
        window = extended[:, DMAX - lag_hours : DMAX - lag_hours + length]
        result = result + jnp.where((travel_delay == lag_hours)[:, None, None], window, 0.0)
    return result


def bring_forward(field, travel_delay, later_rim):
    length = field.shape[1]
    extended = jnp.concatenate([field, later_rim], 1)
    result = jnp.zeros_like(field)
    for lag_hours in range(1, DMAX + 1):
        window = extended[:, lag_hours : lag_hours + length]
        result = result + jnp.where((travel_delay == lag_hours)[:, None, None], window, 0.0)
    return result


def route_down(matrix, field):
    return jnp.einsum("ij,jtw->itw", matrix, field, precision=lax.Precision.HIGHEST)


def route_up(matrix, field):
    return jnp.einsum("ij,itw->jtw", matrix, field, precision=lax.Precision.HIGHEST)


def iterate(fields, statics, scales, prefix_sum, suffix_sum, from_earlier, from_later):
    release, storage_dual, demand_dual, cost, inflow, demand = fields
    (
        storage_start,
        storage_low,
        storage_high,
        release_cap,
        efficiency,
        travel_delay,
        to_own,
        to_next,
    ) = statics
    scale_time, scale_sum = scales
    suffix = suffix_sum(storage_dual)
    beyond = passed_along(suffix, "river", -1)
    at_sink = route_up(to_own, suffix) + route_up(to_next, beyond)
    later_duals = bring_forward(at_sink, travel_delay, from_later(at_sink[:, :DMAX]))
    gradient = (
        cost
        + scale_time * (later_duals - suffix)
        + scale_sum * efficiency[:, None, None] * demand_dual[None]
    )
    release_new = jnp.clip(release - primal_step * gradient, 0.0, release_cap[:, None, None])
    extrapolated = 2.0 * release_new - release
    length = extrapolated.shape[1]
    delayed = hold_back(extrapolated, travel_delay, from_earlier(extrapolated[:, length - DMAX :]))
    incoming = passed_along(route_down(to_next, delayed), "river", 1)
    routed = route_down(to_own, delayed) + incoming
    storage = storage_start[:, None, None] + scale_time * prefix_sum(inflow + routed - extrapolated)
    lower_bound = storage_low[:, None, None]
    upper_bound = storage_high[:, None, None]
    storage_dual_new = (
        storage_dual
        + dual_step * storage
        - dual_step * jnp.clip(storage_dual / dual_step + storage, lower_bound, upper_bound)
    )
    storage_excess = storage - jnp.clip(storage, lower_bound, upper_bound)
    partial_power = jnp.sum(scale_sum * efficiency[:, None, None] * extrapolated, 0)
    supplied = exchange(partial_power, "river", "sum")
    demand_dual_new = jnp.minimum(demand_dual + dual_step * (supplied - demand), 0.0)
    return (release_new, storage_dual_new, demand_dual_new, storage_excess)


def suffix_local(field):
    return jnp.flip(jnp.cumsum(jnp.flip(field, 1), 1), 1)


def shards(
    release,
    storage_dual,
    demand_dual,
    cost,
    inflow,
    demand,
    storage_start,
    storage_low,
    storage_high,
    release_cap,
    efficiency,
    downstream,
    travel_delay,
):
    res_dev = release.shape[0]
    scale_time = 1.0 / (release.shape[1] * lax.axis_size("hours"))
    scale_sum = 1.0 / math.sqrt(res_dev * lax.axis_size("river"))
    base_index = lax.axis_index("river") * res_dev
    target = downstream - base_index
    indices = jnp.arange(res_dev, dtype=jnp.int32)
    to_own = (target[None, :] == indices[:, None]).astype(jnp.float32)
    to_next = (target[None, :] == indices[:, None] + res_dev).astype(jnp.float32)
    statics = (
        storage_start,
        storage_low,
        storage_high,
        release_cap,
        efficiency,
        travel_delay,
        to_own,
        to_next,
    )
    scales = (scale_time, scale_sum)

    def prefix_blocks(field):
        local_sum = jnp.cumsum(field, 1)
        totals = local_sum[:, -1]
        offset = exchange(totals, "hours", "prefix")
        return local_sum + offset[:, None]

    def suffix_blocks(field):
        local_sum = suffix_local(field)
        totals = local_sum[:, 0]
        offset = exchange(totals, "hours", "suffix")
        return local_sum + offset[:, None]

    def earlier_block(part):
        return passed_along(part, "hours", 1)

    def later_block(part):
        return passed_along(part, "hours", -1)

    fields = (release, storage_dual, demand_dual, cost, inflow, demand)
    return iterate(
        fields, statics, scales, prefix_blocks, suffix_blocks, earlier_block, later_block
    )


def solution(mesh):
    return jax.shard_map(
        shards,
        mesh=mesh,
        in_specs=(
            P("river", "hours", None),
            P("river", "hours", None),
            P("hours", None),
            P("river", "hours", None),
            P("river", "hours", None),
            P("hours", None),
            P("river"),
            P("river"),
            P("river"),
            P("river"),
            P("river"),
            P("river"),
            P("river"),
        ),
        out_specs=(
            P("river", "hours", None),
            P("river", "hours", None),
            P("hours", None),
            P("river", "hours", None),
        ),
        check_vma=False,
    )
```

```python
import functools
import math

import jax
import jax.numpy as jnp
from jax import lax
from jax.experimental import pallas as pl
from jax.experimental.pallas import tpu as pltpu
from jax.sharding import PartitionSpec as P

DMAX = 6


primal_step = 1.0
dual_step = 0.1


def passed_along(block, axis, distance):
    devices = range(lax.axis_size(axis))
    route = [(i - distance, i) for i in devices if i - distance in devices]
    return lax.ppermute(block, axis, route)


MESH = pl.DeviceIdType.MESH


def two_level_kernel(inner, outer, axis, other, mode, x_ref, out_ref, near, far, group, s1, r1, s2, r2):
    me = lax.axis_index(axis)
    fixed = lax.axis_index(other)
    o = me // inner
    i = me % inner

    def device(p):
        return (fixed, p) if axis == "hours" else (p, fixed)

    def wanted(src, dst):
        if mode == "prefix":
            return src < dst
        if mode == "suffix":
            return src > dst
        return src != dst

    barrier = pltpu.get_barrier_semaphore()
    for step in range(1, inner):
        pl.semaphore_signal(barrier, 1, device_id=device(o * inner + lax.rem(i + step, inner)), device_id_type=MESH)
    for step in range(1, outer):
        pl.semaphore_signal(barrier, 1, device_id=device(lax.rem(o + step, outer) * inner + i), device_id_type=MESH)
    pl.semaphore_wait(barrier, inner + outer - 2)

    def across(step):
        p = lax.rem(i + step, inner)
        return pltpu.make_async_remote_copy(
            src_ref=x_ref, dst_ref=near.at[i], send_sem=s1.at[p], recv_sem=r1.at[i],
            device_id=device(o * inner + p), device_id_type=MESH)

    def arrived(step):
        p = lax.rem(i + step, inner)
        return pltpu.make_async_remote_copy(
            src_ref=x_ref, dst_ref=near.at[p], send_sem=s1.at[p], recv_sem=r1.at[p],
            device_id=device(o * inner + p), device_id_type=MESH)

    for step in range(1, inner):
        across(step).start()
    for step in range(1, inner):
        across(step).wait_send()
        arrived(step).wait_recv()

    own = x_ref[...]
    total = own
    part = own if mode == "sum" else jnp.zeros_like(own)
    for step in range(1, inner):
        p = lax.rem(i + step, inner)
        block = near[p]
        total = total + block
        if mode == "sum":
            part = part + block
        else:
            part = part + jnp.where(wanted(p, i), block, 0.0)
    group[...] = total

    def up(step):
        q = lax.rem(o + step, outer)
        return pltpu.make_async_remote_copy(
            src_ref=group, dst_ref=far.at[o], send_sem=s2.at[q], recv_sem=r2.at[o],
            device_id=device(q * inner + i), device_id_type=MESH)

    def got(step):
        q = lax.rem(o + step, outer)
        return pltpu.make_async_remote_copy(
            src_ref=group, dst_ref=far.at[q], send_sem=s2.at[q], recv_sem=r2.at[q],
            device_id=device(q * inner + i), device_id_type=MESH)

    for step in range(1, outer):
        q = lax.rem(o + step, outer)

        @pl.when(wanted(o, q))
        def _():
            up(step).start()

    for step in range(1, outer):
        q = lax.rem(o + step, outer)

        @pl.when(wanted(o, q))
        def _():
            up(step).wait_send()

        @pl.when(wanted(q, o))
        def _():
            got(step).wait_recv()

    for step in range(1, outer):
        q = lax.rem(o + step, outer)
        part = part + jnp.where(wanted(q, o), far[q], 0.0)
    out_ref[...] = part


IDS = {"prefix": 0, "suffix": 1, "sum": 2}


def two_level(part, axis, mode, inner):
    n = lax.axis_size(axis)
    outer = n // inner
    other = "river" if axis == "hours" else "hours"
    return pl.pallas_call(
        functools.partial(two_level_kernel, inner, outer, axis, other, mode),
        out_shape=jax.ShapeDtypeStruct(part.shape, part.dtype),
        in_specs=[pl.BlockSpec(memory_space=pltpu.VMEM)],
        out_specs=pl.BlockSpec(memory_space=pltpu.VMEM),
        scratch_shapes=[
            pltpu.VMEM((inner,) + part.shape, part.dtype),
            pltpu.VMEM((outer,) + part.shape, part.dtype),
            pltpu.VMEM(part.shape, part.dtype),
            pltpu.SemaphoreType.DMA((inner,)),
            pltpu.SemaphoreType.DMA((inner,)),
            pltpu.SemaphoreType.DMA((outer,)),
            pltpu.SemaphoreType.DMA((outer,)),
        ],
        compiler_params=pltpu.CompilerParams(collective_id=IDS[mode], has_side_effects=True),
    )(part)


def add_pair(earlier_part, later_part):
    return earlier_part + later_part


def hold_back(field, travel_delay, earlier_rim):
    length = field.shape[1]
    extended = jnp.concatenate([earlier_rim, field], 1)
    result = jnp.zeros_like(field)
    for lag_hours in range(1, DMAX + 1):
        window = extended[:, DMAX - lag_hours : DMAX - lag_hours + length]
        result = result + jnp.where((travel_delay == lag_hours)[:, None, None], window, 0.0)
    return result


def bring_forward(field, travel_delay, later_rim):
    length = field.shape[1]
    extended = jnp.concatenate([field, later_rim], 1)
    result = jnp.zeros_like(field)
    for lag_hours in range(1, DMAX + 1):
        window = extended[:, lag_hours : lag_hours + length]
        result = result + jnp.where((travel_delay == lag_hours)[:, None, None], window, 0.0)
    return result


def route_down(matrix, field):
    return jnp.einsum("ij,jtw->itw", matrix, field, precision=lax.Precision.HIGHEST)


def route_up(matrix, field):
    return jnp.einsum("ij,itw->jtw", matrix, field, precision=lax.Precision.HIGHEST)


def iterate(fields, statics, scales, prefix_sum, suffix_sum, from_earlier, from_later):
    release, storage_dual, demand_dual, cost, inflow, demand = fields
    (
        storage_start,
        storage_low,
        storage_high,
        release_cap,
        efficiency,
        travel_delay,
        to_own,
        to_next,
    ) = statics
    scale_time, scale_sum = scales
    suffix = suffix_sum(storage_dual)
    beyond = passed_along(suffix, "river", -1)
    at_sink = route_up(to_own, suffix) + route_up(to_next, beyond)
    later_duals = bring_forward(at_sink, travel_delay, from_later(at_sink[:, :DMAX]))
    gradient = (
        cost
        + scale_time * (later_duals - suffix)
        + scale_sum * efficiency[:, None, None] * demand_dual[None]
    )
    release_new = jnp.clip(release - primal_step * gradient, 0.0, release_cap[:, None, None])
    extrapolated = 2.0 * release_new - release
    length = extrapolated.shape[1]
    delayed = hold_back(extrapolated, travel_delay, from_earlier(extrapolated[:, length - DMAX :]))
    incoming = passed_along(route_down(to_next, delayed), "river", 1)
    routed = route_down(to_own, delayed) + incoming
    storage = storage_start[:, None, None] + scale_time * prefix_sum(inflow + routed - extrapolated)
    lower_bound = storage_low[:, None, None]
    upper_bound = storage_high[:, None, None]
    storage_dual_new = (
        storage_dual
        + dual_step * storage
        - dual_step * jnp.clip(storage_dual / dual_step + storage, lower_bound, upper_bound)
    )
    storage_excess = storage - jnp.clip(storage, lower_bound, upper_bound)
    partial_power = jnp.sum(scale_sum * efficiency[:, None, None] * extrapolated, 0)
    supplied = two_level(partial_power, "river", "sum", 8)
    demand_dual_new = jnp.minimum(demand_dual + dual_step * (supplied - demand), 0.0)
    return (release_new, storage_dual_new, demand_dual_new, storage_excess)


def suffix_local(field):
    return jnp.flip(jnp.cumsum(jnp.flip(field, 1), 1), 1)


def shards(
    release,
    storage_dual,
    demand_dual,
    cost,
    inflow,
    demand,
    storage_start,
    storage_low,
    storage_high,
    release_cap,
    efficiency,
    downstream,
    travel_delay,
):
    res_dev = release.shape[0]
    scale_time = 1.0 / (release.shape[1] * lax.axis_size("hours"))
    scale_sum = 1.0 / math.sqrt(res_dev * lax.axis_size("river"))
    base_index = lax.axis_index("river") * res_dev
    target = downstream - base_index
    indices = jnp.arange(res_dev, dtype=jnp.int32)
    to_own = (target[None, :] == indices[:, None]).astype(jnp.float32)
    to_next = (target[None, :] == indices[:, None] + res_dev).astype(jnp.float32)
    statics = (
        storage_start,
        storage_low,
        storage_high,
        release_cap,
        efficiency,
        travel_delay,
        to_own,
        to_next,
    )
    scales = (scale_time, scale_sum)

    def prefix_blocks(field):
        local_sum = jnp.cumsum(field, 1)
        totals = local_sum[:, -1]
        offset = two_level(totals, "hours", "prefix", 8)
        return local_sum + offset[:, None]

    def suffix_blocks(field):
        local_sum = suffix_local(field)
        totals = local_sum[:, 0]
        offset = two_level(totals, "hours", "suffix", 8)
        return local_sum + offset[:, None]

    def earlier_block(part):
        return passed_along(part, "hours", 1)

    def later_block(part):
        return passed_along(part, "hours", -1)

    fields = (release, storage_dual, demand_dual, cost, inflow, demand)
    return iterate(
        fields, statics, scales, prefix_blocks, suffix_blocks, earlier_block, later_block
    )


def solution(mesh):
    return jax.shard_map(
        shards,
        mesh=mesh,
        in_specs=(
            P("river", "hours", None),
            P("river", "hours", None),
            P("hours", None),
            P("river", "hours", None),
            P("river", "hours", None),
            P("hours", None),
            P("river"),
            P("river"),
            P("river"),
            P("river"),
            P("river"),
            P("river"),
            P("river"),
        ),
        out_specs=(
            P("river", "hours", None),
            P("river", "hours", None),
            P("hours", None),
            P("river", "hours", None),
        ),
        check_vma=False,
    )
```

```python
import functools
import math

import jax
import jax.numpy as jnp
from jax import lax
from jax.experimental import pallas as pl
from jax.experimental.pallas import tpu as pltpu
from jax.sharding import PartitionSpec as P

DMAX = 6


primal_step = 1.0
dual_step = 0.1


def passed_along(block, axis, distance):
    devices = range(lax.axis_size(axis))
    route = [(i - distance, i) for i in devices if i - distance in devices]
    return lax.ppermute(block, axis, route)


MESH = pl.DeviceIdType.MESH


def wanted(mode, src, dst):
    if mode == "prefix":
        return src < dst
    if mode == "suffix":
        return src > dst
    return src != dst


class Job:
    def __init__(self, axis, mode, inner, n):
        self.axis, self.mode, self.inner = axis, mode, inner
        self.outer = n // inner
        self.other = "river" if axis == "hours" else "hours"

    def place(self):
        me = lax.axis_index(self.axis)
        self.fixed = lax.axis_index(self.other)
        self.o = me // self.inner
        self.i = me % self.inner

    def device(self, p):
        return (self.fixed, p) if self.axis == "hours" else (p, self.fixed)

    def peers(self):
        inner, outer, o, i = self.inner, self.outer, self.o, self.i
        near = [self.device(o * inner + lax.rem(i + s, inner)) for s in range(1, inner)]
        far = [self.device(lax.rem(o + s, outer) * inner + i) for s in range(1, outer)]
        return near + far


def multi_kernel(jobs, *refs):
    count = len(jobs)
    ins, outs, rest = refs[:count], refs[count:2 * count], refs[2 * count:]
    for job in jobs:
        job.place()
    barrier = pltpu.get_barrier_semaphore()
    partners = 0
    for job in jobs:
        for dev in job.peers():
            pl.semaphore_signal(barrier, 1, device_id=dev, device_id_type=MESH)
            partners += 1
    pl.semaphore_wait(barrier, partners)

    def across(job, x_ref, near, s1, r1, p, landing):
        return pltpu.make_async_remote_copy(
            src_ref=x_ref, dst_ref=near.at[landing], send_sem=s1.at[p], recv_sem=r1.at[landing],
            device_id=job.device(job.o * job.inner + p), device_id_type=MESH)

    for k, job in enumerate(jobs):
        near, far, group, s1, r1, s2, r2 = rest[7 * k:7 * k + 7]
        for s in range(1, job.inner):
            p = lax.rem(job.i + s, job.inner)
            across(job, ins[k], near, s1, r1, p, job.i).start()
    parts = []
    for k, job in enumerate(jobs):
        near, far, group, s1, r1, s2, r2 = rest[7 * k:7 * k + 7]
        for s in range(1, job.inner):
            p = lax.rem(job.i + s, job.inner)
            across(job, ins[k], near, s1, r1, p, job.i).wait_send()
            across(job, ins[k], near, s1, r1, p, p).wait_recv()
        own = ins[k][...]
        total = own
        part = own if job.mode == "sum" else jnp.zeros_like(own)
        for s in range(1, job.inner):
            p = lax.rem(job.i + s, job.inner)
            block = near[p]
            total = total + block
            if job.mode == "sum":
                part = part + block
            else:
                part = part + jnp.where(wanted(job.mode, p, job.i), block, 0.0)
        group[...] = total
        parts.append(part)

    def up(job, group, far, s2, r2, q, landing):
        return pltpu.make_async_remote_copy(
            src_ref=group, dst_ref=far.at[landing], send_sem=s2.at[q], recv_sem=r2.at[landing],
            device_id=job.device(q * job.inner + job.i), device_id_type=MESH)

    for k, job in enumerate(jobs):
        near, far, group, s1, r1, s2, r2 = rest[7 * k:7 * k + 7]
        for s in range(1, job.outer):
            q = lax.rem(job.o + s, job.outer)

            @pl.when(wanted(job.mode, job.o, q))
            def _():
                up(job, group, far, s2, r2, q, job.o).start()

    for k, job in enumerate(jobs):
        near, far, group, s1, r1, s2, r2 = rest[7 * k:7 * k + 7]
        part = parts[k]
        for s in range(1, job.outer):
            q = lax.rem(job.o + s, job.outer)

            @pl.when(wanted(job.mode, job.o, q))
            def _():
                up(job, group, far, s2, r2, q, job.o).wait_send()

            @pl.when(wanted(job.mode, q, job.o))
            def _():
                up(job, group, far, s2, r2, q, q).wait_recv()

        for s in range(1, job.outer):
            q = lax.rem(job.o + s, job.outer)
            part = part + jnp.where(wanted(job.mode, q, job.o), far[q], 0.0)
        outs[k][...] = part


def combine(parts, specs, collective):
    jobs = [Job(axis, mode, inner, lax.axis_size(axis)) for axis, mode, inner in specs]
    scratch = []
    for part, job in zip(parts, jobs):
        scratch += [
            pltpu.VMEM((job.inner,) + part.shape, part.dtype),
            pltpu.VMEM((job.outer,) + part.shape, part.dtype),
            pltpu.VMEM(part.shape, part.dtype),
            pltpu.SemaphoreType.DMA((job.inner,)),
            pltpu.SemaphoreType.DMA((job.inner,)),
            pltpu.SemaphoreType.DMA((job.outer,)),
            pltpu.SemaphoreType.DMA((job.outer,)),
        ]
    return pl.pallas_call(
        functools.partial(multi_kernel, jobs),
        out_shape=[jax.ShapeDtypeStruct(part.shape, part.dtype) for part in parts],
        in_specs=[pl.BlockSpec(memory_space=pltpu.VMEM)] * len(parts),
        out_specs=[pl.BlockSpec(memory_space=pltpu.VMEM)] * len(parts),
        scratch_shapes=scratch,
        compiler_params=pltpu.CompilerParams(collective_id=collective, has_side_effects=True),
    )(*parts)


def add_pair(earlier_part, later_part):
    return earlier_part + later_part


def hold_back(field, travel_delay, earlier_rim):
    length = field.shape[1]
    extended = jnp.concatenate([earlier_rim, field], 1)
    result = jnp.zeros_like(field)
    for lag_hours in range(1, DMAX + 1):
        window = extended[:, DMAX - lag_hours : DMAX - lag_hours + length]
        result = result + jnp.where((travel_delay == lag_hours)[:, None, None], window, 0.0)
    return result


def bring_forward(field, travel_delay, later_rim):
    length = field.shape[1]
    extended = jnp.concatenate([field, later_rim], 1)
    result = jnp.zeros_like(field)
    for lag_hours in range(1, DMAX + 1):
        window = extended[:, lag_hours : lag_hours + length]
        result = result + jnp.where((travel_delay == lag_hours)[:, None, None], window, 0.0)
    return result


def route_down(matrix, field):
    return jnp.einsum("ij,jtw->itw", matrix, field, precision=lax.Precision.HIGHEST)


def route_up(matrix, field):
    return jnp.einsum("ij,itw->jtw", matrix, field, precision=lax.Precision.HIGHEST)


def iterate(fields, statics, scales, suffix_sum, from_earlier, from_later):
    release, storage_dual, demand_dual, cost, inflow, demand = fields
    (
        storage_start,
        storage_low,
        storage_high,
        release_cap,
        efficiency,
        travel_delay,
        to_own,
        to_next,
    ) = statics
    scale_time, scale_sum = scales
    suffix = suffix_sum(storage_dual)
    beyond = passed_along(suffix, "river", -1)
    at_sink = route_up(to_own, suffix) + route_up(to_next, beyond)
    later_duals = bring_forward(at_sink, travel_delay, from_later(at_sink[:, :DMAX]))
    gradient = (
        cost
        + scale_time * (later_duals - suffix)
        + scale_sum * efficiency[:, None, None] * demand_dual[None]
    )
    release_new = jnp.clip(release - primal_step * gradient, 0.0, release_cap[:, None, None])
    extrapolated = 2.0 * release_new - release
    length = extrapolated.shape[1]
    delayed = hold_back(extrapolated, travel_delay, from_earlier(extrapolated[:, length - DMAX :]))
    incoming = passed_along(route_down(to_next, delayed), "river", 1)
    routed = route_down(to_own, delayed) + incoming
    local_sum = jnp.cumsum(inflow + routed - extrapolated, 1)
    partial_power = jnp.sum(scale_sum * efficiency[:, None, None] * extrapolated, 0)
    offset, supplied = combine(
        [local_sum[:, -1], partial_power], [("hours", "prefix", 8), ("river", "sum", 8)], 1
    )
    storage = storage_start[:, None, None] + scale_time * (local_sum + offset[:, None])
    lower_bound = storage_low[:, None, None]
    upper_bound = storage_high[:, None, None]
    storage_dual_new = (
        storage_dual
        + dual_step * storage
        - dual_step * jnp.clip(storage_dual / dual_step + storage, lower_bound, upper_bound)
    )
    storage_excess = storage - jnp.clip(storage, lower_bound, upper_bound)
    demand_dual_new = jnp.minimum(demand_dual + dual_step * (supplied - demand), 0.0)
    return (release_new, storage_dual_new, demand_dual_new, storage_excess)


def suffix_local(field):
    return jnp.flip(jnp.cumsum(jnp.flip(field, 1), 1), 1)


def shards(
    release,
    storage_dual,
    demand_dual,
    cost,
    inflow,
    demand,
    storage_start,
    storage_low,
    storage_high,
    release_cap,
    efficiency,
    downstream,
    travel_delay,
):
    res_dev = release.shape[0]
    scale_time = 1.0 / (release.shape[1] * lax.axis_size("hours"))
    scale_sum = 1.0 / math.sqrt(res_dev * lax.axis_size("river"))
    base_index = lax.axis_index("river") * res_dev
    target = downstream - base_index
    indices = jnp.arange(res_dev, dtype=jnp.int32)
    to_own = (target[None, :] == indices[:, None]).astype(jnp.float32)
    to_next = (target[None, :] == indices[:, None] + res_dev).astype(jnp.float32)
    statics = (
        storage_start,
        storage_low,
        storage_high,
        release_cap,
        efficiency,
        travel_delay,
        to_own,
        to_next,
    )
    scales = (scale_time, scale_sum)

    def suffix_blocks(field):
        local_sum = suffix_local(field)
        totals = local_sum[:, 0]
        (offset,) = combine([totals], [("hours", "suffix", 8)], 0)
        return local_sum + offset[:, None]

    def earlier_block(part):
        return passed_along(part, "hours", 1)

    def later_block(part):
        return passed_along(part, "hours", -1)

    fields = (release, storage_dual, demand_dual, cost, inflow, demand)
    return iterate(
        fields, statics, scales, suffix_blocks, earlier_block, later_block
    )


def solution(mesh):
    return jax.shard_map(
        shards,
        mesh=mesh,
        in_specs=(
            P("river", "hours", None),
            P("river", "hours", None),
            P("hours", None),
            P("river", "hours", None),
            P("river", "hours", None),
            P("hours", None),
            P("river"),
            P("river"),
            P("river"),
            P("river"),
            P("river"),
            P("river"),
            P("river"),
        ),
        out_specs=(
            P("river", "hours", None),
            P("river", "hours", None),
            P("hours", None),
            P("river", "hours", None),
        ),
        check_vma=False,
    )
```

```python
import functools
import math

import jax
import jax.numpy as jnp
from jax import lax
from jax.experimental import pallas as pl
from jax.experimental.pallas import tpu as pltpu
from jax.sharding import PartitionSpec as P

DMAX = 6


primal_step = 1.0
dual_step = 0.1


def passed_along(block, axis, distance):
    devices = range(lax.axis_size(axis))
    route = [(i - distance, i) for i in devices if i - distance in devices]
    return lax.ppermute(block, axis, route)


MESH = pl.DeviceIdType.MESH


def wanted(mode, src, dst):
    if mode == "prefix":
        return src < dst
    if mode == "suffix":
        return src > dst
    return src != dst


class Job:
    def __init__(self, axis, mode, inner, n):
        self.axis, self.mode, self.inner = axis, mode, inner
        self.outer = n // inner
        self.other = "river" if axis == "hours" else "hours"

    def place(self):
        me = lax.axis_index(self.axis)
        self.fixed = lax.axis_index(self.other)
        self.o = me // self.inner
        self.i = me % self.inner

    def device(self, p):
        return (self.fixed, p) if self.axis == "hours" else (p, self.fixed)

    def peers(self):
        inner, outer, o, i = self.inner, self.outer, self.o, self.i
        near = [self.device(o * inner + lax.rem(i + s, inner)) for s in range(1, inner)]
        far = [self.device(lax.rem(o + s, outer) * inner + i) for s in range(1, outer)]
        return near + far


def multi_kernel(jobs, *refs):
    count = len(jobs)
    ins, outs, rest = refs[:count], refs[count:2 * count], refs[2 * count:]
    for job in jobs:
        job.place()
    barrier = pltpu.get_barrier_semaphore()
    partners = 0
    for job in jobs:
        for dev in job.peers():
            pl.semaphore_signal(barrier, 1, device_id=dev, device_id_type=MESH)
            partners += 1
    pl.semaphore_wait(barrier, partners)

    def across(job, x_ref, near, s1, r1, p, landing):
        return pltpu.make_async_remote_copy(
            src_ref=x_ref, dst_ref=near.at[landing], send_sem=s1.at[p], recv_sem=r1.at[landing],
            device_id=job.device(job.o * job.inner + p), device_id_type=MESH)

    for k, job in enumerate(jobs):
        near, far, group, s1, r1, s2, r2 = rest[7 * k:7 * k + 7]
        for s in range(1, job.inner):
            p = lax.rem(job.i + s, job.inner)
            across(job, ins[k], near, s1, r1, p, job.i).start()
    parts = []
    for k, job in enumerate(jobs):
        near, far, group, s1, r1, s2, r2 = rest[7 * k:7 * k + 7]
        for s in range(1, job.inner):
            p = lax.rem(job.i + s, job.inner)
            across(job, ins[k], near, s1, r1, p, job.i).wait_send()
            across(job, ins[k], near, s1, r1, p, p).wait_recv()
        own = ins[k][...]
        total = own
        part = own if job.mode == "sum" else jnp.zeros_like(own)
        for s in range(1, job.inner):
            p = lax.rem(job.i + s, job.inner)
            block = near[p]
            total = total + block
            if job.mode == "sum":
                part = part + block
            else:
                part = part + jnp.where(wanted(job.mode, p, job.i), block, 0.0)
        group[...] = total
        parts.append(part)

    def up(job, group, far, s2, r2, q, landing):
        return pltpu.make_async_remote_copy(
            src_ref=group, dst_ref=far.at[landing], send_sem=s2.at[q], recv_sem=r2.at[landing],
            device_id=job.device(q * job.inner + job.i), device_id_type=MESH)

    for k, job in enumerate(jobs):
        near, far, group, s1, r1, s2, r2 = rest[7 * k:7 * k + 7]
        for s in range(1, job.outer):
            q = lax.rem(job.o + s, job.outer)

            @pl.when(wanted(job.mode, job.o, q))
            def _():
                up(job, group, far, s2, r2, q, job.o).start()

    for k, job in enumerate(jobs):
        near, far, group, s1, r1, s2, r2 = rest[7 * k:7 * k + 7]
        part = parts[k]
        for s in range(1, job.outer):
            q = lax.rem(job.o + s, job.outer)

            @pl.when(wanted(job.mode, job.o, q))
            def _():
                up(job, group, far, s2, r2, q, job.o).wait_send()

            @pl.when(wanted(job.mode, q, job.o))
            def _():
                up(job, group, far, s2, r2, q, q).wait_recv()

        for s in range(1, job.outer):
            q = lax.rem(job.o + s, job.outer)
            part = part + jnp.where(wanted(job.mode, q, job.o), far[q], 0.0)
        outs[k][...] = part


def combine(parts, specs, collective):
    shapes = [part.shape for part in parts]
    parts = [part.reshape(-1, 128) for part in parts]
    jobs = [Job(axis, mode, inner, lax.axis_size(axis)) for axis, mode, inner in specs]
    scratch = []
    for part, job in zip(parts, jobs):
        scratch += [
            pltpu.VMEM((job.inner,) + part.shape, part.dtype),
            pltpu.VMEM((job.outer,) + part.shape, part.dtype),
            pltpu.VMEM(part.shape, part.dtype),
            pltpu.SemaphoreType.DMA((job.inner,)),
            pltpu.SemaphoreType.DMA((job.inner,)),
            pltpu.SemaphoreType.DMA((job.outer,)),
            pltpu.SemaphoreType.DMA((job.outer,)),
        ]
    results = pl.pallas_call(
        functools.partial(multi_kernel, jobs),
        out_shape=[jax.ShapeDtypeStruct(part.shape, part.dtype) for part in parts],
        in_specs=[pl.BlockSpec(memory_space=pltpu.VMEM)] * len(parts),
        out_specs=[pl.BlockSpec(memory_space=pltpu.VMEM)] * len(parts),
        scratch_shapes=scratch,
        compiler_params=pltpu.CompilerParams(collective_id=collective, has_side_effects=True),
    )(*parts)
    return [result.reshape(shape) for result, shape in zip(results, shapes)]


def add_pair(earlier_part, later_part):
    return earlier_part + later_part


def hold_back(field, travel_delay, earlier_rim):
    length = field.shape[1]
    extended = jnp.concatenate([earlier_rim, field], 1)
    result = jnp.zeros_like(field)
    for lag_hours in range(1, DMAX + 1):
        window = extended[:, DMAX - lag_hours : DMAX - lag_hours + length]
        result = result + jnp.where((travel_delay == lag_hours)[:, None, None], window, 0.0)
    return result


def bring_forward(field, travel_delay, later_rim):
    length = field.shape[1]
    extended = jnp.concatenate([field, later_rim], 1)
    result = jnp.zeros_like(field)
    for lag_hours in range(1, DMAX + 1):
        window = extended[:, lag_hours : lag_hours + length]
        result = result + jnp.where((travel_delay == lag_hours)[:, None, None], window, 0.0)
    return result


def route_down(matrix, field):
    return jnp.einsum("ij,jtw->itw", matrix, field, precision=lax.Precision.HIGHEST)


def route_up(matrix, field):
    return jnp.einsum("ij,itw->jtw", matrix, field, precision=lax.Precision.HIGHEST)


def iterate(fields, statics, scales, suffix_sum, from_earlier, from_later):
    release, storage_dual, demand_dual, cost, inflow, demand = fields
    (
        storage_start,
        storage_low,
        storage_high,
        release_cap,
        efficiency,
        travel_delay,
        to_own,
        to_next,
    ) = statics
    scale_time, scale_sum = scales
    suffix = suffix_sum(storage_dual)
    beyond = passed_along(suffix, "river", -1)
    at_sink = route_up(to_own, suffix) + route_up(to_next, beyond)
    later_duals = bring_forward(at_sink, travel_delay, from_later(at_sink[:, :DMAX]))
    gradient = (
        cost
        + scale_time * (later_duals - suffix)
        + scale_sum * efficiency[:, None, None] * demand_dual[None]
    )
    release_new = jnp.clip(release - primal_step * gradient, 0.0, release_cap[:, None, None])
    extrapolated = 2.0 * release_new - release
    length = extrapolated.shape[1]
    delayed = hold_back(extrapolated, travel_delay, from_earlier(extrapolated[:, length - DMAX :]))
    incoming = passed_along(route_down(to_next, delayed), "river", 1)
    routed = route_down(to_own, delayed) + incoming
    local_sum = jnp.cumsum(inflow + routed - extrapolated, 1)
    partial_power = jnp.sum(scale_sum * efficiency[:, None, None] * extrapolated, 0)
    offset, supplied = combine(
        [local_sum[:, -1], partial_power], [("hours", "prefix", 8), ("river", "sum", 8)], 1
    )
    storage = storage_start[:, None, None] + scale_time * (local_sum + offset[:, None])
    lower_bound = storage_low[:, None, None]
    upper_bound = storage_high[:, None, None]
    storage_dual_new = (
        storage_dual
        + dual_step * storage
        - dual_step * jnp.clip(storage_dual / dual_step + storage, lower_bound, upper_bound)
    )
    storage_excess = storage - jnp.clip(storage, lower_bound, upper_bound)
    demand_dual_new = jnp.minimum(demand_dual + dual_step * (supplied - demand), 0.0)
    return (release_new, storage_dual_new, demand_dual_new, storage_excess)


def suffix_local(field):
    return jnp.flip(jnp.cumsum(jnp.flip(field, 1), 1), 1)


def shards(
    release,
    storage_dual,
    demand_dual,
    cost,
    inflow,
    demand,
    storage_start,
    storage_low,
    storage_high,
    release_cap,
    efficiency,
    downstream,
    travel_delay,
):
    res_dev = release.shape[0]
    scale_time = 1.0 / (release.shape[1] * lax.axis_size("hours"))
    scale_sum = 1.0 / math.sqrt(res_dev * lax.axis_size("river"))
    base_index = lax.axis_index("river") * res_dev
    target = downstream - base_index
    indices = jnp.arange(res_dev, dtype=jnp.int32)
    to_own = (target[None, :] == indices[:, None]).astype(jnp.float32)
    to_next = (target[None, :] == indices[:, None] + res_dev).astype(jnp.float32)
    statics = (
        storage_start,
        storage_low,
        storage_high,
        release_cap,
        efficiency,
        travel_delay,
        to_own,
        to_next,
    )
    scales = (scale_time, scale_sum)

    def suffix_blocks(field):
        local_sum = suffix_local(field)
        totals = local_sum[:, 0]
        (offset,) = combine([totals], [("hours", "suffix", 8)], 0)
        return local_sum + offset[:, None]

    def earlier_block(part):
        return passed_along(part, "hours", 1)

    def later_block(part):
        return passed_along(part, "hours", -1)

    fields = (release, storage_dual, demand_dual, cost, inflow, demand)
    return iterate(
        fields, statics, scales, suffix_blocks, earlier_block, later_block
    )


def solution(mesh):
    return jax.shard_map(
        shards,
        mesh=mesh,
        in_specs=(
            P("river", "hours", None),
            P("river", "hours", None),
            P("hours", None),
            P("river", "hours", None),
            P("river", "hours", None),
            P("hours", None),
            P("river"),
            P("river"),
            P("river"),
            P("river"),
            P("river"),
            P("river"),
            P("river"),
        ),
        out_specs=(
            P("river", "hours", None),
            P("river", "hours", None),
            P("hours", None),
            P("river", "hours", None),
        ),
        check_vma=False,
    )
```

```python
import functools
import math

import jax
import jax.numpy as jnp
from jax import lax
from jax.experimental import pallas as pl
from jax.experimental.pallas import tpu as pltpu
from jax.sharding import PartitionSpec as P

DMAX = 6


primal_step = 1.0
dual_step = 0.1


def passed_along(block, axis, distance):
    devices = range(lax.axis_size(axis))
    route = [(i - distance, i) for i in devices if i - distance in devices]
    return lax.ppermute(block, axis, route)


MESH = pl.DeviceIdType.MESH


def wanted(mode, src, dst):
    if mode == "prefix":
        return src < dst
    if mode == "suffix":
        return src > dst
    return src != dst


class Job:
    def __init__(self, axis, mode, inner, n):
        self.axis, self.mode, self.inner = axis, mode, inner
        self.outer = n // inner
        self.other = "river" if axis == "hours" else "hours"

    def place(self):
        me = lax.axis_index(self.axis)
        self.fixed = lax.axis_index(self.other)
        self.o = me // self.inner
        self.i = me % self.inner

    def device(self, p):
        return (self.fixed, p) if self.axis == "hours" else (p, self.fixed)

    def peers(self):
        inner, outer, o, i = self.inner, self.outer, self.o, self.i
        near = [self.device(o * inner + lax.rem(i + s, inner)) for s in range(1, inner)]
        far = [self.device(lax.rem(o + s, outer) * inner + i) for s in range(1, outer)]
        return near + far


def multi_kernel(jobs, *refs):
    count = len(jobs)
    ins, outs, rest = refs[:count], refs[count:2 * count], refs[2 * count:]
    for job in jobs:
        job.place()
    barrier = pltpu.get_barrier_semaphore()
    partners = 0
    for job in jobs:
        for dev in job.peers():
            pl.semaphore_signal(barrier, 1, device_id=dev, device_id_type=MESH)
            partners += 1
    pl.semaphore_wait(barrier, partners)

    def across(job, x_ref, near, s1, r1, p, landing):
        return pltpu.make_async_remote_copy(
            src_ref=x_ref, dst_ref=near.at[landing], send_sem=s1.at[p], recv_sem=r1.at[landing],
            device_id=job.device(job.o * job.inner + p), device_id_type=MESH)

    for k, job in enumerate(jobs):
        near, far, group, s1, r1, s2, r2 = rest[7 * k:7 * k + 7]
        for s in range(1, job.inner):
            p = lax.rem(job.i + s, job.inner)
            across(job, ins[k], near, s1, r1, p, job.i).start()
    parts = []
    for k, job in enumerate(jobs):
        near, far, group, s1, r1, s2, r2 = rest[7 * k:7 * k + 7]
        for s in range(1, job.inner):
            p = lax.rem(job.i + s, job.inner)
            across(job, ins[k], near, s1, r1, p, job.i).wait_send()
            across(job, ins[k], near, s1, r1, p, p).wait_recv()
        own = ins[k][...]
        total = own
        part = own if job.mode == "sum" else jnp.zeros_like(own)
        for s in range(1, job.inner):
            p = lax.rem(job.i + s, job.inner)
            block = near[p]
            total = total + block
            if job.mode == "sum":
                part = part + block
            else:
                part = part + jnp.where(wanted(job.mode, p, job.i), block, 0.0)
        group[...] = total
        parts.append(part)

    def up(job, group, far, s2, r2, q, landing):
        return pltpu.make_async_remote_copy(
            src_ref=group, dst_ref=far.at[landing], send_sem=s2.at[q], recv_sem=r2.at[landing],
            device_id=job.device(q * job.inner + job.i), device_id_type=MESH)

    for k, job in enumerate(jobs):
        near, far, group, s1, r1, s2, r2 = rest[7 * k:7 * k + 7]
        for s in range(1, job.outer):
            q = lax.rem(job.o + s, job.outer)

            @pl.when(wanted(job.mode, job.o, q))
            def _():
                up(job, group, far, s2, r2, q, job.o).start()

    for k, job in enumerate(jobs):
        near, far, group, s1, r1, s2, r2 = rest[7 * k:7 * k + 7]
        part = parts[k]
        for s in range(1, job.outer):
            q = lax.rem(job.o + s, job.outer)

            @pl.when(wanted(job.mode, job.o, q))
            def _():
                up(job, group, far, s2, r2, q, job.o).wait_send()

            @pl.when(wanted(job.mode, q, job.o))
            def _():
                up(job, group, far, s2, r2, q, q).wait_recv()

        for s in range(1, job.outer):
            q = lax.rem(job.o + s, job.outer)
            part = part + jnp.where(wanted(job.mode, q, job.o), far[q], 0.0)
        outs[k][...] = part


def dual_kernel(
    sloc_ref, t_ref, off_ref, off_next_ref, beyond_ref, rim_own_ref, rim_next_ref,
    near, far, group, beyond_buf, rim_src_own, rim_src_next, rim_own_buf, rim_next_buf,
    off_src, off_next_buf, s1, r1, s2, r2, sems,
):
    job = Job("hours", "suffix", 8, lax.axis_size("hours"))
    job.place()
    n_r = lax.axis_size("river")
    n_h = lax.axis_size("hours")
    r = lax.axis_index("river")
    h = lax.axis_index("hours")
    has_up, has_down = r > 0, r < n_r - 1
    has_before, has_after = h > 0, h < n_h - 1

    barrier = pltpu.get_barrier_semaphore()
    for dev in job.peers():
        pl.semaphore_signal(barrier, 1, device_id=dev, device_id_type=MESH)
    for flag, dev in ((has_up, (r - 1, h)), (has_down, (r + 1, h)), (has_before, (r, h - 1)), (has_after, (r, h + 1))):

        @pl.when(flag)
        def _():
            pl.semaphore_signal(barrier, 1, device_id=dev, device_id_type=MESH)

    extra = sum(jnp.where(flag, 1, 0) for flag in (has_up, has_down, has_before, has_after))
    pl.semaphore_wait(barrier, job.inner + job.outer - 2 + extra)

    def link(src, dst, k, dev):
        return pltpu.make_async_remote_copy(
            src_ref=src, dst_ref=dst, send_sem=sems.at[2 * k], recv_sem=sems.at[2 * k + 1],
            device_id=dev, device_id_type=MESH)

    to_up = lambda src, dst, k: link(src, dst, k, (r - 1, h))
    to_before = lambda src, dst, k: link(src, dst, k, (r, h - 1))

    def across(p, landing):
        return pltpu.make_async_remote_copy(
            src_ref=t_ref, dst_ref=near.at[landing], send_sem=s1.at[p], recv_sem=r1.at[landing],
            device_id=job.device(job.o * job.inner + p), device_id_type=MESH)

    for s in range(1, job.inner):
        across(lax.rem(job.i + s, job.inner), job.i).start()

    @pl.when(has_up)
    def _():
        to_up(sloc_ref, beyond_buf, 0).start()

    rim_src_own[...] = sloc_ref[:, 0:DMAX, :] - sloc_ref[:, 0:1, :]

    @pl.when(has_before)
    def _():
        to_before(rim_src_own, rim_own_buf, 1).start()

    for s in range(1, job.inner):
        p = lax.rem(job.i + s, job.inner)
        across(p, job.i).wait_send()
        across(p, p).wait_recv()
    own = t_ref[...]
    total = own
    part = jnp.zeros_like(own)
    for s in range(1, job.inner):
        p = lax.rem(job.i + s, job.inner)
        block = near[p]
        total = total + block
        part = part + jnp.where(p > job.i, block, 0.0)
    group[...] = total

    def up(q, landing):
        return pltpu.make_async_remote_copy(
            src_ref=group, dst_ref=far.at[landing], send_sem=s2.at[q], recv_sem=r2.at[landing],
            device_id=job.device(q * job.inner + job.i), device_id_type=MESH)

    for s in range(1, job.outer):
        q = lax.rem(job.o + s, job.outer)

        @pl.when(job.o > q)
        def _():
            up(q, job.o).start()

    @pl.when(has_down)
    def _():
        to_up(sloc_ref, beyond_buf, 0).wait_recv()
        rim_src_next[...] = beyond_buf[:, 0:DMAX, :] - beyond_buf[:, 0:1, :]

    @pl.when(jnp.logical_and(has_down, has_before))
    def _():
        to_before(rim_src_next, rim_next_buf, 2).start()

    for s in range(1, job.outer):
        q = lax.rem(job.o + s, job.outer)

        @pl.when(job.o > q)
        def _():
            up(q, job.o).wait_send()

        @pl.when(q > job.o)
        def _():
            up(q, q).wait_recv()

    for s in range(1, job.outer):
        q = lax.rem(job.o + s, job.outer)
        part = part + jnp.where(q > job.o, far[q], 0.0)
    off_src[...] = part
    off_ref[...] = part

    @pl.when(has_up)
    def _():
        to_up(off_src, off_next_buf, 3).start()

    @pl.when(has_up)
    def _():
        to_up(sloc_ref, beyond_buf, 0).wait_send()
        to_up(off_src, off_next_buf, 3).wait_send()

    @pl.when(has_before)
    def _():
        to_before(rim_src_own, rim_own_buf, 1).wait_send()

    @pl.when(jnp.logical_and(has_down, has_before))
    def _():
        to_before(rim_src_next, rim_next_buf, 2).wait_send()

    @pl.when(has_after)
    def _():
        to_before(rim_src_own, rim_own_buf, 1).wait_recv()
        rim_own_ref[...] = rim_own_buf[...]

    @pl.when(jnp.logical_not(has_after))
    def _():
        rim_own_ref[...] = jnp.zeros_like(rim_own_ref)

    @pl.when(jnp.logical_and(has_down, has_after))
    def _():
        to_before(rim_src_next, rim_next_buf, 2).wait_recv()
        rim_next_ref[...] = rim_next_buf[...]

    @pl.when(jnp.logical_not(jnp.logical_and(has_down, has_after)))
    def _():
        rim_next_ref[...] = jnp.zeros_like(rim_next_ref)

    @pl.when(has_down)
    def _():
        to_up(off_src, off_next_buf, 3).wait_recv()
        off_next_ref[...] = off_next_buf[...]
        beyond_ref[...] = beyond_buf[...]

    @pl.when(jnp.logical_not(has_down))
    def _():
        off_next_ref[...] = jnp.zeros_like(off_next_ref)
        beyond_ref[...] = jnp.zeros_like(beyond_ref)


def dual_exchange(sloc):
    res, length, width = sloc.shape
    t = sloc[:, 0].reshape(-1, 128)
    inner = 8
    outer = lax.axis_size("hours") // inner
    rim = (res, DMAX, width)
    vmem = pl.BlockSpec(memory_space=pltpu.VMEM)
    off, off_next, beyond, rim_own, rim_next = pl.pallas_call(
        dual_kernel,
        out_shape=[
            jax.ShapeDtypeStruct(t.shape, t.dtype),
            jax.ShapeDtypeStruct(t.shape, t.dtype),
            jax.ShapeDtypeStruct(sloc.shape, sloc.dtype),
            jax.ShapeDtypeStruct(rim, sloc.dtype),
            jax.ShapeDtypeStruct(rim, sloc.dtype),
        ],
        in_specs=[vmem, vmem],
        out_specs=[vmem] * 5,
        scratch_shapes=[
            pltpu.VMEM((inner,) + t.shape, t.dtype),
            pltpu.VMEM((outer,) + t.shape, t.dtype),
            pltpu.VMEM(t.shape, t.dtype),
            pltpu.VMEM(sloc.shape, sloc.dtype),
            pltpu.VMEM(rim, sloc.dtype),
            pltpu.VMEM(rim, sloc.dtype),
            pltpu.VMEM(rim, sloc.dtype),
            pltpu.VMEM(rim, sloc.dtype),
            pltpu.VMEM(t.shape, t.dtype),
            pltpu.VMEM(t.shape, t.dtype),
            pltpu.SemaphoreType.DMA((inner,)),
            pltpu.SemaphoreType.DMA((inner,)),
            pltpu.SemaphoreType.DMA((outer,)),
            pltpu.SemaphoreType.DMA((outer,)),
            pltpu.SemaphoreType.DMA((8,)),
        ],
        compiler_params=pltpu.CompilerParams(collective_id=0, has_side_effects=True, vmem_limit_bytes=48 * 1024 * 1024),
    )(sloc, t)
    return off.reshape(res, width), off_next.reshape(res, width), beyond, rim_own, rim_next


def combine(parts, specs, collective):
    shapes = [part.shape for part in parts]
    parts = [part.reshape(-1, 128) for part in parts]
    jobs = [Job(axis, mode, inner, lax.axis_size(axis)) for axis, mode, inner in specs]
    scratch = []
    for part, job in zip(parts, jobs):
        scratch += [
            pltpu.VMEM((job.inner,) + part.shape, part.dtype),
            pltpu.VMEM((job.outer,) + part.shape, part.dtype),
            pltpu.VMEM(part.shape, part.dtype),
            pltpu.SemaphoreType.DMA((job.inner,)),
            pltpu.SemaphoreType.DMA((job.inner,)),
            pltpu.SemaphoreType.DMA((job.outer,)),
            pltpu.SemaphoreType.DMA((job.outer,)),
        ]
    results = pl.pallas_call(
        functools.partial(multi_kernel, jobs),
        out_shape=[jax.ShapeDtypeStruct(part.shape, part.dtype) for part in parts],
        in_specs=[pl.BlockSpec(memory_space=pltpu.VMEM)] * len(parts),
        out_specs=[pl.BlockSpec(memory_space=pltpu.VMEM)] * len(parts),
        scratch_shapes=scratch,
        compiler_params=pltpu.CompilerParams(collective_id=collective, has_side_effects=True),
    )(*parts)
    return [result.reshape(shape) for result, shape in zip(results, shapes)]


def add_pair(earlier_part, later_part):
    return earlier_part + later_part


def hold_back(field, travel_delay, earlier_rim):
    length = field.shape[1]
    extended = jnp.concatenate([earlier_rim, field], 1)
    result = jnp.zeros_like(field)
    for lag_hours in range(1, DMAX + 1):
        window = extended[:, DMAX - lag_hours : DMAX - lag_hours + length]
        result = result + jnp.where((travel_delay == lag_hours)[:, None, None], window, 0.0)
    return result


def bring_forward(field, travel_delay, later_rim):
    length = field.shape[1]
    extended = jnp.concatenate([field, later_rim], 1)
    result = jnp.zeros_like(field)
    for lag_hours in range(1, DMAX + 1):
        window = extended[:, lag_hours : lag_hours + length]
        result = result + jnp.where((travel_delay == lag_hours)[:, None, None], window, 0.0)
    return result


def route_down(matrix, field):
    return jnp.einsum("ij,jtw->itw", matrix, field, precision=lax.Precision.HIGHEST)


def route_up(matrix, field):
    return jnp.einsum("ij,itw->jtw", matrix, field, precision=lax.Precision.HIGHEST)


def iterate(fields, statics, scales, suffix_sum, from_earlier, from_later):
    release, storage_dual, demand_dual, cost, inflow, demand = fields
    (
        storage_start,
        storage_low,
        storage_high,
        release_cap,
        efficiency,
        travel_delay,
        to_own,
        to_next,
    ) = statics
    scale_time, scale_sum = scales
    local = suffix_local(storage_dual)
    off, off_next, beyond, rim_own, rim_next = dual_exchange(local)
    suffix = local + off[:, None]
    at_sink = route_up(to_own, suffix) + route_up(to_next, beyond + off_next[:, None])
    last = lax.axis_index("hours") == lax.axis_size("hours") - 1
    rim_sink = route_up(to_own, rim_own + off[:, None]) + route_up(to_next, rim_next + off_next[:, None])
    later_duals = bring_forward(at_sink, travel_delay, jnp.where(last, 0.0, rim_sink))
    gradient = (
        cost
        + scale_time * (later_duals - suffix)
        + scale_sum * efficiency[:, None, None] * demand_dual[None]
    )
    release_new = jnp.clip(release - primal_step * gradient, 0.0, release_cap[:, None, None])
    extrapolated = 2.0 * release_new - release
    length = extrapolated.shape[1]
    delayed = hold_back(extrapolated, travel_delay, from_earlier(extrapolated[:, length - DMAX :]))
    incoming = passed_along(route_down(to_next, delayed), "river", 1)
    routed = route_down(to_own, delayed) + incoming
    local_sum = jnp.cumsum(inflow + routed - extrapolated, 1)
    partial_power = jnp.sum(scale_sum * efficiency[:, None, None] * extrapolated, 0)
    offset, supplied = combine(
        [local_sum[:, -1], partial_power], [("hours", "prefix", 8), ("river", "sum", 8)], 1
    )
    storage = storage_start[:, None, None] + scale_time * (local_sum + offset[:, None])
    lower_bound = storage_low[:, None, None]
    upper_bound = storage_high[:, None, None]
    storage_dual_new = (
        storage_dual
        + dual_step * storage
        - dual_step * jnp.clip(storage_dual / dual_step + storage, lower_bound, upper_bound)
    )
    storage_excess = storage - jnp.clip(storage, lower_bound, upper_bound)
    demand_dual_new = jnp.minimum(demand_dual + dual_step * (supplied - demand), 0.0)
    return (release_new, storage_dual_new, demand_dual_new, storage_excess)


def suffix_local(field):
    return jnp.flip(jnp.cumsum(jnp.flip(field, 1), 1), 1)


def shards(
    release,
    storage_dual,
    demand_dual,
    cost,
    inflow,
    demand,
    storage_start,
    storage_low,
    storage_high,
    release_cap,
    efficiency,
    downstream,
    travel_delay,
):
    res_dev = release.shape[0]
    scale_time = 1.0 / (release.shape[1] * lax.axis_size("hours"))
    scale_sum = 1.0 / math.sqrt(res_dev * lax.axis_size("river"))
    base_index = lax.axis_index("river") * res_dev
    target = downstream - base_index
    indices = jnp.arange(res_dev, dtype=jnp.int32)
    to_own = (target[None, :] == indices[:, None]).astype(jnp.float32)
    to_next = (target[None, :] == indices[:, None] + res_dev).astype(jnp.float32)
    statics = (
        storage_start,
        storage_low,
        storage_high,
        release_cap,
        efficiency,
        travel_delay,
        to_own,
        to_next,
    )
    scales = (scale_time, scale_sum)

    def suffix_blocks(field):
        local_sum = suffix_local(field)
        totals = local_sum[:, 0]
        (offset,) = combine([totals], [("hours", "suffix", 8)], 0)
        return local_sum + offset[:, None]

    def earlier_block(part):
        return passed_along(part, "hours", 1)

    def later_block(part):
        return passed_along(part, "hours", -1)

    fields = (release, storage_dual, demand_dual, cost, inflow, demand)
    return iterate(
        fields, statics, scales, suffix_blocks, earlier_block, later_block
    )


def solution(mesh):
    return jax.shard_map(
        shards,
        mesh=mesh,
        in_specs=(
            P("river", "hours", None),
            P("river", "hours", None),
            P("hours", None),
            P("river", "hours", None),
            P("river", "hours", None),
            P("hours", None),
            P("river"),
            P("river"),
            P("river"),
            P("river"),
            P("river"),
            P("river"),
            P("river"),
        ),
        out_specs=(
            P("river", "hours", None),
            P("river", "hours", None),
            P("hours", None),
            P("river", "hours", None),
        ),
        check_vma=False,
    )
```

```python
import functools
import math

import jax
import jax.numpy as jnp
from jax import lax
from jax.experimental import pallas as pl
from jax.experimental.pallas import tpu as pltpu
from jax.sharding import PartitionSpec as P

DMAX = 6


primal_step = 1.0
dual_step = 0.1


def passed_along(block, axis, distance):
    devices = range(lax.axis_size(axis))
    route = [(i - distance, i) for i in devices if i - distance in devices]
    return lax.ppermute(block, axis, route)


MESH = pl.DeviceIdType.MESH


def wanted(mode, src, dst):
    if mode == "prefix":
        return src < dst
    if mode == "suffix":
        return src > dst
    return src != dst


class Job:
    def __init__(self, axis, mode, inner, n):
        self.axis, self.mode, self.inner = axis, mode, inner
        self.outer = n // inner
        self.other = "river" if axis == "hours" else "hours"

    def place(self):
        me = lax.axis_index(self.axis)
        self.fixed = lax.axis_index(self.other)
        self.o = me // self.inner
        self.i = me % self.inner

    def device(self, p):
        return (self.fixed, p) if self.axis == "hours" else (p, self.fixed)

    def peers(self):
        inner, outer, o, i = self.inner, self.outer, self.o, self.i
        near = [self.device(o * inner + lax.rem(i + s, inner)) for s in range(1, inner)]
        far = [self.device(lax.rem(o + s, outer) * inner + i) for s in range(1, outer)]
        return near + far


def multi_kernel(jobs, *refs):
    count = len(jobs)
    ins, outs, rest = refs[:count], refs[count:2 * count], refs[2 * count:]
    for job in jobs:
        job.place()
    barrier = pltpu.get_barrier_semaphore()
    partners = 0
    for job in jobs:
        for dev in job.peers():
            pl.semaphore_signal(barrier, 1, device_id=dev, device_id_type=MESH)
            partners += 1
    pl.semaphore_wait(barrier, partners)

    def across(job, x_ref, near, s1, r1, p, landing):
        return pltpu.make_async_remote_copy(
            src_ref=x_ref, dst_ref=near.at[landing], send_sem=s1.at[p], recv_sem=r1.at[landing],
            device_id=job.device(job.o * job.inner + p), device_id_type=MESH)

    for k, job in enumerate(jobs):
        near, far, group, s1, r1, s2, r2 = rest[7 * k:7 * k + 7]
        for s in range(1, job.inner):
            p = lax.rem(job.i + s, job.inner)
            across(job, ins[k], near, s1, r1, p, job.i).start()
    parts = []
    for k, job in enumerate(jobs):
        near, far, group, s1, r1, s2, r2 = rest[7 * k:7 * k + 7]
        for s in range(1, job.inner):
            p = lax.rem(job.i + s, job.inner)
            across(job, ins[k], near, s1, r1, p, job.i).wait_send()
            across(job, ins[k], near, s1, r1, p, p).wait_recv()
        own = ins[k][...]
        total = own
        part = own if job.mode == "sum" else jnp.zeros_like(own)
        for s in range(1, job.inner):
            p = lax.rem(job.i + s, job.inner)
            block = near[p]
            total = total + block
            if job.mode == "sum":
                part = part + block
            else:
                part = part + jnp.where(wanted(job.mode, p, job.i), block, 0.0)
        group[...] = total
        parts.append(part)

    def up(job, group, far, s2, r2, q, landing):
        return pltpu.make_async_remote_copy(
            src_ref=group, dst_ref=far.at[landing], send_sem=s2.at[q], recv_sem=r2.at[landing],
            device_id=job.device(q * job.inner + job.i), device_id_type=MESH)

    for k, job in enumerate(jobs):
        near, far, group, s1, r1, s2, r2 = rest[7 * k:7 * k + 7]
        for s in range(1, job.outer):
            q = lax.rem(job.o + s, job.outer)

            @pl.when(wanted(job.mode, job.o, q))
            def _():
                up(job, group, far, s2, r2, q, job.o).start()

    for k, job in enumerate(jobs):
        near, far, group, s1, r1, s2, r2 = rest[7 * k:7 * k + 7]
        part = parts[k]
        for s in range(1, job.outer):
            q = lax.rem(job.o + s, job.outer)

            @pl.when(wanted(job.mode, job.o, q))
            def _():
                up(job, group, far, s2, r2, q, job.o).wait_send()

            @pl.when(wanted(job.mode, q, job.o))
            def _():
                up(job, group, far, s2, r2, q, q).wait_recv()

        for s in range(1, job.outer):
            q = lax.rem(job.o + s, job.outer)
            part = part + jnp.where(wanted(job.mode, q, job.o), far[q], 0.0)
        outs[k][...] = part


def dual_kernel(
    sloc_ref, t_ref, off_ref, off_next_ref, beyond_ref, rim_own_ref, rim_next_ref,
    near, far, group, beyond_buf, rim_src_own, rim_src_next, rim_own_buf, rim_next_buf,
    off_src, off_next_buf, s1, r1, s2, r2, sems,
):
    job = Job("hours", "suffix", 8, lax.axis_size("hours"))
    job.place()
    n_r = lax.axis_size("river")
    n_h = lax.axis_size("hours")
    r = lax.axis_index("river")
    h = lax.axis_index("hours")
    has_up, has_down = r > 0, r < n_r - 1
    has_before, has_after = h > 0, h < n_h - 1

    barrier = pltpu.get_barrier_semaphore()
    for dev in job.peers():
        pl.semaphore_signal(barrier, 1, device_id=dev, device_id_type=MESH)
    for flag, dev in ((has_up, (r - 1, h)), (has_down, (r + 1, h)), (has_before, (r, h - 1)), (has_after, (r, h + 1))):

        @pl.when(flag)
        def _():
            pl.semaphore_signal(barrier, 1, device_id=dev, device_id_type=MESH)

    extra = sum(jnp.where(flag, 1, 0) for flag in (has_up, has_down, has_before, has_after))
    pl.semaphore_wait(barrier, job.inner + job.outer - 2 + extra)

    def link(src, dst, k, dev):
        return pltpu.make_async_remote_copy(
            src_ref=src, dst_ref=dst, send_sem=sems.at[2 * k], recv_sem=sems.at[2 * k + 1],
            device_id=dev, device_id_type=MESH)

    to_up = lambda src, dst, k: link(src, dst, k, (r - 1, h))
    to_before = lambda src, dst, k: link(src, dst, k, (r, h - 1))

    def across(p, landing):
        return pltpu.make_async_remote_copy(
            src_ref=t_ref, dst_ref=near.at[landing], send_sem=s1.at[p], recv_sem=r1.at[landing],
            device_id=job.device(job.o * job.inner + p), device_id_type=MESH)

    for s in range(1, job.inner):
        across(lax.rem(job.i + s, job.inner), job.i).start()

    @pl.when(has_up)
    def _():
        to_up(sloc_ref, beyond_buf, 0).start()

    rim_src_own[...] = sloc_ref[:, 0:DMAX, :] - sloc_ref[:, 0:1, :]

    @pl.when(has_before)
    def _():
        to_before(rim_src_own, rim_own_buf, 1).start()

    for s in range(1, job.inner):
        p = lax.rem(job.i + s, job.inner)
        across(p, job.i).wait_send()
        across(p, p).wait_recv()
    own = t_ref[...]
    total = own
    part = jnp.zeros_like(own)
    for s in range(1, job.inner):
        p = lax.rem(job.i + s, job.inner)
        block = near[p]
        total = total + block
        part = part + jnp.where(p > job.i, block, 0.0)
    group[...] = total

    def up(q, landing):
        return pltpu.make_async_remote_copy(
            src_ref=group, dst_ref=far.at[landing], send_sem=s2.at[q], recv_sem=r2.at[landing],
            device_id=job.device(q * job.inner + job.i), device_id_type=MESH)

    for s in range(1, job.outer):
        q = lax.rem(job.o + s, job.outer)

        @pl.when(job.o > q)
        def _():
            up(q, job.o).start()

    @pl.when(has_down)
    def _():
        to_up(sloc_ref, beyond_buf, 0).wait_recv()
        rim_src_next[...] = beyond_buf[:, 0:DMAX, :] - beyond_buf[:, 0:1, :]

    @pl.when(jnp.logical_and(has_down, has_before))
    def _():
        to_before(rim_src_next, rim_next_buf, 2).start()

    for s in range(1, job.outer):
        q = lax.rem(job.o + s, job.outer)

        @pl.when(job.o > q)
        def _():
            up(q, job.o).wait_send()

        @pl.when(q > job.o)
        def _():
            up(q, q).wait_recv()

    for s in range(1, job.outer):
        q = lax.rem(job.o + s, job.outer)
        part = part + jnp.where(q > job.o, far[q], 0.0)
    off_src[...] = part
    off_ref[...] = part

    @pl.when(has_up)
    def _():
        to_up(off_src, off_next_buf, 3).start()

    @pl.when(has_up)
    def _():
        to_up(sloc_ref, beyond_buf, 0).wait_send()
        to_up(off_src, off_next_buf, 3).wait_send()

    @pl.when(has_before)
    def _():
        to_before(rim_src_own, rim_own_buf, 1).wait_send()

    @pl.when(jnp.logical_and(has_down, has_before))
    def _():
        to_before(rim_src_next, rim_next_buf, 2).wait_send()

    @pl.when(has_after)
    def _():
        to_before(rim_src_own, rim_own_buf, 1).wait_recv()
        rim_own_ref[...] = rim_own_buf[...]

    @pl.when(jnp.logical_not(has_after))
    def _():
        rim_own_ref[...] = jnp.zeros_like(rim_own_ref)

    @pl.when(jnp.logical_and(has_down, has_after))
    def _():
        to_before(rim_src_next, rim_next_buf, 2).wait_recv()
        rim_next_ref[...] = rim_next_buf[...]

    @pl.when(jnp.logical_not(jnp.logical_and(has_down, has_after)))
    def _():
        rim_next_ref[...] = jnp.zeros_like(rim_next_ref)

    @pl.when(has_down)
    def _():
        to_up(off_src, off_next_buf, 3).wait_recv()
        off_next_ref[...] = off_next_buf[...]
        beyond_ref[...] = beyond_buf[...]

    @pl.when(jnp.logical_not(has_down))
    def _():
        off_next_ref[...] = jnp.zeros_like(off_next_ref)
        beyond_ref[...] = jnp.zeros_like(beyond_ref)


def dual_exchange(sloc):
    res, length, width = sloc.shape
    t = sloc[:, 0].reshape(-1, 128)
    inner = 8
    outer = lax.axis_size("hours") // inner
    rim = (res, DMAX, width)
    vmem = pl.BlockSpec(memory_space=pltpu.VMEM)
    off, off_next, beyond, rim_own, rim_next = pl.pallas_call(
        dual_kernel,
        out_shape=[
            jax.ShapeDtypeStruct(t.shape, t.dtype),
            jax.ShapeDtypeStruct(t.shape, t.dtype),
            jax.ShapeDtypeStruct(sloc.shape, sloc.dtype),
            jax.ShapeDtypeStruct(rim, sloc.dtype),
            jax.ShapeDtypeStruct(rim, sloc.dtype),
        ],
        in_specs=[vmem, vmem],
        out_specs=[vmem] * 5,
        scratch_shapes=[
            pltpu.VMEM((inner,) + t.shape, t.dtype),
            pltpu.VMEM((outer,) + t.shape, t.dtype),
            pltpu.VMEM(t.shape, t.dtype),
            pltpu.VMEM(sloc.shape, sloc.dtype),
            pltpu.VMEM(rim, sloc.dtype),
            pltpu.VMEM(rim, sloc.dtype),
            pltpu.VMEM(rim, sloc.dtype),
            pltpu.VMEM(rim, sloc.dtype),
            pltpu.VMEM(t.shape, t.dtype),
            pltpu.VMEM(t.shape, t.dtype),
            pltpu.SemaphoreType.DMA((inner,)),
            pltpu.SemaphoreType.DMA((inner,)),
            pltpu.SemaphoreType.DMA((outer,)),
            pltpu.SemaphoreType.DMA((outer,)),
            pltpu.SemaphoreType.DMA((8,)),
        ],
        compiler_params=pltpu.CompilerParams(collective_id=0, has_side_effects=True, vmem_limit_bytes=48 * 1024 * 1024),
    )(sloc, t)
    return off.reshape(res, width), off_next.reshape(res, width), beyond, rim_own, rim_next


def flow_kernel(
    main_ref, rim_own_ref, rim_next_ref, ab_ref, power_ref,
    incoming_ref, rim_own_in_ref, rim_next_in_ref, pa_ref, pb_up_ref, supplied_ref,
    near_h, far_h, group_h, near_r, far_r, group_r, incoming_buf, rim_own_buf, rim_next_buf,
    pb_src, pb_buf, s1h, r1h, s2h, r2h, s1r, r1r, s2r, r2r, sems,
):
    jobs = [Job("hours", "prefix", 8, lax.axis_size("hours")), Job("river", "sum", 8, lax.axis_size("river"))]
    for job in jobs:
        job.place()
    n_r = lax.axis_size("river")
    n_h = lax.axis_size("hours")
    r = lax.axis_index("river")
    h = lax.axis_index("hours")
    has_up, has_down = r > 0, r < n_r - 1
    has_before, has_after = h > 0, h < n_h - 1
    diag_down = jnp.logical_and(has_down, has_after)
    diag_up = jnp.logical_and(has_up, has_before)

    barrier = pltpu.get_barrier_semaphore()
    fixed = 0
    for job in jobs:
        for dev in job.peers():
            pl.semaphore_signal(barrier, 1, device_id=dev, device_id_type=MESH)
            fixed += 1
    links = (
        (has_up, (r - 1, h)), (has_down, (r + 1, h)), (has_before, (r, h - 1)), (has_after, (r, h + 1)),
        (diag_down, (r + 1, h + 1)), (diag_up, (r - 1, h - 1)),
    )
    for flag, dev in links:

        @pl.when(flag)
        def _():
            pl.semaphore_signal(barrier, 1, device_id=dev, device_id_type=MESH)

    extra = sum(jnp.where(flag, 1, 0) for flag, _ in links)
    pl.semaphore_wait(barrier, fixed + extra)

    def link(src, dst, k, dev):
        return pltpu.make_async_remote_copy(
            src_ref=src, dst_ref=dst, send_sem=sems.at[2 * k], recv_sem=sems.at[2 * k + 1],
            device_id=dev, device_id_type=MESH)

    main_copy = link(main_ref, incoming_buf, 0, (r + 1, h))
    rim_own_copy = link(rim_own_ref, rim_own_buf, 1, (r, h + 1))
    rim_next_copy = link(rim_next_ref, rim_next_buf, 2, (r + 1, h + 1))
    pb_copy = link(pb_src, pb_buf, 3, (r + 1, h))

    @pl.when(has_down)
    def _():
        main_copy.start()

    @pl.when(has_after)
    def _():
        rim_own_copy.start()

    @pl.when(diag_down)
    def _():
        rim_next_copy.start()

    bufs = [(ab_ref, near_h, far_h, group_h, s1h, r1h, s2h, r2h), (power_ref, near_r, far_r, group_r, s1r, r1r, s2r, r2r)]

    def across(job, x_ref, near, s1, r1, p, landing):
        return pltpu.make_async_remote_copy(
            src_ref=x_ref, dst_ref=near.at[landing], send_sem=s1.at[p], recv_sem=r1.at[landing],
            device_id=job.device(job.o * job.inner + p), device_id_type=MESH)

    for job, (x_ref, near, far, group, s1, r1, s2, r2) in zip(jobs, bufs):
        for s in range(1, job.inner):
            across(job, x_ref, near, s1, r1, lax.rem(job.i + s, job.inner), job.i).start()
    parts = []
    for job, (x_ref, near, far, group, s1, r1, s2, r2) in zip(jobs, bufs):
        for s in range(1, job.inner):
            p = lax.rem(job.i + s, job.inner)
            across(job, x_ref, near, s1, r1, p, job.i).wait_send()
            across(job, x_ref, near, s1, r1, p, p).wait_recv()
        own = x_ref[...]
        total = own
        part = own if job.mode == "sum" else jnp.zeros_like(own)
        for s in range(1, job.inner):
            p = lax.rem(job.i + s, job.inner)
            block = near[p]
            total = total + block
            if job.mode == "sum":
                part = part + block
            else:
                part = part + jnp.where(wanted(job.mode, p, job.i), block, 0.0)
        group[...] = total
        parts.append(part)

    def up(job, group, far, s2, r2, q, landing):
        return pltpu.make_async_remote_copy(
            src_ref=group, dst_ref=far.at[landing], send_sem=s2.at[q], recv_sem=r2.at[landing],
            device_id=job.device(q * job.inner + job.i), device_id_type=MESH)

    for job, (x_ref, near, far, group, s1, r1, s2, r2) in zip(jobs, bufs):
        for s in range(1, job.outer):
            q = lax.rem(job.o + s, job.outer)

            @pl.when(wanted(job.mode, job.o, q))
            def _():
                up(job, group, far, s2, r2, q, job.o).start()

    results = []
    for job, part, (x_ref, near, far, group, s1, r1, s2, r2) in zip(jobs, parts, bufs):
        for s in range(1, job.outer):
            q = lax.rem(job.o + s, job.outer)

            @pl.when(wanted(job.mode, job.o, q))
            def _():
                up(job, group, far, s2, r2, q, job.o).wait_send()

            @pl.when(wanted(job.mode, q, job.o))
            def _():
                up(job, group, far, s2, r2, q, q).wait_recv()

        for s in range(1, job.outer):
            q = lax.rem(job.o + s, job.outer)
            part = part + jnp.where(wanted(job.mode, q, job.o), far[q], 0.0)
        results.append(part)
    scanned, supplied = results
    half = pb_src.shape[0]
    pa_ref[...] = scanned
    supplied_ref[...] = supplied
    pb_src[...] = scanned[half:]

    @pl.when(has_down)
    def _():
        pb_copy.start()
        main_copy.wait_send()
        pb_copy.wait_send()

    @pl.when(has_after)
    def _():
        rim_own_copy.wait_send()

    @pl.when(diag_down)
    def _():
        rim_next_copy.wait_send()

    @pl.when(has_up)
    def _():
        main_copy.wait_recv()
        pb_copy.wait_recv()
        incoming_ref[...] = incoming_buf[...]
        pb_up_ref[...] = pb_buf[...]

    @pl.when(jnp.logical_not(has_up))
    def _():
        incoming_ref[...] = jnp.zeros_like(incoming_ref)
        pb_up_ref[...] = jnp.zeros_like(pb_up_ref)

    @pl.when(has_before)
    def _():
        rim_own_copy.wait_recv()
        rim_own_in_ref[...] = rim_own_buf[...]

    @pl.when(jnp.logical_not(has_before))
    def _():
        rim_own_in_ref[...] = jnp.zeros_like(rim_own_in_ref)

    @pl.when(diag_up)
    def _():
        rim_next_copy.wait_recv()
        rim_next_in_ref[...] = rim_next_buf[...]

    @pl.when(jnp.logical_not(diag_up))
    def _():
        rim_next_in_ref[...] = jnp.zeros_like(rim_next_in_ref)


def flow_exchange(main_next, rim_own, rim_next, own_totals, next_totals, power):
    res, width = own_totals.shape
    ab = jnp.concatenate([own_totals, next_totals], 0).reshape(-1, 128)
    flat_power = power.reshape(-1, 128)
    half = ab.shape[0] // 2
    inner = 8
    outer_h = lax.axis_size("hours") // inner
    outer_r = lax.axis_size("river") // inner
    vmem = pl.BlockSpec(memory_space=pltpu.VMEM)
    shape = lambda a: jax.ShapeDtypeStruct(a.shape, a.dtype)
    incoming, rim_own_in, rim_next_in, pa, pb_up, supplied = pl.pallas_call(
        flow_kernel,
        out_shape=[
            shape(main_next), shape(rim_own), shape(rim_next), shape(ab),
            jax.ShapeDtypeStruct((half, 128), ab.dtype), shape(flat_power),
        ],
        in_specs=[vmem] * 5,
        out_specs=[vmem] * 6,
        scratch_shapes=[
            pltpu.VMEM((inner,) + ab.shape, ab.dtype),
            pltpu.VMEM((outer_h,) + ab.shape, ab.dtype),
            pltpu.VMEM(ab.shape, ab.dtype),
            pltpu.VMEM((inner,) + flat_power.shape, ab.dtype),
            pltpu.VMEM((outer_r,) + flat_power.shape, ab.dtype),
            pltpu.VMEM(flat_power.shape, ab.dtype),
            pltpu.VMEM(main_next.shape, ab.dtype),
            pltpu.VMEM(rim_own.shape, ab.dtype),
            pltpu.VMEM(rim_next.shape, ab.dtype),
            pltpu.VMEM((half, 128), ab.dtype),
            pltpu.VMEM((half, 128), ab.dtype),
            pltpu.SemaphoreType.DMA((inner,)),
            pltpu.SemaphoreType.DMA((inner,)),
            pltpu.SemaphoreType.DMA((outer_h,)),
            pltpu.SemaphoreType.DMA((outer_h,)),
            pltpu.SemaphoreType.DMA((inner,)),
            pltpu.SemaphoreType.DMA((inner,)),
            pltpu.SemaphoreType.DMA((outer_r,)),
            pltpu.SemaphoreType.DMA((outer_r,)),
            pltpu.SemaphoreType.DMA((8,)),
        ],
        compiler_params=pltpu.CompilerParams(collective_id=1, has_side_effects=True, vmem_limit_bytes=48 * 1024 * 1024),
    )(main_next, rim_own, rim_next, ab, flat_power)
    offset = pa[:half].reshape(res, width) + pb_up.reshape(res, width)
    return incoming, rim_own_in, rim_next_in, offset, supplied.reshape(power.shape)


def combine(parts, specs, collective):
    shapes = [part.shape for part in parts]
    parts = [part.reshape(-1, 128) for part in parts]
    jobs = [Job(axis, mode, inner, lax.axis_size(axis)) for axis, mode, inner in specs]
    scratch = []
    for part, job in zip(parts, jobs):
        scratch += [
            pltpu.VMEM((job.inner,) + part.shape, part.dtype),
            pltpu.VMEM((job.outer,) + part.shape, part.dtype),
            pltpu.VMEM(part.shape, part.dtype),
            pltpu.SemaphoreType.DMA((job.inner,)),
            pltpu.SemaphoreType.DMA((job.inner,)),
            pltpu.SemaphoreType.DMA((job.outer,)),
            pltpu.SemaphoreType.DMA((job.outer,)),
        ]
    results = pl.pallas_call(
        functools.partial(multi_kernel, jobs),
        out_shape=[jax.ShapeDtypeStruct(part.shape, part.dtype) for part in parts],
        in_specs=[pl.BlockSpec(memory_space=pltpu.VMEM)] * len(parts),
        out_specs=[pl.BlockSpec(memory_space=pltpu.VMEM)] * len(parts),
        scratch_shapes=scratch,
        compiler_params=pltpu.CompilerParams(collective_id=collective, has_side_effects=True),
    )(*parts)
    return [result.reshape(shape) for result, shape in zip(results, shapes)]


def add_pair(earlier_part, later_part):
    return earlier_part + later_part


def hold_back(field, travel_delay, earlier_rim):
    length = field.shape[1]
    extended = jnp.concatenate([earlier_rim, field], 1)
    result = jnp.zeros_like(field)
    for lag_hours in range(1, DMAX + 1):
        window = extended[:, DMAX - lag_hours : DMAX - lag_hours + length]
        result = result + jnp.where((travel_delay == lag_hours)[:, None, None], window, 0.0)
    return result


def bring_forward(field, travel_delay, later_rim):
    length = field.shape[1]
    extended = jnp.concatenate([field, later_rim], 1)
    result = jnp.zeros_like(field)
    for lag_hours in range(1, DMAX + 1):
        window = extended[:, lag_hours : lag_hours + length]
        result = result + jnp.where((travel_delay == lag_hours)[:, None, None], window, 0.0)
    return result


def route_down(matrix, field):
    return jnp.einsum("ij,jtw->itw", matrix, field, precision=lax.Precision.HIGHEST)


def route_up(matrix, field):
    return jnp.einsum("ij,itw->jtw", matrix, field, precision=lax.Precision.HIGHEST)


def iterate(fields, statics, scales, suffix_sum, from_earlier, from_later):
    release, storage_dual, demand_dual, cost, inflow, demand = fields
    (
        storage_start,
        storage_low,
        storage_high,
        release_cap,
        efficiency,
        travel_delay,
        to_own,
        to_next,
    ) = statics
    scale_time, scale_sum = scales
    local = suffix_local(storage_dual)
    off, off_next, beyond, rim_own, rim_next = dual_exchange(local)
    suffix = local + off[:, None]
    at_sink = route_up(to_own, suffix) + route_up(to_next, beyond + off_next[:, None])
    last = lax.axis_index("hours") == lax.axis_size("hours") - 1
    rim_sink = route_up(to_own, rim_own + off[:, None]) + route_up(to_next, rim_next + off_next[:, None])
    later_duals = bring_forward(at_sink, travel_delay, jnp.where(last, 0.0, rim_sink))
    gradient = (
        cost
        + scale_time * (later_duals - suffix)
        + scale_sum * efficiency[:, None, None] * demand_dual[None]
    )
    release_new = jnp.clip(release - primal_step * gradient, 0.0, release_cap[:, None, None])
    extrapolated = 2.0 * release_new - release
    length = extrapolated.shape[1]
    tail = extrapolated[:, length - DMAX :]
    settled = hold_back(extrapolated, travel_delay, jnp.zeros_like(tail))
    rim_delayed = hold_back(jnp.zeros_like(extrapolated), travel_delay, tail)[:, :DMAX]
    main_own = route_down(to_own, settled)
    main_next = route_down(to_next, settled)
    rim_own = route_down(to_own, rim_delayed)
    rim_next = route_down(to_next, rim_delayed)
    base = inflow + main_own - extrapolated
    own_totals = jnp.sum(base, 1) + jnp.sum(rim_own, 1)
    next_totals = jnp.sum(main_next, 1) + jnp.sum(rim_next, 1)
    partial_power = jnp.sum(scale_sum * efficiency[:, None, None] * extrapolated, 0)
    incoming, rim_own_in, rim_next_in, offset, supplied = flow_exchange(
        main_next, rim_own, rim_next, own_totals, next_totals, partial_power
    )
    arrived = jnp.concatenate([rim_own_in + rim_next_in, jnp.zeros_like(base[:, DMAX:])], 1)
    local_sum = jnp.cumsum(base + incoming + arrived, 1)
    offset = offset - jnp.sum(rim_own_in, 1) - jnp.sum(rim_next_in, 1)
    storage = storage_start[:, None, None] + scale_time * (local_sum + offset[:, None])
    lower_bound = storage_low[:, None, None]
    upper_bound = storage_high[:, None, None]
    storage_dual_new = (
        storage_dual
        + dual_step * storage
        - dual_step * jnp.clip(storage_dual / dual_step + storage, lower_bound, upper_bound)
    )
    storage_excess = storage - jnp.clip(storage, lower_bound, upper_bound)
    demand_dual_new = jnp.minimum(demand_dual + dual_step * (supplied - demand), 0.0)
    return (release_new, storage_dual_new, demand_dual_new, storage_excess)


def suffix_local(field):
    return jnp.flip(jnp.cumsum(jnp.flip(field, 1), 1), 1)


def shards(
    release,
    storage_dual,
    demand_dual,
    cost,
    inflow,
    demand,
    storage_start,
    storage_low,
    storage_high,
    release_cap,
    efficiency,
    downstream,
    travel_delay,
):
    res_dev = release.shape[0]
    scale_time = 1.0 / (release.shape[1] * lax.axis_size("hours"))
    scale_sum = 1.0 / math.sqrt(res_dev * lax.axis_size("river"))
    base_index = lax.axis_index("river") * res_dev
    target = downstream - base_index
    indices = jnp.arange(res_dev, dtype=jnp.int32)
    to_own = (target[None, :] == indices[:, None]).astype(jnp.float32)
    to_next = (target[None, :] == indices[:, None] + res_dev).astype(jnp.float32)
    statics = (
        storage_start,
        storage_low,
        storage_high,
        release_cap,
        efficiency,
        travel_delay,
        to_own,
        to_next,
    )
    scales = (scale_time, scale_sum)

    def suffix_blocks(field):
        local_sum = suffix_local(field)
        totals = local_sum[:, 0]
        (offset,) = combine([totals], [("hours", "suffix", 8)], 0)
        return local_sum + offset[:, None]

    def earlier_block(part):
        return passed_along(part, "hours", 1)

    def later_block(part):
        return passed_along(part, "hours", -1)

    fields = (release, storage_dual, demand_dual, cost, inflow, demand)
    return iterate(
        fields, statics, scales, suffix_blocks, earlier_block, later_block
    )


def solution(mesh):
    return jax.shard_map(
        shards,
        mesh=mesh,
        in_specs=(
            P("river", "hours", None),
            P("river", "hours", None),
            P("hours", None),
            P("river", "hours", None),
            P("river", "hours", None),
            P("hours", None),
            P("river"),
            P("river"),
            P("river"),
            P("river"),
            P("river"),
            P("river"),
            P("river"),
        ),
        out_specs=(
            P("river", "hours", None),
            P("river", "hours", None),
            P("hours", None),
            P("river", "hours", None),
        ),
        check_vma=False,
    )
```

```python
import functools
import math

import jax
import jax.numpy as jnp
from jax import lax
from jax.experimental import pallas as pl
from jax.experimental.pallas import tpu as pltpu
from jax.sharding import PartitionSpec as P

DMAX = 6


primal_step = 1.0
dual_step = 0.1


def passed_along(block, axis, distance):
    devices = range(lax.axis_size(axis))
    route = [(i - distance, i) for i in devices if i - distance in devices]
    return lax.ppermute(block, axis, route)


MESH = pl.DeviceIdType.MESH


def wanted(mode, src, dst):
    if mode == "prefix":
        return src < dst
    if mode == "suffix":
        return src > dst
    return src != dst


class Job:
    def __init__(self, axis, mode, inner, n):
        self.axis, self.mode, self.inner = axis, mode, inner
        self.outer = n // inner
        self.other = "river" if axis == "hours" else "hours"

    def place(self):
        me = lax.axis_index(self.axis)
        self.fixed = lax.axis_index(self.other)
        self.o = me // self.inner
        self.i = me % self.inner

    def device(self, p):
        return (self.fixed, p) if self.axis == "hours" else (p, self.fixed)

    def peers(self):
        inner, outer, o, i = self.inner, self.outer, self.o, self.i
        near = [self.device(o * inner + lax.rem(i + s, inner)) for s in range(1, inner)]
        far = [self.device(lax.rem(o + s, outer) * inner + i) for s in range(1, outer)]
        return near + far


def multi_kernel(jobs, *refs):
    count = len(jobs)
    ins, outs, rest = refs[:count], refs[count:2 * count], refs[2 * count:]
    for job in jobs:
        job.place()
    barrier = pltpu.get_barrier_semaphore()
    partners = 0
    for job in jobs:
        for dev in job.peers():
            pl.semaphore_signal(barrier, 1, device_id=dev, device_id_type=MESH)
            partners += 1
    pl.semaphore_wait(barrier, partners)

    def across(job, x_ref, near, s1, r1, p, landing):
        return pltpu.make_async_remote_copy(
            src_ref=x_ref, dst_ref=near.at[landing], send_sem=s1.at[p], recv_sem=r1.at[landing],
            device_id=job.device(job.o * job.inner + p), device_id_type=MESH)

    for k, job in enumerate(jobs):
        near, far, group, s1, r1, s2, r2 = rest[7 * k:7 * k + 7]
        for s in range(1, job.inner):
            p = lax.rem(job.i + s, job.inner)
            across(job, ins[k], near, s1, r1, p, job.i).start()
    parts = []
    for k, job in enumerate(jobs):
        near, far, group, s1, r1, s2, r2 = rest[7 * k:7 * k + 7]
        for s in range(1, job.inner):
            p = lax.rem(job.i + s, job.inner)
            across(job, ins[k], near, s1, r1, p, job.i).wait_send()
            across(job, ins[k], near, s1, r1, p, p).wait_recv()
        own = ins[k][...]
        total = own
        part = own if job.mode == "sum" else jnp.zeros_like(own)
        for s in range(1, job.inner):
            p = lax.rem(job.i + s, job.inner)
            block = near[p]
            total = total + block
            if job.mode == "sum":
                part = part + block
            else:
                part = part + jnp.where(wanted(job.mode, p, job.i), block, 0.0)
        group[...] = total
        parts.append(part)

    def up(job, group, far, s2, r2, q, landing):
        return pltpu.make_async_remote_copy(
            src_ref=group, dst_ref=far.at[landing], send_sem=s2.at[q], recv_sem=r2.at[landing],
            device_id=job.device(q * job.inner + job.i), device_id_type=MESH)

    for k, job in enumerate(jobs):
        near, far, group, s1, r1, s2, r2 = rest[7 * k:7 * k + 7]
        for s in range(1, job.outer):
            q = lax.rem(job.o + s, job.outer)

            @pl.when(wanted(job.mode, job.o, q))
            def _():
                up(job, group, far, s2, r2, q, job.o).start()

    for k, job in enumerate(jobs):
        near, far, group, s1, r1, s2, r2 = rest[7 * k:7 * k + 7]
        part = parts[k]
        for s in range(1, job.outer):
            q = lax.rem(job.o + s, job.outer)

            @pl.when(wanted(job.mode, job.o, q))
            def _():
                up(job, group, far, s2, r2, q, job.o).wait_send()

            @pl.when(wanted(job.mode, q, job.o))
            def _():
                up(job, group, far, s2, r2, q, q).wait_recv()

        for s in range(1, job.outer):
            q = lax.rem(job.o + s, job.outer)
            part = part + jnp.where(wanted(job.mode, q, job.o), far[q], 0.0)
        outs[k][...] = part


def dual_kernel(
    sloc_ref, t_ref, off_ref, off_next_ref, beyond_ref, rim_own_ref, rim_next_ref,
    near, far, group, beyond_buf, rim_src_own, rim_src_next, rim_own_buf, rim_next_buf,
    off_src, off_next_buf, s1, r1, s2, r2, sems,
):
    job = Job("hours", "suffix", 8, lax.axis_size("hours"))
    job.place()
    n_r = lax.axis_size("river")
    n_h = lax.axis_size("hours")
    r = lax.axis_index("river")
    h = lax.axis_index("hours")
    has_up, has_down = r > 0, r < n_r - 1
    has_before, has_after = h > 0, h < n_h - 1

    barrier = pltpu.get_barrier_semaphore()
    for dev in job.peers():
        pl.semaphore_signal(barrier, 1, device_id=dev, device_id_type=MESH)
    for flag, dev in ((has_up, (r - 1, h)), (has_down, (r + 1, h)), (has_before, (r, h - 1)), (has_after, (r, h + 1))):

        @pl.when(flag)
        def _():
            pl.semaphore_signal(barrier, 1, device_id=dev, device_id_type=MESH)

    extra = sum(jnp.where(flag, 1, 0) for flag in (has_up, has_down, has_before, has_after))
    pl.semaphore_wait(barrier, job.inner + job.outer - 2 + extra)

    def link(src, dst, k, dev):
        return pltpu.make_async_remote_copy(
            src_ref=src, dst_ref=dst, send_sem=sems.at[2 * k], recv_sem=sems.at[2 * k + 1],
            device_id=dev, device_id_type=MESH)

    to_up = lambda src, dst, k: link(src, dst, k, (r - 1, h))
    to_before = lambda src, dst, k: link(src, dst, k, (r, h - 1))

    def across(p, landing):
        return pltpu.make_async_remote_copy(
            src_ref=t_ref, dst_ref=near.at[landing], send_sem=s1.at[p], recv_sem=r1.at[landing],
            device_id=job.device(job.o * job.inner + p), device_id_type=MESH)

    for s in range(1, job.inner):
        across(lax.rem(job.i + s, job.inner), job.i).start()

    @pl.when(has_up)
    def _():
        to_up(sloc_ref, beyond_buf, 0).start()

    rim_src_own[...] = sloc_ref[:, 0:DMAX, :] - sloc_ref[:, 0:1, :]

    @pl.when(has_before)
    def _():
        to_before(rim_src_own, rim_own_buf, 1).start()

    for s in range(1, job.inner):
        p = lax.rem(job.i + s, job.inner)
        across(p, job.i).wait_send()
        across(p, p).wait_recv()
    own = t_ref[...]
    total = own
    part = jnp.zeros_like(own)
    for s in range(1, job.inner):
        p = lax.rem(job.i + s, job.inner)
        block = near[p]
        total = total + block
        part = part + jnp.where(p > job.i, block, 0.0)
    group[...] = total

    def up(q, landing):
        return pltpu.make_async_remote_copy(
            src_ref=group, dst_ref=far.at[landing], send_sem=s2.at[q], recv_sem=r2.at[landing],
            device_id=job.device(q * job.inner + job.i), device_id_type=MESH)

    for s in range(1, job.outer):
        q = lax.rem(job.o + s, job.outer)

        @pl.when(job.o > q)
        def _():
            up(q, job.o).start()

    @pl.when(has_down)
    def _():
        to_up(sloc_ref, beyond_buf, 0).wait_recv()
        rim_src_next[...] = beyond_buf[:, 0:DMAX, :] - beyond_buf[:, 0:1, :]

    @pl.when(jnp.logical_and(has_down, has_before))
    def _():
        to_before(rim_src_next, rim_next_buf, 2).start()

    for s in range(1, job.outer):
        q = lax.rem(job.o + s, job.outer)

        @pl.when(job.o > q)
        def _():
            up(q, job.o).wait_send()

        @pl.when(q > job.o)
        def _():
            up(q, q).wait_recv()

    for s in range(1, job.outer):
        q = lax.rem(job.o + s, job.outer)
        part = part + jnp.where(q > job.o, far[q], 0.0)
    off_src[...] = part
    off_ref[...] = part

    @pl.when(has_up)
    def _():
        to_up(off_src, off_next_buf, 3).start()

    @pl.when(has_up)
    def _():
        to_up(sloc_ref, beyond_buf, 0).wait_send()
        to_up(off_src, off_next_buf, 3).wait_send()

    @pl.when(has_before)
    def _():
        to_before(rim_src_own, rim_own_buf, 1).wait_send()

    @pl.when(jnp.logical_and(has_down, has_before))
    def _():
        to_before(rim_src_next, rim_next_buf, 2).wait_send()

    @pl.when(has_after)
    def _():
        to_before(rim_src_own, rim_own_buf, 1).wait_recv()
        rim_own_ref[...] = rim_own_buf[...]

    @pl.when(jnp.logical_not(has_after))
    def _():
        rim_own_ref[...] = jnp.zeros_like(rim_own_ref)

    @pl.when(jnp.logical_and(has_down, has_after))
    def _():
        to_before(rim_src_next, rim_next_buf, 2).wait_recv()
        rim_next_ref[...] = rim_next_buf[...]

    @pl.when(jnp.logical_not(jnp.logical_and(has_down, has_after)))
    def _():
        rim_next_ref[...] = jnp.zeros_like(rim_next_ref)

    @pl.when(has_down)
    def _():
        to_up(off_src, off_next_buf, 3).wait_recv()
        off_next_ref[...] = off_next_buf[...]
        beyond_ref[...] = beyond_buf[...]

    @pl.when(jnp.logical_not(has_down))
    def _():
        off_next_ref[...] = jnp.zeros_like(off_next_ref)
        beyond_ref[...] = jnp.zeros_like(beyond_ref)


def dual_exchange(sloc):
    res, length, width = sloc.shape
    t = sloc[:, 0].reshape(-1, 128)
    inner = 8
    outer = lax.axis_size("hours") // inner
    rim = (res, DMAX, width)
    vmem = pl.BlockSpec(memory_space=pltpu.VMEM)
    off, off_next, beyond, rim_own, rim_next = pl.pallas_call(
        dual_kernel,
        out_shape=[
            jax.ShapeDtypeStruct(t.shape, t.dtype),
            jax.ShapeDtypeStruct(t.shape, t.dtype),
            jax.ShapeDtypeStruct(sloc.shape, sloc.dtype),
            jax.ShapeDtypeStruct(rim, sloc.dtype),
            jax.ShapeDtypeStruct(rim, sloc.dtype),
        ],
        in_specs=[vmem, vmem],
        out_specs=[vmem] * 5,
        scratch_shapes=[
            pltpu.VMEM((inner,) + t.shape, t.dtype),
            pltpu.VMEM((outer,) + t.shape, t.dtype),
            pltpu.VMEM(t.shape, t.dtype),
            pltpu.VMEM(sloc.shape, sloc.dtype),
            pltpu.VMEM(rim, sloc.dtype),
            pltpu.VMEM(rim, sloc.dtype),
            pltpu.VMEM(rim, sloc.dtype),
            pltpu.VMEM(rim, sloc.dtype),
            pltpu.VMEM(t.shape, t.dtype),
            pltpu.VMEM(t.shape, t.dtype),
            pltpu.SemaphoreType.DMA((inner,)),
            pltpu.SemaphoreType.DMA((inner,)),
            pltpu.SemaphoreType.DMA((outer,)),
            pltpu.SemaphoreType.DMA((outer,)),
            pltpu.SemaphoreType.DMA((8,)),
        ],
        compiler_params=pltpu.CompilerParams(collective_id=0, has_side_effects=True, vmem_limit_bytes=48 * 1024 * 1024),
    )(sloc, t)
    return off.reshape(res, width), off_next.reshape(res, width), beyond, rim_own, rim_next


def flow_kernel(
    main_ref, rim_own_ref, rim_next_ref, a_ref, b_ref, power_ref,
    incoming_ref, rim_own_in_ref, rim_next_in_ref, pa_ref, supplied_ref,
    near_h, far_h, group_h, near_r, far_r, group_r, incoming_buf, rim_own_buf, rim_next_buf,
    a_src, b_buf, s1h, r1h, s2h, r2h, s1r, r1r, s2r, r2r, sems,
):
    jobs = [Job("hours", "prefix", 8, lax.axis_size("hours")), Job("river", "sum", 8, lax.axis_size("river"))]
    for job in jobs:
        job.place()
    n_r = lax.axis_size("river")
    n_h = lax.axis_size("hours")
    r = lax.axis_index("river")
    h = lax.axis_index("hours")
    has_up, has_down = r > 0, r < n_r - 1
    has_before, has_after = h > 0, h < n_h - 1
    diag_down = jnp.logical_and(has_down, has_after)
    diag_up = jnp.logical_and(has_up, has_before)

    barrier = pltpu.get_barrier_semaphore()
    fixed = 0
    for job in jobs:
        for dev in job.peers():
            pl.semaphore_signal(barrier, 1, device_id=dev, device_id_type=MESH)
            fixed += 1
    links = (
        (has_up, (r - 1, h)), (has_down, (r + 1, h)), (has_before, (r, h - 1)), (has_after, (r, h + 1)),
        (diag_down, (r + 1, h + 1)), (diag_up, (r - 1, h - 1)),
    )
    for flag, dev in links:

        @pl.when(flag)
        def _():
            pl.semaphore_signal(barrier, 1, device_id=dev, device_id_type=MESH)

    extra = sum(jnp.where(flag, 1, 0) for flag, _ in links)
    pl.semaphore_wait(barrier, fixed + extra)

    def link(src, dst, k, dev):
        return pltpu.make_async_remote_copy(
            src_ref=src, dst_ref=dst, send_sem=sems.at[2 * k], recv_sem=sems.at[2 * k + 1],
            device_id=dev, device_id_type=MESH)

    main_copy = link(main_ref, incoming_buf, 0, (r + 1, h))
    rim_own_copy = link(rim_own_ref, rim_own_buf, 1, (r, h + 1))
    rim_next_copy = link(rim_next_ref, rim_next_buf, 2, (r + 1, h + 1))
    b_copy = link(b_ref, b_buf, 3, (r + 1, h))

    @pl.when(has_down)
    def _():
        b_copy.start()
        main_copy.start()

    @pl.when(has_after)
    def _():
        rim_own_copy.start()

    @pl.when(diag_down)
    def _():
        rim_next_copy.start()

    bufs = [(a_src, near_h, far_h, group_h, s1h, r1h, s2h, r2h), (power_ref, near_r, far_r, group_r, s1r, r1r, s2r, r2r)]

    def across(job, x_ref, near, s1, r1, p, landing):
        return pltpu.make_async_remote_copy(
            src_ref=x_ref, dst_ref=near.at[landing], send_sem=s1.at[p], recv_sem=r1.at[landing],
            device_id=job.device(job.o * job.inner + p), device_id_type=MESH)

    for job, (x_ref, near, far, group, s1, r1, s2, r2) in zip(jobs[::-1], bufs[::-1]):
        if job.axis == "hours":

            @pl.when(has_up)
            def _():
                b_copy.wait_recv()
                a_src[...] = a_ref[...] + b_buf[...]

            @pl.when(jnp.logical_not(has_up))
            def _():
                a_src[...] = a_ref[...]

        for s in range(1, job.inner):
            across(job, x_ref, near, s1, r1, lax.rem(job.i + s, job.inner), job.i).start()
    parts = []
    for job, (x_ref, near, far, group, s1, r1, s2, r2) in zip(jobs, bufs):
        for s in range(1, job.inner):
            p = lax.rem(job.i + s, job.inner)
            across(job, x_ref, near, s1, r1, p, job.i).wait_send()
            across(job, x_ref, near, s1, r1, p, p).wait_recv()
        own = x_ref[...]
        total = own
        part = own if job.mode == "sum" else jnp.zeros_like(own)
        for s in range(1, job.inner):
            p = lax.rem(job.i + s, job.inner)
            block = near[p]
            total = total + block
            if job.mode == "sum":
                part = part + block
            else:
                part = part + jnp.where(wanted(job.mode, p, job.i), block, 0.0)
        group[...] = total
        parts.append(part)

    def up(job, group, far, s2, r2, q, landing):
        return pltpu.make_async_remote_copy(
            src_ref=group, dst_ref=far.at[landing], send_sem=s2.at[q], recv_sem=r2.at[landing],
            device_id=job.device(q * job.inner + job.i), device_id_type=MESH)

    for job, (x_ref, near, far, group, s1, r1, s2, r2) in zip(jobs, bufs):
        for s in range(1, job.outer):
            q = lax.rem(job.o + s, job.outer)

            @pl.when(wanted(job.mode, job.o, q))
            def _():
                up(job, group, far, s2, r2, q, job.o).start()

    results = []
    for job, part, (x_ref, near, far, group, s1, r1, s2, r2) in zip(jobs, parts, bufs):
        for s in range(1, job.outer):
            q = lax.rem(job.o + s, job.outer)

            @pl.when(wanted(job.mode, job.o, q))
            def _():
                up(job, group, far, s2, r2, q, job.o).wait_send()

            @pl.when(wanted(job.mode, q, job.o))
            def _():
                up(job, group, far, s2, r2, q, q).wait_recv()

        for s in range(1, job.outer):
            q = lax.rem(job.o + s, job.outer)
            part = part + jnp.where(wanted(job.mode, q, job.o), far[q], 0.0)
        results.append(part)
    scanned, supplied = results
    pa_ref[...] = scanned
    supplied_ref[...] = supplied

    @pl.when(has_down)
    def _():
        main_copy.wait_send()
        b_copy.wait_send()

    @pl.when(has_after)
    def _():
        rim_own_copy.wait_send()

    @pl.when(diag_down)
    def _():
        rim_next_copy.wait_send()

    @pl.when(has_up)
    def _():
        main_copy.wait_recv()
        incoming_ref[...] = incoming_buf[...]

    @pl.when(jnp.logical_not(has_up))
    def _():
        incoming_ref[...] = jnp.zeros_like(incoming_ref)

    @pl.when(has_before)
    def _():
        rim_own_copy.wait_recv()
        rim_own_in_ref[...] = rim_own_buf[...]

    @pl.when(jnp.logical_not(has_before))
    def _():
        rim_own_in_ref[...] = jnp.zeros_like(rim_own_in_ref)

    @pl.when(diag_up)
    def _():
        rim_next_copy.wait_recv()
        rim_next_in_ref[...] = rim_next_buf[...]

    @pl.when(jnp.logical_not(diag_up))
    def _():
        rim_next_in_ref[...] = jnp.zeros_like(rim_next_in_ref)


def flow_exchange(main_next, rim_own, rim_next, own_totals, next_totals, power):
    res, width = own_totals.shape
    a = own_totals.reshape(-1, 128)
    b = next_totals.reshape(-1, 128)
    flat_power = power.reshape(-1, 128)
    inner = 8
    outer_h = lax.axis_size("hours") // inner
    outer_r = lax.axis_size("river") // inner
    vmem = pl.BlockSpec(memory_space=pltpu.VMEM)
    shape = lambda x: jax.ShapeDtypeStruct(x.shape, x.dtype)
    incoming, rim_own_in, rim_next_in, pa, supplied = pl.pallas_call(
        flow_kernel,
        out_shape=[shape(main_next), shape(rim_own), shape(rim_next), shape(a), shape(flat_power)],
        in_specs=[vmem] * 6,
        out_specs=[vmem] * 5,
        scratch_shapes=[
            pltpu.VMEM((inner,) + a.shape, a.dtype),
            pltpu.VMEM((outer_h,) + a.shape, a.dtype),
            pltpu.VMEM(a.shape, a.dtype),
            pltpu.VMEM((inner,) + flat_power.shape, a.dtype),
            pltpu.VMEM((outer_r,) + flat_power.shape, a.dtype),
            pltpu.VMEM(flat_power.shape, a.dtype),
            pltpu.VMEM(main_next.shape, a.dtype),
            pltpu.VMEM(rim_own.shape, a.dtype),
            pltpu.VMEM(rim_next.shape, a.dtype),
            pltpu.VMEM(a.shape, a.dtype),
            pltpu.VMEM(a.shape, a.dtype),
            pltpu.SemaphoreType.DMA((inner,)),
            pltpu.SemaphoreType.DMA((inner,)),
            pltpu.SemaphoreType.DMA((outer_h,)),
            pltpu.SemaphoreType.DMA((outer_h,)),
            pltpu.SemaphoreType.DMA((inner,)),
            pltpu.SemaphoreType.DMA((inner,)),
            pltpu.SemaphoreType.DMA((outer_r,)),
            pltpu.SemaphoreType.DMA((outer_r,)),
            pltpu.SemaphoreType.DMA((8,)),
        ],
        compiler_params=pltpu.CompilerParams(collective_id=1, has_side_effects=True, vmem_limit_bytes=48 * 1024 * 1024),
    )(main_next, rim_own, rim_next, a, b, flat_power)
    return incoming, rim_own_in, rim_next_in, pa.reshape(res, width), supplied.reshape(power.shape)


def combine(parts, specs, collective):
    shapes = [part.shape for part in parts]
    parts = [part.reshape(-1, 128) for part in parts]
    jobs = [Job(axis, mode, inner, lax.axis_size(axis)) for axis, mode, inner in specs]
    scratch = []
    for part, job in zip(parts, jobs):
        scratch += [
            pltpu.VMEM((job.inner,) + part.shape, part.dtype),
            pltpu.VMEM((job.outer,) + part.shape, part.dtype),
            pltpu.VMEM(part.shape, part.dtype),
            pltpu.SemaphoreType.DMA((job.inner,)),
            pltpu.SemaphoreType.DMA((job.inner,)),
            pltpu.SemaphoreType.DMA((job.outer,)),
            pltpu.SemaphoreType.DMA((job.outer,)),
        ]
    results = pl.pallas_call(
        functools.partial(multi_kernel, jobs),
        out_shape=[jax.ShapeDtypeStruct(part.shape, part.dtype) for part in parts],
        in_specs=[pl.BlockSpec(memory_space=pltpu.VMEM)] * len(parts),
        out_specs=[pl.BlockSpec(memory_space=pltpu.VMEM)] * len(parts),
        scratch_shapes=scratch,
        compiler_params=pltpu.CompilerParams(collective_id=collective, has_side_effects=True),
    )(*parts)
    return [result.reshape(shape) for result, shape in zip(results, shapes)]


def add_pair(earlier_part, later_part):
    return earlier_part + later_part


def hold_back(field, travel_delay, earlier_rim):
    length = field.shape[1]
    extended = jnp.concatenate([earlier_rim, field], 1)
    result = jnp.zeros_like(field)
    for lag_hours in range(1, DMAX + 1):
        window = extended[:, DMAX - lag_hours : DMAX - lag_hours + length]
        result = result + jnp.where((travel_delay == lag_hours)[:, None, None], window, 0.0)
    return result


def bring_forward(field, travel_delay, later_rim):
    length = field.shape[1]
    extended = jnp.concatenate([field, later_rim], 1)
    result = jnp.zeros_like(field)
    for lag_hours in range(1, DMAX + 1):
        window = extended[:, lag_hours : lag_hours + length]
        result = result + jnp.where((travel_delay == lag_hours)[:, None, None], window, 0.0)
    return result


def route_down(matrix, field):
    return jnp.einsum("ij,jtw->itw", matrix, field, precision=lax.Precision.HIGHEST)


def route_up(matrix, field):
    return jnp.einsum("ij,itw->jtw", matrix, field, precision=lax.Precision.HIGHEST)


def iterate(fields, statics, scales, suffix_sum, from_earlier, from_later):
    release, storage_dual, demand_dual, cost, inflow, demand = fields
    (
        storage_start,
        storage_low,
        storage_high,
        release_cap,
        efficiency,
        travel_delay,
        to_own,
        to_next,
    ) = statics
    scale_time, scale_sum = scales
    local = suffix_local(storage_dual)
    off, off_next, beyond, rim_own, rim_next = dual_exchange(local)
    suffix = local + off[:, None]
    at_sink = route_up(to_own, suffix) + route_up(to_next, beyond + off_next[:, None])
    last = lax.axis_index("hours") == lax.axis_size("hours") - 1
    rim_sink = route_up(to_own, rim_own + off[:, None]) + route_up(to_next, rim_next + off_next[:, None])
    later_duals = bring_forward(at_sink, travel_delay, jnp.where(last, 0.0, rim_sink))
    gradient = (
        cost
        + scale_time * (later_duals - suffix)
        + scale_sum * efficiency[:, None, None] * demand_dual[None]
    )
    release_new = jnp.clip(release - primal_step * gradient, 0.0, release_cap[:, None, None])
    extrapolated = 2.0 * release_new - release
    length = extrapolated.shape[1]
    tail = extrapolated[:, length - DMAX :]
    settled = hold_back(extrapolated, travel_delay, jnp.zeros_like(tail))
    rim_delayed = hold_back(jnp.zeros_like(extrapolated), travel_delay, tail)[:, :DMAX]
    main_own = route_down(to_own, settled)
    main_next = route_down(to_next, settled)
    rim_own = route_down(to_own, rim_delayed)
    rim_next = route_down(to_next, rim_delayed)
    base = inflow + main_own - extrapolated
    own_totals = jnp.sum(base, 1) + jnp.sum(rim_own, 1)
    next_totals = jnp.sum(main_next, 1) + jnp.sum(rim_next, 1)
    partial_power = jnp.sum(scale_sum * efficiency[:, None, None] * extrapolated, 0)
    incoming, rim_own_in, rim_next_in, offset, supplied = flow_exchange(
        main_next, rim_own, rim_next, own_totals, next_totals, partial_power
    )
    arrived = jnp.concatenate([rim_own_in + rim_next_in, jnp.zeros_like(base[:, DMAX:])], 1)
    local_sum = jnp.cumsum(base + incoming + arrived, 1)
    offset = offset - jnp.sum(rim_own_in, 1) - jnp.sum(rim_next_in, 1)
    storage = storage_start[:, None, None] + scale_time * (local_sum + offset[:, None])
    lower_bound = storage_low[:, None, None]
    upper_bound = storage_high[:, None, None]
    storage_dual_new = (
        storage_dual
        + dual_step * storage
        - dual_step * jnp.clip(storage_dual / dual_step + storage, lower_bound, upper_bound)
    )
    storage_excess = storage - jnp.clip(storage, lower_bound, upper_bound)
    demand_dual_new = jnp.minimum(demand_dual + dual_step * (supplied - demand), 0.0)
    return (release_new, storage_dual_new, demand_dual_new, storage_excess)


def suffix_local(field):
    return jnp.flip(jnp.cumsum(jnp.flip(field, 1), 1), 1)


def shards(
    release,
    storage_dual,
    demand_dual,
    cost,
    inflow,
    demand,
    storage_start,
    storage_low,
    storage_high,
    release_cap,
    efficiency,
    downstream,
    travel_delay,
):
    res_dev = release.shape[0]
    scale_time = 1.0 / (release.shape[1] * lax.axis_size("hours"))
    scale_sum = 1.0 / math.sqrt(res_dev * lax.axis_size("river"))
    base_index = lax.axis_index("river") * res_dev
    target = downstream - base_index
    indices = jnp.arange(res_dev, dtype=jnp.int32)
    to_own = (target[None, :] == indices[:, None]).astype(jnp.float32)
    to_next = (target[None, :] == indices[:, None] + res_dev).astype(jnp.float32)
    statics = (
        storage_start,
        storage_low,
        storage_high,
        release_cap,
        efficiency,
        travel_delay,
        to_own,
        to_next,
    )
    scales = (scale_time, scale_sum)

    def suffix_blocks(field):
        local_sum = suffix_local(field)
        totals = local_sum[:, 0]
        (offset,) = combine([totals], [("hours", "suffix", 8)], 0)
        return local_sum + offset[:, None]

    def earlier_block(part):
        return passed_along(part, "hours", 1)

    def later_block(part):
        return passed_along(part, "hours", -1)

    fields = (release, storage_dual, demand_dual, cost, inflow, demand)
    return iterate(
        fields, statics, scales, suffix_blocks, earlier_block, later_block
    )


def solution(mesh):
    return jax.shard_map(
        shards,
        mesh=mesh,
        in_specs=(
            P("river", "hours", None),
            P("river", "hours", None),
            P("hours", None),
            P("river", "hours", None),
            P("river", "hours", None),
            P("hours", None),
            P("river"),
            P("river"),
            P("river"),
            P("river"),
            P("river"),
            P("river"),
            P("river"),
        ),
        out_specs=(
            P("river", "hours", None),
            P("river", "hours", None),
            P("hours", None),
            P("river", "hours", None),
        ),
        check_vma=False,
    )
```

```python
import functools
import math

import jax
import jax.numpy as jnp
from jax import lax
from jax.experimental import pallas as pl
from jax.experimental.pallas import tpu as pltpu
from jax.sharding import PartitionSpec as P

DMAX = 6


primal_step = 1.0
dual_step = 0.1


def passed_along(block, axis, distance):
    devices = range(lax.axis_size(axis))
    route = [(i - distance, i) for i in devices if i - distance in devices]
    return lax.ppermute(block, axis, route)


MESH = pl.DeviceIdType.MESH


def wanted(mode, src, dst):
    if mode == "prefix":
        return src < dst
    if mode == "suffix":
        return src > dst
    return src != dst


class Job:
    def __init__(self, axis, mode, inner, n):
        self.axis, self.mode, self.inner = axis, mode, inner
        self.outer = n // inner
        self.other = "river" if axis == "hours" else "hours"

    def place(self):
        me = lax.axis_index(self.axis)
        self.fixed = lax.axis_index(self.other)
        self.o = me // self.inner
        self.i = me % self.inner

    def device(self, p):
        return (self.fixed, p) if self.axis == "hours" else (p, self.fixed)

    def peers(self):
        inner, outer, o, i = self.inner, self.outer, self.o, self.i
        near = [self.device(o * inner + lax.rem(i + s, inner)) for s in range(1, inner)]
        far = [self.device(lax.rem(o + s, outer) * inner + i) for s in range(1, outer)]
        return near + far


def multi_kernel(jobs, *refs):
    count = len(jobs)
    ins, outs, rest = refs[:count], refs[count:2 * count], refs[2 * count:]
    for job in jobs:
        job.place()
    barrier = pltpu.get_barrier_semaphore()
    partners = 0
    for job in jobs:
        for dev in job.peers():
            pl.semaphore_signal(barrier, 1, device_id=dev, device_id_type=MESH)
            partners += 1
    pl.semaphore_wait(barrier, partners)

    def across(job, x_ref, near, s1, r1, p, landing):
        return pltpu.make_async_remote_copy(
            src_ref=x_ref, dst_ref=near.at[landing], send_sem=s1.at[p], recv_sem=r1.at[landing],
            device_id=job.device(job.o * job.inner + p), device_id_type=MESH)

    for k, job in enumerate(jobs):
        near, far, group, s1, r1, s2, r2 = rest[7 * k:7 * k + 7]
        for s in range(1, job.inner):
            p = lax.rem(job.i + s, job.inner)
            across(job, ins[k], near, s1, r1, p, job.i).start()
    parts = []
    for k, job in enumerate(jobs):
        near, far, group, s1, r1, s2, r2 = rest[7 * k:7 * k + 7]
        for s in range(1, job.inner):
            p = lax.rem(job.i + s, job.inner)
            across(job, ins[k], near, s1, r1, p, job.i).wait_send()
            across(job, ins[k], near, s1, r1, p, p).wait_recv()
        own = ins[k][...]
        total = own
        part = own if job.mode == "sum" else jnp.zeros_like(own)
        for s in range(1, job.inner):
            p = lax.rem(job.i + s, job.inner)
            block = near[p]
            total = total + block
            if job.mode == "sum":
                part = part + block
            else:
                part = part + jnp.where(wanted(job.mode, p, job.i), block, 0.0)
        group[...] = total
        parts.append(part)

    def up(job, group, far, s2, r2, q, landing):
        return pltpu.make_async_remote_copy(
            src_ref=group, dst_ref=far.at[landing], send_sem=s2.at[q], recv_sem=r2.at[landing],
            device_id=job.device(q * job.inner + job.i), device_id_type=MESH)

    for k, job in enumerate(jobs):
        near, far, group, s1, r1, s2, r2 = rest[7 * k:7 * k + 7]
        for s in range(1, job.outer):
            q = lax.rem(job.o + s, job.outer)

            @pl.when(wanted(job.mode, job.o, q))
            def _():
                up(job, group, far, s2, r2, q, job.o).start()

    for k, job in enumerate(jobs):
        near, far, group, s1, r1, s2, r2 = rest[7 * k:7 * k + 7]
        part = parts[k]
        for s in range(1, job.outer):
            q = lax.rem(job.o + s, job.outer)

            @pl.when(wanted(job.mode, job.o, q))
            def _():
                up(job, group, far, s2, r2, q, job.o).wait_send()

            @pl.when(wanted(job.mode, q, job.o))
            def _():
                up(job, group, far, s2, r2, q, q).wait_recv()

        for s in range(1, job.outer):
            q = lax.rem(job.o + s, job.outer)
            part = part + jnp.where(wanted(job.mode, q, job.o), far[q], 0.0)
        outs[k][...] = part


def dual_kernel(
    sloc_ref, t_ref, off_ref, off_next_ref, beyond_ref, rim_own_ref, rim_next_ref,
    near, far, group, beyond_buf, rim_src_own, rim_src_next, rim_own_buf, rim_next_buf,
    off_src, off_next_buf, s1, r1, s2, r2, sems,
):
    job = Job("hours", "suffix", 8, lax.axis_size("hours"))
    job.place()
    n_r = lax.axis_size("river")
    n_h = lax.axis_size("hours")
    r = lax.axis_index("river")
    h = lax.axis_index("hours")
    has_up, has_down = r > 0, r < n_r - 1
    has_before, has_after = h > 0, h < n_h - 1

    barrier = pltpu.get_barrier_semaphore()
    for dev in job.peers():
        pl.semaphore_signal(barrier, 1, device_id=dev, device_id_type=MESH)
    for flag, dev in ((has_up, (r - 1, h)), (has_down, (r + 1, h)), (has_before, (r, h - 1)), (has_after, (r, h + 1))):

        @pl.when(flag)
        def _():
            pl.semaphore_signal(barrier, 1, device_id=dev, device_id_type=MESH)

    extra = sum(jnp.where(flag, 1, 0) for flag in (has_up, has_down, has_before, has_after))
    pl.semaphore_wait(barrier, job.inner + job.outer - 2 + extra)

    def link(src, dst, k, dev):
        return pltpu.make_async_remote_copy(
            src_ref=src, dst_ref=dst, send_sem=sems.at[2 * k], recv_sem=sems.at[2 * k + 1],
            device_id=dev, device_id_type=MESH)

    to_up = lambda src, dst, k: link(src, dst, k, (r - 1, h))
    to_before = lambda src, dst, k: link(src, dst, k, (r, h - 1))

    def across(p, landing):
        return pltpu.make_async_remote_copy(
            src_ref=t_ref, dst_ref=near.at[landing], send_sem=s1.at[p], recv_sem=r1.at[landing],
            device_id=job.device(job.o * job.inner + p), device_id_type=MESH)

    for s in range(1, job.inner):
        across(lax.rem(job.i + s, job.inner), job.i).start()

    @pl.when(has_up)
    def _():
        to_up(sloc_ref, beyond_buf, 0).start()

    rim_src_own[...] = sloc_ref[:, 0:DMAX, :] - sloc_ref[:, 0:1, :]

    @pl.when(has_before)
    def _():
        to_before(rim_src_own, rim_own_buf, 1).start()

    for s in range(1, job.inner):
        p = lax.rem(job.i + s, job.inner)
        across(p, job.i).wait_send()
        across(p, p).wait_recv()
    own = t_ref[...]
    total = own
    part = jnp.zeros_like(own)
    for s in range(1, job.inner):
        p = lax.rem(job.i + s, job.inner)
        block = near[p]
        total = total + block
        part = part + jnp.where(p > job.i, block, 0.0)
    group[...] = total

    def up(q, landing):
        return pltpu.make_async_remote_copy(
            src_ref=group, dst_ref=far.at[landing], send_sem=s2.at[q], recv_sem=r2.at[landing],
            device_id=job.device(q * job.inner + job.i), device_id_type=MESH)

    for s in range(1, job.outer):
        q = lax.rem(job.o + s, job.outer)

        @pl.when(job.o > q)
        def _():
            up(q, job.o).start()

    @pl.when(has_down)
    def _():
        to_up(sloc_ref, beyond_buf, 0).wait_recv()
        rim_src_next[...] = beyond_buf[:, 0:DMAX, :] - beyond_buf[:, 0:1, :]

    @pl.when(jnp.logical_and(has_down, has_before))
    def _():
        to_before(rim_src_next, rim_next_buf, 2).start()

    for s in range(1, job.outer):
        q = lax.rem(job.o + s, job.outer)

        @pl.when(job.o > q)
        def _():
            up(q, job.o).wait_send()

        @pl.when(q > job.o)
        def _():
            up(q, q).wait_recv()

    for s in range(1, job.outer):
        q = lax.rem(job.o + s, job.outer)
        part = part + jnp.where(q > job.o, far[q], 0.0)
    off_src[...] = part
    off_ref[...] = part

    @pl.when(has_up)
    def _():
        to_up(off_src, off_next_buf, 3).start()

    @pl.when(has_up)
    def _():
        to_up(sloc_ref, beyond_buf, 0).wait_send()
        to_up(off_src, off_next_buf, 3).wait_send()

    @pl.when(has_before)
    def _():
        to_before(rim_src_own, rim_own_buf, 1).wait_send()

    @pl.when(jnp.logical_and(has_down, has_before))
    def _():
        to_before(rim_src_next, rim_next_buf, 2).wait_send()

    @pl.when(has_after)
    def _():
        to_before(rim_src_own, rim_own_buf, 1).wait_recv()
        rim_own_ref[...] = rim_own_buf[...]

    @pl.when(jnp.logical_not(has_after))
    def _():
        rim_own_ref[...] = jnp.zeros_like(rim_own_ref)

    @pl.when(jnp.logical_and(has_down, has_after))
    def _():
        to_before(rim_src_next, rim_next_buf, 2).wait_recv()
        rim_next_ref[...] = rim_next_buf[...]

    @pl.when(jnp.logical_not(jnp.logical_and(has_down, has_after)))
    def _():
        rim_next_ref[...] = jnp.zeros_like(rim_next_ref)

    @pl.when(has_down)
    def _():
        to_up(off_src, off_next_buf, 3).wait_recv()
        off_next_ref[...] = off_next_buf[...]
        beyond_ref[...] = beyond_buf[...]

    @pl.when(jnp.logical_not(has_down))
    def _():
        off_next_ref[...] = jnp.zeros_like(off_next_ref)
        beyond_ref[...] = jnp.zeros_like(beyond_ref)


def dual_exchange(sloc):
    res, length, width = sloc.shape
    t = sloc[:, 0].reshape(-1, 128)
    inner = 8
    outer = lax.axis_size("hours") // inner
    rim = (res, DMAX, width)
    vmem = pl.BlockSpec(memory_space=pltpu.VMEM)
    off, off_next, beyond, rim_own, rim_next = pl.pallas_call(
        dual_kernel,
        out_shape=[
            jax.ShapeDtypeStruct(t.shape, t.dtype),
            jax.ShapeDtypeStruct(t.shape, t.dtype),
            jax.ShapeDtypeStruct(sloc.shape, sloc.dtype),
            jax.ShapeDtypeStruct(rim, sloc.dtype),
            jax.ShapeDtypeStruct(rim, sloc.dtype),
        ],
        in_specs=[vmem, vmem],
        out_specs=[vmem] * 5,
        scratch_shapes=[
            pltpu.VMEM((inner,) + t.shape, t.dtype),
            pltpu.VMEM((outer,) + t.shape, t.dtype),
            pltpu.VMEM(t.shape, t.dtype),
            pltpu.VMEM(sloc.shape, sloc.dtype),
            pltpu.VMEM(rim, sloc.dtype),
            pltpu.VMEM(rim, sloc.dtype),
            pltpu.VMEM(rim, sloc.dtype),
            pltpu.VMEM(rim, sloc.dtype),
            pltpu.VMEM(t.shape, t.dtype),
            pltpu.VMEM(t.shape, t.dtype),
            pltpu.SemaphoreType.DMA((inner,)),
            pltpu.SemaphoreType.DMA((inner,)),
            pltpu.SemaphoreType.DMA((outer,)),
            pltpu.SemaphoreType.DMA((outer,)),
            pltpu.SemaphoreType.DMA((8,)),
        ],
        compiler_params=pltpu.CompilerParams(collective_id=0, has_side_effects=True, vmem_limit_bytes=48 * 1024 * 1024),
    )(sloc, t)
    return off.reshape(res, width), off_next.reshape(res, width), beyond, rim_own, rim_next


def flow_kernel(
    main_ref, rim_own_ref, rim_next_ref, a_ref, b_ref, power_ref,
    incoming_ref, rim_own_in_ref, rim_next_in_ref, pa_ref, supplied_ref,
    near_h, far_h, group_h, rs_buf, red, x_buf, full, incoming_buf, rim_own_buf, rim_next_buf,
    a_src, b_buf, s1h, r1h, s2h, r2h, s1r, r1r, s2r, r2r, sems,
):
    jobs = [Job("hours", "prefix", 8, lax.axis_size("hours")), Job("river", "sum", 8, lax.axis_size("river"))]
    for job in jobs:
        job.place()
    n_r = lax.axis_size("river")
    n_h = lax.axis_size("hours")
    r = lax.axis_index("river")
    h = lax.axis_index("hours")
    has_up, has_down = r > 0, r < n_r - 1
    has_before, has_after = h > 0, h < n_h - 1
    diag_down = jnp.logical_and(has_down, has_after)
    diag_up = jnp.logical_and(has_up, has_before)

    barrier = pltpu.get_barrier_semaphore()
    fixed = 0
    for job in jobs:
        for dev in job.peers():
            pl.semaphore_signal(barrier, 1, device_id=dev, device_id_type=MESH)
            fixed += 1
    links = (
        (has_up, (r - 1, h)), (has_down, (r + 1, h)), (has_before, (r, h - 1)), (has_after, (r, h + 1)),
        (diag_down, (r + 1, h + 1)), (diag_up, (r - 1, h - 1)),
    )
    for flag, dev in links:

        @pl.when(flag)
        def _():
            pl.semaphore_signal(barrier, 1, device_id=dev, device_id_type=MESH)

    extra = sum(jnp.where(flag, 1, 0) for flag, _ in links)
    pl.semaphore_wait(barrier, fixed + extra)

    def link(src, dst, k, dev):
        return pltpu.make_async_remote_copy(
            src_ref=src, dst_ref=dst, send_sem=sems.at[2 * k], recv_sem=sems.at[2 * k + 1],
            device_id=dev, device_id_type=MESH)

    main_copy = link(main_ref, incoming_buf, 0, (r + 1, h))
    rim_own_copy = link(rim_own_ref, rim_own_buf, 1, (r, h + 1))
    rim_next_copy = link(rim_next_ref, rim_next_buf, 2, (r + 1, h + 1))
    b_copy = link(b_ref, b_buf, 3, (r + 1, h))

    @pl.when(has_down)
    def _():
        b_copy.start()
        main_copy.start()

    @pl.when(has_after)
    def _():
        rim_own_copy.start()

    @pl.when(diag_down)
    def _():
        rim_next_copy.start()

    bufs = [(a_src, near_h, far_h, group_h, s1h, r1h, s2h, r2h)]
    river = jobs.pop()
    tile = rs_buf.shape[1]

    def scatter(c, landing):
        return pltpu.make_async_remote_copy(
            src_ref=power_ref.at[pl.ds(c * tile, tile)], dst_ref=rs_buf.at[landing], send_sem=s1r.at[c],
            recv_sem=r1r.at[landing], device_id=river.device(river.o * river.inner + c), device_id_type=MESH)

    for s in range(1, river.inner):
        scatter(lax.rem(river.i + s, river.inner), river.i).start()

    def across(job, x_ref, near, s1, r1, p, landing):
        return pltpu.make_async_remote_copy(
            src_ref=x_ref, dst_ref=near.at[landing], send_sem=s1.at[p], recv_sem=r1.at[landing],
            device_id=job.device(job.o * job.inner + p), device_id_type=MESH)

    for job, (x_ref, near, far, group, s1, r1, s2, r2) in zip(jobs, bufs):
        if job.axis == "hours":

            @pl.when(has_up)
            def _():
                b_copy.wait_recv()
                a_src[...] = a_ref[...] + b_buf[...]

            @pl.when(jnp.logical_not(has_up))
            def _():
                a_src[...] = a_ref[...]

        for s in range(1, job.inner):
            across(job, x_ref, near, s1, r1, lax.rem(job.i + s, job.inner), job.i).start()
    parts = []
    for job, (x_ref, near, far, group, s1, r1, s2, r2) in zip(jobs, bufs):
        for s in range(1, job.inner):
            p = lax.rem(job.i + s, job.inner)
            across(job, x_ref, near, s1, r1, p, job.i).wait_send()
            across(job, x_ref, near, s1, r1, p, p).wait_recv()
        own = x_ref[...]
        total = own
        part = own if job.mode == "sum" else jnp.zeros_like(own)
        for s in range(1, job.inner):
            p = lax.rem(job.i + s, job.inner)
            block = near[p]
            total = total + block
            if job.mode == "sum":
                part = part + block
            else:
                part = part + jnp.where(wanted(job.mode, p, job.i), block, 0.0)
        group[...] = total
        parts.append(part)

    def up(job, group, far, s2, r2, q, landing):
        return pltpu.make_async_remote_copy(
            src_ref=group, dst_ref=far.at[landing], send_sem=s2.at[q], recv_sem=r2.at[landing],
            device_id=job.device(q * job.inner + job.i), device_id_type=MESH)

    for job, (x_ref, near, far, group, s1, r1, s2, r2) in zip(jobs, bufs):
        for s in range(1, job.outer):
            q = lax.rem(job.o + s, job.outer)

            @pl.when(wanted(job.mode, job.o, q))
            def _():
                up(job, group, far, s2, r2, q, job.o).start()

    results = []
    for job, part, (x_ref, near, far, group, s1, r1, s2, r2) in zip(jobs, parts, bufs):
        for s in range(1, job.outer):
            q = lax.rem(job.o + s, job.outer)

            @pl.when(wanted(job.mode, job.o, q))
            def _():
                up(job, group, far, s2, r2, q, job.o).wait_send()

            @pl.when(wanted(job.mode, q, job.o))
            def _():
                up(job, group, far, s2, r2, q, q).wait_recv()

        for s in range(1, job.outer):
            q = lax.rem(job.o + s, job.outer)
            part = part + jnp.where(wanted(job.mode, q, job.o), far[q], 0.0)
        results.append(part)
    (scanned,) = results
    pa_ref[...] = scanned

    for s in range(1, river.inner):
        c = lax.rem(river.i + s, river.inner)
        scatter(c, river.i).wait_send()
        scatter(c, c).wait_recv()
    mine = power_ref[pl.ds(river.i * tile, tile)]
    for s in range(1, river.inner):
        mine = mine + rs_buf[lax.rem(river.i + s, river.inner)]
    red[...] = mine
    partner = river.device(lax.rem(river.o + 1, river.outer) * river.inner + river.i)
    swap = pltpu.make_async_remote_copy(
        src_ref=red, dst_ref=x_buf, send_sem=s2r.at[0], recv_sem=r2r.at[0], device_id=partner, device_id_type=MESH)
    swap.start()
    swap.wait_send()
    swap.wait_recv()
    full[river.i] = mine + x_buf[...]

    def gather(c, landing):
        return pltpu.make_async_remote_copy(
            src_ref=full.at[river.i], dst_ref=full.at[landing], send_sem=s2r.at[1 + c], recv_sem=r1r.at[river.inner + landing],
            device_id=river.device(river.o * river.inner + c), device_id_type=MESH)

    for s in range(1, river.inner):
        gather(lax.rem(river.i + s, river.inner), river.i).start()
    for s in range(1, river.inner):
        c = lax.rem(river.i + s, river.inner)
        gather(c, river.i).wait_send()
        gather(c, c).wait_recv()
    for c in range(river.inner):
        supplied_ref[pl.ds(c * tile, tile)] = full[c]

    @pl.when(has_down)
    def _():
        main_copy.wait_send()
        b_copy.wait_send()

    @pl.when(has_after)
    def _():
        rim_own_copy.wait_send()

    @pl.when(diag_down)
    def _():
        rim_next_copy.wait_send()

    @pl.when(has_up)
    def _():
        main_copy.wait_recv()
        incoming_ref[...] = incoming_buf[...]

    @pl.when(jnp.logical_not(has_up))
    def _():
        incoming_ref[...] = jnp.zeros_like(incoming_ref)

    @pl.when(has_before)
    def _():
        rim_own_copy.wait_recv()
        rim_own_in_ref[...] = rim_own_buf[...]

    @pl.when(jnp.logical_not(has_before))
    def _():
        rim_own_in_ref[...] = jnp.zeros_like(rim_own_in_ref)

    @pl.when(diag_up)
    def _():
        rim_next_copy.wait_recv()
        rim_next_in_ref[...] = rim_next_buf[...]

    @pl.when(jnp.logical_not(diag_up))
    def _():
        rim_next_in_ref[...] = jnp.zeros_like(rim_next_in_ref)


def flow_exchange(main_next, rim_own, rim_next, own_totals, next_totals, power):
    res, width = own_totals.shape
    a = own_totals.reshape(-1, 128)
    b = next_totals.reshape(-1, 128)
    flat_power = power.reshape(-1, 128)
    inner = 8
    outer_h = lax.axis_size("hours") // inner
    outer_r = lax.axis_size("river") // inner
    vmem = pl.BlockSpec(memory_space=pltpu.VMEM)
    shape = lambda x: jax.ShapeDtypeStruct(x.shape, x.dtype)
    incoming, rim_own_in, rim_next_in, pa, supplied = pl.pallas_call(
        flow_kernel,
        out_shape=[shape(main_next), shape(rim_own), shape(rim_next), shape(a), shape(flat_power)],
        in_specs=[vmem] * 6,
        out_specs=[vmem] * 5,
        scratch_shapes=[
            pltpu.VMEM((inner,) + a.shape, a.dtype),
            pltpu.VMEM((outer_h,) + a.shape, a.dtype),
            pltpu.VMEM(a.shape, a.dtype),
            pltpu.VMEM((inner, flat_power.shape[0] // inner, 128), a.dtype),
            pltpu.VMEM((flat_power.shape[0] // inner, 128), a.dtype),
            pltpu.VMEM((flat_power.shape[0] // inner, 128), a.dtype),
            pltpu.VMEM((inner, flat_power.shape[0] // inner, 128), a.dtype),
            pltpu.VMEM(main_next.shape, a.dtype),
            pltpu.VMEM(rim_own.shape, a.dtype),
            pltpu.VMEM(rim_next.shape, a.dtype),
            pltpu.VMEM(a.shape, a.dtype),
            pltpu.VMEM(a.shape, a.dtype),
            pltpu.SemaphoreType.DMA((inner,)),
            pltpu.SemaphoreType.DMA((inner,)),
            pltpu.SemaphoreType.DMA((outer_h,)),
            pltpu.SemaphoreType.DMA((outer_h,)),
            pltpu.SemaphoreType.DMA((inner,)),
            pltpu.SemaphoreType.DMA((2 * inner,)),
            pltpu.SemaphoreType.DMA((inner + 1,)),
            pltpu.SemaphoreType.DMA((1,)),
            pltpu.SemaphoreType.DMA((8,)),
        ],
        compiler_params=pltpu.CompilerParams(collective_id=1, has_side_effects=True, vmem_limit_bytes=48 * 1024 * 1024),
    )(main_next, rim_own, rim_next, a, b, flat_power)
    return incoming, rim_own_in, rim_next_in, pa.reshape(res, width), supplied.reshape(power.shape)


def combine(parts, specs, collective):
    shapes = [part.shape for part in parts]
    parts = [part.reshape(-1, 128) for part in parts]
    jobs = [Job(axis, mode, inner, lax.axis_size(axis)) for axis, mode, inner in specs]
    scratch = []
    for part, job in zip(parts, jobs):
        scratch += [
            pltpu.VMEM((job.inner,) + part.shape, part.dtype),
            pltpu.VMEM((job.outer,) + part.shape, part.dtype),
            pltpu.VMEM(part.shape, part.dtype),
            pltpu.SemaphoreType.DMA((job.inner,)),
            pltpu.SemaphoreType.DMA((job.inner,)),
            pltpu.SemaphoreType.DMA((job.outer,)),
            pltpu.SemaphoreType.DMA((job.outer,)),
        ]
    results = pl.pallas_call(
        functools.partial(multi_kernel, jobs),
        out_shape=[jax.ShapeDtypeStruct(part.shape, part.dtype) for part in parts],
        in_specs=[pl.BlockSpec(memory_space=pltpu.VMEM)] * len(parts),
        out_specs=[pl.BlockSpec(memory_space=pltpu.VMEM)] * len(parts),
        scratch_shapes=scratch,
        compiler_params=pltpu.CompilerParams(collective_id=collective, has_side_effects=True),
    )(*parts)
    return [result.reshape(shape) for result, shape in zip(results, shapes)]


def add_pair(earlier_part, later_part):
    return earlier_part + later_part


def hold_back(field, travel_delay, earlier_rim):
    length = field.shape[1]
    extended = jnp.concatenate([earlier_rim, field], 1)
    result = jnp.zeros_like(field)
    for lag_hours in range(1, DMAX + 1):
        window = extended[:, DMAX - lag_hours : DMAX - lag_hours + length]
        result = result + jnp.where((travel_delay == lag_hours)[:, None, None], window, 0.0)
    return result


def bring_forward(field, travel_delay, later_rim):
    length = field.shape[1]
    extended = jnp.concatenate([field, later_rim], 1)
    result = jnp.zeros_like(field)
    for lag_hours in range(1, DMAX + 1):
        window = extended[:, lag_hours : lag_hours + length]
        result = result + jnp.where((travel_delay == lag_hours)[:, None, None], window, 0.0)
    return result


def route_down(matrix, field):
    return jnp.einsum("ij,jtw->itw", matrix, field, precision=lax.Precision.HIGHEST)


def route_up(matrix, field):
    return jnp.einsum("ij,itw->jtw", matrix, field, precision=lax.Precision.HIGHEST)


def iterate(fields, statics, scales, suffix_sum, from_earlier, from_later):
    release, storage_dual, demand_dual, cost, inflow, demand = fields
    (
        storage_start,
        storage_low,
        storage_high,
        release_cap,
        efficiency,
        travel_delay,
        to_own,
        to_next,
    ) = statics
    scale_time, scale_sum = scales
    local = suffix_local(storage_dual)
    off, off_next, beyond, rim_own, rim_next = dual_exchange(local)
    suffix = local + off[:, None]
    at_sink = route_up(to_own, suffix) + route_up(to_next, beyond + off_next[:, None])
    last = lax.axis_index("hours") == lax.axis_size("hours") - 1
    rim_sink = route_up(to_own, rim_own + off[:, None]) + route_up(to_next, rim_next + off_next[:, None])
    later_duals = bring_forward(at_sink, travel_delay, jnp.where(last, 0.0, rim_sink))
    gradient = (
        cost
        + scale_time * (later_duals - suffix)
        + scale_sum * efficiency[:, None, None] * demand_dual[None]
    )
    release_new = jnp.clip(release - primal_step * gradient, 0.0, release_cap[:, None, None])
    extrapolated = 2.0 * release_new - release
    length = extrapolated.shape[1]
    tail = extrapolated[:, length - DMAX :]
    settled = hold_back(extrapolated, travel_delay, jnp.zeros_like(tail))
    rim_delayed = hold_back(jnp.zeros_like(extrapolated), travel_delay, tail)[:, :DMAX]
    main_own = route_down(to_own, settled)
    main_next = route_down(to_next, settled)
    rim_own = route_down(to_own, rim_delayed)
    rim_next = route_down(to_next, rim_delayed)
    base = inflow + main_own - extrapolated
    own_totals = jnp.sum(base, 1) + jnp.sum(rim_own, 1)
    next_totals = jnp.sum(main_next, 1) + jnp.sum(rim_next, 1)
    partial_power = jnp.sum(scale_sum * efficiency[:, None, None] * extrapolated, 0)
    incoming, rim_own_in, rim_next_in, offset, supplied = flow_exchange(
        main_next, rim_own, rim_next, own_totals, next_totals, partial_power
    )
    arrived = jnp.concatenate([rim_own_in + rim_next_in, jnp.zeros_like(base[:, DMAX:])], 1)
    local_sum = jnp.cumsum(base + incoming + arrived, 1)
    offset = offset - jnp.sum(rim_own_in, 1) - jnp.sum(rim_next_in, 1)
    storage = storage_start[:, None, None] + scale_time * (local_sum + offset[:, None])
    lower_bound = storage_low[:, None, None]
    upper_bound = storage_high[:, None, None]
    storage_dual_new = (
        storage_dual
        + dual_step * storage
        - dual_step * jnp.clip(storage_dual / dual_step + storage, lower_bound, upper_bound)
    )
    storage_excess = storage - jnp.clip(storage, lower_bound, upper_bound)
    demand_dual_new = jnp.minimum(demand_dual + dual_step * (supplied - demand), 0.0)
    return (release_new, storage_dual_new, demand_dual_new, storage_excess)


def suffix_local(field):
    return jnp.flip(jnp.cumsum(jnp.flip(field, 1), 1), 1)


def shards(
    release,
    storage_dual,
    demand_dual,
    cost,
    inflow,
    demand,
    storage_start,
    storage_low,
    storage_high,
    release_cap,
    efficiency,
    downstream,
    travel_delay,
):
    res_dev = release.shape[0]
    scale_time = 1.0 / (release.shape[1] * lax.axis_size("hours"))
    scale_sum = 1.0 / math.sqrt(res_dev * lax.axis_size("river"))
    base_index = lax.axis_index("river") * res_dev
    target = downstream - base_index
    indices = jnp.arange(res_dev, dtype=jnp.int32)
    to_own = (target[None, :] == indices[:, None]).astype(jnp.float32)
    to_next = (target[None, :] == indices[:, None] + res_dev).astype(jnp.float32)
    statics = (
        storage_start,
        storage_low,
        storage_high,
        release_cap,
        efficiency,
        travel_delay,
        to_own,
        to_next,
    )
    scales = (scale_time, scale_sum)

    def suffix_blocks(field):
        local_sum = suffix_local(field)
        totals = local_sum[:, 0]
        (offset,) = combine([totals], [("hours", "suffix", 8)], 0)
        return local_sum + offset[:, None]

    def earlier_block(part):
        return passed_along(part, "hours", 1)

    def later_block(part):
        return passed_along(part, "hours", -1)

    fields = (release, storage_dual, demand_dual, cost, inflow, demand)
    return iterate(
        fields, statics, scales, suffix_blocks, earlier_block, later_block
    )


def solution(mesh):
    return jax.shard_map(
        shards,
        mesh=mesh,
        in_specs=(
            P("river", "hours", None),
            P("river", "hours", None),
            P("hours", None),
            P("river", "hours", None),
            P("river", "hours", None),
            P("hours", None),
            P("river"),
            P("river"),
            P("river"),
            P("river"),
            P("river"),
            P("river"),
            P("river"),
        ),
        out_specs=(
            P("river", "hours", None),
            P("river", "hours", None),
            P("hours", None),
            P("river", "hours", None),
        ),
        check_vma=False,
    )
```

```python
import functools
import math

import jax
import jax.numpy as jnp
from jax import lax
from jax.experimental import pallas as pl
from jax.experimental.pallas import tpu as pltpu
from jax.sharding import PartitionSpec as P

DMAX = 6


primal_step = 1.0
dual_step = 0.1


def passed_along(block, axis, distance):
    devices = range(lax.axis_size(axis))
    route = [(i - distance, i) for i in devices if i - distance in devices]
    return lax.ppermute(block, axis, route)


MESH = pl.DeviceIdType.MESH


def wanted(mode, src, dst):
    if mode == "prefix":
        return src < dst
    if mode == "suffix":
        return src > dst
    return src != dst


class Job:
    def __init__(self, axis, mode, inner, n):
        self.axis, self.mode, self.inner = axis, mode, inner
        self.outer = n // inner
        self.other = "river" if axis == "hours" else "hours"

    def place(self):
        me = lax.axis_index(self.axis)
        self.fixed = lax.axis_index(self.other)
        self.o = me // self.inner
        self.i = me % self.inner

    def device(self, p):
        return (self.fixed, p) if self.axis == "hours" else (p, self.fixed)

    def peers(self):
        inner, outer, o, i = self.inner, self.outer, self.o, self.i
        near = [self.device(o * inner + lax.rem(i + s, inner)) for s in range(1, inner)]
        far = [self.device(lax.rem(o + s, outer) * inner + i) for s in range(1, outer)]
        return near + far


def multi_kernel(jobs, *refs):
    count = len(jobs)
    ins, outs, rest = refs[:count], refs[count:2 * count], refs[2 * count:]
    for job in jobs:
        job.place()
    barrier = pltpu.get_barrier_semaphore()
    partners = 0
    for job in jobs:
        for dev in job.peers():
            pl.semaphore_signal(barrier, 1, device_id=dev, device_id_type=MESH)
            partners += 1
    pl.semaphore_wait(barrier, partners)

    def across(job, x_ref, near, s1, r1, p, landing):
        return pltpu.make_async_remote_copy(
            src_ref=x_ref, dst_ref=near.at[landing], send_sem=s1.at[p], recv_sem=r1.at[landing],
            device_id=job.device(job.o * job.inner + p), device_id_type=MESH)

    for k, job in enumerate(jobs):
        near, far, group, s1, r1, s2, r2 = rest[7 * k:7 * k + 7]
        for s in range(1, job.inner):
            p = lax.rem(job.i + s, job.inner)
            across(job, ins[k], near, s1, r1, p, job.i).start()
    parts = []
    for k, job in enumerate(jobs):
        near, far, group, s1, r1, s2, r2 = rest[7 * k:7 * k + 7]
        for s in range(1, job.inner):
            p = lax.rem(job.i + s, job.inner)
            across(job, ins[k], near, s1, r1, p, job.i).wait_send()
            across(job, ins[k], near, s1, r1, p, p).wait_recv()
        own = ins[k][...]
        total = own
        part = own if job.mode == "sum" else jnp.zeros_like(own)
        for s in range(1, job.inner):
            p = lax.rem(job.i + s, job.inner)
            block = near[p]
            total = total + block
            if job.mode == "sum":
                part = part + block
            else:
                part = part + jnp.where(wanted(job.mode, p, job.i), block, 0.0)
        group[...] = total
        parts.append(part)

    def up(job, group, far, s2, r2, q, landing):
        return pltpu.make_async_remote_copy(
            src_ref=group, dst_ref=far.at[landing], send_sem=s2.at[q], recv_sem=r2.at[landing],
            device_id=job.device(q * job.inner + job.i), device_id_type=MESH)

    for k, job in enumerate(jobs):
        near, far, group, s1, r1, s2, r2 = rest[7 * k:7 * k + 7]
        for s in range(1, job.outer):
            q = lax.rem(job.o + s, job.outer)

            @pl.when(wanted(job.mode, job.o, q))
            def _():
                up(job, group, far, s2, r2, q, job.o).start()

    for k, job in enumerate(jobs):
        near, far, group, s1, r1, s2, r2 = rest[7 * k:7 * k + 7]
        part = parts[k]
        for s in range(1, job.outer):
            q = lax.rem(job.o + s, job.outer)

            @pl.when(wanted(job.mode, job.o, q))
            def _():
                up(job, group, far, s2, r2, q, job.o).wait_send()

            @pl.when(wanted(job.mode, q, job.o))
            def _():
                up(job, group, far, s2, r2, q, q).wait_recv()

        for s in range(1, job.outer):
            q = lax.rem(job.o + s, job.outer)
            part = part + jnp.where(wanted(job.mode, q, job.o), far[q], 0.0)
        outs[k][...] = part


def dual_kernel(
    sloc_ref, t_ref, off_ref, off_next_ref, beyond_ref, rim_own_ref, rim_next_ref,
    near, far, group, beyond_buf, rim_src_own, rim_src_next, rim_own_buf, rim_next_buf,
    off_src, off_next_buf, s1, r1, s2, r2, sems,
):
    job = Job("hours", "suffix", 8, lax.axis_size("hours"))
    job.place()
    n_r = lax.axis_size("river")
    n_h = lax.axis_size("hours")
    r = lax.axis_index("river")
    h = lax.axis_index("hours")
    has_up, has_down = r > 0, r < n_r - 1
    has_before, has_after = h > 0, h < n_h - 1

    barrier = pltpu.get_barrier_semaphore()
    for dev in job.peers():
        pl.semaphore_signal(barrier, 1, device_id=dev, device_id_type=MESH)
    for flag, dev in ((has_up, (r - 1, h)), (has_down, (r + 1, h)), (has_before, (r, h - 1)), (has_after, (r, h + 1))):

        @pl.when(flag)
        def _():
            pl.semaphore_signal(barrier, 1, device_id=dev, device_id_type=MESH)

    extra = sum(jnp.where(flag, 1, 0) for flag in (has_up, has_down, has_before, has_after))
    pl.semaphore_wait(barrier, job.inner + job.outer - 2 + extra)

    def link(src, dst, k, dev):
        return pltpu.make_async_remote_copy(
            src_ref=src, dst_ref=dst, send_sem=sems.at[2 * k], recv_sem=sems.at[2 * k + 1],
            device_id=dev, device_id_type=MESH)

    to_up = lambda src, dst, k: link(src, dst, k, (r - 1, h))
    to_before = lambda src, dst, k: link(src, dst, k, (r, h - 1))

    def across(p, landing):
        return pltpu.make_async_remote_copy(
            src_ref=t_ref, dst_ref=near.at[landing], send_sem=s1.at[p], recv_sem=r1.at[landing],
            device_id=job.device(job.o * job.inner + p), device_id_type=MESH)

    for s in range(1, job.inner):
        across(lax.rem(job.i + s, job.inner), job.i).start()

    @pl.when(has_up)
    def _():
        to_up(sloc_ref, beyond_buf, 0).start()

    rim_src_own[...] = sloc_ref[:, 0:DMAX, :] - sloc_ref[:, 0:1, :]

    @pl.when(has_before)
    def _():
        to_before(rim_src_own, rim_own_buf, 1).start()

    for s in range(1, job.inner):
        p = lax.rem(job.i + s, job.inner)
        across(p, job.i).wait_send()
        across(p, p).wait_recv()
    own = t_ref[...]
    total = own
    part = jnp.zeros_like(own)
    for s in range(1, job.inner):
        p = lax.rem(job.i + s, job.inner)
        block = near[p]
        total = total + block
        part = part + jnp.where(p > job.i, block, 0.0)
    group[...] = total

    def up(q, landing):
        return pltpu.make_async_remote_copy(
            src_ref=group, dst_ref=far.at[landing], send_sem=s2.at[q], recv_sem=r2.at[landing],
            device_id=job.device(q * job.inner + job.i), device_id_type=MESH)

    for s in range(1, job.outer):
        q = lax.rem(job.o + s, job.outer)

        @pl.when(job.o > q)
        def _():
            up(q, job.o).start()

    @pl.when(has_down)
    def _():
        to_up(sloc_ref, beyond_buf, 0).wait_recv()
        rim_src_next[...] = beyond_buf[:, 0:DMAX, :] - beyond_buf[:, 0:1, :]

    @pl.when(jnp.logical_and(has_down, has_before))
    def _():
        to_before(rim_src_next, rim_next_buf, 2).start()

    for s in range(1, job.outer):
        q = lax.rem(job.o + s, job.outer)

        @pl.when(job.o > q)
        def _():
            up(q, job.o).wait_send()

        @pl.when(q > job.o)
        def _():
            up(q, q).wait_recv()

    for s in range(1, job.outer):
        q = lax.rem(job.o + s, job.outer)
        part = part + jnp.where(q > job.o, far[q], 0.0)
    off_src[...] = part
    off_ref[...] = part

    @pl.when(has_up)
    def _():
        to_up(off_src, off_next_buf, 3).start()

    @pl.when(has_up)
    def _():
        to_up(sloc_ref, beyond_buf, 0).wait_send()
        to_up(off_src, off_next_buf, 3).wait_send()

    @pl.when(has_before)
    def _():
        to_before(rim_src_own, rim_own_buf, 1).wait_send()

    @pl.when(jnp.logical_and(has_down, has_before))
    def _():
        to_before(rim_src_next, rim_next_buf, 2).wait_send()

    @pl.when(has_after)
    def _():
        to_before(rim_src_own, rim_own_buf, 1).wait_recv()
        rim_own_ref[...] = rim_own_buf[...]

    @pl.when(jnp.logical_not(has_after))
    def _():
        rim_own_ref[...] = jnp.zeros_like(rim_own_ref)

    @pl.when(jnp.logical_and(has_down, has_after))
    def _():
        to_before(rim_src_next, rim_next_buf, 2).wait_recv()
        rim_next_ref[...] = rim_next_buf[...]

    @pl.when(jnp.logical_not(jnp.logical_and(has_down, has_after)))
    def _():
        rim_next_ref[...] = jnp.zeros_like(rim_next_ref)

    @pl.when(has_down)
    def _():
        to_up(off_src, off_next_buf, 3).wait_recv()
        off_next_ref[...] = off_next_buf[...]
        beyond_ref[...] = beyond_buf[...]

    @pl.when(jnp.logical_not(has_down))
    def _():
        off_next_ref[...] = jnp.zeros_like(off_next_ref)
        beyond_ref[...] = jnp.zeros_like(beyond_ref)


def dual_exchange(sloc):
    res, length, width = sloc.shape
    t = sloc[:, 0].reshape(-1, 128)
    inner = 8
    outer = lax.axis_size("hours") // inner
    rim = (res, DMAX, width)
    vmem = pl.BlockSpec(memory_space=pltpu.VMEM)
    off, off_next, beyond, rim_own, rim_next = pl.pallas_call(
        dual_kernel,
        out_shape=[
            jax.ShapeDtypeStruct(t.shape, t.dtype),
            jax.ShapeDtypeStruct(t.shape, t.dtype),
            jax.ShapeDtypeStruct(sloc.shape, sloc.dtype),
            jax.ShapeDtypeStruct(rim, sloc.dtype),
            jax.ShapeDtypeStruct(rim, sloc.dtype),
        ],
        in_specs=[vmem, vmem],
        out_specs=[vmem] * 5,
        scratch_shapes=[
            pltpu.VMEM((inner,) + t.shape, t.dtype),
            pltpu.VMEM((outer,) + t.shape, t.dtype),
            pltpu.VMEM(t.shape, t.dtype),
            pltpu.VMEM(sloc.shape, sloc.dtype),
            pltpu.VMEM(rim, sloc.dtype),
            pltpu.VMEM(rim, sloc.dtype),
            pltpu.VMEM(rim, sloc.dtype),
            pltpu.VMEM(rim, sloc.dtype),
            pltpu.VMEM(t.shape, t.dtype),
            pltpu.VMEM(t.shape, t.dtype),
            pltpu.SemaphoreType.DMA((inner,)),
            pltpu.SemaphoreType.DMA((inner,)),
            pltpu.SemaphoreType.DMA((outer,)),
            pltpu.SemaphoreType.DMA((outer,)),
            pltpu.SemaphoreType.DMA((8,)),
        ],
        compiler_params=pltpu.CompilerParams(collective_id=0, has_side_effects=True, vmem_limit_bytes=48 * 1024 * 1024),
    )(sloc, t)
    return off.reshape(res, width), off_next.reshape(res, width), beyond, rim_own, rim_next


def flow_kernel(
    main_ref, rim_own_ref, rim_next_ref, a_ref, b_ref, power_ref,
    incoming_ref, rim_own_in_ref, rim_next_in_ref, pa_ref, supplied_ref,
    near_h, far_h, group_h, near_r, far_r, group_r, incoming_buf, rim_own_buf, rim_next_buf,
    a_src, b_buf, s1h, r1h, s2h, r2h, s1r, r1r, s2r, r2r, sems,
):
    jobs = [Job("hours", "prefix", 8, lax.axis_size("hours")), Job("river", "sum", 8, lax.axis_size("river"))]
    for job in jobs:
        job.place()
    n_r = lax.axis_size("river")
    n_h = lax.axis_size("hours")
    r = lax.axis_index("river")
    h = lax.axis_index("hours")
    has_up, has_down = r > 0, r < n_r - 1
    has_before, has_after = h > 0, h < n_h - 1
    diag_down = jnp.logical_and(has_down, has_after)
    diag_up = jnp.logical_and(has_up, has_before)

    barrier = pltpu.get_barrier_semaphore()
    fixed = 0
    for job in jobs:
        for dev in job.peers():
            pl.semaphore_signal(barrier, 1, device_id=dev, device_id_type=MESH)
            fixed += 1
    links = (
        (has_up, (r - 1, h)), (has_down, (r + 1, h)), (has_before, (r, h - 1)), (has_after, (r, h + 1)),
        (diag_down, (r + 1, h + 1)), (diag_up, (r - 1, h - 1)),
    )
    for flag, dev in links:

        @pl.when(flag)
        def _():
            pl.semaphore_signal(barrier, 1, device_id=dev, device_id_type=MESH)

    extra = sum(jnp.where(flag, 1, 0) for flag, _ in links)
    pl.semaphore_wait(barrier, fixed + extra)

    def link(src, dst, k, dev):
        return pltpu.make_async_remote_copy(
            src_ref=src, dst_ref=dst, send_sem=sems.at[2 * k], recv_sem=sems.at[2 * k + 1],
            device_id=dev, device_id_type=MESH)

    main_copy = link(main_ref, incoming_buf, 0, (r + 1, h))
    rim_own_copy = link(rim_own_ref, rim_own_buf, 1, (r, h + 1))
    rim_next_copy = link(rim_next_ref, rim_next_buf, 2, (r + 1, h + 1))
    b_copy = link(b_ref, b_buf, 3, (r + 1, h))

    @pl.when(has_down)
    def _():
        b_copy.start()
        main_copy.start()

    @pl.when(has_after)
    def _():
        rim_own_copy.start()

    @pl.when(diag_down)
    def _():
        rim_next_copy.start()

    bufs = [(a_src, near_h, far_h, group_h, s1h, r1h, s2h, r2h), (power_ref, near_r, far_r, group_r, s1r, r1r, s2r, r2r)]

    def across(job, x_ref, near, s1, r1, p, landing):
        return pltpu.make_async_remote_copy(
            src_ref=x_ref, dst_ref=near.at[landing], send_sem=s1.at[p], recv_sem=r1.at[landing],
            device_id=job.device(job.o * job.inner + p), device_id_type=MESH)

    for job, (x_ref, near, far, group, s1, r1, s2, r2) in zip(jobs[::-1], bufs[::-1]):
        if job.axis == "hours":

            @pl.when(has_up)
            def _():
                b_copy.wait_recv()
                a_src[...] = a_ref[...] + b_buf[...]

            @pl.when(jnp.logical_not(has_up))
            def _():
                a_src[...] = a_ref[...]

        for s in range(1, job.inner):
            across(job, x_ref, near, s1, r1, lax.rem(job.i + s, job.inner), job.i).start()
    parts = []
    for job, (x_ref, near, far, group, s1, r1, s2, r2) in zip(jobs, bufs):
        for s in range(1, job.inner):
            p = lax.rem(job.i + s, job.inner)
            across(job, x_ref, near, s1, r1, p, job.i).wait_send()
            across(job, x_ref, near, s1, r1, p, p).wait_recv()
        own = x_ref[...]
        total = own
        part = own if job.mode == "sum" else jnp.zeros_like(own)
        for s in range(1, job.inner):
            p = lax.rem(job.i + s, job.inner)
            block = near[p]
            total = total + block
            if job.mode == "sum":
                part = part + block
            else:
                part = part + jnp.where(wanted(job.mode, p, job.i), block, 0.0)
        group[...] = total
        parts.append(part)

    def up(job, group, far, s2, r2, q, landing):
        return pltpu.make_async_remote_copy(
            src_ref=group, dst_ref=far.at[landing], send_sem=s2.at[q], recv_sem=r2.at[landing],
            device_id=job.device(q * job.inner + job.i), device_id_type=MESH)

    for job, (x_ref, near, far, group, s1, r1, s2, r2) in zip(jobs, bufs):
        for s in range(1, job.outer):
            q = lax.rem(job.o + s, job.outer)

            @pl.when(wanted(job.mode, job.o, q))
            def _():
                up(job, group, far, s2, r2, q, job.o).start()

    results = []
    for job, part, (x_ref, near, far, group, s1, r1, s2, r2) in zip(jobs, parts, bufs):
        for s in range(1, job.outer):
            q = lax.rem(job.o + s, job.outer)

            @pl.when(wanted(job.mode, job.o, q))
            def _():
                up(job, group, far, s2, r2, q, job.o).wait_send()

            @pl.when(wanted(job.mode, q, job.o))
            def _():
                up(job, group, far, s2, r2, q, q).wait_recv()

        for s in range(1, job.outer):
            q = lax.rem(job.o + s, job.outer)
            part = part + jnp.where(wanted(job.mode, q, job.o), far[q], 0.0)
        results.append(part)
    scanned, supplied = results
    pa_ref[...] = scanned
    supplied_ref[...] = supplied

    @pl.when(has_down)
    def _():
        main_copy.wait_send()
        b_copy.wait_send()

    @pl.when(has_after)
    def _():
        rim_own_copy.wait_send()

    @pl.when(diag_down)
    def _():
        rim_next_copy.wait_send()

    @pl.when(has_up)
    def _():
        main_copy.wait_recv()
        incoming_ref[...] = incoming_buf[...]

    @pl.when(jnp.logical_not(has_up))
    def _():
        incoming_ref[...] = jnp.zeros_like(incoming_ref)

    @pl.when(has_before)
    def _():
        rim_own_copy.wait_recv()
        rim_own_in_ref[...] = rim_own_buf[...]

    @pl.when(jnp.logical_not(has_before))
    def _():
        rim_own_in_ref[...] = jnp.zeros_like(rim_own_in_ref)

    @pl.when(diag_up)
    def _():
        rim_next_copy.wait_recv()
        rim_next_in_ref[...] = rim_next_buf[...]

    @pl.when(jnp.logical_not(diag_up))
    def _():
        rim_next_in_ref[...] = jnp.zeros_like(rim_next_in_ref)


def flow_exchange(main_next, rim_own, rim_next, own_totals, next_totals, power):
    res, width = own_totals.shape
    a = own_totals.reshape(-1, 128)
    b = next_totals.reshape(-1, 128)
    flat_power = power.reshape(-1, 128)
    inner = 8
    outer_h = lax.axis_size("hours") // inner
    outer_r = lax.axis_size("river") // inner
    vmem = pl.BlockSpec(memory_space=pltpu.VMEM)
    shape = lambda x: jax.ShapeDtypeStruct(x.shape, x.dtype)
    incoming, rim_own_in, rim_next_in, pa, supplied = pl.pallas_call(
        flow_kernel,
        out_shape=[shape(main_next), shape(rim_own), shape(rim_next), shape(a), shape(flat_power)],
        in_specs=[vmem] * 6,
        out_specs=[vmem] * 5,
        scratch_shapes=[
            pltpu.VMEM((inner,) + a.shape, a.dtype),
            pltpu.VMEM((outer_h,) + a.shape, a.dtype),
            pltpu.VMEM(a.shape, a.dtype),
            pltpu.VMEM((inner,) + flat_power.shape, a.dtype),
            pltpu.VMEM((outer_r,) + flat_power.shape, a.dtype),
            pltpu.VMEM(flat_power.shape, a.dtype),
            pltpu.VMEM(main_next.shape, a.dtype),
            pltpu.VMEM(rim_own.shape, a.dtype),
            pltpu.VMEM(rim_next.shape, a.dtype),
            pltpu.VMEM(a.shape, a.dtype),
            pltpu.VMEM(a.shape, a.dtype),
            pltpu.SemaphoreType.DMA((inner,)),
            pltpu.SemaphoreType.DMA((inner,)),
            pltpu.SemaphoreType.DMA((outer_h,)),
            pltpu.SemaphoreType.DMA((outer_h,)),
            pltpu.SemaphoreType.DMA((inner,)),
            pltpu.SemaphoreType.DMA((inner,)),
            pltpu.SemaphoreType.DMA((outer_r,)),
            pltpu.SemaphoreType.DMA((outer_r,)),
            pltpu.SemaphoreType.DMA((8,)),
        ],
        compiler_params=pltpu.CompilerParams(collective_id=1, has_side_effects=True, vmem_limit_bytes=48 * 1024 * 1024),
    )(main_next, rim_own, rim_next, a, b, flat_power)
    return incoming, rim_own_in, rim_next_in, pa.reshape(res, width), supplied.reshape(power.shape)


def combine(parts, specs, collective):
    shapes = [part.shape for part in parts]
    parts = [part.reshape(-1, 128) for part in parts]
    jobs = [Job(axis, mode, inner, lax.axis_size(axis)) for axis, mode, inner in specs]
    scratch = []
    for part, job in zip(parts, jobs):
        scratch += [
            pltpu.VMEM((job.inner,) + part.shape, part.dtype),
            pltpu.VMEM((job.outer,) + part.shape, part.dtype),
            pltpu.VMEM(part.shape, part.dtype),
            pltpu.SemaphoreType.DMA((job.inner,)),
            pltpu.SemaphoreType.DMA((job.inner,)),
            pltpu.SemaphoreType.DMA((job.outer,)),
            pltpu.SemaphoreType.DMA((job.outer,)),
        ]
    results = pl.pallas_call(
        functools.partial(multi_kernel, jobs),
        out_shape=[jax.ShapeDtypeStruct(part.shape, part.dtype) for part in parts],
        in_specs=[pl.BlockSpec(memory_space=pltpu.VMEM)] * len(parts),
        out_specs=[pl.BlockSpec(memory_space=pltpu.VMEM)] * len(parts),
        scratch_shapes=scratch,
        compiler_params=pltpu.CompilerParams(collective_id=collective, has_side_effects=True),
    )(*parts)
    return [result.reshape(shape) for result, shape in zip(results, shapes)]


def add_pair(earlier_part, later_part):
    return earlier_part + later_part


def hold_back(field, travel_delay, earlier_rim):
    length = field.shape[1]
    extended = jnp.concatenate([earlier_rim, field], 1)
    result = jnp.zeros_like(field)
    for lag_hours in range(1, DMAX + 1):
        window = extended[:, DMAX - lag_hours : DMAX - lag_hours + length]
        result = result + jnp.where((travel_delay == lag_hours)[:, None, None], window, 0.0)
    return result


def bring_forward(field, travel_delay, later_rim):
    length = field.shape[1]
    extended = jnp.concatenate([field, later_rim], 1)
    result = jnp.zeros_like(field)
    for lag_hours in range(1, DMAX + 1):
        window = extended[:, lag_hours : lag_hours + length]
        result = result + jnp.where((travel_delay == lag_hours)[:, None, None], window, 0.0)
    return result


def route_down(matrix, field):
    return jnp.einsum("ij,jtw->itw", matrix, field, precision=lax.Precision.HIGHEST)


def route_up(matrix, field):
    return jnp.einsum("ij,itw->jtw", matrix, field, precision=lax.Precision.HIGHEST)


def iterate(fields, statics, scales, suffix_sum, from_earlier, from_later):
    release, storage_dual, demand_dual, cost, inflow, demand = fields
    (
        storage_start,
        storage_low,
        storage_high,
        release_cap,
        efficiency,
        travel_delay,
        to_own,
        to_next,
    ) = statics
    scale_time, scale_sum = scales
    local = suffix_local(storage_dual)
    off, off_next, beyond, rim_own, rim_next = dual_exchange(local)
    suffix = local + off[:, None]
    at_sink = route_up(to_own, suffix) + route_up(to_next, beyond + off_next[:, None])
    last = lax.axis_index("hours") == lax.axis_size("hours") - 1
    rim_sink = route_up(to_own, rim_own + off[:, None]) + route_up(to_next, rim_next + off_next[:, None])
    later_duals = bring_forward(at_sink, travel_delay, jnp.where(last, 0.0, rim_sink))
    gradient = (
        cost
        + scale_time * (later_duals - suffix)
        + scale_sum * efficiency[:, None, None] * demand_dual[None]
    )
    release_new = jnp.clip(release - primal_step * gradient, 0.0, release_cap[:, None, None])
    extrapolated = 2.0 * release_new - release
    length = extrapolated.shape[1]
    tail = extrapolated[:, length - DMAX :]
    settled = hold_back(extrapolated, travel_delay, jnp.zeros_like(tail))
    rim_delayed = hold_back(jnp.zeros_like(extrapolated), travel_delay, tail)[:, :DMAX]
    main_own = route_down(to_own, settled)
    main_next = route_down(to_next, settled)
    rim_own = route_down(to_own, rim_delayed)
    rim_next = route_down(to_next, rim_delayed)
    base = inflow + main_own - extrapolated
    own_totals = jnp.sum(base, 1) + jnp.sum(rim_own, 1)
    next_totals = jnp.sum(main_next, 1) + jnp.sum(rim_next, 1)
    partial_power = jnp.sum(scale_sum * efficiency[:, None, None] * extrapolated, 0)
    incoming, rim_own_in, rim_next_in, offset, supplied = flow_exchange(
        main_next, rim_own, rim_next, own_totals, next_totals, partial_power
    )
    arrived = jnp.concatenate([rim_own_in + rim_next_in, jnp.zeros_like(base[:, DMAX:])], 1)
    local_sum = jnp.cumsum(base + incoming + arrived, 1)
    offset = offset - jnp.sum(rim_own_in, 1) - jnp.sum(rim_next_in, 1)
    storage = storage_start[:, None, None] + scale_time * (local_sum + offset[:, None])
    lower_bound = storage_low[:, None, None]
    upper_bound = storage_high[:, None, None]
    storage_dual_new = (
        storage_dual
        + dual_step * storage
        - dual_step * jnp.clip(storage_dual / dual_step + storage, lower_bound, upper_bound)
    )
    storage_excess = storage - jnp.clip(storage, lower_bound, upper_bound)
    demand_dual_new = jnp.minimum(demand_dual + dual_step * (supplied - demand), 0.0)
    return (release_new, storage_dual_new, demand_dual_new, storage_excess)


def suffix_local(field):
    return lax.cumsum(field, 1, reverse=True)


def shards(
    release,
    storage_dual,
    demand_dual,
    cost,
    inflow,
    demand,
    storage_start,
    storage_low,
    storage_high,
    release_cap,
    efficiency,
    downstream,
    travel_delay,
):
    res_dev = release.shape[0]
    scale_time = 1.0 / (release.shape[1] * lax.axis_size("hours"))
    scale_sum = 1.0 / math.sqrt(res_dev * lax.axis_size("river"))
    base_index = lax.axis_index("river") * res_dev
    target = downstream - base_index
    indices = jnp.arange(res_dev, dtype=jnp.int32)
    to_own = (target[None, :] == indices[:, None]).astype(jnp.float32)
    to_next = (target[None, :] == indices[:, None] + res_dev).astype(jnp.float32)
    statics = (
        storage_start,
        storage_low,
        storage_high,
        release_cap,
        efficiency,
        travel_delay,
        to_own,
        to_next,
    )
    scales = (scale_time, scale_sum)

    def suffix_blocks(field):
        local_sum = suffix_local(field)
        totals = local_sum[:, 0]
        (offset,) = combine([totals], [("hours", "suffix", 8)], 0)
        return local_sum + offset[:, None]

    def earlier_block(part):
        return passed_along(part, "hours", 1)

    def later_block(part):
        return passed_along(part, "hours", -1)

    fields = (release, storage_dual, demand_dual, cost, inflow, demand)
    return iterate(
        fields, statics, scales, suffix_blocks, earlier_block, later_block
    )


def solution(mesh):
    return jax.shard_map(
        shards,
        mesh=mesh,
        in_specs=(
            P("river", "hours", None),
            P("river", "hours", None),
            P("hours", None),
            P("river", "hours", None),
            P("river", "hours", None),
            P("hours", None),
            P("river"),
            P("river"),
            P("river"),
            P("river"),
            P("river"),
            P("river"),
            P("river"),
        ),
        out_specs=(
            P("river", "hours", None),
            P("river", "hours", None),
            P("hours", None),
            P("river", "hours", None),
        ),
        check_vma=False,
    )
```

```python
import functools
import math

import jax
import jax.numpy as jnp
from jax import lax
from jax.experimental import pallas as pl
from jax.experimental.pallas import tpu as pltpu
from jax.sharding import PartitionSpec as P

DMAX = 6
HOURS_INNER = 4


primal_step = 1.0
dual_step = 0.1


def passed_along(block, axis, distance):
    devices = range(lax.axis_size(axis))
    route = [(i - distance, i) for i in devices if i - distance in devices]
    return lax.ppermute(block, axis, route)


MESH = pl.DeviceIdType.MESH


def wanted(mode, src, dst):
    if mode == "prefix":
        return src < dst
    if mode == "suffix":
        return src > dst
    return src != dst


class Job:
    def __init__(self, axis, mode, inner, n):
        self.axis, self.mode, self.inner = axis, mode, inner
        self.outer = n // inner
        self.other = "river" if axis == "hours" else "hours"

    def place(self):
        me = lax.axis_index(self.axis)
        self.fixed = lax.axis_index(self.other)
        self.o = me // self.inner
        self.i = me % self.inner

    def device(self, p):
        return (self.fixed, p) if self.axis == "hours" else (p, self.fixed)

    def peers(self):
        inner, outer, o, i = self.inner, self.outer, self.o, self.i
        near = [self.device(o * inner + lax.rem(i + s, inner)) for s in range(1, inner)]
        far = [self.device(lax.rem(o + s, outer) * inner + i) for s in range(1, outer)]
        return near + far


def multi_kernel(jobs, *refs):
    count = len(jobs)
    ins, outs, rest = refs[:count], refs[count:2 * count], refs[2 * count:]
    for job in jobs:
        job.place()
    barrier = pltpu.get_barrier_semaphore()
    partners = 0
    for job in jobs:
        for dev in job.peers():
            pl.semaphore_signal(barrier, 1, device_id=dev, device_id_type=MESH)
            partners += 1
    pl.semaphore_wait(barrier, partners)

    def across(job, x_ref, near, s1, r1, p, landing):
        return pltpu.make_async_remote_copy(
            src_ref=x_ref, dst_ref=near.at[landing], send_sem=s1.at[p], recv_sem=r1.at[landing],
            device_id=job.device(job.o * job.inner + p), device_id_type=MESH)

    for k, job in enumerate(jobs):
        near, far, group, s1, r1, s2, r2 = rest[7 * k:7 * k + 7]
        for s in range(1, job.inner):
            p = lax.rem(job.i + s, job.inner)
            across(job, ins[k], near, s1, r1, p, job.i).start()
    parts = []
    for k, job in enumerate(jobs):
        near, far, group, s1, r1, s2, r2 = rest[7 * k:7 * k + 7]
        for s in range(1, job.inner):
            p = lax.rem(job.i + s, job.inner)
            across(job, ins[k], near, s1, r1, p, job.i).wait_send()
            across(job, ins[k], near, s1, r1, p, p).wait_recv()
        own = ins[k][...]
        total = own
        part = own if job.mode == "sum" else jnp.zeros_like(own)
        for s in range(1, job.inner):
            p = lax.rem(job.i + s, job.inner)
            block = near[p]
            total = total + block
            if job.mode == "sum":
                part = part + block
            else:
                part = part + jnp.where(wanted(job.mode, p, job.i), block, 0.0)
        group[...] = total
        parts.append(part)

    def up(job, group, far, s2, r2, q, landing):
        return pltpu.make_async_remote_copy(
            src_ref=group, dst_ref=far.at[landing], send_sem=s2.at[q], recv_sem=r2.at[landing],
            device_id=job.device(q * job.inner + job.i), device_id_type=MESH)

    for k, job in enumerate(jobs):
        near, far, group, s1, r1, s2, r2 = rest[7 * k:7 * k + 7]
        for s in range(1, job.outer):
            q = lax.rem(job.o + s, job.outer)

            @pl.when(wanted(job.mode, job.o, q))
            def _():
                up(job, group, far, s2, r2, q, job.o).start()

    for k, job in enumerate(jobs):
        near, far, group, s1, r1, s2, r2 = rest[7 * k:7 * k + 7]
        part = parts[k]
        for s in range(1, job.outer):
            q = lax.rem(job.o + s, job.outer)

            @pl.when(wanted(job.mode, job.o, q))
            def _():
                up(job, group, far, s2, r2, q, job.o).wait_send()

            @pl.when(wanted(job.mode, q, job.o))
            def _():
                up(job, group, far, s2, r2, q, q).wait_recv()

        for s in range(1, job.outer):
            q = lax.rem(job.o + s, job.outer)
            part = part + jnp.where(wanted(job.mode, q, job.o), far[q], 0.0)
        outs[k][...] = part


def dual_kernel(
    sloc_ref, t_ref, off_ref, off_next_ref, beyond_ref, rim_own_ref, rim_next_ref,
    near, far, group, beyond_buf, rim_src_own, rim_src_next, rim_own_buf, rim_next_buf,
    off_src, off_next_buf, s1, r1, s2, r2, sems,
):
    job = Job("hours", "suffix", HOURS_INNER, lax.axis_size("hours"))
    job.place()
    n_r = lax.axis_size("river")
    n_h = lax.axis_size("hours")
    r = lax.axis_index("river")
    h = lax.axis_index("hours")
    has_up, has_down = r > 0, r < n_r - 1
    has_before, has_after = h > 0, h < n_h - 1

    barrier = pltpu.get_barrier_semaphore()
    for dev in job.peers():
        pl.semaphore_signal(barrier, 1, device_id=dev, device_id_type=MESH)
    for flag, dev in ((has_up, (r - 1, h)), (has_down, (r + 1, h)), (has_before, (r, h - 1)), (has_after, (r, h + 1))):

        @pl.when(flag)
        def _():
            pl.semaphore_signal(barrier, 1, device_id=dev, device_id_type=MESH)

    extra = sum(jnp.where(flag, 1, 0) for flag in (has_up, has_down, has_before, has_after))
    pl.semaphore_wait(barrier, job.inner + job.outer - 2 + extra)

    def link(src, dst, k, dev):
        return pltpu.make_async_remote_copy(
            src_ref=src, dst_ref=dst, send_sem=sems.at[2 * k], recv_sem=sems.at[2 * k + 1],
            device_id=dev, device_id_type=MESH)

    to_up = lambda src, dst, k: link(src, dst, k, (r - 1, h))
    to_before = lambda src, dst, k: link(src, dst, k, (r, h - 1))

    def across(p, landing):
        return pltpu.make_async_remote_copy(
            src_ref=t_ref, dst_ref=near.at[landing], send_sem=s1.at[p], recv_sem=r1.at[landing],
            device_id=job.device(job.o * job.inner + p), device_id_type=MESH)

    for s in range(1, job.inner):
        across(lax.rem(job.i + s, job.inner), job.i).start()

    @pl.when(has_up)
    def _():
        to_up(sloc_ref, beyond_buf, 0).start()

    rim_src_own[...] = sloc_ref[:, 0:DMAX, :] - sloc_ref[:, 0:1, :]

    @pl.when(has_before)
    def _():
        to_before(rim_src_own, rim_own_buf, 1).start()

    for s in range(1, job.inner):
        p = lax.rem(job.i + s, job.inner)
        across(p, job.i).wait_send()
        across(p, p).wait_recv()
    own = t_ref[...]
    total = own
    part = jnp.zeros_like(own)
    for s in range(1, job.inner):
        p = lax.rem(job.i + s, job.inner)
        block = near[p]
        total = total + block
        part = part + jnp.where(p > job.i, block, 0.0)
    group[...] = total

    def up(q, landing):
        return pltpu.make_async_remote_copy(
            src_ref=group, dst_ref=far.at[landing], send_sem=s2.at[q], recv_sem=r2.at[landing],
            device_id=job.device(q * job.inner + job.i), device_id_type=MESH)

    for s in range(1, job.outer):
        q = lax.rem(job.o + s, job.outer)

        @pl.when(job.o > q)
        def _():
            up(q, job.o).start()

    @pl.when(has_down)
    def _():
        to_up(sloc_ref, beyond_buf, 0).wait_recv()
        rim_src_next[...] = beyond_buf[:, 0:DMAX, :] - beyond_buf[:, 0:1, :]

    @pl.when(jnp.logical_and(has_down, has_before))
    def _():
        to_before(rim_src_next, rim_next_buf, 2).start()

    for s in range(1, job.outer):
        q = lax.rem(job.o + s, job.outer)

        @pl.when(job.o > q)
        def _():
            up(q, job.o).wait_send()

        @pl.when(q > job.o)
        def _():
            up(q, q).wait_recv()

    for s in range(1, job.outer):
        q = lax.rem(job.o + s, job.outer)
        part = part + jnp.where(q > job.o, far[q], 0.0)
    off_src[...] = part
    off_ref[...] = part

    @pl.when(has_up)
    def _():
        to_up(off_src, off_next_buf, 3).start()

    @pl.when(has_up)
    def _():
        to_up(sloc_ref, beyond_buf, 0).wait_send()
        to_up(off_src, off_next_buf, 3).wait_send()

    @pl.when(has_before)
    def _():
        to_before(rim_src_own, rim_own_buf, 1).wait_send()

    @pl.when(jnp.logical_and(has_down, has_before))
    def _():
        to_before(rim_src_next, rim_next_buf, 2).wait_send()

    @pl.when(has_after)
    def _():
        to_before(rim_src_own, rim_own_buf, 1).wait_recv()
        rim_own_ref[...] = rim_own_buf[...]

    @pl.when(jnp.logical_not(has_after))
    def _():
        rim_own_ref[...] = jnp.zeros_like(rim_own_ref)

    @pl.when(jnp.logical_and(has_down, has_after))
    def _():
        to_before(rim_src_next, rim_next_buf, 2).wait_recv()
        rim_next_ref[...] = rim_next_buf[...]

    @pl.when(jnp.logical_not(jnp.logical_and(has_down, has_after)))
    def _():
        rim_next_ref[...] = jnp.zeros_like(rim_next_ref)

    @pl.when(has_down)
    def _():
        to_up(off_src, off_next_buf, 3).wait_recv()
        off_next_ref[...] = off_next_buf[...]
        beyond_ref[...] = beyond_buf[...]

    @pl.when(jnp.logical_not(has_down))
    def _():
        off_next_ref[...] = jnp.zeros_like(off_next_ref)
        beyond_ref[...] = jnp.zeros_like(beyond_ref)


def dual_exchange(sloc):
    res, length, width = sloc.shape
    t = sloc[:, 0].reshape(-1, 128)
    inner = HOURS_INNER
    outer = lax.axis_size("hours") // inner
    rim = (res, DMAX, width)
    vmem = pl.BlockSpec(memory_space=pltpu.VMEM)
    off, off_next, beyond, rim_own, rim_next = pl.pallas_call(
        dual_kernel,
        out_shape=[
            jax.ShapeDtypeStruct(t.shape, t.dtype),
            jax.ShapeDtypeStruct(t.shape, t.dtype),
            jax.ShapeDtypeStruct(sloc.shape, sloc.dtype),
            jax.ShapeDtypeStruct(rim, sloc.dtype),
            jax.ShapeDtypeStruct(rim, sloc.dtype),
        ],
        in_specs=[vmem, vmem],
        out_specs=[vmem] * 5,
        scratch_shapes=[
            pltpu.VMEM((inner,) + t.shape, t.dtype),
            pltpu.VMEM((outer,) + t.shape, t.dtype),
            pltpu.VMEM(t.shape, t.dtype),
            pltpu.VMEM(sloc.shape, sloc.dtype),
            pltpu.VMEM(rim, sloc.dtype),
            pltpu.VMEM(rim, sloc.dtype),
            pltpu.VMEM(rim, sloc.dtype),
            pltpu.VMEM(rim, sloc.dtype),
            pltpu.VMEM(t.shape, t.dtype),
            pltpu.VMEM(t.shape, t.dtype),
            pltpu.SemaphoreType.DMA((inner,)),
            pltpu.SemaphoreType.DMA((inner,)),
            pltpu.SemaphoreType.DMA((outer,)),
            pltpu.SemaphoreType.DMA((outer,)),
            pltpu.SemaphoreType.DMA((8,)),
        ],
        compiler_params=pltpu.CompilerParams(collective_id=0, has_side_effects=True, vmem_limit_bytes=48 * 1024 * 1024),
    )(sloc, t)
    return off.reshape(res, width), off_next.reshape(res, width), beyond, rim_own, rim_next


def flow_kernel(
    main_ref, rim_own_ref, rim_next_ref, a_ref, b_ref, power_ref,
    incoming_ref, rim_own_in_ref, rim_next_in_ref, pa_ref, supplied_ref,
    near_h, far_h, group_h, near_r, far_r, group_r, incoming_buf, rim_own_buf, rim_next_buf,
    a_src, b_buf, s1h, r1h, s2h, r2h, s1r, r1r, s2r, r2r, sems,
):
    jobs = [Job("hours", "prefix", HOURS_INNER, lax.axis_size("hours")), Job("river", "sum", 8, lax.axis_size("river"))]
    for job in jobs:
        job.place()
    n_r = lax.axis_size("river")
    n_h = lax.axis_size("hours")
    r = lax.axis_index("river")
    h = lax.axis_index("hours")
    has_up, has_down = r > 0, r < n_r - 1
    has_before, has_after = h > 0, h < n_h - 1
    diag_down = jnp.logical_and(has_down, has_after)
    diag_up = jnp.logical_and(has_up, has_before)

    barrier = pltpu.get_barrier_semaphore()
    fixed = 0
    for job in jobs:
        for dev in job.peers():
            pl.semaphore_signal(barrier, 1, device_id=dev, device_id_type=MESH)
            fixed += 1
    links = (
        (has_up, (r - 1, h)), (has_down, (r + 1, h)), (has_before, (r, h - 1)), (has_after, (r, h + 1)),
        (diag_down, (r + 1, h + 1)), (diag_up, (r - 1, h - 1)),
    )
    for flag, dev in links:

        @pl.when(flag)
        def _():
            pl.semaphore_signal(barrier, 1, device_id=dev, device_id_type=MESH)

    extra = sum(jnp.where(flag, 1, 0) for flag, _ in links)
    pl.semaphore_wait(barrier, fixed + extra)

    def link(src, dst, k, dev):
        return pltpu.make_async_remote_copy(
            src_ref=src, dst_ref=dst, send_sem=sems.at[2 * k], recv_sem=sems.at[2 * k + 1],
            device_id=dev, device_id_type=MESH)

    main_copy = link(main_ref, incoming_buf, 0, (r + 1, h))
    rim_own_copy = link(rim_own_ref, rim_own_buf, 1, (r, h + 1))
    rim_next_copy = link(rim_next_ref, rim_next_buf, 2, (r + 1, h + 1))
    b_copy = link(b_ref, b_buf, 3, (r + 1, h))

    @pl.when(has_down)
    def _():
        b_copy.start()
        main_copy.start()

    @pl.when(has_after)
    def _():
        rim_own_copy.start()

    @pl.when(diag_down)
    def _():
        rim_next_copy.start()

    bufs = [(a_src, near_h, far_h, group_h, s1h, r1h, s2h, r2h), (power_ref, near_r, far_r, group_r, s1r, r1r, s2r, r2r)]

    def across(job, x_ref, near, s1, r1, p, landing):
        return pltpu.make_async_remote_copy(
            src_ref=x_ref, dst_ref=near.at[landing], send_sem=s1.at[p], recv_sem=r1.at[landing],
            device_id=job.device(job.o * job.inner + p), device_id_type=MESH)

    for job, (x_ref, near, far, group, s1, r1, s2, r2) in zip(jobs[::-1], bufs[::-1]):
        if job.axis == "hours":

            @pl.when(has_up)
            def _():
                b_copy.wait_recv()
                a_src[...] = a_ref[...] + b_buf[...]

            @pl.when(jnp.logical_not(has_up))
            def _():
                a_src[...] = a_ref[...]

        for s in range(1, job.inner):
            across(job, x_ref, near, s1, r1, lax.rem(job.i + s, job.inner), job.i).start()
    parts = []
    for job, (x_ref, near, far, group, s1, r1, s2, r2) in zip(jobs, bufs):
        for s in range(1, job.inner):
            p = lax.rem(job.i + s, job.inner)
            across(job, x_ref, near, s1, r1, p, job.i).wait_send()
            across(job, x_ref, near, s1, r1, p, p).wait_recv()
        own = x_ref[...]
        total = own
        part = own if job.mode == "sum" else jnp.zeros_like(own)
        for s in range(1, job.inner):
            p = lax.rem(job.i + s, job.inner)
            block = near[p]
            total = total + block
            if job.mode == "sum":
                part = part + block
            else:
                part = part + jnp.where(wanted(job.mode, p, job.i), block, 0.0)
        group[...] = total
        parts.append(part)

    def up(job, group, far, s2, r2, q, landing):
        return pltpu.make_async_remote_copy(
            src_ref=group, dst_ref=far.at[landing], send_sem=s2.at[q], recv_sem=r2.at[landing],
            device_id=job.device(q * job.inner + job.i), device_id_type=MESH)

    for job, (x_ref, near, far, group, s1, r1, s2, r2) in zip(jobs, bufs):
        for s in range(1, job.outer):
            q = lax.rem(job.o + s, job.outer)

            @pl.when(wanted(job.mode, job.o, q))
            def _():
                up(job, group, far, s2, r2, q, job.o).start()

    results = []
    for job, part, (x_ref, near, far, group, s1, r1, s2, r2) in zip(jobs, parts, bufs):
        for s in range(1, job.outer):
            q = lax.rem(job.o + s, job.outer)

            @pl.when(wanted(job.mode, job.o, q))
            def _():
                up(job, group, far, s2, r2, q, job.o).wait_send()

            @pl.when(wanted(job.mode, q, job.o))
            def _():
                up(job, group, far, s2, r2, q, q).wait_recv()

        for s in range(1, job.outer):
            q = lax.rem(job.o + s, job.outer)
            part = part + jnp.where(wanted(job.mode, q, job.o), far[q], 0.0)
        results.append(part)
    scanned, supplied = results
    pa_ref[...] = scanned
    supplied_ref[...] = supplied

    @pl.when(has_down)
    def _():
        main_copy.wait_send()
        b_copy.wait_send()

    @pl.when(has_after)
    def _():
        rim_own_copy.wait_send()

    @pl.when(diag_down)
    def _():
        rim_next_copy.wait_send()

    @pl.when(has_up)
    def _():
        main_copy.wait_recv()
        incoming_ref[...] = incoming_buf[...]

    @pl.when(jnp.logical_not(has_up))
    def _():
        incoming_ref[...] = jnp.zeros_like(incoming_ref)

    @pl.when(has_before)
    def _():
        rim_own_copy.wait_recv()
        rim_own_in_ref[...] = rim_own_buf[...]

    @pl.when(jnp.logical_not(has_before))
    def _():
        rim_own_in_ref[...] = jnp.zeros_like(rim_own_in_ref)

    @pl.when(diag_up)
    def _():
        rim_next_copy.wait_recv()
        rim_next_in_ref[...] = rim_next_buf[...]

    @pl.when(jnp.logical_not(diag_up))
    def _():
        rim_next_in_ref[...] = jnp.zeros_like(rim_next_in_ref)


def flow_exchange(main_next, rim_own, rim_next, own_totals, next_totals, power):
    res, width = own_totals.shape
    a = own_totals.reshape(-1, 128)
    b = next_totals.reshape(-1, 128)
    flat_power = power.reshape(-1, 128)
    inner_h = HOURS_INNER
    inner = 8
    outer_h = lax.axis_size("hours") // inner_h
    outer_r = lax.axis_size("river") // inner
    vmem = pl.BlockSpec(memory_space=pltpu.VMEM)
    shape = lambda x: jax.ShapeDtypeStruct(x.shape, x.dtype)
    incoming, rim_own_in, rim_next_in, pa, supplied = pl.pallas_call(
        flow_kernel,
        out_shape=[shape(main_next), shape(rim_own), shape(rim_next), shape(a), shape(flat_power)],
        in_specs=[vmem] * 6,
        out_specs=[vmem] * 5,
        scratch_shapes=[
            pltpu.VMEM((inner_h,) + a.shape, a.dtype),
            pltpu.VMEM((outer_h,) + a.shape, a.dtype),
            pltpu.VMEM(a.shape, a.dtype),
            pltpu.VMEM((inner,) + flat_power.shape, a.dtype),
            pltpu.VMEM((outer_r,) + flat_power.shape, a.dtype),
            pltpu.VMEM(flat_power.shape, a.dtype),
            pltpu.VMEM(main_next.shape, a.dtype),
            pltpu.VMEM(rim_own.shape, a.dtype),
            pltpu.VMEM(rim_next.shape, a.dtype),
            pltpu.VMEM(a.shape, a.dtype),
            pltpu.VMEM(a.shape, a.dtype),
            pltpu.SemaphoreType.DMA((inner_h,)),
            pltpu.SemaphoreType.DMA((inner_h,)),
            pltpu.SemaphoreType.DMA((outer_h,)),
            pltpu.SemaphoreType.DMA((outer_h,)),
            pltpu.SemaphoreType.DMA((inner,)),
            pltpu.SemaphoreType.DMA((inner,)),
            pltpu.SemaphoreType.DMA((outer_r,)),
            pltpu.SemaphoreType.DMA((outer_r,)),
            pltpu.SemaphoreType.DMA((8,)),
        ],
        compiler_params=pltpu.CompilerParams(collective_id=1, has_side_effects=True, vmem_limit_bytes=48 * 1024 * 1024),
    )(main_next, rim_own, rim_next, a, b, flat_power)
    return incoming, rim_own_in, rim_next_in, pa.reshape(res, width), supplied.reshape(power.shape)


def combine(parts, specs, collective):
    shapes = [part.shape for part in parts]
    parts = [part.reshape(-1, 128) for part in parts]
    jobs = [Job(axis, mode, inner, lax.axis_size(axis)) for axis, mode, inner in specs]
    scratch = []
    for part, job in zip(parts, jobs):
        scratch += [
            pltpu.VMEM((job.inner,) + part.shape, part.dtype),
            pltpu.VMEM((job.outer,) + part.shape, part.dtype),
            pltpu.VMEM(part.shape, part.dtype),
            pltpu.SemaphoreType.DMA((job.inner,)),
            pltpu.SemaphoreType.DMA((job.inner,)),
            pltpu.SemaphoreType.DMA((job.outer,)),
            pltpu.SemaphoreType.DMA((job.outer,)),
        ]
    results = pl.pallas_call(
        functools.partial(multi_kernel, jobs),
        out_shape=[jax.ShapeDtypeStruct(part.shape, part.dtype) for part in parts],
        in_specs=[pl.BlockSpec(memory_space=pltpu.VMEM)] * len(parts),
        out_specs=[pl.BlockSpec(memory_space=pltpu.VMEM)] * len(parts),
        scratch_shapes=scratch,
        compiler_params=pltpu.CompilerParams(collective_id=collective, has_side_effects=True),
    )(*parts)
    return [result.reshape(shape) for result, shape in zip(results, shapes)]


def add_pair(earlier_part, later_part):
    return earlier_part + later_part


def hold_back(field, travel_delay, earlier_rim):
    length = field.shape[1]
    extended = jnp.concatenate([earlier_rim, field], 1)
    result = jnp.zeros_like(field)
    for lag_hours in range(1, DMAX + 1):
        window = extended[:, DMAX - lag_hours : DMAX - lag_hours + length]
        result = result + jnp.where((travel_delay == lag_hours)[:, None, None], window, 0.0)
    return result


def bring_forward(field, travel_delay, later_rim):
    length = field.shape[1]
    extended = jnp.concatenate([field, later_rim], 1)
    result = jnp.zeros_like(field)
    for lag_hours in range(1, DMAX + 1):
        window = extended[:, lag_hours : lag_hours + length]
        result = result + jnp.where((travel_delay == lag_hours)[:, None, None], window, 0.0)
    return result


def route_down(matrix, field):
    return jnp.einsum("ij,jtw->itw", matrix, field, precision=lax.Precision.HIGHEST)


def route_up(matrix, field):
    return jnp.einsum("ij,itw->jtw", matrix, field, precision=lax.Precision.HIGHEST)


def iterate(fields, statics, scales, suffix_sum, from_earlier, from_later):
    release, storage_dual, demand_dual, cost, inflow, demand = fields
    (
        storage_start,
        storage_low,
        storage_high,
        release_cap,
        efficiency,
        travel_delay,
        to_own,
        to_next,
    ) = statics
    scale_time, scale_sum = scales
    local = suffix_local(storage_dual)
    off, off_next, beyond, rim_own, rim_next = dual_exchange(local)
    suffix = local + off[:, None]
    at_sink = route_up(to_own, suffix) + route_up(to_next, beyond + off_next[:, None])
    last = lax.axis_index("hours") == lax.axis_size("hours") - 1
    rim_sink = route_up(to_own, rim_own + off[:, None]) + route_up(to_next, rim_next + off_next[:, None])
    later_duals = bring_forward(at_sink, travel_delay, jnp.where(last, 0.0, rim_sink))
    gradient = (
        cost
        + scale_time * (later_duals - suffix)
        + scale_sum * efficiency[:, None, None] * demand_dual[None]
    )
    release_new = jnp.clip(release - primal_step * gradient, 0.0, release_cap[:, None, None])
    extrapolated = 2.0 * release_new - release
    length = extrapolated.shape[1]
    tail = extrapolated[:, length - DMAX :]
    settled = hold_back(extrapolated, travel_delay, jnp.zeros_like(tail))
    rim_delayed = hold_back(jnp.zeros_like(extrapolated), travel_delay, tail)[:, :DMAX]
    main_own = route_down(to_own, settled)
    main_next = route_down(to_next, settled)
    rim_own = route_down(to_own, rim_delayed)
    rim_next = route_down(to_next, rim_delayed)
    base = inflow + main_own - extrapolated
    own_totals = jnp.sum(base, 1) + jnp.sum(rim_own, 1)
    next_totals = jnp.sum(main_next, 1) + jnp.sum(rim_next, 1)
    partial_power = jnp.sum(scale_sum * efficiency[:, None, None] * extrapolated, 0)
    incoming, rim_own_in, rim_next_in, offset, supplied = flow_exchange(
        main_next, rim_own, rim_next, own_totals, next_totals, partial_power
    )
    arrived = jnp.concatenate([rim_own_in + rim_next_in, jnp.zeros_like(base[:, DMAX:])], 1)
    local_sum = jnp.cumsum(base + incoming + arrived, 1)
    offset = offset - jnp.sum(rim_own_in, 1) - jnp.sum(rim_next_in, 1)
    storage = storage_start[:, None, None] + scale_time * (local_sum + offset[:, None])
    lower_bound = storage_low[:, None, None]
    upper_bound = storage_high[:, None, None]
    storage_dual_new = (
        storage_dual
        + dual_step * storage
        - dual_step * jnp.clip(storage_dual / dual_step + storage, lower_bound, upper_bound)
    )
    storage_excess = storage - jnp.clip(storage, lower_bound, upper_bound)
    demand_dual_new = jnp.minimum(demand_dual + dual_step * (supplied - demand), 0.0)
    return (release_new, storage_dual_new, demand_dual_new, storage_excess)


def suffix_local(field):
    return lax.cumsum(field, 1, reverse=True)


def shards(
    release,
    storage_dual,
    demand_dual,
    cost,
    inflow,
    demand,
    storage_start,
    storage_low,
    storage_high,
    release_cap,
    efficiency,
    downstream,
    travel_delay,
):
    res_dev = release.shape[0]
    scale_time = 1.0 / (release.shape[1] * lax.axis_size("hours"))
    scale_sum = 1.0 / math.sqrt(res_dev * lax.axis_size("river"))
    base_index = lax.axis_index("river") * res_dev
    target = downstream - base_index
    indices = jnp.arange(res_dev, dtype=jnp.int32)
    to_own = (target[None, :] == indices[:, None]).astype(jnp.float32)
    to_next = (target[None, :] == indices[:, None] + res_dev).astype(jnp.float32)
    statics = (
        storage_start,
        storage_low,
        storage_high,
        release_cap,
        efficiency,
        travel_delay,
        to_own,
        to_next,
    )
    scales = (scale_time, scale_sum)

    def suffix_blocks(field):
        local_sum = suffix_local(field)
        totals = local_sum[:, 0]
        (offset,) = combine([totals], [("hours", "suffix", 8)], 0)
        return local_sum + offset[:, None]

    def earlier_block(part):
        return passed_along(part, "hours", 1)

    def later_block(part):
        return passed_along(part, "hours", -1)

    fields = (release, storage_dual, demand_dual, cost, inflow, demand)
    return iterate(
        fields, statics, scales, suffix_blocks, earlier_block, later_block
    )


def solution(mesh):
    return jax.shard_map(
        shards,
        mesh=mesh,
        in_specs=(
            P("river", "hours", None),
            P("river", "hours", None),
            P("hours", None),
            P("river", "hours", None),
            P("river", "hours", None),
            P("hours", None),
            P("river"),
            P("river"),
            P("river"),
            P("river"),
            P("river"),
            P("river"),
            P("river"),
        ),
        out_specs=(
            P("river", "hours", None),
            P("river", "hours", None),
            P("hours", None),
            P("river", "hours", None),
        ),
        check_vma=False,
    )
```

```python
import functools
import math

import jax
import jax.numpy as jnp
from jax import lax
from jax.experimental import pallas as pl
from jax.experimental.pallas import tpu as pltpu
from jax.sharding import PartitionSpec as P

DMAX = 6


primal_step = 1.0
dual_step = 0.1


def passed_along(block, axis, distance):
    devices = range(lax.axis_size(axis))
    route = [(i - distance, i) for i in devices if i - distance in devices]
    return lax.ppermute(block, axis, route)


MESH = pl.DeviceIdType.MESH


def wanted(mode, src, dst):
    if mode == "prefix":
        return src < dst
    if mode == "suffix":
        return src > dst
    return src != dst


class Job:
    def __init__(self, axis, mode, inner, n):
        self.axis, self.mode, self.inner = axis, mode, inner
        self.outer = n // inner
        self.other = "river" if axis == "hours" else "hours"

    def place(self):
        me = lax.axis_index(self.axis)
        self.fixed = lax.axis_index(self.other)
        self.o = me // self.inner
        self.i = me % self.inner

    def device(self, p):
        return (self.fixed, p) if self.axis == "hours" else (p, self.fixed)

    def peers(self):
        inner, outer, o, i = self.inner, self.outer, self.o, self.i
        near = [self.device(o * inner + lax.rem(i + s, inner)) for s in range(1, inner)]
        far = [self.device(lax.rem(o + s, outer) * inner + i) for s in range(1, outer)]
        return near + far


def multi_kernel(jobs, *refs):
    count = len(jobs)
    ins, outs, rest = refs[:count], refs[count:2 * count], refs[2 * count:]
    for job in jobs:
        job.place()
    barrier = pltpu.get_barrier_semaphore()
    partners = 0
    for job in jobs:
        for dev in job.peers():
            pl.semaphore_signal(barrier, 1, device_id=dev, device_id_type=MESH)
            partners += 1
    pl.semaphore_wait(barrier, partners)

    def across(job, x_ref, near, s1, r1, p, landing):
        return pltpu.make_async_remote_copy(
            src_ref=x_ref, dst_ref=near.at[landing], send_sem=s1.at[p], recv_sem=r1.at[landing],
            device_id=job.device(job.o * job.inner + p), device_id_type=MESH)

    for k, job in enumerate(jobs):
        near, far, group, s1, r1, s2, r2 = rest[7 * k:7 * k + 7]
        for s in range(1, job.inner):
            p = lax.rem(job.i + s, job.inner)
            across(job, ins[k], near, s1, r1, p, job.i).start()
    parts = []
    for k, job in enumerate(jobs):
        near, far, group, s1, r1, s2, r2 = rest[7 * k:7 * k + 7]
        for s in range(1, job.inner):
            p = lax.rem(job.i + s, job.inner)
            across(job, ins[k], near, s1, r1, p, job.i).wait_send()
            across(job, ins[k], near, s1, r1, p, p).wait_recv()
        own = ins[k][...]
        total = own
        part = own if job.mode == "sum" else jnp.zeros_like(own)
        for s in range(1, job.inner):
            p = lax.rem(job.i + s, job.inner)
            block = near[p]
            total = total + block
            if job.mode == "sum":
                part = part + block
            else:
                part = part + jnp.where(wanted(job.mode, p, job.i), block, 0.0)
        group[...] = total
        parts.append(part)

    def up(job, group, far, s2, r2, q, landing):
        return pltpu.make_async_remote_copy(
            src_ref=group, dst_ref=far.at[landing], send_sem=s2.at[q], recv_sem=r2.at[landing],
            device_id=job.device(q * job.inner + job.i), device_id_type=MESH)

    for k, job in enumerate(jobs):
        near, far, group, s1, r1, s2, r2 = rest[7 * k:7 * k + 7]
        for s in range(1, job.outer):
            q = lax.rem(job.o + s, job.outer)

            @pl.when(wanted(job.mode, job.o, q))
            def _():
                up(job, group, far, s2, r2, q, job.o).start()

    for k, job in enumerate(jobs):
        near, far, group, s1, r1, s2, r2 = rest[7 * k:7 * k + 7]
        part = parts[k]
        for s in range(1, job.outer):
            q = lax.rem(job.o + s, job.outer)

            @pl.when(wanted(job.mode, job.o, q))
            def _():
                up(job, group, far, s2, r2, q, job.o).wait_send()

            @pl.when(wanted(job.mode, q, job.o))
            def _():
                up(job, group, far, s2, r2, q, q).wait_recv()

        for s in range(1, job.outer):
            q = lax.rem(job.o + s, job.outer)
            part = part + jnp.where(wanted(job.mode, q, job.o), far[q], 0.0)
        outs[k][...] = part


def dual_kernel(
    sloc_ref, t_ref, off_ref, off_next_ref, beyond_ref, rim_own_ref, rim_next_ref,
    near, far, group, beyond_buf, rim_src_own, rim_src_next, rim_own_buf, rim_next_buf,
    s_src, tn_buf, s1, r1, s2, r2, sems,
):
    job = Job("hours", "suffix", 8, lax.axis_size("hours"))
    job.place()
    n_r = lax.axis_size("river")
    n_h = lax.axis_size("hours")
    r = lax.axis_index("river")
    h = lax.axis_index("hours")
    has_up, has_down = r > 0, r < n_r - 1
    has_before, has_after = h > 0, h < n_h - 1

    barrier = pltpu.get_barrier_semaphore()
    for dev in job.peers():
        pl.semaphore_signal(barrier, 1, device_id=dev, device_id_type=MESH)
    for flag, dev in ((has_up, (r - 1, h)), (has_down, (r + 1, h)), (has_before, (r, h - 1)), (has_after, (r, h + 1))):

        @pl.when(flag)
        def _():
            pl.semaphore_signal(barrier, 1, device_id=dev, device_id_type=MESH)

    extra = sum(jnp.where(flag, 1, 0) for flag in (has_up, has_down, has_before, has_after))
    pl.semaphore_wait(barrier, job.inner + job.outer - 2 + extra)

    def link(src, dst, k, dev):
        return pltpu.make_async_remote_copy(
            src_ref=src, dst_ref=dst, send_sem=sems.at[2 * k], recv_sem=sems.at[2 * k + 1],
            device_id=dev, device_id_type=MESH)

    to_up = lambda src, dst, k: link(src, dst, k, (r - 1, h))
    to_before = lambda src, dst, k: link(src, dst, k, (r, h - 1))

    def across(p, landing):
        return pltpu.make_async_remote_copy(
            src_ref=s_src, dst_ref=near.at[landing], send_sem=s1.at[p], recv_sem=r1.at[landing],
            device_id=job.device(job.o * job.inner + p), device_id_type=MESH)

    t_copy = to_up(t_ref, tn_buf, 3)
    half = t_ref.shape[0]

    @pl.when(has_up)
    def _():
        t_copy.start()
        to_up(sloc_ref, beyond_buf, 0).start()

    s_src[0:half] = t_ref[...]

    @pl.when(has_down)
    def _():
        t_copy.wait_recv()
        s_src[half:] = tn_buf[...]

    @pl.when(jnp.logical_not(has_down))
    def _():
        s_src[half:] = jnp.zeros_like(tn_buf)

    for s in range(1, job.inner):
        across(lax.rem(job.i + s, job.inner), job.i).start()

    rim_src_own[...] = sloc_ref[:, 0:DMAX, :] - sloc_ref[:, 0:1, :]

    @pl.when(has_before)
    def _():
        to_before(rim_src_own, rim_own_buf, 1).start()

    for s in range(1, job.inner):
        p = lax.rem(job.i + s, job.inner)
        across(p, job.i).wait_send()
        across(p, p).wait_recv()
    own = s_src[...]
    total = own
    part = jnp.zeros_like(own)
    for s in range(1, job.inner):
        p = lax.rem(job.i + s, job.inner)
        block = near[p]
        total = total + block
        part = part + jnp.where(p > job.i, block, 0.0)
    group[...] = total

    def up(q, landing):
        return pltpu.make_async_remote_copy(
            src_ref=group, dst_ref=far.at[landing], send_sem=s2.at[q], recv_sem=r2.at[landing],
            device_id=job.device(q * job.inner + job.i), device_id_type=MESH)

    for s in range(1, job.outer):
        q = lax.rem(job.o + s, job.outer)

        @pl.when(job.o > q)
        def _():
            up(q, job.o).start()

    @pl.when(has_down)
    def _():
        to_up(sloc_ref, beyond_buf, 0).wait_recv()
        rim_src_next[...] = beyond_buf[:, 0:DMAX, :] - beyond_buf[:, 0:1, :]

    @pl.when(jnp.logical_and(has_down, has_before))
    def _():
        to_before(rim_src_next, rim_next_buf, 2).start()

    for s in range(1, job.outer):
        q = lax.rem(job.o + s, job.outer)

        @pl.when(job.o > q)
        def _():
            up(q, job.o).wait_send()

        @pl.when(q > job.o)
        def _():
            up(q, q).wait_recv()

    for s in range(1, job.outer):
        q = lax.rem(job.o + s, job.outer)
        part = part + jnp.where(q > job.o, far[q], 0.0)
    off_ref[...] = part[:half]
    off_next_ref[...] = part[half:]

    @pl.when(has_up)
    def _():
        to_up(sloc_ref, beyond_buf, 0).wait_send()
        t_copy.wait_send()

    @pl.when(has_before)
    def _():
        to_before(rim_src_own, rim_own_buf, 1).wait_send()

    @pl.when(jnp.logical_and(has_down, has_before))
    def _():
        to_before(rim_src_next, rim_next_buf, 2).wait_send()

    @pl.when(has_after)
    def _():
        to_before(rim_src_own, rim_own_buf, 1).wait_recv()
        rim_own_ref[...] = rim_own_buf[...]

    @pl.when(jnp.logical_not(has_after))
    def _():
        rim_own_ref[...] = jnp.zeros_like(rim_own_ref)

    @pl.when(jnp.logical_and(has_down, has_after))
    def _():
        to_before(rim_src_next, rim_next_buf, 2).wait_recv()
        rim_next_ref[...] = rim_next_buf[...]

    @pl.when(jnp.logical_not(jnp.logical_and(has_down, has_after)))
    def _():
        rim_next_ref[...] = jnp.zeros_like(rim_next_ref)

    @pl.when(has_down)
    def _():
        beyond_ref[...] = beyond_buf[...]

    @pl.when(jnp.logical_not(has_down))
    def _():
        beyond_ref[...] = jnp.zeros_like(beyond_ref)


def dual_exchange(sloc):
    res, length, width = sloc.shape
    t = sloc[:, 0].reshape(-1, 128)
    inner = 8
    outer = lax.axis_size("hours") // inner
    rim = (res, DMAX, width)
    vmem = pl.BlockSpec(memory_space=pltpu.VMEM)
    off, off_next, beyond, rim_own, rim_next = pl.pallas_call(
        dual_kernel,
        out_shape=[
            jax.ShapeDtypeStruct(t.shape, t.dtype),
            jax.ShapeDtypeStruct(t.shape, t.dtype),
            jax.ShapeDtypeStruct(sloc.shape, sloc.dtype),
            jax.ShapeDtypeStruct(rim, sloc.dtype),
            jax.ShapeDtypeStruct(rim, sloc.dtype),
        ],
        in_specs=[vmem, vmem],
        out_specs=[vmem] * 5,
        scratch_shapes=[
            pltpu.VMEM((inner, 2 * t.shape[0], 128), t.dtype),
            pltpu.VMEM((outer, 2 * t.shape[0], 128), t.dtype),
            pltpu.VMEM((2 * t.shape[0], 128), t.dtype),
            pltpu.VMEM(sloc.shape, sloc.dtype),
            pltpu.VMEM(rim, sloc.dtype),
            pltpu.VMEM(rim, sloc.dtype),
            pltpu.VMEM(rim, sloc.dtype),
            pltpu.VMEM(rim, sloc.dtype),
            pltpu.VMEM((2 * t.shape[0], 128), t.dtype),
            pltpu.VMEM(t.shape, t.dtype),
            pltpu.SemaphoreType.DMA((inner,)),
            pltpu.SemaphoreType.DMA((inner,)),
            pltpu.SemaphoreType.DMA((outer,)),
            pltpu.SemaphoreType.DMA((outer,)),
            pltpu.SemaphoreType.DMA((8,)),
        ],
        compiler_params=pltpu.CompilerParams(collective_id=0, has_side_effects=True, vmem_limit_bytes=48 * 1024 * 1024),
    )(sloc, t)
    return off.reshape(res, width), off_next.reshape(res, width), beyond, rim_own, rim_next


def flow_kernel(
    main_ref, rim_own_ref, rim_next_ref, a_ref, b_ref, power_ref,
    incoming_ref, rim_own_in_ref, rim_next_in_ref, pa_ref, supplied_ref,
    near_h, far_h, group_h, near_r, far_r, group_r, incoming_buf, rim_own_buf, rim_next_buf,
    a_src, b_buf, s1h, r1h, s2h, r2h, s1r, r1r, s2r, r2r, sems,
):
    jobs = [Job("hours", "prefix", 8, lax.axis_size("hours")), Job("river", "sum", 8, lax.axis_size("river"))]
    for job in jobs:
        job.place()
    n_r = lax.axis_size("river")
    n_h = lax.axis_size("hours")
    r = lax.axis_index("river")
    h = lax.axis_index("hours")
    has_up, has_down = r > 0, r < n_r - 1
    has_before, has_after = h > 0, h < n_h - 1
    diag_down = jnp.logical_and(has_down, has_after)
    diag_up = jnp.logical_and(has_up, has_before)

    barrier = pltpu.get_barrier_semaphore()
    fixed = 0
    for job in jobs:
        for dev in job.peers():
            pl.semaphore_signal(barrier, 1, device_id=dev, device_id_type=MESH)
            fixed += 1
    links = (
        (has_up, (r - 1, h)), (has_down, (r + 1, h)), (has_before, (r, h - 1)), (has_after, (r, h + 1)),
        (diag_down, (r + 1, h + 1)), (diag_up, (r - 1, h - 1)),
    )
    for flag, dev in links:

        @pl.when(flag)
        def _():
            pl.semaphore_signal(barrier, 1, device_id=dev, device_id_type=MESH)

    extra = sum(jnp.where(flag, 1, 0) for flag, _ in links)
    pl.semaphore_wait(barrier, fixed + extra)

    def link(src, dst, k, dev):
        return pltpu.make_async_remote_copy(
            src_ref=src, dst_ref=dst, send_sem=sems.at[2 * k], recv_sem=sems.at[2 * k + 1],
            device_id=dev, device_id_type=MESH)

    main_copy = link(main_ref, incoming_buf, 0, (r + 1, h))
    rim_own_copy = link(rim_own_ref, rim_own_buf, 1, (r, h + 1))
    rim_next_copy = link(rim_next_ref, rim_next_buf, 2, (r + 1, h + 1))
    b_copy = link(b_ref, b_buf, 3, (r + 1, h))

    @pl.when(has_down)
    def _():
        b_copy.start()
        main_copy.start()

    @pl.when(has_after)
    def _():
        rim_own_copy.start()

    @pl.when(diag_down)
    def _():
        rim_next_copy.start()

    bufs = [(a_src, near_h, far_h, group_h, s1h, r1h, s2h, r2h), (power_ref, near_r, far_r, group_r, s1r, r1r, s2r, r2r)]

    def across(job, x_ref, near, s1, r1, p, landing):
        return pltpu.make_async_remote_copy(
            src_ref=x_ref, dst_ref=near.at[landing], send_sem=s1.at[p], recv_sem=r1.at[landing],
            device_id=job.device(job.o * job.inner + p), device_id_type=MESH)

    for job, (x_ref, near, far, group, s1, r1, s2, r2) in zip(jobs[::-1], bufs[::-1]):
        if job.axis == "hours":

            @pl.when(has_up)
            def _():
                b_copy.wait_recv()
                a_src[...] = a_ref[...] + b_buf[...]

            @pl.when(jnp.logical_not(has_up))
            def _():
                a_src[...] = a_ref[...]

        for s in range(1, job.inner):
            across(job, x_ref, near, s1, r1, lax.rem(job.i + s, job.inner), job.i).start()
    parts = []
    for job, (x_ref, near, far, group, s1, r1, s2, r2) in zip(jobs, bufs):
        for s in range(1, job.inner):
            p = lax.rem(job.i + s, job.inner)
            across(job, x_ref, near, s1, r1, p, job.i).wait_send()
            across(job, x_ref, near, s1, r1, p, p).wait_recv()
        own = x_ref[...]
        total = own
        part = own if job.mode == "sum" else jnp.zeros_like(own)
        for s in range(1, job.inner):
            p = lax.rem(job.i + s, job.inner)
            block = near[p]
            total = total + block
            if job.mode == "sum":
                part = part + block
            else:
                part = part + jnp.where(wanted(job.mode, p, job.i), block, 0.0)
        group[...] = total
        parts.append(part)

    def up(job, group, far, s2, r2, q, landing):
        return pltpu.make_async_remote_copy(
            src_ref=group, dst_ref=far.at[landing], send_sem=s2.at[q], recv_sem=r2.at[landing],
            device_id=job.device(q * job.inner + job.i), device_id_type=MESH)

    for job, (x_ref, near, far, group, s1, r1, s2, r2) in zip(jobs, bufs):
        for s in range(1, job.outer):
            q = lax.rem(job.o + s, job.outer)

            @pl.when(wanted(job.mode, job.o, q))
            def _():
                up(job, group, far, s2, r2, q, job.o).start()

    results = []
    for job, part, (x_ref, near, far, group, s1, r1, s2, r2) in zip(jobs, parts, bufs):
        for s in range(1, job.outer):
            q = lax.rem(job.o + s, job.outer)

            @pl.when(wanted(job.mode, job.o, q))
            def _():
                up(job, group, far, s2, r2, q, job.o).wait_send()

            @pl.when(wanted(job.mode, q, job.o))
            def _():
                up(job, group, far, s2, r2, q, q).wait_recv()

        for s in range(1, job.outer):
            q = lax.rem(job.o + s, job.outer)
            part = part + jnp.where(wanted(job.mode, q, job.o), far[q], 0.0)
        results.append(part)
    scanned, supplied = results
    pa_ref[...] = scanned
    supplied_ref[...] = supplied

    @pl.when(has_down)
    def _():
        main_copy.wait_send()
        b_copy.wait_send()

    @pl.when(has_after)
    def _():
        rim_own_copy.wait_send()

    @pl.when(diag_down)
    def _():
        rim_next_copy.wait_send()

    @pl.when(has_up)
    def _():
        main_copy.wait_recv()
        incoming_ref[...] = incoming_buf[...]

    @pl.when(jnp.logical_not(has_up))
    def _():
        incoming_ref[...] = jnp.zeros_like(incoming_ref)

    @pl.when(has_before)
    def _():
        rim_own_copy.wait_recv()
        rim_own_in_ref[...] = rim_own_buf[...]

    @pl.when(jnp.logical_not(has_before))
    def _():
        rim_own_in_ref[...] = jnp.zeros_like(rim_own_in_ref)

    @pl.when(diag_up)
    def _():
        rim_next_copy.wait_recv()
        rim_next_in_ref[...] = rim_next_buf[...]

    @pl.when(jnp.logical_not(diag_up))
    def _():
        rim_next_in_ref[...] = jnp.zeros_like(rim_next_in_ref)


def flow_exchange(main_next, rim_own, rim_next, own_totals, next_totals, power):
    res, width = own_totals.shape
    a = own_totals.reshape(-1, 128)
    b = next_totals.reshape(-1, 128)
    flat_power = power.reshape(-1, 128)
    inner = 8
    outer_h = lax.axis_size("hours") // inner
    outer_r = lax.axis_size("river") // inner
    vmem = pl.BlockSpec(memory_space=pltpu.VMEM)
    shape = lambda x: jax.ShapeDtypeStruct(x.shape, x.dtype)
    incoming, rim_own_in, rim_next_in, pa, supplied = pl.pallas_call(
        flow_kernel,
        out_shape=[shape(main_next), shape(rim_own), shape(rim_next), shape(a), shape(flat_power)],
        in_specs=[vmem] * 6,
        out_specs=[vmem] * 5,
        scratch_shapes=[
            pltpu.VMEM((inner,) + a.shape, a.dtype),
            pltpu.VMEM((outer_h,) + a.shape, a.dtype),
            pltpu.VMEM(a.shape, a.dtype),
            pltpu.VMEM((inner,) + flat_power.shape, a.dtype),
            pltpu.VMEM((outer_r,) + flat_power.shape, a.dtype),
            pltpu.VMEM(flat_power.shape, a.dtype),
            pltpu.VMEM(main_next.shape, a.dtype),
            pltpu.VMEM(rim_own.shape, a.dtype),
            pltpu.VMEM(rim_next.shape, a.dtype),
            pltpu.VMEM(a.shape, a.dtype),
            pltpu.VMEM(a.shape, a.dtype),
            pltpu.SemaphoreType.DMA((inner,)),
            pltpu.SemaphoreType.DMA((inner,)),
            pltpu.SemaphoreType.DMA((outer_h,)),
            pltpu.SemaphoreType.DMA((outer_h,)),
            pltpu.SemaphoreType.DMA((inner,)),
            pltpu.SemaphoreType.DMA((inner,)),
            pltpu.SemaphoreType.DMA((outer_r,)),
            pltpu.SemaphoreType.DMA((outer_r,)),
            pltpu.SemaphoreType.DMA((8,)),
        ],
        compiler_params=pltpu.CompilerParams(collective_id=1, has_side_effects=True, vmem_limit_bytes=48 * 1024 * 1024),
    )(main_next, rim_own, rim_next, a, b, flat_power)
    return incoming, rim_own_in, rim_next_in, pa.reshape(res, width), supplied.reshape(power.shape)


def combine(parts, specs, collective):
    shapes = [part.shape for part in parts]
    parts = [part.reshape(-1, 128) for part in parts]
    jobs = [Job(axis, mode, inner, lax.axis_size(axis)) for axis, mode, inner in specs]
    scratch = []
    for part, job in zip(parts, jobs):
        scratch += [
            pltpu.VMEM((job.inner,) + part.shape, part.dtype),
            pltpu.VMEM((job.outer,) + part.shape, part.dtype),
            pltpu.VMEM(part.shape, part.dtype),
            pltpu.SemaphoreType.DMA((job.inner,)),
            pltpu.SemaphoreType.DMA((job.inner,)),
            pltpu.SemaphoreType.DMA((job.outer,)),
            pltpu.SemaphoreType.DMA((job.outer,)),
        ]
    results = pl.pallas_call(
        functools.partial(multi_kernel, jobs),
        out_shape=[jax.ShapeDtypeStruct(part.shape, part.dtype) for part in parts],
        in_specs=[pl.BlockSpec(memory_space=pltpu.VMEM)] * len(parts),
        out_specs=[pl.BlockSpec(memory_space=pltpu.VMEM)] * len(parts),
        scratch_shapes=scratch,
        compiler_params=pltpu.CompilerParams(collective_id=collective, has_side_effects=True),
    )(*parts)
    return [result.reshape(shape) for result, shape in zip(results, shapes)]


def add_pair(earlier_part, later_part):
    return earlier_part + later_part


def hold_back(field, travel_delay, earlier_rim):
    length = field.shape[1]
    extended = jnp.concatenate([earlier_rim, field], 1)
    result = jnp.zeros_like(field)
    for lag_hours in range(1, DMAX + 1):
        window = extended[:, DMAX - lag_hours : DMAX - lag_hours + length]
        result = result + jnp.where((travel_delay == lag_hours)[:, None, None], window, 0.0)
    return result


def bring_forward(field, travel_delay, later_rim):
    length = field.shape[1]
    extended = jnp.concatenate([field, later_rim], 1)
    result = jnp.zeros_like(field)
    for lag_hours in range(1, DMAX + 1):
        window = extended[:, lag_hours : lag_hours + length]
        result = result + jnp.where((travel_delay == lag_hours)[:, None, None], window, 0.0)
    return result


def route_down(matrix, field):
    return jnp.einsum("ij,jtw->itw", matrix, field, precision=lax.Precision.HIGHEST)


def route_up(matrix, field):
    return jnp.einsum("ij,itw->jtw", matrix, field, precision=lax.Precision.HIGHEST)


def iterate(fields, statics, scales, suffix_sum, from_earlier, from_later):
    release, storage_dual, demand_dual, cost, inflow, demand = fields
    (
        storage_start,
        storage_low,
        storage_high,
        release_cap,
        efficiency,
        travel_delay,
        to_own,
        to_next,
    ) = statics
    scale_time, scale_sum = scales
    local = suffix_local(storage_dual)
    off, off_next, beyond, rim_own, rim_next = dual_exchange(local)
    suffix = local + off[:, None]
    at_sink = route_up(to_own, suffix) + route_up(to_next, beyond + off_next[:, None])
    last = lax.axis_index("hours") == lax.axis_size("hours") - 1
    rim_sink = route_up(to_own, rim_own + off[:, None]) + route_up(to_next, rim_next + off_next[:, None])
    later_duals = bring_forward(at_sink, travel_delay, jnp.where(last, 0.0, rim_sink))
    gradient = (
        cost
        + scale_time * (later_duals - suffix)
        + scale_sum * efficiency[:, None, None] * demand_dual[None]
    )
    release_new = jnp.clip(release - primal_step * gradient, 0.0, release_cap[:, None, None])
    extrapolated = 2.0 * release_new - release
    length = extrapolated.shape[1]
    tail = extrapolated[:, length - DMAX :]
    settled = hold_back(extrapolated, travel_delay, jnp.zeros_like(tail))
    rim_delayed = hold_back(jnp.zeros_like(extrapolated), travel_delay, tail)[:, :DMAX]
    main_own = route_down(to_own, settled)
    main_next = route_down(to_next, settled)
    rim_own = route_down(to_own, rim_delayed)
    rim_next = route_down(to_next, rim_delayed)
    base = inflow + main_own - extrapolated
    own_totals = jnp.sum(base, 1) + jnp.sum(rim_own, 1)
    next_totals = jnp.sum(main_next, 1) + jnp.sum(rim_next, 1)
    partial_power = jnp.sum(scale_sum * efficiency[:, None, None] * extrapolated, 0)
    incoming, rim_own_in, rim_next_in, offset, supplied = flow_exchange(
        main_next, rim_own, rim_next, own_totals, next_totals, partial_power
    )
    arrived = jnp.concatenate([rim_own_in + rim_next_in, jnp.zeros_like(base[:, DMAX:])], 1)
    local_sum = jnp.cumsum(base + incoming + arrived, 1)
    offset = offset - jnp.sum(rim_own_in, 1) - jnp.sum(rim_next_in, 1)
    storage = storage_start[:, None, None] + scale_time * (local_sum + offset[:, None])
    lower_bound = storage_low[:, None, None]
    upper_bound = storage_high[:, None, None]
    storage_dual_new = (
        storage_dual
        + dual_step * storage
        - dual_step * jnp.clip(storage_dual / dual_step + storage, lower_bound, upper_bound)
    )
    storage_excess = storage - jnp.clip(storage, lower_bound, upper_bound)
    demand_dual_new = jnp.minimum(demand_dual + dual_step * (supplied - demand), 0.0)
    return (release_new, storage_dual_new, demand_dual_new, storage_excess)


def suffix_local(field):
    return lax.cumsum(field, 1, reverse=True)


def shards(
    release,
    storage_dual,
    demand_dual,
    cost,
    inflow,
    demand,
    storage_start,
    storage_low,
    storage_high,
    release_cap,
    efficiency,
    downstream,
    travel_delay,
):
    res_dev = release.shape[0]
    scale_time = 1.0 / (release.shape[1] * lax.axis_size("hours"))
    scale_sum = 1.0 / math.sqrt(res_dev * lax.axis_size("river"))
    base_index = lax.axis_index("river") * res_dev
    target = downstream - base_index
    indices = jnp.arange(res_dev, dtype=jnp.int32)
    to_own = (target[None, :] == indices[:, None]).astype(jnp.float32)
    to_next = (target[None, :] == indices[:, None] + res_dev).astype(jnp.float32)
    statics = (
        storage_start,
        storage_low,
        storage_high,
        release_cap,
        efficiency,
        travel_delay,
        to_own,
        to_next,
    )
    scales = (scale_time, scale_sum)

    def suffix_blocks(field):
        local_sum = suffix_local(field)
        totals = local_sum[:, 0]
        (offset,) = combine([totals], [("hours", "suffix", 8)], 0)
        return local_sum + offset[:, None]

    def earlier_block(part):
        return passed_along(part, "hours", 1)

    def later_block(part):
        return passed_along(part, "hours", -1)

    fields = (release, storage_dual, demand_dual, cost, inflow, demand)
    return iterate(
        fields, statics, scales, suffix_blocks, earlier_block, later_block
    )


def solution(mesh):
    return jax.shard_map(
        shards,
        mesh=mesh,
        in_specs=(
            P("river", "hours", None),
            P("river", "hours", None),
            P("hours", None),
            P("river", "hours", None),
            P("river", "hours", None),
            P("hours", None),
            P("river"),
            P("river"),
            P("river"),
            P("river"),
            P("river"),
            P("river"),
            P("river"),
        ),
        out_specs=(
            P("river", "hours", None),
            P("river", "hours", None),
            P("hours", None),
            P("river", "hours", None),
        ),
        check_vma=False,
    )
```

```python
import functools
import math

import jax
import jax.numpy as jnp
from jax import lax
from jax.experimental import pallas as pl
from jax.experimental.pallas import tpu as pltpu
from jax.sharding import PartitionSpec as P

DMAX = 6
RIVER_INNER = 2


primal_step = 1.0
dual_step = 0.1


def passed_along(block, axis, distance):
    devices = range(lax.axis_size(axis))
    route = [(i - distance, i) for i in devices if i - distance in devices]
    return lax.ppermute(block, axis, route)


MESH = pl.DeviceIdType.MESH


def wanted(mode, src, dst):
    if mode == "prefix":
        return src < dst
    if mode == "suffix":
        return src > dst
    return src != dst


class Job:
    def __init__(self, axis, mode, inner, n):
        self.axis, self.mode, self.inner = axis, mode, inner
        self.outer = n // inner
        self.other = "river" if axis == "hours" else "hours"

    def place(self):
        me = lax.axis_index(self.axis)
        self.fixed = lax.axis_index(self.other)
        self.o = me // self.inner
        self.i = me % self.inner

    def device(self, p):
        return (self.fixed, p) if self.axis == "hours" else (p, self.fixed)

    def peers(self):
        inner, outer, o, i = self.inner, self.outer, self.o, self.i
        near = [self.device(o * inner + lax.rem(i + s, inner)) for s in range(1, inner)]
        far = [self.device(lax.rem(o + s, outer) * inner + i) for s in range(1, outer)]
        return near + far


def multi_kernel(jobs, *refs):
    count = len(jobs)
    ins, outs, rest = refs[:count], refs[count:2 * count], refs[2 * count:]
    for job in jobs:
        job.place()
    barrier = pltpu.get_barrier_semaphore()
    partners = 0
    for job in jobs:
        for dev in job.peers():
            pl.semaphore_signal(barrier, 1, device_id=dev, device_id_type=MESH)
            partners += 1
    pl.semaphore_wait(barrier, partners)

    def across(job, x_ref, near, s1, r1, p, landing):
        return pltpu.make_async_remote_copy(
            src_ref=x_ref, dst_ref=near.at[landing], send_sem=s1.at[p], recv_sem=r1.at[landing],
            device_id=job.device(job.o * job.inner + p), device_id_type=MESH)

    for k, job in enumerate(jobs):
        near, far, group, s1, r1, s2, r2 = rest[7 * k:7 * k + 7]
        for s in range(1, job.inner):
            p = lax.rem(job.i + s, job.inner)
            across(job, ins[k], near, s1, r1, p, job.i).start()
    parts = []
    for k, job in enumerate(jobs):
        near, far, group, s1, r1, s2, r2 = rest[7 * k:7 * k + 7]
        for s in range(1, job.inner):
            p = lax.rem(job.i + s, job.inner)
            across(job, ins[k], near, s1, r1, p, job.i).wait_send()
            across(job, ins[k], near, s1, r1, p, p).wait_recv()
        own = ins[k][...]
        total = own
        part = own if job.mode == "sum" else jnp.zeros_like(own)
        for s in range(1, job.inner):
            p = lax.rem(job.i + s, job.inner)
            block = near[p]
            total = total + block
            if job.mode == "sum":
                part = part + block
            else:
                part = part + jnp.where(wanted(job.mode, p, job.i), block, 0.0)
        group[...] = total
        parts.append(part)

    def up(job, group, far, s2, r2, q, landing):
        return pltpu.make_async_remote_copy(
            src_ref=group, dst_ref=far.at[landing], send_sem=s2.at[q], recv_sem=r2.at[landing],
            device_id=job.device(q * job.inner + job.i), device_id_type=MESH)

    for k, job in enumerate(jobs):
        near, far, group, s1, r1, s2, r2 = rest[7 * k:7 * k + 7]
        for s in range(1, job.outer):
            q = lax.rem(job.o + s, job.outer)

            @pl.when(wanted(job.mode, job.o, q))
            def _():
                up(job, group, far, s2, r2, q, job.o).start()

    for k, job in enumerate(jobs):
        near, far, group, s1, r1, s2, r2 = rest[7 * k:7 * k + 7]
        part = parts[k]
        for s in range(1, job.outer):
            q = lax.rem(job.o + s, job.outer)

            @pl.when(wanted(job.mode, job.o, q))
            def _():
                up(job, group, far, s2, r2, q, job.o).wait_send()

            @pl.when(wanted(job.mode, q, job.o))
            def _():
                up(job, group, far, s2, r2, q, q).wait_recv()

        for s in range(1, job.outer):
            q = lax.rem(job.o + s, job.outer)
            part = part + jnp.where(wanted(job.mode, q, job.o), far[q], 0.0)
        outs[k][...] = part


def dual_kernel(
    sloc_ref, t_ref, off_ref, off_next_ref, beyond_ref, rim_own_ref, rim_next_ref,
    near, far, group, beyond_buf, rim_src_own, rim_src_next, rim_own_buf, rim_next_buf,
    off_src, off_next_buf, s1, r1, s2, r2, sems,
):
    job = Job("hours", "suffix", 8, lax.axis_size("hours"))
    job.place()
    n_r = lax.axis_size("river")
    n_h = lax.axis_size("hours")
    r = lax.axis_index("river")
    h = lax.axis_index("hours")
    has_up, has_down = r > 0, r < n_r - 1
    has_before, has_after = h > 0, h < n_h - 1

    barrier = pltpu.get_barrier_semaphore()
    for dev in job.peers():
        pl.semaphore_signal(barrier, 1, device_id=dev, device_id_type=MESH)
    for flag, dev in ((has_up, (r - 1, h)), (has_down, (r + 1, h)), (has_before, (r, h - 1)), (has_after, (r, h + 1))):

        @pl.when(flag)
        def _():
            pl.semaphore_signal(barrier, 1, device_id=dev, device_id_type=MESH)

    extra = sum(jnp.where(flag, 1, 0) for flag in (has_up, has_down, has_before, has_after))
    pl.semaphore_wait(barrier, job.inner + job.outer - 2 + extra)

    def link(src, dst, k, dev):
        return pltpu.make_async_remote_copy(
            src_ref=src, dst_ref=dst, send_sem=sems.at[2 * k], recv_sem=sems.at[2 * k + 1],
            device_id=dev, device_id_type=MESH)

    to_up = lambda src, dst, k: link(src, dst, k, (r - 1, h))
    to_before = lambda src, dst, k: link(src, dst, k, (r, h - 1))

    def across(p, landing):
        return pltpu.make_async_remote_copy(
            src_ref=t_ref, dst_ref=near.at[landing], send_sem=s1.at[p], recv_sem=r1.at[landing],
            device_id=job.device(job.o * job.inner + p), device_id_type=MESH)

    for s in range(1, job.inner):
        across(lax.rem(job.i + s, job.inner), job.i).start()

    @pl.when(has_up)
    def _():
        to_up(sloc_ref, beyond_buf, 0).start()

    rim_src_own[...] = sloc_ref[:, 0:DMAX, :] - sloc_ref[:, 0:1, :]

    @pl.when(has_before)
    def _():
        to_before(rim_src_own, rim_own_buf, 1).start()

    for s in range(1, job.inner):
        p = lax.rem(job.i + s, job.inner)
        across(p, job.i).wait_send()
        across(p, p).wait_recv()
    own = t_ref[...]
    total = own
    part = jnp.zeros_like(own)
    for s in range(1, job.inner):
        p = lax.rem(job.i + s, job.inner)
        block = near[p]
        total = total + block
        part = part + jnp.where(p > job.i, block, 0.0)
    group[...] = total

    def up(q, landing):
        return pltpu.make_async_remote_copy(
            src_ref=group, dst_ref=far.at[landing], send_sem=s2.at[q], recv_sem=r2.at[landing],
            device_id=job.device(q * job.inner + job.i), device_id_type=MESH)

    for s in range(1, job.outer):
        q = lax.rem(job.o + s, job.outer)

        @pl.when(job.o > q)
        def _():
            up(q, job.o).start()

    @pl.when(has_down)
    def _():
        to_up(sloc_ref, beyond_buf, 0).wait_recv()
        rim_src_next[...] = beyond_buf[:, 0:DMAX, :] - beyond_buf[:, 0:1, :]

    @pl.when(jnp.logical_and(has_down, has_before))
    def _():
        to_before(rim_src_next, rim_next_buf, 2).start()

    for s in range(1, job.outer):
        q = lax.rem(job.o + s, job.outer)

        @pl.when(job.o > q)
        def _():
            up(q, job.o).wait_send()

        @pl.when(q > job.o)
        def _():
            up(q, q).wait_recv()

    for s in range(1, job.outer):
        q = lax.rem(job.o + s, job.outer)
        part = part + jnp.where(q > job.o, far[q], 0.0)
    off_src[...] = part
    off_ref[...] = part

    @pl.when(has_up)
    def _():
        to_up(off_src, off_next_buf, 3).start()

    @pl.when(has_up)
    def _():
        to_up(sloc_ref, beyond_buf, 0).wait_send()
        to_up(off_src, off_next_buf, 3).wait_send()

    @pl.when(has_before)
    def _():
        to_before(rim_src_own, rim_own_buf, 1).wait_send()

    @pl.when(jnp.logical_and(has_down, has_before))
    def _():
        to_before(rim_src_next, rim_next_buf, 2).wait_send()

    @pl.when(has_after)
    def _():
        to_before(rim_src_own, rim_own_buf, 1).wait_recv()
        rim_own_ref[...] = rim_own_buf[...]

    @pl.when(jnp.logical_not(has_after))
    def _():
        rim_own_ref[...] = jnp.zeros_like(rim_own_ref)

    @pl.when(jnp.logical_and(has_down, has_after))
    def _():
        to_before(rim_src_next, rim_next_buf, 2).wait_recv()
        rim_next_ref[...] = rim_next_buf[...]

    @pl.when(jnp.logical_not(jnp.logical_and(has_down, has_after)))
    def _():
        rim_next_ref[...] = jnp.zeros_like(rim_next_ref)

    @pl.when(has_down)
    def _():
        to_up(off_src, off_next_buf, 3).wait_recv()
        off_next_ref[...] = off_next_buf[...]
        beyond_ref[...] = beyond_buf[...]

    @pl.when(jnp.logical_not(has_down))
    def _():
        off_next_ref[...] = jnp.zeros_like(off_next_ref)
        beyond_ref[...] = jnp.zeros_like(beyond_ref)


def dual_exchange(sloc):
    res, length, width = sloc.shape
    t = sloc[:, 0].reshape(-1, 128)
    inner = 8
    outer = lax.axis_size("hours") // inner
    rim = (res, DMAX, width)
    vmem = pl.BlockSpec(memory_space=pltpu.VMEM)
    off, off_next, beyond, rim_own, rim_next = pl.pallas_call(
        dual_kernel,
        out_shape=[
            jax.ShapeDtypeStruct(t.shape, t.dtype),
            jax.ShapeDtypeStruct(t.shape, t.dtype),
            jax.ShapeDtypeStruct(sloc.shape, sloc.dtype),
            jax.ShapeDtypeStruct(rim, sloc.dtype),
            jax.ShapeDtypeStruct(rim, sloc.dtype),
        ],
        in_specs=[vmem, vmem],
        out_specs=[vmem] * 5,
        scratch_shapes=[
            pltpu.VMEM((inner,) + t.shape, t.dtype),
            pltpu.VMEM((outer,) + t.shape, t.dtype),
            pltpu.VMEM(t.shape, t.dtype),
            pltpu.VMEM(sloc.shape, sloc.dtype),
            pltpu.VMEM(rim, sloc.dtype),
            pltpu.VMEM(rim, sloc.dtype),
            pltpu.VMEM(rim, sloc.dtype),
            pltpu.VMEM(rim, sloc.dtype),
            pltpu.VMEM(t.shape, t.dtype),
            pltpu.VMEM(t.shape, t.dtype),
            pltpu.SemaphoreType.DMA((inner,)),
            pltpu.SemaphoreType.DMA((inner,)),
            pltpu.SemaphoreType.DMA((outer,)),
            pltpu.SemaphoreType.DMA((outer,)),
            pltpu.SemaphoreType.DMA((8,)),
        ],
        compiler_params=pltpu.CompilerParams(collective_id=0, has_side_effects=True, vmem_limit_bytes=48 * 1024 * 1024),
    )(sloc, t)
    return off.reshape(res, width), off_next.reshape(res, width), beyond, rim_own, rim_next


def flow_kernel(
    main_ref, rim_own_ref, rim_next_ref, a_ref, b_ref, power_ref,
    incoming_ref, rim_own_in_ref, rim_next_in_ref, pa_ref, supplied_ref,
    near_h, far_h, group_h, near_r, far_r, group_r, incoming_buf, rim_own_buf, rim_next_buf,
    a_src, b_buf, s1h, r1h, s2h, r2h, s1r, r1r, s2r, r2r, sems,
):
    jobs = [Job("hours", "prefix", 8, lax.axis_size("hours")), Job("river", "sum", RIVER_INNER, lax.axis_size("river"))]
    for job in jobs:
        job.place()
    n_r = lax.axis_size("river")
    n_h = lax.axis_size("hours")
    r = lax.axis_index("river")
    h = lax.axis_index("hours")
    has_up, has_down = r > 0, r < n_r - 1
    has_before, has_after = h > 0, h < n_h - 1
    diag_down = jnp.logical_and(has_down, has_after)
    diag_up = jnp.logical_and(has_up, has_before)

    barrier = pltpu.get_barrier_semaphore()
    fixed = 0
    for job in jobs:
        for dev in job.peers():
            pl.semaphore_signal(barrier, 1, device_id=dev, device_id_type=MESH)
            fixed += 1
    links = (
        (has_up, (r - 1, h)), (has_down, (r + 1, h)), (has_before, (r, h - 1)), (has_after, (r, h + 1)),
        (diag_down, (r + 1, h + 1)), (diag_up, (r - 1, h - 1)),
    )
    for flag, dev in links:

        @pl.when(flag)
        def _():
            pl.semaphore_signal(barrier, 1, device_id=dev, device_id_type=MESH)

    extra = sum(jnp.where(flag, 1, 0) for flag, _ in links)
    pl.semaphore_wait(barrier, fixed + extra)

    def link(src, dst, k, dev):
        return pltpu.make_async_remote_copy(
            src_ref=src, dst_ref=dst, send_sem=sems.at[2 * k], recv_sem=sems.at[2 * k + 1],
            device_id=dev, device_id_type=MESH)

    main_copy = link(main_ref, incoming_buf, 0, (r + 1, h))
    rim_own_copy = link(rim_own_ref, rim_own_buf, 1, (r, h + 1))
    rim_next_copy = link(rim_next_ref, rim_next_buf, 2, (r + 1, h + 1))
    b_copy = link(b_ref, b_buf, 3, (r + 1, h))

    @pl.when(has_down)
    def _():
        b_copy.start()
        main_copy.start()

    @pl.when(has_after)
    def _():
        rim_own_copy.start()

    @pl.when(diag_down)
    def _():
        rim_next_copy.start()

    bufs = [(a_src, near_h, far_h, group_h, s1h, r1h, s2h, r2h), (power_ref, near_r, far_r, group_r, s1r, r1r, s2r, r2r)]

    def across(job, x_ref, near, s1, r1, p, landing):
        return pltpu.make_async_remote_copy(
            src_ref=x_ref, dst_ref=near.at[landing], send_sem=s1.at[p], recv_sem=r1.at[landing],
            device_id=job.device(job.o * job.inner + p), device_id_type=MESH)

    for job, (x_ref, near, far, group, s1, r1, s2, r2) in zip(jobs[::-1], bufs[::-1]):
        if job.axis == "hours":

            @pl.when(has_up)
            def _():
                b_copy.wait_recv()
                a_src[...] = a_ref[...] + b_buf[...]

            @pl.when(jnp.logical_not(has_up))
            def _():
                a_src[...] = a_ref[...]

        for s in range(1, job.inner):
            across(job, x_ref, near, s1, r1, lax.rem(job.i + s, job.inner), job.i).start()
    parts = []
    for job, (x_ref, near, far, group, s1, r1, s2, r2) in zip(jobs, bufs):
        for s in range(1, job.inner):
            p = lax.rem(job.i + s, job.inner)
            across(job, x_ref, near, s1, r1, p, job.i).wait_send()
            across(job, x_ref, near, s1, r1, p, p).wait_recv()
        own = x_ref[...]
        total = own
        part = own if job.mode == "sum" else jnp.zeros_like(own)
        for s in range(1, job.inner):
            p = lax.rem(job.i + s, job.inner)
            block = near[p]
            total = total + block
            if job.mode == "sum":
                part = part + block
            else:
                part = part + jnp.where(wanted(job.mode, p, job.i), block, 0.0)
        group[...] = total
        parts.append(part)

    def up(job, group, far, s2, r2, q, landing):
        return pltpu.make_async_remote_copy(
            src_ref=group, dst_ref=far.at[landing], send_sem=s2.at[q], recv_sem=r2.at[landing],
            device_id=job.device(q * job.inner + job.i), device_id_type=MESH)

    for job, (x_ref, near, far, group, s1, r1, s2, r2) in zip(jobs, bufs):
        for s in range(1, job.outer):
            q = lax.rem(job.o + s, job.outer)

            @pl.when(wanted(job.mode, job.o, q))
            def _():
                up(job, group, far, s2, r2, q, job.o).start()

    results = []
    for job, part, (x_ref, near, far, group, s1, r1, s2, r2) in zip(jobs, parts, bufs):
        for s in range(1, job.outer):
            q = lax.rem(job.o + s, job.outer)

            @pl.when(wanted(job.mode, job.o, q))
            def _():
                up(job, group, far, s2, r2, q, job.o).wait_send()

            @pl.when(wanted(job.mode, q, job.o))
            def _():
                up(job, group, far, s2, r2, q, q).wait_recv()

        for s in range(1, job.outer):
            q = lax.rem(job.o + s, job.outer)
            part = part + jnp.where(wanted(job.mode, q, job.o), far[q], 0.0)
        results.append(part)
    scanned, supplied = results
    pa_ref[...] = scanned
    supplied_ref[...] = supplied

    @pl.when(has_down)
    def _():
        main_copy.wait_send()
        b_copy.wait_send()

    @pl.when(has_after)
    def _():
        rim_own_copy.wait_send()

    @pl.when(diag_down)
    def _():
        rim_next_copy.wait_send()

    @pl.when(has_up)
    def _():
        main_copy.wait_recv()
        incoming_ref[...] = incoming_buf[...]

    @pl.when(jnp.logical_not(has_up))
    def _():
        incoming_ref[...] = jnp.zeros_like(incoming_ref)

    @pl.when(has_before)
    def _():
        rim_own_copy.wait_recv()
        rim_own_in_ref[...] = rim_own_buf[...]

    @pl.when(jnp.logical_not(has_before))
    def _():
        rim_own_in_ref[...] = jnp.zeros_like(rim_own_in_ref)

    @pl.when(diag_up)
    def _():
        rim_next_copy.wait_recv()
        rim_next_in_ref[...] = rim_next_buf[...]

    @pl.when(jnp.logical_not(diag_up))
    def _():
        rim_next_in_ref[...] = jnp.zeros_like(rim_next_in_ref)


def flow_exchange(main_next, rim_own, rim_next, own_totals, next_totals, power):
    res, width = own_totals.shape
    a = own_totals.reshape(-1, 128)
    b = next_totals.reshape(-1, 128)
    flat_power = power.reshape(-1, 128)
    inner = 8
    inner_r = RIVER_INNER
    outer_h = lax.axis_size("hours") // inner
    outer_r = lax.axis_size("river") // inner_r
    vmem = pl.BlockSpec(memory_space=pltpu.VMEM)
    shape = lambda x: jax.ShapeDtypeStruct(x.shape, x.dtype)
    incoming, rim_own_in, rim_next_in, pa, supplied = pl.pallas_call(
        flow_kernel,
        out_shape=[shape(main_next), shape(rim_own), shape(rim_next), shape(a), shape(flat_power)],
        in_specs=[vmem] * 6,
        out_specs=[vmem] * 5,
        scratch_shapes=[
            pltpu.VMEM((inner,) + a.shape, a.dtype),
            pltpu.VMEM((outer_h,) + a.shape, a.dtype),
            pltpu.VMEM(a.shape, a.dtype),
            pltpu.VMEM((inner_r,) + flat_power.shape, a.dtype),
            pltpu.VMEM((outer_r,) + flat_power.shape, a.dtype),
            pltpu.VMEM(flat_power.shape, a.dtype),
            pltpu.VMEM(main_next.shape, a.dtype),
            pltpu.VMEM(rim_own.shape, a.dtype),
            pltpu.VMEM(rim_next.shape, a.dtype),
            pltpu.VMEM(a.shape, a.dtype),
            pltpu.VMEM(a.shape, a.dtype),
            pltpu.SemaphoreType.DMA((inner,)),
            pltpu.SemaphoreType.DMA((inner,)),
            pltpu.SemaphoreType.DMA((outer_h,)),
            pltpu.SemaphoreType.DMA((outer_h,)),
            pltpu.SemaphoreType.DMA((inner_r,)),
            pltpu.SemaphoreType.DMA((inner_r,)),
            pltpu.SemaphoreType.DMA((outer_r,)),
            pltpu.SemaphoreType.DMA((outer_r,)),
            pltpu.SemaphoreType.DMA((8,)),
        ],
        compiler_params=pltpu.CompilerParams(collective_id=1, has_side_effects=True, vmem_limit_bytes=48 * 1024 * 1024),
    )(main_next, rim_own, rim_next, a, b, flat_power)
    return incoming, rim_own_in, rim_next_in, pa.reshape(res, width), supplied.reshape(power.shape)


def combine(parts, specs, collective):
    shapes = [part.shape for part in parts]
    parts = [part.reshape(-1, 128) for part in parts]
    jobs = [Job(axis, mode, inner, lax.axis_size(axis)) for axis, mode, inner in specs]
    scratch = []
    for part, job in zip(parts, jobs):
        scratch += [
            pltpu.VMEM((job.inner,) + part.shape, part.dtype),
            pltpu.VMEM((job.outer,) + part.shape, part.dtype),
            pltpu.VMEM(part.shape, part.dtype),
            pltpu.SemaphoreType.DMA((job.inner,)),
            pltpu.SemaphoreType.DMA((job.inner,)),
            pltpu.SemaphoreType.DMA((job.outer,)),
            pltpu.SemaphoreType.DMA((job.outer,)),
        ]
    results = pl.pallas_call(
        functools.partial(multi_kernel, jobs),
        out_shape=[jax.ShapeDtypeStruct(part.shape, part.dtype) for part in parts],
        in_specs=[pl.BlockSpec(memory_space=pltpu.VMEM)] * len(parts),
        out_specs=[pl.BlockSpec(memory_space=pltpu.VMEM)] * len(parts),
        scratch_shapes=scratch,
        compiler_params=pltpu.CompilerParams(collective_id=collective, has_side_effects=True),
    )(*parts)
    return [result.reshape(shape) for result, shape in zip(results, shapes)]


def add_pair(earlier_part, later_part):
    return earlier_part + later_part


def hold_back(field, travel_delay, earlier_rim):
    length = field.shape[1]
    extended = jnp.concatenate([earlier_rim, field], 1)
    result = jnp.zeros_like(field)
    for lag_hours in range(1, DMAX + 1):
        window = extended[:, DMAX - lag_hours : DMAX - lag_hours + length]
        result = result + jnp.where((travel_delay == lag_hours)[:, None, None], window, 0.0)
    return result


def bring_forward(field, travel_delay, later_rim):
    length = field.shape[1]
    extended = jnp.concatenate([field, later_rim], 1)
    result = jnp.zeros_like(field)
    for lag_hours in range(1, DMAX + 1):
        window = extended[:, lag_hours : lag_hours + length]
        result = result + jnp.where((travel_delay == lag_hours)[:, None, None], window, 0.0)
    return result


def route_down(matrix, field):
    return jnp.einsum("ij,jtw->itw", matrix, field, precision=lax.Precision.HIGHEST)


def route_up(matrix, field):
    return jnp.einsum("ij,itw->jtw", matrix, field, precision=lax.Precision.HIGHEST)


def iterate(fields, statics, scales, suffix_sum, from_earlier, from_later):
    release, storage_dual, demand_dual, cost, inflow, demand = fields
    (
        storage_start,
        storage_low,
        storage_high,
        release_cap,
        efficiency,
        travel_delay,
        to_own,
        to_next,
    ) = statics
    scale_time, scale_sum = scales
    local = suffix_local(storage_dual)
    off, off_next, beyond, rim_own, rim_next = dual_exchange(local)
    suffix = local + off[:, None]
    at_sink = route_up(to_own, suffix) + route_up(to_next, beyond + off_next[:, None])
    last = lax.axis_index("hours") == lax.axis_size("hours") - 1
    rim_sink = route_up(to_own, rim_own + off[:, None]) + route_up(to_next, rim_next + off_next[:, None])
    later_duals = bring_forward(at_sink, travel_delay, jnp.where(last, 0.0, rim_sink))
    gradient = (
        cost
        + scale_time * (later_duals - suffix)
        + scale_sum * efficiency[:, None, None] * demand_dual[None]
    )
    release_new = jnp.clip(release - primal_step * gradient, 0.0, release_cap[:, None, None])
    extrapolated = 2.0 * release_new - release
    length = extrapolated.shape[1]
    tail = extrapolated[:, length - DMAX :]
    settled = hold_back(extrapolated, travel_delay, jnp.zeros_like(tail))
    rim_delayed = hold_back(jnp.zeros_like(extrapolated), travel_delay, tail)[:, :DMAX]
    main_own = route_down(to_own, settled)
    main_next = route_down(to_next, settled)
    rim_own = route_down(to_own, rim_delayed)
    rim_next = route_down(to_next, rim_delayed)
    base = inflow + main_own - extrapolated
    own_totals = jnp.sum(base, 1) + jnp.sum(rim_own, 1)
    next_totals = jnp.sum(main_next, 1) + jnp.sum(rim_next, 1)
    partial_power = jnp.sum(scale_sum * efficiency[:, None, None] * extrapolated, 0)
    incoming, rim_own_in, rim_next_in, offset, supplied = flow_exchange(
        main_next, rim_own, rim_next, own_totals, next_totals, partial_power
    )
    arrived = jnp.concatenate([rim_own_in + rim_next_in, jnp.zeros_like(base[:, DMAX:])], 1)
    local_sum = jnp.cumsum(base + incoming + arrived, 1)
    offset = offset - jnp.sum(rim_own_in, 1) - jnp.sum(rim_next_in, 1)
    storage = storage_start[:, None, None] + scale_time * (local_sum + offset[:, None])
    lower_bound = storage_low[:, None, None]
    upper_bound = storage_high[:, None, None]
    storage_dual_new = (
        storage_dual
        + dual_step * storage
        - dual_step * jnp.clip(storage_dual / dual_step + storage, lower_bound, upper_bound)
    )
    storage_excess = storage - jnp.clip(storage, lower_bound, upper_bound)
    demand_dual_new = jnp.minimum(demand_dual + dual_step * (supplied - demand), 0.0)
    return (release_new, storage_dual_new, demand_dual_new, storage_excess)


def suffix_local(field):
    return lax.cumsum(field, 1, reverse=True)


def shards(
    release,
    storage_dual,
    demand_dual,
    cost,
    inflow,
    demand,
    storage_start,
    storage_low,
    storage_high,
    release_cap,
    efficiency,
    downstream,
    travel_delay,
):
    res_dev = release.shape[0]
    scale_time = 1.0 / (release.shape[1] * lax.axis_size("hours"))
    scale_sum = 1.0 / math.sqrt(res_dev * lax.axis_size("river"))
    base_index = lax.axis_index("river") * res_dev
    target = downstream - base_index
    indices = jnp.arange(res_dev, dtype=jnp.int32)
    to_own = (target[None, :] == indices[:, None]).astype(jnp.float32)
    to_next = (target[None, :] == indices[:, None] + res_dev).astype(jnp.float32)
    statics = (
        storage_start,
        storage_low,
        storage_high,
        release_cap,
        efficiency,
        travel_delay,
        to_own,
        to_next,
    )
    scales = (scale_time, scale_sum)

    def suffix_blocks(field):
        local_sum = suffix_local(field)
        totals = local_sum[:, 0]
        (offset,) = combine([totals], [("hours", "suffix", 8)], 0)
        return local_sum + offset[:, None]

    def earlier_block(part):
        return passed_along(part, "hours", 1)

    def later_block(part):
        return passed_along(part, "hours", -1)

    fields = (release, storage_dual, demand_dual, cost, inflow, demand)
    return iterate(
        fields, statics, scales, suffix_blocks, earlier_block, later_block
    )


def solution(mesh):
    return jax.shard_map(
        shards,
        mesh=mesh,
        in_specs=(
            P("river", "hours", None),
            P("river", "hours", None),
            P("hours", None),
            P("river", "hours", None),
            P("river", "hours", None),
            P("hours", None),
            P("river"),
            P("river"),
            P("river"),
            P("river"),
            P("river"),
            P("river"),
            P("river"),
        ),
        out_specs=(
            P("river", "hours", None),
            P("river", "hours", None),
            P("hours", None),
            P("river", "hours", None),
        ),
        check_vma=False,
    )
```

```python
import functools
import math

import jax
import jax.numpy as jnp
from jax import lax
from jax.experimental import pallas as pl
from jax.experimental.pallas import tpu as pltpu
from jax.sharding import PartitionSpec as P

DMAX = 6


primal_step = 1.0
dual_step = 0.1


def passed_along(block, axis, distance):
    devices = range(lax.axis_size(axis))
    route = [(i - distance, i) for i in devices if i - distance in devices]
    return lax.ppermute(block, axis, route)


MESH = pl.DeviceIdType.MESH


def wanted(mode, src, dst):
    if mode == "prefix":
        return src < dst
    if mode == "suffix":
        return src > dst
    return src != dst


class Job:
    def __init__(self, axis, mode, inner, n):
        self.axis, self.mode, self.inner = axis, mode, inner
        self.outer = n // inner
        self.other = "river" if axis == "hours" else "hours"

    def place(self):
        me = lax.axis_index(self.axis)
        self.fixed = lax.axis_index(self.other)
        self.o = me // self.inner
        self.i = me % self.inner

    def device(self, p):
        return (self.fixed, p) if self.axis == "hours" else (p, self.fixed)

    def peers(self):
        inner, outer, o, i = self.inner, self.outer, self.o, self.i
        near = [self.device(o * inner + lax.rem(i + s, inner)) for s in range(1, inner)]
        far = [self.device(lax.rem(o + s, outer) * inner + i) for s in range(1, outer)]
        return near + far


def multi_kernel(jobs, *refs):
    count = len(jobs)
    ins, outs, rest = refs[:count], refs[count:2 * count], refs[2 * count:]
    for job in jobs:
        job.place()
    barrier = pltpu.get_barrier_semaphore()
    partners = 0
    for job in jobs:
        for dev in job.peers():
            pl.semaphore_signal(barrier, 1, device_id=dev, device_id_type=MESH)
            partners += 1
    pl.semaphore_wait(barrier, partners)

    def across(job, x_ref, near, s1, r1, p, landing):
        return pltpu.make_async_remote_copy(
            src_ref=x_ref, dst_ref=near.at[landing], send_sem=s1.at[p], recv_sem=r1.at[landing],
            device_id=job.device(job.o * job.inner + p), device_id_type=MESH)

    for k, job in enumerate(jobs):
        near, far, group, s1, r1, s2, r2 = rest[7 * k:7 * k + 7]
        for s in range(1, job.inner):
            p = lax.rem(job.i + s, job.inner)
            across(job, ins[k], near, s1, r1, p, job.i).start()
    parts = []
    for k, job in enumerate(jobs):
        near, far, group, s1, r1, s2, r2 = rest[7 * k:7 * k + 7]
        for s in range(1, job.inner):
            p = lax.rem(job.i + s, job.inner)
            across(job, ins[k], near, s1, r1, p, job.i).wait_send()
            across(job, ins[k], near, s1, r1, p, p).wait_recv()
        own = ins[k][...]
        total = own
        part = own if job.mode == "sum" else jnp.zeros_like(own)
        for s in range(1, job.inner):
            p = lax.rem(job.i + s, job.inner)
            block = near[p]
            total = total + block
            if job.mode == "sum":
                part = part + block
            else:
                part = part + jnp.where(wanted(job.mode, p, job.i), block, 0.0)
        group[...] = total
        parts.append(part)

    def up(job, group, far, s2, r2, q, landing):
        return pltpu.make_async_remote_copy(
            src_ref=group, dst_ref=far.at[landing], send_sem=s2.at[q], recv_sem=r2.at[landing],
            device_id=job.device(q * job.inner + job.i), device_id_type=MESH)

    for k, job in enumerate(jobs):
        near, far, group, s1, r1, s2, r2 = rest[7 * k:7 * k + 7]
        for s in range(1, job.outer):
            q = lax.rem(job.o + s, job.outer)

            @pl.when(wanted(job.mode, job.o, q))
            def _():
                up(job, group, far, s2, r2, q, job.o).start()

    for k, job in enumerate(jobs):
        near, far, group, s1, r1, s2, r2 = rest[7 * k:7 * k + 7]
        part = parts[k]
        for s in range(1, job.outer):
            q = lax.rem(job.o + s, job.outer)

            @pl.when(wanted(job.mode, job.o, q))
            def _():
                up(job, group, far, s2, r2, q, job.o).wait_send()

            @pl.when(wanted(job.mode, q, job.o))
            def _():
                up(job, group, far, s2, r2, q, q).wait_recv()

        for s in range(1, job.outer):
            q = lax.rem(job.o + s, job.outer)
            part = part + jnp.where(wanted(job.mode, q, job.o), far[q], 0.0)
        outs[k][...] = part


def dual_kernel(
    sloc_ref, t_ref, off_ref, off_next_ref, beyond_ref, rim_own_ref, rim_next_ref,
    near, far, group, beyond_buf, rim_src_own, rim_src_next, rim_own_buf, rim_next_buf,
    off_src, off_next_buf, s1, r1, s2, r2, sems,
):
    job = Job("hours", "suffix", 8, lax.axis_size("hours"))
    job.place()
    n_r = lax.axis_size("river")
    n_h = lax.axis_size("hours")
    r = lax.axis_index("river")
    h = lax.axis_index("hours")
    has_up, has_down = r > 0, r < n_r - 1
    has_before, has_after = h > 0, h < n_h - 1

    barrier = pltpu.get_barrier_semaphore()
    for dev in job.peers():
        pl.semaphore_signal(barrier, 1, device_id=dev, device_id_type=MESH)
    for flag, dev in ((has_up, (r - 1, h)), (has_down, (r + 1, h)), (has_before, (r, h - 1)), (has_after, (r, h + 1))):

        @pl.when(flag)
        def _():
            pl.semaphore_signal(barrier, 1, device_id=dev, device_id_type=MESH)

    extra = sum(jnp.where(flag, 1, 0) for flag in (has_up, has_down, has_before, has_after))
    pl.semaphore_wait(barrier, job.inner + job.outer - 2 + extra)

    def link(src, dst, k, dev):
        return pltpu.make_async_remote_copy(
            src_ref=src, dst_ref=dst, send_sem=sems.at[2 * k], recv_sem=sems.at[2 * k + 1],
            device_id=dev, device_id_type=MESH)

    to_up = lambda src, dst, k: link(src, dst, k, (r - 1, h))
    to_before = lambda src, dst, k: link(src, dst, k, (r, h - 1))

    def across(p, landing):
        return pltpu.make_async_remote_copy(
            src_ref=t_ref, dst_ref=near.at[landing], send_sem=s1.at[p], recv_sem=r1.at[landing],
            device_id=job.device(job.o * job.inner + p), device_id_type=MESH)

    for s in range(1, job.inner):
        across(lax.rem(job.i + s, job.inner), job.i).start()

    @pl.when(has_up)
    def _():
        to_up(sloc_ref, beyond_buf, 0).start()

    rim_src_own[...] = sloc_ref[:, 0:DMAX, :] - sloc_ref[:, 0:1, :]

    @pl.when(has_before)
    def _():
        to_before(rim_src_own, rim_own_buf, 1).start()

    for s in range(1, job.inner):
        p = lax.rem(job.i + s, job.inner)
        across(p, job.i).wait_send()
        across(p, p).wait_recv()
    own = t_ref[...]
    total = own
    part = jnp.zeros_like(own)
    for s in range(1, job.inner):
        p = lax.rem(job.i + s, job.inner)
        block = near[p]
        total = total + block
        part = part + jnp.where(p > job.i, block, 0.0)
    group[...] = total

    def up(q, landing):
        return pltpu.make_async_remote_copy(
            src_ref=group, dst_ref=far.at[landing], send_sem=s2.at[q], recv_sem=r2.at[landing],
            device_id=job.device(q * job.inner + job.i), device_id_type=MESH)

    for s in range(1, job.outer):
        q = lax.rem(job.o + s, job.outer)

        @pl.when(job.o > q)
        def _():
            up(q, job.o).start()

    @pl.when(has_down)
    def _():
        to_up(sloc_ref, beyond_buf, 0).wait_recv()
        rim_src_next[...] = beyond_buf[:, 0:DMAX, :] - beyond_buf[:, 0:1, :]

    @pl.when(jnp.logical_and(has_down, has_before))
    def _():
        to_before(rim_src_next, rim_next_buf, 2).start()

    for s in range(1, job.outer):
        q = lax.rem(job.o + s, job.outer)

        @pl.when(job.o > q)
        def _():
            up(q, job.o).wait_send()

        @pl.when(q > job.o)
        def _():
            up(q, q).wait_recv()

    for s in range(1, job.outer):
        q = lax.rem(job.o + s, job.outer)
        part = part + jnp.where(q > job.o, far[q], 0.0)
    off_src[...] = part
    off_ref[...] = part

    @pl.when(has_up)
    def _():
        to_up(off_src, off_next_buf, 3).start()

    @pl.when(has_up)
    def _():
        to_up(sloc_ref, beyond_buf, 0).wait_send()
        to_up(off_src, off_next_buf, 3).wait_send()

    @pl.when(has_before)
    def _():
        to_before(rim_src_own, rim_own_buf, 1).wait_send()

    @pl.when(jnp.logical_and(has_down, has_before))
    def _():
        to_before(rim_src_next, rim_next_buf, 2).wait_send()

    @pl.when(has_after)
    def _():
        to_before(rim_src_own, rim_own_buf, 1).wait_recv()
        rim_own_ref[...] = rim_own_buf[...]

    @pl.when(jnp.logical_not(has_after))
    def _():
        rim_own_ref[...] = jnp.zeros_like(rim_own_ref)

    @pl.when(jnp.logical_and(has_down, has_after))
    def _():
        to_before(rim_src_next, rim_next_buf, 2).wait_recv()
        rim_next_ref[...] = rim_next_buf[...]

    @pl.when(jnp.logical_not(jnp.logical_and(has_down, has_after)))
    def _():
        rim_next_ref[...] = jnp.zeros_like(rim_next_ref)

    @pl.when(has_down)
    def _():
        to_up(off_src, off_next_buf, 3).wait_recv()
        off_next_ref[...] = off_next_buf[...]
        beyond_ref[...] = beyond_buf[...]

    @pl.when(jnp.logical_not(has_down))
    def _():
        off_next_ref[...] = jnp.zeros_like(off_next_ref)
        beyond_ref[...] = jnp.zeros_like(beyond_ref)


def dual_exchange(sloc):
    res, length, width = sloc.shape
    t = sloc[:, 0].reshape(-1, 128)
    inner = 8
    outer = lax.axis_size("hours") // inner
    rim = (res, DMAX, width)
    vmem = pl.BlockSpec(memory_space=pltpu.VMEM)
    off, off_next, beyond, rim_own, rim_next = pl.pallas_call(
        dual_kernel,
        out_shape=[
            jax.ShapeDtypeStruct(t.shape, t.dtype),
            jax.ShapeDtypeStruct(t.shape, t.dtype),
            jax.ShapeDtypeStruct(sloc.shape, sloc.dtype),
            jax.ShapeDtypeStruct(rim, sloc.dtype),
            jax.ShapeDtypeStruct(rim, sloc.dtype),
        ],
        in_specs=[vmem, vmem],
        out_specs=[vmem] * 5,
        scratch_shapes=[
            pltpu.VMEM((inner,) + t.shape, t.dtype),
            pltpu.VMEM((outer,) + t.shape, t.dtype),
            pltpu.VMEM(t.shape, t.dtype),
            pltpu.VMEM(sloc.shape, sloc.dtype),
            pltpu.VMEM(rim, sloc.dtype),
            pltpu.VMEM(rim, sloc.dtype),
            pltpu.VMEM(rim, sloc.dtype),
            pltpu.VMEM(rim, sloc.dtype),
            pltpu.VMEM(t.shape, t.dtype),
            pltpu.VMEM(t.shape, t.dtype),
            pltpu.SemaphoreType.DMA((inner,)),
            pltpu.SemaphoreType.DMA((inner,)),
            pltpu.SemaphoreType.DMA((outer,)),
            pltpu.SemaphoreType.DMA((outer,)),
            pltpu.SemaphoreType.DMA((8,)),
        ],
        compiler_params=pltpu.CompilerParams(collective_id=0, has_side_effects=True, vmem_limit_bytes=48 * 1024 * 1024),
    )(sloc, t)
    return off.reshape(res, width), off_next.reshape(res, width), beyond, rim_own, rim_next


def flow_kernel(
    main_ref, rim_own_ref, rim_next_ref, a_ref, b_ref, power_ref,
    incoming_ref, rim_own_in_ref, rim_next_in_ref, pa_ref, supplied_ref,
    near_h, far_h, group_h, near_r, far_r, group_r, incoming_buf, rim_own_buf, rim_next_buf,
    a_src, b_buf, s1h, r1h, s2h, r2h, s1r, r1r, s2r, r2r, sems,
):
    jobs = [Job("hours", "prefix", 8, lax.axis_size("hours")), Job("river", "sum", 8, lax.axis_size("river"))]
    for job in jobs:
        job.place()
    n_r = lax.axis_size("river")
    n_h = lax.axis_size("hours")
    r = lax.axis_index("river")
    h = lax.axis_index("hours")
    has_up, has_down = r > 0, r < n_r - 1
    has_before, has_after = h > 0, h < n_h - 1
    diag_down = jnp.logical_and(has_down, has_after)
    diag_up = jnp.logical_and(has_up, has_before)

    barrier = pltpu.get_barrier_semaphore()
    fixed = 0
    for job in jobs:
        for dev in job.peers():
            pl.semaphore_signal(barrier, 1, device_id=dev, device_id_type=MESH)
            fixed += 1
    links = (
        (has_up, (r - 1, h)), (has_down, (r + 1, h)), (has_before, (r, h - 1)), (has_after, (r, h + 1)),
        (diag_down, (r + 1, h + 1)), (diag_up, (r - 1, h - 1)),
    )
    for flag, dev in links:

        @pl.when(flag)
        def _():
            pl.semaphore_signal(barrier, 1, device_id=dev, device_id_type=MESH)

    extra = sum(jnp.where(flag, 1, 0) for flag, _ in links)
    pl.semaphore_wait(barrier, fixed + extra)

    def link(src, dst, k, dev):
        return pltpu.make_async_remote_copy(
            src_ref=src, dst_ref=dst, send_sem=sems.at[2 * k], recv_sem=sems.at[2 * k + 1],
            device_id=dev, device_id_type=MESH)

    main_copy = link(main_ref, incoming_buf, 0, (r + 1, h))
    rim_own_copy = link(rim_own_ref, rim_own_buf, 1, (r, h + 1))
    rim_next_copy = link(rim_next_ref, rim_next_buf, 2, (r + 1, h + 1))
    b_copy = link(b_ref, b_buf, 3, (r + 1, h))

    @pl.when(has_down)
    def _():
        b_copy.start()

    @pl.when(has_after)
    def _():
        rim_own_copy.start()

    @pl.when(diag_down)
    def _():
        rim_next_copy.start()

    bufs = [(a_src, near_h, far_h, group_h, s1h, r1h, s2h, r2h), (power_ref, near_r, far_r, group_r, s1r, r1r, s2r, r2r)]

    def across(job, x_ref, near, s1, r1, p, landing):
        return pltpu.make_async_remote_copy(
            src_ref=x_ref, dst_ref=near.at[landing], send_sem=s1.at[p], recv_sem=r1.at[landing],
            device_id=job.device(job.o * job.inner + p), device_id_type=MESH)

    for job, (x_ref, near, far, group, s1, r1, s2, r2) in zip(jobs[::-1], bufs[::-1]):
        if job.axis == "hours":

            @pl.when(has_up)
            def _():
                b_copy.wait_recv()
                a_src[...] = a_ref[...] + b_buf[...]

            @pl.when(jnp.logical_not(has_up))
            def _():
                a_src[...] = a_ref[...]

        for s in range(1, job.inner):
            across(job, x_ref, near, s1, r1, lax.rem(job.i + s, job.inner), job.i).start()

    @pl.when(has_down)
    def _():
        main_copy.start()

    parts = []
    for job, (x_ref, near, far, group, s1, r1, s2, r2) in zip(jobs, bufs):
        for s in range(1, job.inner):
            p = lax.rem(job.i + s, job.inner)
            across(job, x_ref, near, s1, r1, p, job.i).wait_send()
            across(job, x_ref, near, s1, r1, p, p).wait_recv()
        own = x_ref[...]
        total = own
        part = own if job.mode == "sum" else jnp.zeros_like(own)
        for s in range(1, job.inner):
            p = lax.rem(job.i + s, job.inner)
            block = near[p]
            total = total + block
            if job.mode == "sum":
                part = part + block
            else:
                part = part + jnp.where(wanted(job.mode, p, job.i), block, 0.0)
        group[...] = total
        parts.append(part)

    def up(job, group, far, s2, r2, q, landing):
        return pltpu.make_async_remote_copy(
            src_ref=group, dst_ref=far.at[landing], send_sem=s2.at[q], recv_sem=r2.at[landing],
            device_id=job.device(q * job.inner + job.i), device_id_type=MESH)

    for job, (x_ref, near, far, group, s1, r1, s2, r2) in zip(jobs, bufs):
        for s in range(1, job.outer):
            q = lax.rem(job.o + s, job.outer)

            @pl.when(wanted(job.mode, job.o, q))
            def _():
                up(job, group, far, s2, r2, q, job.o).start()

    results = []
    for job, part, (x_ref, near, far, group, s1, r1, s2, r2) in zip(jobs, parts, bufs):
        for s in range(1, job.outer):
            q = lax.rem(job.o + s, job.outer)

            @pl.when(wanted(job.mode, job.o, q))
            def _():
                up(job, group, far, s2, r2, q, job.o).wait_send()

            @pl.when(wanted(job.mode, q, job.o))
            def _():
                up(job, group, far, s2, r2, q, q).wait_recv()

        for s in range(1, job.outer):
            q = lax.rem(job.o + s, job.outer)
            part = part + jnp.where(wanted(job.mode, q, job.o), far[q], 0.0)
        results.append(part)
    scanned, supplied = results
    pa_ref[...] = scanned
    supplied_ref[...] = supplied

    @pl.when(has_down)
    def _():
        main_copy.wait_send()
        b_copy.wait_send()

    @pl.when(has_after)
    def _():
        rim_own_copy.wait_send()

    @pl.when(diag_down)
    def _():
        rim_next_copy.wait_send()

    @pl.when(has_up)
    def _():
        main_copy.wait_recv()
        incoming_ref[...] = incoming_buf[...]

    @pl.when(jnp.logical_not(has_up))
    def _():
        incoming_ref[...] = jnp.zeros_like(incoming_ref)

    @pl.when(has_before)
    def _():
        rim_own_copy.wait_recv()
        rim_own_in_ref[...] = rim_own_buf[...]

    @pl.when(jnp.logical_not(has_before))
    def _():
        rim_own_in_ref[...] = jnp.zeros_like(rim_own_in_ref)

    @pl.when(diag_up)
    def _():
        rim_next_copy.wait_recv()
        rim_next_in_ref[...] = rim_next_buf[...]

    @pl.when(jnp.logical_not(diag_up))
    def _():
        rim_next_in_ref[...] = jnp.zeros_like(rim_next_in_ref)


def flow_exchange(main_next, rim_own, rim_next, own_totals, next_totals, power):
    res, width = own_totals.shape
    a = own_totals.reshape(-1, 128)
    b = next_totals.reshape(-1, 128)
    flat_power = power.reshape(-1, 128)
    inner = 8
    outer_h = lax.axis_size("hours") // inner
    outer_r = lax.axis_size("river") // inner
    vmem = pl.BlockSpec(memory_space=pltpu.VMEM)
    shape = lambda x: jax.ShapeDtypeStruct(x.shape, x.dtype)
    incoming, rim_own_in, rim_next_in, pa, supplied = pl.pallas_call(
        flow_kernel,
        out_shape=[shape(main_next), shape(rim_own), shape(rim_next), shape(a), shape(flat_power)],
        in_specs=[vmem] * 6,
        out_specs=[vmem] * 5,
        scratch_shapes=[
            pltpu.VMEM((inner,) + a.shape, a.dtype),
            pltpu.VMEM((outer_h,) + a.shape, a.dtype),
            pltpu.VMEM(a.shape, a.dtype),
            pltpu.VMEM((inner,) + flat_power.shape, a.dtype),
            pltpu.VMEM((outer_r,) + flat_power.shape, a.dtype),
            pltpu.VMEM(flat_power.shape, a.dtype),
            pltpu.VMEM(main_next.shape, a.dtype),
            pltpu.VMEM(rim_own.shape, a.dtype),
            pltpu.VMEM(rim_next.shape, a.dtype),
            pltpu.VMEM(a.shape, a.dtype),
            pltpu.VMEM(a.shape, a.dtype),
            pltpu.SemaphoreType.DMA((inner,)),
            pltpu.SemaphoreType.DMA((inner,)),
            pltpu.SemaphoreType.DMA((outer_h,)),
            pltpu.SemaphoreType.DMA((outer_h,)),
            pltpu.SemaphoreType.DMA((inner,)),
            pltpu.SemaphoreType.DMA((inner,)),
            pltpu.SemaphoreType.DMA((outer_r,)),
            pltpu.SemaphoreType.DMA((outer_r,)),
            pltpu.SemaphoreType.DMA((8,)),
        ],
        compiler_params=pltpu.CompilerParams(collective_id=1, has_side_effects=True, vmem_limit_bytes=48 * 1024 * 1024),
    )(main_next, rim_own, rim_next, a, b, flat_power)
    return incoming, rim_own_in, rim_next_in, pa.reshape(res, width), supplied.reshape(power.shape)


def combine(parts, specs, collective):
    shapes = [part.shape for part in parts]
    parts = [part.reshape(-1, 128) for part in parts]
    jobs = [Job(axis, mode, inner, lax.axis_size(axis)) for axis, mode, inner in specs]
    scratch = []
    for part, job in zip(parts, jobs):
        scratch += [
            pltpu.VMEM((job.inner,) + part.shape, part.dtype),
            pltpu.VMEM((job.outer,) + part.shape, part.dtype),
            pltpu.VMEM(part.shape, part.dtype),
            pltpu.SemaphoreType.DMA((job.inner,)),
            pltpu.SemaphoreType.DMA((job.inner,)),
            pltpu.SemaphoreType.DMA((job.outer,)),
            pltpu.SemaphoreType.DMA((job.outer,)),
        ]
    results = pl.pallas_call(
        functools.partial(multi_kernel, jobs),
        out_shape=[jax.ShapeDtypeStruct(part.shape, part.dtype) for part in parts],
        in_specs=[pl.BlockSpec(memory_space=pltpu.VMEM)] * len(parts),
        out_specs=[pl.BlockSpec(memory_space=pltpu.VMEM)] * len(parts),
        scratch_shapes=scratch,
        compiler_params=pltpu.CompilerParams(collective_id=collective, has_side_effects=True),
    )(*parts)
    return [result.reshape(shape) for result, shape in zip(results, shapes)]


def add_pair(earlier_part, later_part):
    return earlier_part + later_part


def hold_back(field, travel_delay, earlier_rim):
    length = field.shape[1]
    extended = jnp.concatenate([earlier_rim, field], 1)
    result = jnp.zeros_like(field)
    for lag_hours in range(1, DMAX + 1):
        window = extended[:, DMAX - lag_hours : DMAX - lag_hours + length]
        result = result + jnp.where((travel_delay == lag_hours)[:, None, None], window, 0.0)
    return result


def bring_forward(field, travel_delay, later_rim):
    length = field.shape[1]
    extended = jnp.concatenate([field, later_rim], 1)
    result = jnp.zeros_like(field)
    for lag_hours in range(1, DMAX + 1):
        window = extended[:, lag_hours : lag_hours + length]
        result = result + jnp.where((travel_delay == lag_hours)[:, None, None], window, 0.0)
    return result


def route_down(matrix, field):
    return jnp.einsum("ij,jtw->itw", matrix, field, precision=lax.Precision.HIGHEST)


def route_up(matrix, field):
    return jnp.einsum("ij,itw->jtw", matrix, field, precision=lax.Precision.HIGHEST)


def iterate(fields, statics, scales, suffix_sum, from_earlier, from_later):
    release, storage_dual, demand_dual, cost, inflow, demand = fields
    (
        storage_start,
        storage_low,
        storage_high,
        release_cap,
        efficiency,
        travel_delay,
        to_own,
        to_next,
    ) = statics
    scale_time, scale_sum = scales
    local = suffix_local(storage_dual)
    off, off_next, beyond, rim_own, rim_next = dual_exchange(local)
    suffix = local + off[:, None]
    at_sink = route_up(to_own, suffix) + route_up(to_next, beyond + off_next[:, None])
    last = lax.axis_index("hours") == lax.axis_size("hours") - 1
    rim_sink = route_up(to_own, rim_own + off[:, None]) + route_up(to_next, rim_next + off_next[:, None])
    later_duals = bring_forward(at_sink, travel_delay, jnp.where(last, 0.0, rim_sink))
    gradient = (
        cost
        + scale_time * (later_duals - suffix)
        + scale_sum * efficiency[:, None, None] * demand_dual[None]
    )
    release_new = jnp.clip(release - primal_step * gradient, 0.0, release_cap[:, None, None])
    extrapolated = 2.0 * release_new - release
    length = extrapolated.shape[1]
    tail = extrapolated[:, length - DMAX :]
    settled = hold_back(extrapolated, travel_delay, jnp.zeros_like(tail))
    rim_delayed = hold_back(jnp.zeros_like(extrapolated), travel_delay, tail)[:, :DMAX]
    main_own = route_down(to_own, settled)
    main_next = route_down(to_next, settled)
    rim_own = route_down(to_own, rim_delayed)
    rim_next = route_down(to_next, rim_delayed)
    base = inflow + main_own - extrapolated
    own_totals = jnp.sum(base, 1) + jnp.sum(rim_own, 1)
    next_totals = jnp.sum(main_next, 1) + jnp.sum(rim_next, 1)
    partial_power = jnp.sum(scale_sum * efficiency[:, None, None] * extrapolated, 0)
    incoming, rim_own_in, rim_next_in, offset, supplied = flow_exchange(
        main_next, rim_own, rim_next, own_totals, next_totals, partial_power
    )
    arrived = jnp.concatenate([rim_own_in + rim_next_in, jnp.zeros_like(base[:, DMAX:])], 1)
    local_sum = jnp.cumsum(base + incoming + arrived, 1)
    offset = offset - jnp.sum(rim_own_in, 1) - jnp.sum(rim_next_in, 1)
    storage = storage_start[:, None, None] + scale_time * (local_sum + offset[:, None])
    lower_bound = storage_low[:, None, None]
    upper_bound = storage_high[:, None, None]
    storage_dual_new = (
        storage_dual
        + dual_step * storage
        - dual_step * jnp.clip(storage_dual / dual_step + storage, lower_bound, upper_bound)
    )
    storage_excess = storage - jnp.clip(storage, lower_bound, upper_bound)
    demand_dual_new = jnp.minimum(demand_dual + dual_step * (supplied - demand), 0.0)
    return (release_new, storage_dual_new, demand_dual_new, storage_excess)


def suffix_local(field):
    return lax.cumsum(field, 1, reverse=True)


def shards(
    release,
    storage_dual,
    demand_dual,
    cost,
    inflow,
    demand,
    storage_start,
    storage_low,
    storage_high,
    release_cap,
    efficiency,
    downstream,
    travel_delay,
):
    res_dev = release.shape[0]
    scale_time = 1.0 / (release.shape[1] * lax.axis_size("hours"))
    scale_sum = 1.0 / math.sqrt(res_dev * lax.axis_size("river"))
    base_index = lax.axis_index("river") * res_dev
    target = downstream - base_index
    indices = jnp.arange(res_dev, dtype=jnp.int32)
    to_own = (target[None, :] == indices[:, None]).astype(jnp.float32)
    to_next = (target[None, :] == indices[:, None] + res_dev).astype(jnp.float32)
    statics = (
        storage_start,
        storage_low,
        storage_high,
        release_cap,
        efficiency,
        travel_delay,
        to_own,
        to_next,
    )
    scales = (scale_time, scale_sum)

    def suffix_blocks(field):
        local_sum = suffix_local(field)
        totals = local_sum[:, 0]
        (offset,) = combine([totals], [("hours", "suffix", 8)], 0)
        return local_sum + offset[:, None]

    def earlier_block(part):
        return passed_along(part, "hours", 1)

    def later_block(part):
        return passed_along(part, "hours", -1)

    fields = (release, storage_dual, demand_dual, cost, inflow, demand)
    return iterate(
        fields, statics, scales, suffix_blocks, earlier_block, later_block
    )


def solution(mesh):
    return jax.shard_map(
        shards,
        mesh=mesh,
        in_specs=(
            P("river", "hours", None),
            P("river", "hours", None),
            P("hours", None),
            P("river", "hours", None),
            P("river", "hours", None),
            P("hours", None),
            P("river"),
            P("river"),
            P("river"),
            P("river"),
            P("river"),
            P("river"),
            P("river"),
        ),
        out_specs=(
            P("river", "hours", None),
            P("river", "hours", None),
            P("hours", None),
            P("river", "hours", None),
        ),
        check_vma=False,
    )
```

```python
import functools
import math

import jax
import jax.numpy as jnp
from jax import lax
from jax.experimental import pallas as pl
from jax.experimental.pallas import tpu as pltpu
from jax.sharding import PartitionSpec as P

DMAX = 6


primal_step = 1.0
dual_step = 0.1


def passed_along(block, axis, distance):
    devices = range(lax.axis_size(axis))
    route = [(i - distance, i) for i in devices if i - distance in devices]
    return lax.ppermute(block, axis, route)


MESH = pl.DeviceIdType.MESH


def wanted(mode, src, dst):
    if mode == "prefix":
        return src < dst
    if mode == "suffix":
        return src > dst
    return src != dst


class Job:
    def __init__(self, axis, mode, inner, n):
        self.axis, self.mode, self.inner = axis, mode, inner
        self.outer = n // inner
        self.other = "river" if axis == "hours" else "hours"

    def place(self):
        me = lax.axis_index(self.axis)
        self.fixed = lax.axis_index(self.other)
        self.o = me // self.inner
        self.i = me % self.inner

    def device(self, p):
        return (self.fixed, p) if self.axis == "hours" else (p, self.fixed)

    def peers(self):
        inner, outer, o, i = self.inner, self.outer, self.o, self.i
        near = [self.device(o * inner + lax.rem(i + s, inner)) for s in range(1, inner)]
        far = [self.device(lax.rem(o + s, outer) * inner + i) for s in range(1, outer)]
        return near + far


def multi_kernel(jobs, *refs):
    count = len(jobs)
    ins, outs, rest = refs[:count], refs[count:2 * count], refs[2 * count:]
    for job in jobs:
        job.place()
    barrier = pltpu.get_barrier_semaphore()
    partners = 0
    for job in jobs:
        for dev in job.peers():
            pl.semaphore_signal(barrier, 1, device_id=dev, device_id_type=MESH)
            partners += 1
    pl.semaphore_wait(barrier, partners)

    def across(job, x_ref, near, s1, r1, p, landing):
        return pltpu.make_async_remote_copy(
            src_ref=x_ref, dst_ref=near.at[landing], send_sem=s1.at[p], recv_sem=r1.at[landing],
            device_id=job.device(job.o * job.inner + p), device_id_type=MESH)

    for k, job in enumerate(jobs):
        near, far, group, s1, r1, s2, r2 = rest[7 * k:7 * k + 7]
        for s in range(1, job.inner):
            p = lax.rem(job.i + s, job.inner)
            across(job, ins[k], near, s1, r1, p, job.i).start()
    parts = []
    for k, job in enumerate(jobs):
        near, far, group, s1, r1, s2, r2 = rest[7 * k:7 * k + 7]
        for s in range(1, job.inner):
            p = lax.rem(job.i + s, job.inner)
            across(job, ins[k], near, s1, r1, p, job.i).wait_send()
            across(job, ins[k], near, s1, r1, p, p).wait_recv()
        own = ins[k][...]
        total = own
        part = own if job.mode == "sum" else jnp.zeros_like(own)
        for s in range(1, job.inner):
            p = lax.rem(job.i + s, job.inner)
            block = near[p]
            total = total + block
            if job.mode == "sum":
                part = part + block
            else:
                part = part + jnp.where(wanted(job.mode, p, job.i), block, 0.0)
        group[...] = total
        parts.append(part)

    def up(job, group, far, s2, r2, q, landing):
        return pltpu.make_async_remote_copy(
            src_ref=group, dst_ref=far.at[landing], send_sem=s2.at[q], recv_sem=r2.at[landing],
            device_id=job.device(q * job.inner + job.i), device_id_type=MESH)

    for k, job in enumerate(jobs):
        near, far, group, s1, r1, s2, r2 = rest[7 * k:7 * k + 7]
        for s in range(1, job.outer):
            q = lax.rem(job.o + s, job.outer)

            @pl.when(wanted(job.mode, job.o, q))
            def _():
                up(job, group, far, s2, r2, q, job.o).start()

    for k, job in enumerate(jobs):
        near, far, group, s1, r1, s2, r2 = rest[7 * k:7 * k + 7]
        part = parts[k]
        for s in range(1, job.outer):
            q = lax.rem(job.o + s, job.outer)

            @pl.when(wanted(job.mode, job.o, q))
            def _():
                up(job, group, far, s2, r2, q, job.o).wait_send()

            @pl.when(wanted(job.mode, q, job.o))
            def _():
                up(job, group, far, s2, r2, q, q).wait_recv()

        for s in range(1, job.outer):
            q = lax.rem(job.o + s, job.outer)
            part = part + jnp.where(wanted(job.mode, q, job.o), far[q], 0.0)
        outs[k][...] = part


def dual_kernel(
    sloc_ref, t_ref, off_ref, off_next_ref, beyond_ref, rim_own_ref, rim_next_ref,
    near, far, group, beyond_buf, rim_src_own, rim_src_next, rim_own_buf, rim_next_buf,
    off_src, off_next_buf, s1, r1, s2, r2, sems,
):
    job = Job("hours", "suffix", 8, lax.axis_size("hours"))
    job.place()
    n_r = lax.axis_size("river")
    n_h = lax.axis_size("hours")
    r = lax.axis_index("river")
    h = lax.axis_index("hours")
    has_up, has_down = r > 0, r < n_r - 1
    has_before, has_after = h > 0, h < n_h - 1

    barrier = pltpu.get_barrier_semaphore()
    for dev in job.peers():
        pl.semaphore_signal(barrier, 1, device_id=dev, device_id_type=MESH)
    for flag, dev in ((has_up, (r - 1, h)), (has_down, (r + 1, h)), (has_before, (r, h - 1)), (has_after, (r, h + 1))):

        @pl.when(flag)
        def _():
            pl.semaphore_signal(barrier, 1, device_id=dev, device_id_type=MESH)

    extra = sum(jnp.where(flag, 1, 0) for flag in (has_up, has_down, has_before, has_after))
    pl.semaphore_wait(barrier, job.inner + job.outer - 2 + extra)

    def link(src, dst, k, dev):
        return pltpu.make_async_remote_copy(
            src_ref=src, dst_ref=dst, send_sem=sems.at[2 * k], recv_sem=sems.at[2 * k + 1],
            device_id=dev, device_id_type=MESH)

    to_up = lambda src, dst, k: link(src, dst, k, (r - 1, h))
    to_before = lambda src, dst, k: link(src, dst, k, (r, h - 1))

    def across(p, landing):
        return pltpu.make_async_remote_copy(
            src_ref=t_ref, dst_ref=near.at[landing], send_sem=s1.at[p], recv_sem=r1.at[landing],
            device_id=job.device(job.o * job.inner + p), device_id_type=MESH)

    for s in range(1, job.inner):
        across(lax.rem(job.i + s, job.inner), job.i).start()

    @pl.when(has_up)
    def _():
        to_up(sloc_ref, beyond_buf, 0).start()

    rim_src_own[...] = sloc_ref[:, 0:DMAX, :] - sloc_ref[:, 0:1, :]

    @pl.when(has_before)
    def _():
        to_before(rim_src_own, rim_own_buf, 1).start()

    for s in range(1, job.inner):
        p = lax.rem(job.i + s, job.inner)
        across(p, job.i).wait_send()
        across(p, p).wait_recv()
    own = t_ref[...]
    total = own
    part = jnp.zeros_like(own)
    for s in range(1, job.inner):
        p = lax.rem(job.i + s, job.inner)
        block = near[p]
        total = total + block
        part = part + jnp.where(p > job.i, block, 0.0)
    group[...] = total

    def up(q, landing):
        return pltpu.make_async_remote_copy(
            src_ref=group, dst_ref=far.at[landing], send_sem=s2.at[q], recv_sem=r2.at[landing],
            device_id=job.device(q * job.inner + job.i), device_id_type=MESH)

    for s in range(1, job.outer):
        q = lax.rem(job.o + s, job.outer)

        @pl.when(job.o > q)
        def _():
            up(q, job.o).start()

    @pl.when(has_down)
    def _():
        to_up(sloc_ref, beyond_buf, 0).wait_recv()
        rim_src_next[...] = beyond_buf[:, 0:DMAX, :] - beyond_buf[:, 0:1, :]

    @pl.when(jnp.logical_and(has_down, has_before))
    def _():
        to_before(rim_src_next, rim_next_buf, 2).start()

    for s in range(1, job.outer):
        q = lax.rem(job.o + s, job.outer)

        @pl.when(job.o > q)
        def _():
            up(q, job.o).wait_send()

        @pl.when(q > job.o)
        def _():
            up(q, q).wait_recv()

    for s in range(1, job.outer):
        q = lax.rem(job.o + s, job.outer)
        part = part + jnp.where(q > job.o, far[q], 0.0)
    off_src[...] = part
    off_ref[...] = part

    @pl.when(has_up)
    def _():
        to_up(off_src, off_next_buf, 3).start()

    @pl.when(has_up)
    def _():
        to_up(sloc_ref, beyond_buf, 0).wait_send()
        to_up(off_src, off_next_buf, 3).wait_send()

    @pl.when(has_before)
    def _():
        to_before(rim_src_own, rim_own_buf, 1).wait_send()

    @pl.when(jnp.logical_and(has_down, has_before))
    def _():
        to_before(rim_src_next, rim_next_buf, 2).wait_send()

    @pl.when(has_after)
    def _():
        to_before(rim_src_own, rim_own_buf, 1).wait_recv()
        rim_own_ref[...] = rim_own_buf[...]

    @pl.when(jnp.logical_not(has_after))
    def _():
        rim_own_ref[...] = jnp.zeros_like(rim_own_ref)

    @pl.when(jnp.logical_and(has_down, has_after))
    def _():
        to_before(rim_src_next, rim_next_buf, 2).wait_recv()
        rim_next_ref[...] = rim_next_buf[...]

    @pl.when(jnp.logical_not(jnp.logical_and(has_down, has_after)))
    def _():
        rim_next_ref[...] = jnp.zeros_like(rim_next_ref)

    @pl.when(has_down)
    def _():
        to_up(off_src, off_next_buf, 3).wait_recv()
        off_next_ref[...] = off_next_buf[...]
        beyond_ref[...] = beyond_buf[...]

    @pl.when(jnp.logical_not(has_down))
    def _():
        off_next_ref[...] = jnp.zeros_like(off_next_ref)
        beyond_ref[...] = jnp.zeros_like(beyond_ref)


def dual_exchange(sloc):
    res, length, width = sloc.shape
    t = sloc[:, 0].reshape(-1, 128)
    inner = 8
    outer = lax.axis_size("hours") // inner
    rim = (res, DMAX, width)
    vmem = pl.BlockSpec(memory_space=pltpu.VMEM)
    off, off_next, beyond, rim_own, rim_next = pl.pallas_call(
        dual_kernel,
        out_shape=[
            jax.ShapeDtypeStruct(t.shape, t.dtype),
            jax.ShapeDtypeStruct(t.shape, t.dtype),
            jax.ShapeDtypeStruct(sloc.shape, sloc.dtype),
            jax.ShapeDtypeStruct(rim, sloc.dtype),
            jax.ShapeDtypeStruct(rim, sloc.dtype),
        ],
        in_specs=[vmem, vmem],
        out_specs=[vmem] * 5,
        scratch_shapes=[
            pltpu.VMEM((inner,) + t.shape, t.dtype),
            pltpu.VMEM((outer,) + t.shape, t.dtype),
            pltpu.VMEM(t.shape, t.dtype),
            pltpu.VMEM(sloc.shape, sloc.dtype),
            pltpu.VMEM(rim, sloc.dtype),
            pltpu.VMEM(rim, sloc.dtype),
            pltpu.VMEM(rim, sloc.dtype),
            pltpu.VMEM(rim, sloc.dtype),
            pltpu.VMEM(t.shape, t.dtype),
            pltpu.VMEM(t.shape, t.dtype),
            pltpu.SemaphoreType.DMA((inner,)),
            pltpu.SemaphoreType.DMA((inner,)),
            pltpu.SemaphoreType.DMA((outer,)),
            pltpu.SemaphoreType.DMA((outer,)),
            pltpu.SemaphoreType.DMA((8,)),
        ],
        compiler_params=pltpu.CompilerParams(collective_id=0, has_side_effects=True, vmem_limit_bytes=48 * 1024 * 1024),
    )(sloc, t)
    return off.reshape(res, width), off_next.reshape(res, width), beyond, rim_own, rim_next


def flow_kernel(
    main_ref, rim_own_ref, rim_next_ref, a_ref, b_ref, power_ref,
    incoming_ref, rim_own_in_ref, rim_next_in_ref, pa_ref, supplied_ref,
    near_h, far_h, group_h, near_r, far_r, group_r, incoming_buf, rim_own_buf, rim_next_buf,
    a_src, b_buf, s1h, r1h, s2h, r2h, s1r, r1r, s2r, r2r, sems,
):
    jobs = [Job("hours", "prefix", 8, lax.axis_size("hours")), Job("river", "sum", 8, lax.axis_size("river"))]
    for job in jobs:
        job.place()
    n_r = lax.axis_size("river")
    n_h = lax.axis_size("hours")
    r = lax.axis_index("river")
    h = lax.axis_index("hours")
    has_up, has_down = r > 0, r < n_r - 1
    has_before, has_after = h > 0, h < n_h - 1
    diag_down = jnp.logical_and(has_down, has_after)
    diag_up = jnp.logical_and(has_up, has_before)

    barrier = pltpu.get_barrier_semaphore()
    fixed = 0
    for job in jobs:
        for dev in job.peers():
            pl.semaphore_signal(barrier, 1, device_id=dev, device_id_type=MESH)
            fixed += 1
    links = (
        (has_up, (r - 1, h)), (has_down, (r + 1, h)), (has_before, (r, h - 1)), (has_after, (r, h + 1)),
        (diag_down, (r + 1, h + 1)), (diag_up, (r - 1, h - 1)),
    )
    for flag, dev in links:

        @pl.when(flag)
        def _():
            pl.semaphore_signal(barrier, 1, device_id=dev, device_id_type=MESH)

    extra = sum(jnp.where(flag, 1, 0) for flag, _ in links)
    pl.semaphore_wait(barrier, fixed + extra)

    def link(src, dst, k, dev):
        return pltpu.make_async_remote_copy(
            src_ref=src, dst_ref=dst, send_sem=sems.at[2 * k], recv_sem=sems.at[2 * k + 1],
            device_id=dev, device_id_type=MESH)

    main_copy = link(main_ref, incoming_buf, 0, (r + 1, h))
    rim_own_copy = link(rim_own_ref, rim_own_buf, 1, (r, h + 1))
    rim_next_copy = link(rim_next_ref, rim_next_buf, 2, (r + 1, h + 1))
    b_copy = link(b_ref, b_buf, 3, (r + 1, h))

    @pl.when(has_down)
    def _():
        b_copy.start()
        main_copy.start()

    @pl.when(has_after)
    def _():
        rim_own_copy.start()

    @pl.when(diag_down)
    def _():
        rim_next_copy.start()

    bufs = [(a_src, near_h, far_h, group_h, s1h, r1h, s2h, r2h), (power_ref, near_r, far_r, group_r, s1r, r1r, s2r, r2r)]

    def across(job, x_ref, near, s1, r1, p, landing):
        return pltpu.make_async_remote_copy(
            src_ref=x_ref, dst_ref=near.at[landing], send_sem=s1.at[p], recv_sem=r1.at[landing],
            device_id=job.device(job.o * job.inner + p), device_id_type=MESH)

    for job, (x_ref, near, far, group, s1, r1, s2, r2) in zip(jobs[::-1], bufs[::-1]):
        if job.axis == "hours":

            @pl.when(has_up)
            def _():
                b_copy.wait_recv()
                a_src[...] = a_ref[...] + b_buf[...]

            @pl.when(jnp.logical_not(has_up))
            def _():
                a_src[...] = a_ref[...]

        for s in range(1, job.inner):
            across(job, x_ref, near, s1, r1, lax.rem(job.i + s, job.inner), job.i).start()
    parts = []
    for job, (x_ref, near, far, group, s1, r1, s2, r2) in zip(jobs, bufs):
        for s in range(1, job.inner):
            p = lax.rem(job.i + s, job.inner)
            across(job, x_ref, near, s1, r1, p, job.i).wait_send()
            across(job, x_ref, near, s1, r1, p, p).wait_recv()
        own = x_ref[...]
        total = own
        part = own if job.mode == "sum" else jnp.zeros_like(own)
        for s in range(1, job.inner):
            p = lax.rem(job.i + s, job.inner)
            block = near[p]
            total = total + block
            if job.mode == "sum":
                part = part + block
            else:
                part = part + jnp.where(wanted(job.mode, p, job.i), block, 0.0)
        group[...] = total
        parts.append(part)

    def up(job, group, far, s2, r2, q, landing):
        return pltpu.make_async_remote_copy(
            src_ref=group, dst_ref=far.at[landing], send_sem=s2.at[q], recv_sem=r2.at[landing],
            device_id=job.device(q * job.inner + job.i), device_id_type=MESH)

    for job, (x_ref, near, far, group, s1, r1, s2, r2) in zip(jobs, bufs):
        for s in range(1, job.outer):
            q = lax.rem(job.o + s, job.outer)

            @pl.when(wanted(job.mode, job.o, q))
            def _():
                up(job, group, far, s2, r2, q, job.o).start()

    results = []
    for job, part, (x_ref, near, far, group, s1, r1, s2, r2) in zip(jobs, parts, bufs):
        for s in range(1, job.outer):
            q = lax.rem(job.o + s, job.outer)

            @pl.when(wanted(job.mode, job.o, q))
            def _():
                up(job, group, far, s2, r2, q, job.o).wait_send()

            @pl.when(wanted(job.mode, q, job.o))
            def _():
                up(job, group, far, s2, r2, q, q).wait_recv()

        for s in range(1, job.outer):
            q = lax.rem(job.o + s, job.outer)
            part = part + jnp.where(wanted(job.mode, q, job.o), far[q], 0.0)
        results.append(part)
    scanned, supplied = results
    pa_ref[...] = scanned
    supplied_ref[...] = supplied

    @pl.when(has_down)
    def _():
        main_copy.wait_send()
        b_copy.wait_send()

    @pl.when(has_after)
    def _():
        rim_own_copy.wait_send()

    @pl.when(diag_down)
    def _():
        rim_next_copy.wait_send()

    @pl.when(has_up)
    def _():
        main_copy.wait_recv()
        incoming_ref[...] = incoming_buf[...]

    @pl.when(jnp.logical_not(has_up))
    def _():
        incoming_ref[...] = jnp.zeros_like(incoming_ref)

    @pl.when(has_before)
    def _():
        rim_own_copy.wait_recv()
        rim_own_in_ref[...] = rim_own_buf[...]

    @pl.when(jnp.logical_not(has_before))
    def _():
        rim_own_in_ref[...] = jnp.zeros_like(rim_own_in_ref)

    @pl.when(diag_up)
    def _():
        rim_next_copy.wait_recv()
        rim_next_in_ref[...] = rim_next_buf[...]

    @pl.when(jnp.logical_not(diag_up))
    def _():
        rim_next_in_ref[...] = jnp.zeros_like(rim_next_in_ref)


def flow_exchange(main_next, rim_own, rim_next, own_totals, next_totals, power):
    res, width = own_totals.shape
    a = own_totals.reshape(-1, 128)
    b = next_totals.reshape(-1, 128)
    flat_power = power.reshape(-1, 128)
    inner = 8
    outer_h = lax.axis_size("hours") // inner
    outer_r = lax.axis_size("river") // inner
    vmem = pl.BlockSpec(memory_space=pltpu.VMEM)
    shape = lambda x: jax.ShapeDtypeStruct(x.shape, x.dtype)
    incoming, rim_own_in, rim_next_in, pa, supplied = pl.pallas_call(
        flow_kernel,
        out_shape=[shape(main_next), shape(rim_own), shape(rim_next), shape(a), shape(flat_power)],
        in_specs=[vmem] * 6,
        out_specs=[vmem] * 5,
        scratch_shapes=[
            pltpu.VMEM((inner,) + a.shape, a.dtype),
            pltpu.VMEM((outer_h,) + a.shape, a.dtype),
            pltpu.VMEM(a.shape, a.dtype),
            pltpu.VMEM((inner,) + flat_power.shape, a.dtype),
            pltpu.VMEM((outer_r,) + flat_power.shape, a.dtype),
            pltpu.VMEM(flat_power.shape, a.dtype),
            pltpu.VMEM(main_next.shape, a.dtype),
            pltpu.VMEM(rim_own.shape, a.dtype),
            pltpu.VMEM(rim_next.shape, a.dtype),
            pltpu.VMEM(a.shape, a.dtype),
            pltpu.VMEM(a.shape, a.dtype),
            pltpu.SemaphoreType.DMA((inner,)),
            pltpu.SemaphoreType.DMA((inner,)),
            pltpu.SemaphoreType.DMA((outer_h,)),
            pltpu.SemaphoreType.DMA((outer_h,)),
            pltpu.SemaphoreType.DMA((inner,)),
            pltpu.SemaphoreType.DMA((inner,)),
            pltpu.SemaphoreType.DMA((outer_r,)),
            pltpu.SemaphoreType.DMA((outer_r,)),
            pltpu.SemaphoreType.DMA((8,)),
        ],
        compiler_params=pltpu.CompilerParams(collective_id=1, has_side_effects=True, vmem_limit_bytes=48 * 1024 * 1024),
    )(main_next, rim_own, rim_next, a, b, flat_power)
    return incoming, rim_own_in, rim_next_in, pa.reshape(res, width), supplied.reshape(power.shape)


def combine(parts, specs, collective):
    shapes = [part.shape for part in parts]
    parts = [part.reshape(-1, 128) for part in parts]
    jobs = [Job(axis, mode, inner, lax.axis_size(axis)) for axis, mode, inner in specs]
    scratch = []
    for part, job in zip(parts, jobs):
        scratch += [
            pltpu.VMEM((job.inner,) + part.shape, part.dtype),
            pltpu.VMEM((job.outer,) + part.shape, part.dtype),
            pltpu.VMEM(part.shape, part.dtype),
            pltpu.SemaphoreType.DMA((job.inner,)),
            pltpu.SemaphoreType.DMA((job.inner,)),
            pltpu.SemaphoreType.DMA((job.outer,)),
            pltpu.SemaphoreType.DMA((job.outer,)),
        ]
    results = pl.pallas_call(
        functools.partial(multi_kernel, jobs),
        out_shape=[jax.ShapeDtypeStruct(part.shape, part.dtype) for part in parts],
        in_specs=[pl.BlockSpec(memory_space=pltpu.VMEM)] * len(parts),
        out_specs=[pl.BlockSpec(memory_space=pltpu.VMEM)] * len(parts),
        scratch_shapes=scratch,
        compiler_params=pltpu.CompilerParams(collective_id=collective, has_side_effects=True),
    )(*parts)
    return [result.reshape(shape) for result, shape in zip(results, shapes)]


def add_pair(earlier_part, later_part):
    return earlier_part + later_part


def hold_back(field, travel_delay, earlier_rim):
    length = field.shape[1]
    extended = jnp.concatenate([earlier_rim, field], 1)
    result = jnp.zeros_like(field)
    for lag_hours in range(1, DMAX + 1):
        window = extended[:, DMAX - lag_hours : DMAX - lag_hours + length]
        result = result + jnp.where((travel_delay == lag_hours)[:, None, None], window, 0.0)
    return result


def bring_forward(field, travel_delay, later_rim):
    length = field.shape[1]
    extended = jnp.concatenate([field, later_rim], 1)
    result = jnp.zeros_like(field)
    for lag_hours in range(1, DMAX + 1):
        window = extended[:, lag_hours : lag_hours + length]
        result = result + jnp.where((travel_delay == lag_hours)[:, None, None], window, 0.0)
    return result


def route_down(matrix, field):
    return jnp.einsum("ij,jtw->itw", matrix, field, precision=lax.Precision.HIGHEST)


def route_up(matrix, field):
    return jnp.einsum("ij,itw->jtw", matrix, field, precision=lax.Precision.HIGHEST)


def iterate(fields, statics, scales, suffix_sum, from_earlier, from_later):
    release, storage_dual, demand_dual, cost, inflow, demand = fields
    (
        storage_start,
        storage_low,
        storage_high,
        release_cap,
        efficiency,
        travel_delay,
        to_own,
        to_next,
    ) = statics
    scale_time, scale_sum = scales
    local = suffix_local(storage_dual)
    off, off_next, beyond, rim_own, rim_next = dual_exchange(local)
    suffix = local + off[:, None]
    both = jnp.concatenate([to_own, to_next], 0)
    at_sink = route_up(both, jnp.concatenate([suffix, beyond + off_next[:, None]], 0))
    last = lax.axis_index("hours") == lax.axis_size("hours") - 1
    rim_sink = route_up(both, jnp.concatenate([rim_own + off[:, None], rim_next + off_next[:, None]], 0))
    later_duals = bring_forward(at_sink, travel_delay, jnp.where(last, 0.0, rim_sink))
    gradient = (
        cost
        + scale_time * (later_duals - suffix)
        + scale_sum * efficiency[:, None, None] * demand_dual[None]
    )
    release_new = jnp.clip(release - primal_step * gradient, 0.0, release_cap[:, None, None])
    extrapolated = 2.0 * release_new - release
    length = extrapolated.shape[1]
    tail = extrapolated[:, length - DMAX :]
    settled = hold_back(extrapolated, travel_delay, jnp.zeros_like(tail))
    rim_delayed = hold_back(jnp.zeros_like(extrapolated), travel_delay, tail)[:, :DMAX]
    res = settled.shape[0]
    main = route_down(both, settled)
    main_own, main_next = main[:res], main[res:]
    rims = route_down(both, rim_delayed)
    rim_own, rim_next = rims[:res], rims[res:]
    base = inflow + main_own - extrapolated
    own_totals = jnp.sum(base, 1) + jnp.sum(rim_own, 1)
    next_totals = jnp.sum(main_next, 1) + jnp.sum(rim_next, 1)
    partial_power = jnp.sum(scale_sum * efficiency[:, None, None] * extrapolated, 0)
    incoming, rim_own_in, rim_next_in, offset, supplied = flow_exchange(
        main_next, rim_own, rim_next, own_totals, next_totals, partial_power
    )
    arrived = jnp.concatenate([rim_own_in + rim_next_in, jnp.zeros_like(base[:, DMAX:])], 1)
    local_sum = jnp.cumsum(base + incoming + arrived, 1)
    offset = offset - jnp.sum(rim_own_in, 1) - jnp.sum(rim_next_in, 1)
    storage = storage_start[:, None, None] + scale_time * (local_sum + offset[:, None])
    lower_bound = storage_low[:, None, None]
    upper_bound = storage_high[:, None, None]
    storage_dual_new = (
        storage_dual
        + dual_step * storage
        - dual_step * jnp.clip(storage_dual / dual_step + storage, lower_bound, upper_bound)
    )
    storage_excess = storage - jnp.clip(storage, lower_bound, upper_bound)
    demand_dual_new = jnp.minimum(demand_dual + dual_step * (supplied - demand), 0.0)
    return (release_new, storage_dual_new, demand_dual_new, storage_excess)


def suffix_local(field):
    return lax.cumsum(field, 1, reverse=True)


def shards(
    release,
    storage_dual,
    demand_dual,
    cost,
    inflow,
    demand,
    storage_start,
    storage_low,
    storage_high,
    release_cap,
    efficiency,
    downstream,
    travel_delay,
):
    res_dev = release.shape[0]
    scale_time = 1.0 / (release.shape[1] * lax.axis_size("hours"))
    scale_sum = 1.0 / math.sqrt(res_dev * lax.axis_size("river"))
    base_index = lax.axis_index("river") * res_dev
    target = downstream - base_index
    indices = jnp.arange(res_dev, dtype=jnp.int32)
    to_own = (target[None, :] == indices[:, None]).astype(jnp.float32)
    to_next = (target[None, :] == indices[:, None] + res_dev).astype(jnp.float32)
    statics = (
        storage_start,
        storage_low,
        storage_high,
        release_cap,
        efficiency,
        travel_delay,
        to_own,
        to_next,
    )
    scales = (scale_time, scale_sum)

    def suffix_blocks(field):
        local_sum = suffix_local(field)
        totals = local_sum[:, 0]
        (offset,) = combine([totals], [("hours", "suffix", 8)], 0)
        return local_sum + offset[:, None]

    def earlier_block(part):
        return passed_along(part, "hours", 1)

    def later_block(part):
        return passed_along(part, "hours", -1)

    fields = (release, storage_dual, demand_dual, cost, inflow, demand)
    return iterate(
        fields, statics, scales, suffix_blocks, earlier_block, later_block
    )


def solution(mesh):
    return jax.shard_map(
        shards,
        mesh=mesh,
        in_specs=(
            P("river", "hours", None),
            P("river", "hours", None),
            P("hours", None),
            P("river", "hours", None),
            P("river", "hours", None),
            P("hours", None),
            P("river"),
            P("river"),
            P("river"),
            P("river"),
            P("river"),
            P("river"),
            P("river"),
        ),
        out_specs=(
            P("river", "hours", None),
            P("river", "hours", None),
            P("hours", None),
            P("river", "hours", None),
        ),
        check_vma=False,
    )
```

```python
import functools
import math

import jax
import jax.numpy as jnp
from jax import lax
from jax.experimental import pallas as pl
from jax.experimental.pallas import tpu as pltpu
from jax.sharding import PartitionSpec as P

DMAX = 6


primal_step = 1.0
dual_step = 0.1


def passed_along(block, axis, distance):
    devices = range(lax.axis_size(axis))
    route = [(i - distance, i) for i in devices if i - distance in devices]
    return lax.ppermute(block, axis, route)


MESH = pl.DeviceIdType.MESH


def wanted(mode, src, dst):
    if mode == "prefix":
        return src < dst
    if mode == "suffix":
        return src > dst
    return src != dst


class Job:
    def __init__(self, axis, mode, inner, n):
        self.axis, self.mode, self.inner = axis, mode, inner
        self.outer = n // inner
        self.other = "river" if axis == "hours" else "hours"

    def place(self):
        me = lax.axis_index(self.axis)
        self.fixed = lax.axis_index(self.other)
        self.o = me // self.inner
        self.i = me % self.inner

    def device(self, p):
        return (self.fixed, p) if self.axis == "hours" else (p, self.fixed)

    def peers(self):
        inner, outer, o, i = self.inner, self.outer, self.o, self.i
        near = [self.device(o * inner + lax.rem(i + s, inner)) for s in range(1, inner)]
        far = [self.device(lax.rem(o + s, outer) * inner + i) for s in range(1, outer)]
        return near + far


def multi_kernel(jobs, *refs):
    count = len(jobs)
    ins, outs, rest = refs[:count], refs[count:2 * count], refs[2 * count:]
    for job in jobs:
        job.place()
    barrier = pltpu.get_barrier_semaphore()
    partners = 0
    for job in jobs:
        for dev in job.peers():
            pl.semaphore_signal(barrier, 1, device_id=dev, device_id_type=MESH)
            partners += 1
    pl.semaphore_wait(barrier, partners)

    def across(job, x_ref, near, s1, r1, p, landing):
        return pltpu.make_async_remote_copy(
            src_ref=x_ref, dst_ref=near.at[landing], send_sem=s1.at[p], recv_sem=r1.at[landing],
            device_id=job.device(job.o * job.inner + p), device_id_type=MESH)

    for k, job in enumerate(jobs):
        near, far, group, s1, r1, s2, r2 = rest[7 * k:7 * k + 7]
        for s in range(1, job.inner):
            p = lax.rem(job.i + s, job.inner)
            across(job, ins[k], near, s1, r1, p, job.i).start()
    parts = []
    for k, job in enumerate(jobs):
        near, far, group, s1, r1, s2, r2 = rest[7 * k:7 * k + 7]
        for s in range(1, job.inner):
            p = lax.rem(job.i + s, job.inner)
            across(job, ins[k], near, s1, r1, p, job.i).wait_send()
            across(job, ins[k], near, s1, r1, p, p).wait_recv()
        own = ins[k][...]
        total = own
        part = own if job.mode == "sum" else jnp.zeros_like(own)
        for s in range(1, job.inner):
            p = lax.rem(job.i + s, job.inner)
            block = near[p]
            total = total + block
            if job.mode == "sum":
                part = part + block
            else:
                part = part + jnp.where(wanted(job.mode, p, job.i), block, 0.0)
        group[...] = total
        parts.append(part)

    def up(job, group, far, s2, r2, q, landing):
        return pltpu.make_async_remote_copy(
            src_ref=group, dst_ref=far.at[landing], send_sem=s2.at[q], recv_sem=r2.at[landing],
            device_id=job.device(q * job.inner + job.i), device_id_type=MESH)

    for k, job in enumerate(jobs):
        near, far, group, s1, r1, s2, r2 = rest[7 * k:7 * k + 7]
        for s in range(1, job.outer):
            q = lax.rem(job.o + s, job.outer)

            @pl.when(wanted(job.mode, job.o, q))
            def _():
                up(job, group, far, s2, r2, q, job.o).start()

    for k, job in enumerate(jobs):
        near, far, group, s1, r1, s2, r2 = rest[7 * k:7 * k + 7]
        part = parts[k]
        for s in range(1, job.outer):
            q = lax.rem(job.o + s, job.outer)

            @pl.when(wanted(job.mode, job.o, q))
            def _():
                up(job, group, far, s2, r2, q, job.o).wait_send()

            @pl.when(wanted(job.mode, q, job.o))
            def _():
                up(job, group, far, s2, r2, q, q).wait_recv()

        for s in range(1, job.outer):
            q = lax.rem(job.o + s, job.outer)
            part = part + jnp.where(wanted(job.mode, q, job.o), far[q], 0.0)
        outs[k][...] = part


def dual_kernel(
    sloc_ref, t_ref, *refs,
):
    count = (len(refs) - 21) // 2
    held_in, refs = refs[:count], refs[count:]
    off_ref, off_next_ref, beyond_ref, rim_own_ref, rim_next_ref = refs[:5]
    held_out, refs = refs[5:5 + count], refs[5 + count:]
    (near, far, group, beyond_buf, rim_src_own, rim_src_next, rim_own_buf, rim_next_buf,
     off_src, off_next_buf, s1, r1, s2, r2, sems, local) = refs
    fetches = [pltpu.make_async_copy(a, b, local.at[k]) for k, (a, b) in enumerate(zip(held_in, held_out))]
    for fetch in fetches:
        fetch.start()
    job = Job("hours", "suffix", 8, lax.axis_size("hours"))
    job.place()
    n_r = lax.axis_size("river")
    n_h = lax.axis_size("hours")
    r = lax.axis_index("river")
    h = lax.axis_index("hours")
    has_up, has_down = r > 0, r < n_r - 1
    has_before, has_after = h > 0, h < n_h - 1

    barrier = pltpu.get_barrier_semaphore()
    for dev in job.peers():
        pl.semaphore_signal(barrier, 1, device_id=dev, device_id_type=MESH)
    for flag, dev in ((has_up, (r - 1, h)), (has_down, (r + 1, h)), (has_before, (r, h - 1)), (has_after, (r, h + 1))):

        @pl.when(flag)
        def _():
            pl.semaphore_signal(barrier, 1, device_id=dev, device_id_type=MESH)

    extra = sum(jnp.where(flag, 1, 0) for flag in (has_up, has_down, has_before, has_after))
    pl.semaphore_wait(barrier, job.inner + job.outer - 2 + extra)

    def link(src, dst, k, dev):
        return pltpu.make_async_remote_copy(
            src_ref=src, dst_ref=dst, send_sem=sems.at[2 * k], recv_sem=sems.at[2 * k + 1],
            device_id=dev, device_id_type=MESH)

    to_up = lambda src, dst, k: link(src, dst, k, (r - 1, h))
    to_before = lambda src, dst, k: link(src, dst, k, (r, h - 1))

    def across(p, landing):
        return pltpu.make_async_remote_copy(
            src_ref=t_ref, dst_ref=near.at[landing], send_sem=s1.at[p], recv_sem=r1.at[landing],
            device_id=job.device(job.o * job.inner + p), device_id_type=MESH)

    for s in range(1, job.inner):
        across(lax.rem(job.i + s, job.inner), job.i).start()

    @pl.when(has_up)
    def _():
        to_up(sloc_ref, beyond_buf, 0).start()

    rim_src_own[...] = sloc_ref[:, 0:DMAX, :] - sloc_ref[:, 0:1, :]

    @pl.when(has_before)
    def _():
        to_before(rim_src_own, rim_own_buf, 1).start()

    for s in range(1, job.inner):
        p = lax.rem(job.i + s, job.inner)
        across(p, job.i).wait_send()
        across(p, p).wait_recv()
    own = t_ref[...]
    total = own
    part = jnp.zeros_like(own)
    for s in range(1, job.inner):
        p = lax.rem(job.i + s, job.inner)
        block = near[p]
        total = total + block
        part = part + jnp.where(p > job.i, block, 0.0)
    group[...] = total

    def up(q, landing):
        return pltpu.make_async_remote_copy(
            src_ref=group, dst_ref=far.at[landing], send_sem=s2.at[q], recv_sem=r2.at[landing],
            device_id=job.device(q * job.inner + job.i), device_id_type=MESH)

    for s in range(1, job.outer):
        q = lax.rem(job.o + s, job.outer)

        @pl.when(job.o > q)
        def _():
            up(q, job.o).start()

    @pl.when(has_down)
    def _():
        to_up(sloc_ref, beyond_buf, 0).wait_recv()
        rim_src_next[...] = beyond_buf[:, 0:DMAX, :] - beyond_buf[:, 0:1, :]

    @pl.when(jnp.logical_and(has_down, has_before))
    def _():
        to_before(rim_src_next, rim_next_buf, 2).start()

    for s in range(1, job.outer):
        q = lax.rem(job.o + s, job.outer)

        @pl.when(job.o > q)
        def _():
            up(q, job.o).wait_send()

        @pl.when(q > job.o)
        def _():
            up(q, q).wait_recv()

    for s in range(1, job.outer):
        q = lax.rem(job.o + s, job.outer)
        part = part + jnp.where(q > job.o, far[q], 0.0)
    off_src[...] = part
    off_ref[...] = part

    @pl.when(has_up)
    def _():
        to_up(off_src, off_next_buf, 3).start()

    @pl.when(has_up)
    def _():
        to_up(sloc_ref, beyond_buf, 0).wait_send()
        to_up(off_src, off_next_buf, 3).wait_send()

    @pl.when(has_before)
    def _():
        to_before(rim_src_own, rim_own_buf, 1).wait_send()

    @pl.when(jnp.logical_and(has_down, has_before))
    def _():
        to_before(rim_src_next, rim_next_buf, 2).wait_send()

    @pl.when(has_after)
    def _():
        to_before(rim_src_own, rim_own_buf, 1).wait_recv()
        rim_own_ref[...] = rim_own_buf[...]

    @pl.when(jnp.logical_not(has_after))
    def _():
        rim_own_ref[...] = jnp.zeros_like(rim_own_ref)

    @pl.when(jnp.logical_and(has_down, has_after))
    def _():
        to_before(rim_src_next, rim_next_buf, 2).wait_recv()
        rim_next_ref[...] = rim_next_buf[...]

    @pl.when(jnp.logical_not(jnp.logical_and(has_down, has_after)))
    def _():
        rim_next_ref[...] = jnp.zeros_like(rim_next_ref)

    @pl.when(has_down)
    def _():
        to_up(off_src, off_next_buf, 3).wait_recv()
        off_next_ref[...] = off_next_buf[...]
        beyond_ref[...] = beyond_buf[...]

    @pl.when(jnp.logical_not(has_down))
    def _():
        off_next_ref[...] = jnp.zeros_like(off_next_ref)
        beyond_ref[...] = jnp.zeros_like(beyond_ref)

    for fetch in fetches:
        fetch.wait()


def dual_exchange(sloc, held):
    res, length, width = sloc.shape
    t = sloc[:, 0].reshape(-1, 128)
    inner = 8
    outer = lax.axis_size("hours") // inner
    rim = (res, DMAX, width)
    vmem = pl.BlockSpec(memory_space=pltpu.VMEM)
    outs = pl.pallas_call(
        dual_kernel,
        out_shape=[
            jax.ShapeDtypeStruct(t.shape, t.dtype),
            jax.ShapeDtypeStruct(t.shape, t.dtype),
            jax.ShapeDtypeStruct(sloc.shape, sloc.dtype),
            jax.ShapeDtypeStruct(rim, sloc.dtype),
            jax.ShapeDtypeStruct(rim, sloc.dtype),
        ] + [jax.ShapeDtypeStruct(a.shape, a.dtype) for a in held],
        in_specs=[vmem, vmem] + [pl.BlockSpec(memory_space=pl.ANY)] * len(held),
        out_specs=[vmem] * (5 + len(held)),
        scratch_shapes=[
            pltpu.VMEM((inner,) + t.shape, t.dtype),
            pltpu.VMEM((outer,) + t.shape, t.dtype),
            pltpu.VMEM(t.shape, t.dtype),
            pltpu.VMEM(sloc.shape, sloc.dtype),
            pltpu.VMEM(rim, sloc.dtype),
            pltpu.VMEM(rim, sloc.dtype),
            pltpu.VMEM(rim, sloc.dtype),
            pltpu.VMEM(rim, sloc.dtype),
            pltpu.VMEM(t.shape, t.dtype),
            pltpu.VMEM(t.shape, t.dtype),
            pltpu.SemaphoreType.DMA((inner,)),
            pltpu.SemaphoreType.DMA((inner,)),
            pltpu.SemaphoreType.DMA((outer,)),
            pltpu.SemaphoreType.DMA((outer,)),
            pltpu.SemaphoreType.DMA((8,)),
            pltpu.SemaphoreType.DMA((len(held),)),
        ],
        compiler_params=pltpu.CompilerParams(collective_id=0, has_side_effects=True, vmem_limit_bytes=48 * 1024 * 1024),
    )(sloc, t, *held)
    off, off_next, beyond, rim_own, rim_next = outs[:5]
    return off.reshape(res, width), off_next.reshape(res, width), beyond, rim_own, rim_next, outs[5:]


def flow_kernel(
    main_ref, rim_own_ref, rim_next_ref, a_ref, b_ref, power_ref,
    incoming_ref, rim_own_in_ref, rim_next_in_ref, pa_ref, supplied_ref,
    near_h, far_h, group_h, near_r, far_r, group_r, incoming_buf, rim_own_buf, rim_next_buf,
    a_src, b_buf, s1h, r1h, s2h, r2h, s1r, r1r, s2r, r2r, sems,
):
    jobs = [Job("hours", "prefix", 8, lax.axis_size("hours")), Job("river", "sum", 8, lax.axis_size("river"))]
    for job in jobs:
        job.place()
    n_r = lax.axis_size("river")
    n_h = lax.axis_size("hours")
    r = lax.axis_index("river")
    h = lax.axis_index("hours")
    has_up, has_down = r > 0, r < n_r - 1
    has_before, has_after = h > 0, h < n_h - 1
    diag_down = jnp.logical_and(has_down, has_after)
    diag_up = jnp.logical_and(has_up, has_before)

    barrier = pltpu.get_barrier_semaphore()
    fixed = 0
    for job in jobs:
        for dev in job.peers():
            pl.semaphore_signal(barrier, 1, device_id=dev, device_id_type=MESH)
            fixed += 1
    links = (
        (has_up, (r - 1, h)), (has_down, (r + 1, h)), (has_before, (r, h - 1)), (has_after, (r, h + 1)),
        (diag_down, (r + 1, h + 1)), (diag_up, (r - 1, h - 1)),
    )
    for flag, dev in links:

        @pl.when(flag)
        def _():
            pl.semaphore_signal(barrier, 1, device_id=dev, device_id_type=MESH)

    extra = sum(jnp.where(flag, 1, 0) for flag, _ in links)
    pl.semaphore_wait(barrier, fixed + extra)

    def link(src, dst, k, dev):
        return pltpu.make_async_remote_copy(
            src_ref=src, dst_ref=dst, send_sem=sems.at[2 * k], recv_sem=sems.at[2 * k + 1],
            device_id=dev, device_id_type=MESH)

    main_copy = link(main_ref, incoming_buf, 0, (r + 1, h))
    rim_own_copy = link(rim_own_ref, rim_own_buf, 1, (r, h + 1))
    rim_next_copy = link(rim_next_ref, rim_next_buf, 2, (r + 1, h + 1))
    b_copy = link(b_ref, b_buf, 3, (r + 1, h))

    @pl.when(has_down)
    def _():
        b_copy.start()
        main_copy.start()

    @pl.when(has_after)
    def _():
        rim_own_copy.start()

    @pl.when(diag_down)
    def _():
        rim_next_copy.start()

    bufs = [(a_src, near_h, far_h, group_h, s1h, r1h, s2h, r2h), (power_ref, near_r, far_r, group_r, s1r, r1r, s2r, r2r)]

    def across(job, x_ref, near, s1, r1, p, landing):
        return pltpu.make_async_remote_copy(
            src_ref=x_ref, dst_ref=near.at[landing], send_sem=s1.at[p], recv_sem=r1.at[landing],
            device_id=job.device(job.o * job.inner + p), device_id_type=MESH)

    for job, (x_ref, near, far, group, s1, r1, s2, r2) in zip(jobs[::-1], bufs[::-1]):
        if job.axis == "hours":

            @pl.when(has_up)
            def _():
                b_copy.wait_recv()
                a_src[...] = a_ref[...] + b_buf[...]

            @pl.when(jnp.logical_not(has_up))
            def _():
                a_src[...] = a_ref[...]

        for s in range(1, job.inner):
            across(job, x_ref, near, s1, r1, lax.rem(job.i + s, job.inner), job.i).start()
    parts = []
    for job, (x_ref, near, far, group, s1, r1, s2, r2) in zip(jobs, bufs):
        for s in range(1, job.inner):
            p = lax.rem(job.i + s, job.inner)
            across(job, x_ref, near, s1, r1, p, job.i).wait_send()
            across(job, x_ref, near, s1, r1, p, p).wait_recv()
        own = x_ref[...]
        total = own
        part = own if job.mode == "sum" else jnp.zeros_like(own)
        for s in range(1, job.inner):
            p = lax.rem(job.i + s, job.inner)
            block = near[p]
            total = total + block
            if job.mode == "sum":
                part = part + block
            else:
                part = part + jnp.where(wanted(job.mode, p, job.i), block, 0.0)
        group[...] = total
        parts.append(part)

    def up(job, group, far, s2, r2, q, landing):
        return pltpu.make_async_remote_copy(
            src_ref=group, dst_ref=far.at[landing], send_sem=s2.at[q], recv_sem=r2.at[landing],
            device_id=job.device(q * job.inner + job.i), device_id_type=MESH)

    for job, (x_ref, near, far, group, s1, r1, s2, r2) in zip(jobs, bufs):
        for s in range(1, job.outer):
            q = lax.rem(job.o + s, job.outer)

            @pl.when(wanted(job.mode, job.o, q))
            def _():
                up(job, group, far, s2, r2, q, job.o).start()

    results = []
    for job, part, (x_ref, near, far, group, s1, r1, s2, r2) in zip(jobs, parts, bufs):
        for s in range(1, job.outer):
            q = lax.rem(job.o + s, job.outer)

            @pl.when(wanted(job.mode, job.o, q))
            def _():
                up(job, group, far, s2, r2, q, job.o).wait_send()

            @pl.when(wanted(job.mode, q, job.o))
            def _():
                up(job, group, far, s2, r2, q, q).wait_recv()

        for s in range(1, job.outer):
            q = lax.rem(job.o + s, job.outer)
            part = part + jnp.where(wanted(job.mode, q, job.o), far[q], 0.0)
        results.append(part)
    scanned, supplied = results
    pa_ref[...] = scanned
    supplied_ref[...] = supplied

    @pl.when(has_down)
    def _():
        main_copy.wait_send()
        b_copy.wait_send()

    @pl.when(has_after)
    def _():
        rim_own_copy.wait_send()

    @pl.when(diag_down)
    def _():
        rim_next_copy.wait_send()

    @pl.when(has_up)
    def _():
        main_copy.wait_recv()
        incoming_ref[...] = incoming_buf[...]

    @pl.when(jnp.logical_not(has_up))
    def _():
        incoming_ref[...] = jnp.zeros_like(incoming_ref)

    @pl.when(has_before)
    def _():
        rim_own_copy.wait_recv()
        rim_own_in_ref[...] = rim_own_buf[...]

    @pl.when(jnp.logical_not(has_before))
    def _():
        rim_own_in_ref[...] = jnp.zeros_like(rim_own_in_ref)

    @pl.when(diag_up)
    def _():
        rim_next_copy.wait_recv()
        rim_next_in_ref[...] = rim_next_buf[...]

    @pl.when(jnp.logical_not(diag_up))
    def _():
        rim_next_in_ref[...] = jnp.zeros_like(rim_next_in_ref)


def flow_exchange(main_next, rim_own, rim_next, own_totals, next_totals, power):
    res, width = own_totals.shape
    a = own_totals.reshape(-1, 128)
    b = next_totals.reshape(-1, 128)
    flat_power = power.reshape(-1, 128)
    inner = 8
    outer_h = lax.axis_size("hours") // inner
    outer_r = lax.axis_size("river") // inner
    vmem = pl.BlockSpec(memory_space=pltpu.VMEM)
    shape = lambda x: jax.ShapeDtypeStruct(x.shape, x.dtype)
    incoming, rim_own_in, rim_next_in, pa, supplied = pl.pallas_call(
        flow_kernel,
        out_shape=[shape(main_next), shape(rim_own), shape(rim_next), shape(a), shape(flat_power)],
        in_specs=[vmem] * 6,
        out_specs=[vmem] * 5,
        scratch_shapes=[
            pltpu.VMEM((inner,) + a.shape, a.dtype),
            pltpu.VMEM((outer_h,) + a.shape, a.dtype),
            pltpu.VMEM(a.shape, a.dtype),
            pltpu.VMEM((inner,) + flat_power.shape, a.dtype),
            pltpu.VMEM((outer_r,) + flat_power.shape, a.dtype),
            pltpu.VMEM(flat_power.shape, a.dtype),
            pltpu.VMEM(main_next.shape, a.dtype),
            pltpu.VMEM(rim_own.shape, a.dtype),
            pltpu.VMEM(rim_next.shape, a.dtype),
            pltpu.VMEM(a.shape, a.dtype),
            pltpu.VMEM(a.shape, a.dtype),
            pltpu.SemaphoreType.DMA((inner,)),
            pltpu.SemaphoreType.DMA((inner,)),
            pltpu.SemaphoreType.DMA((outer_h,)),
            pltpu.SemaphoreType.DMA((outer_h,)),
            pltpu.SemaphoreType.DMA((inner,)),
            pltpu.SemaphoreType.DMA((inner,)),
            pltpu.SemaphoreType.DMA((outer_r,)),
            pltpu.SemaphoreType.DMA((outer_r,)),
            pltpu.SemaphoreType.DMA((8,)),
        ],
        compiler_params=pltpu.CompilerParams(collective_id=1, has_side_effects=True, vmem_limit_bytes=48 * 1024 * 1024),
    )(main_next, rim_own, rim_next, a, b, flat_power)
    return incoming, rim_own_in, rim_next_in, pa.reshape(res, width), supplied.reshape(power.shape)


def combine(parts, specs, collective):
    shapes = [part.shape for part in parts]
    parts = [part.reshape(-1, 128) for part in parts]
    jobs = [Job(axis, mode, inner, lax.axis_size(axis)) for axis, mode, inner in specs]
    scratch = []
    for part, job in zip(parts, jobs):
        scratch += [
            pltpu.VMEM((job.inner,) + part.shape, part.dtype),
            pltpu.VMEM((job.outer,) + part.shape, part.dtype),
            pltpu.VMEM(part.shape, part.dtype),
            pltpu.SemaphoreType.DMA((job.inner,)),
            pltpu.SemaphoreType.DMA((job.inner,)),
            pltpu.SemaphoreType.DMA((job.outer,)),
            pltpu.SemaphoreType.DMA((job.outer,)),
        ]
    results = pl.pallas_call(
        functools.partial(multi_kernel, jobs),
        out_shape=[jax.ShapeDtypeStruct(part.shape, part.dtype) for part in parts],
        in_specs=[pl.BlockSpec(memory_space=pltpu.VMEM)] * len(parts),
        out_specs=[pl.BlockSpec(memory_space=pltpu.VMEM)] * len(parts),
        scratch_shapes=scratch,
        compiler_params=pltpu.CompilerParams(collective_id=collective, has_side_effects=True),
    )(*parts)
    return [result.reshape(shape) for result, shape in zip(results, shapes)]


def add_pair(earlier_part, later_part):
    return earlier_part + later_part


def hold_back(field, travel_delay, earlier_rim):
    length = field.shape[1]
    extended = jnp.concatenate([earlier_rim, field], 1)
    result = jnp.zeros_like(field)
    for lag_hours in range(1, DMAX + 1):
        window = extended[:, DMAX - lag_hours : DMAX - lag_hours + length]
        result = result + jnp.where((travel_delay == lag_hours)[:, None, None], window, 0.0)
    return result


def bring_forward(field, travel_delay, later_rim):
    length = field.shape[1]
    extended = jnp.concatenate([field, later_rim], 1)
    result = jnp.zeros_like(field)
    for lag_hours in range(1, DMAX + 1):
        window = extended[:, lag_hours : lag_hours + length]
        result = result + jnp.where((travel_delay == lag_hours)[:, None, None], window, 0.0)
    return result


def route_down(matrix, field):
    return jnp.einsum("ij,jtw->itw", matrix, field, precision=lax.Precision.HIGHEST)


def route_up(matrix, field):
    return jnp.einsum("ij,itw->jtw", matrix, field, precision=lax.Precision.HIGHEST)


def iterate(fields, statics, scales, suffix_sum, from_earlier, from_later):
    release, storage_dual, demand_dual, cost, inflow, demand = fields
    (
        storage_start,
        storage_low,
        storage_high,
        release_cap,
        efficiency,
        travel_delay,
        to_own,
        to_next,
    ) = statics
    scale_time, scale_sum = scales
    local = suffix_local(storage_dual)
    off, off_next, beyond, rim_own, rim_next, held = dual_exchange(local, [release, cost, inflow, storage_dual])
    release, cost, inflow, storage_dual = held
    suffix = local + off[:, None]
    both = jnp.concatenate([to_own, to_next], 0)
    at_sink = route_up(both, jnp.concatenate([suffix, beyond + off_next[:, None]], 0))
    last = lax.axis_index("hours") == lax.axis_size("hours") - 1
    rim_sink = route_up(both, jnp.concatenate([rim_own + off[:, None], rim_next + off_next[:, None]], 0))
    later_duals = bring_forward(at_sink, travel_delay, jnp.where(last, 0.0, rim_sink))
    gradient = (
        cost
        + scale_time * (later_duals - suffix)
        + scale_sum * efficiency[:, None, None] * demand_dual[None]
    )
    release_new = jnp.clip(release - primal_step * gradient, 0.0, release_cap[:, None, None])
    extrapolated = 2.0 * release_new - release
    length = extrapolated.shape[1]
    tail = extrapolated[:, length - DMAX :]
    settled = hold_back(extrapolated, travel_delay, jnp.zeros_like(tail))
    rim_delayed = hold_back(jnp.zeros_like(extrapolated), travel_delay, tail)[:, :DMAX]
    res = settled.shape[0]
    main = route_down(both, settled)
    main_own, main_next = main[:res], main[res:]
    rims = route_down(both, rim_delayed)
    rim_own, rim_next = rims[:res], rims[res:]
    base = inflow + main_own - extrapolated
    own_totals = jnp.sum(base, 1) + jnp.sum(rim_own, 1)
    next_totals = jnp.sum(main_next, 1) + jnp.sum(rim_next, 1)
    partial_power = jnp.sum(scale_sum * efficiency[:, None, None] * extrapolated, 0)
    incoming, rim_own_in, rim_next_in, offset, supplied = flow_exchange(
        main_next, rim_own, rim_next, own_totals, next_totals, partial_power
    )
    arrived = jnp.concatenate([rim_own_in + rim_next_in, jnp.zeros_like(base[:, DMAX:])], 1)
    local_sum = jnp.cumsum(base + incoming + arrived, 1)
    offset = offset - jnp.sum(rim_own_in, 1) - jnp.sum(rim_next_in, 1)
    storage = storage_start[:, None, None] + scale_time * (local_sum + offset[:, None])
    lower_bound = storage_low[:, None, None]
    upper_bound = storage_high[:, None, None]
    storage_dual_new = (
        storage_dual
        + dual_step * storage
        - dual_step * jnp.clip(storage_dual / dual_step + storage, lower_bound, upper_bound)
    )
    storage_excess = storage - jnp.clip(storage, lower_bound, upper_bound)
    demand_dual_new = jnp.minimum(demand_dual + dual_step * (supplied - demand), 0.0)
    return (release_new, storage_dual_new, demand_dual_new, storage_excess)


def suffix_local(field):
    return lax.cumsum(field, 1, reverse=True)


def shards(
    release,
    storage_dual,
    demand_dual,
    cost,
    inflow,
    demand,
    storage_start,
    storage_low,
    storage_high,
    release_cap,
    efficiency,
    downstream,
    travel_delay,
):
    res_dev = release.shape[0]
    scale_time = 1.0 / (release.shape[1] * lax.axis_size("hours"))
    scale_sum = 1.0 / math.sqrt(res_dev * lax.axis_size("river"))
    base_index = lax.axis_index("river") * res_dev
    target = downstream - base_index
    indices = jnp.arange(res_dev, dtype=jnp.int32)
    to_own = (target[None, :] == indices[:, None]).astype(jnp.float32)
    to_next = (target[None, :] == indices[:, None] + res_dev).astype(jnp.float32)
    statics = (
        storage_start,
        storage_low,
        storage_high,
        release_cap,
        efficiency,
        travel_delay,
        to_own,
        to_next,
    )
    scales = (scale_time, scale_sum)

    def suffix_blocks(field):
        local_sum = suffix_local(field)
        totals = local_sum[:, 0]
        (offset,) = combine([totals], [("hours", "suffix", 8)], 0)
        return local_sum + offset[:, None]

    def earlier_block(part):
        return passed_along(part, "hours", 1)

    def later_block(part):
        return passed_along(part, "hours", -1)

    fields = (release, storage_dual, demand_dual, cost, inflow, demand)
    return iterate(
        fields, statics, scales, suffix_blocks, earlier_block, later_block
    )


def solution(mesh):
    return jax.shard_map(
        shards,
        mesh=mesh,
        in_specs=(
            P("river", "hours", None),
            P("river", "hours", None),
            P("hours", None),
            P("river", "hours", None),
            P("river", "hours", None),
            P("hours", None),
            P("river"),
            P("river"),
            P("river"),
            P("river"),
            P("river"),
            P("river"),
            P("river"),
        ),
        out_specs=(
            P("river", "hours", None),
            P("river", "hours", None),
            P("hours", None),
            P("river", "hours", None),
        ),
        check_vma=False,
    )
```

```python
import functools
import math

import jax
import jax.numpy as jnp
from jax import lax
from jax.experimental import pallas as pl
from jax.experimental.pallas import tpu as pltpu
from jax.sharding import PartitionSpec as P

DMAX = 6


primal_step = 1.0
dual_step = 0.1


def passed_along(block, axis, distance):
    devices = range(lax.axis_size(axis))
    route = [(i - distance, i) for i in devices if i - distance in devices]
    return lax.ppermute(block, axis, route)


MESH = pl.DeviceIdType.MESH


def wanted(mode, src, dst):
    if mode == "prefix":
        return src < dst
    if mode == "suffix":
        return src > dst
    return src != dst


class Job:
    def __init__(self, axis, mode, inner, n):
        self.axis, self.mode, self.inner = axis, mode, inner
        self.outer = n // inner
        self.other = "river" if axis == "hours" else "hours"

    def place(self):
        me = lax.axis_index(self.axis)
        self.fixed = lax.axis_index(self.other)
        self.o = me // self.inner
        self.i = me % self.inner

    def device(self, p):
        return (self.fixed, p) if self.axis == "hours" else (p, self.fixed)

    def peers(self):
        inner, outer, o, i = self.inner, self.outer, self.o, self.i
        near = [self.device(o * inner + lax.rem(i + s, inner)) for s in range(1, inner)]
        far = [self.device(lax.rem(o + s, outer) * inner + i) for s in range(1, outer)]
        return near + far


def multi_kernel(jobs, *refs):
    count = len(jobs)
    ins, outs, rest = refs[:count], refs[count:2 * count], refs[2 * count:]
    for job in jobs:
        job.place()
    barrier = pltpu.get_barrier_semaphore()
    partners = 0
    for job in jobs:
        for dev in job.peers():
            pl.semaphore_signal(barrier, 1, device_id=dev, device_id_type=MESH)
            partners += 1
    pl.semaphore_wait(barrier, partners)

    def across(job, x_ref, near, s1, r1, p, landing):
        return pltpu.make_async_remote_copy(
            src_ref=x_ref, dst_ref=near.at[landing], send_sem=s1.at[p], recv_sem=r1.at[landing],
            device_id=job.device(job.o * job.inner + p), device_id_type=MESH)

    for k, job in enumerate(jobs):
        near, far, group, s1, r1, s2, r2 = rest[7 * k:7 * k + 7]
        for s in range(1, job.inner):
            p = lax.rem(job.i + s, job.inner)
            across(job, ins[k], near, s1, r1, p, job.i).start()
    parts = []
    for k, job in enumerate(jobs):
        near, far, group, s1, r1, s2, r2 = rest[7 * k:7 * k + 7]
        for s in range(1, job.inner):
            p = lax.rem(job.i + s, job.inner)
            across(job, ins[k], near, s1, r1, p, job.i).wait_send()
            across(job, ins[k], near, s1, r1, p, p).wait_recv()
        own = ins[k][...]
        total = own
        part = own if job.mode == "sum" else jnp.zeros_like(own)
        for s in range(1, job.inner):
            p = lax.rem(job.i + s, job.inner)
            block = near[p]
            total = total + block
            if job.mode == "sum":
                part = part + block
            else:
                part = part + jnp.where(wanted(job.mode, p, job.i), block, 0.0)
        group[...] = total
        parts.append(part)

    def up(job, group, far, s2, r2, q, landing):
        return pltpu.make_async_remote_copy(
            src_ref=group, dst_ref=far.at[landing], send_sem=s2.at[q], recv_sem=r2.at[landing],
            device_id=job.device(q * job.inner + job.i), device_id_type=MESH)

    for k, job in enumerate(jobs):
        near, far, group, s1, r1, s2, r2 = rest[7 * k:7 * k + 7]
        for s in range(1, job.outer):
            q = lax.rem(job.o + s, job.outer)

            @pl.when(wanted(job.mode, job.o, q))
            def _():
                up(job, group, far, s2, r2, q, job.o).start()

    for k, job in enumerate(jobs):
        near, far, group, s1, r1, s2, r2 = rest[7 * k:7 * k + 7]
        part = parts[k]
        for s in range(1, job.outer):
            q = lax.rem(job.o + s, job.outer)

            @pl.when(wanted(job.mode, job.o, q))
            def _():
                up(job, group, far, s2, r2, q, job.o).wait_send()

            @pl.when(wanted(job.mode, q, job.o))
            def _():
                up(job, group, far, s2, r2, q, q).wait_recv()

        for s in range(1, job.outer):
            q = lax.rem(job.o + s, job.outer)
            part = part + jnp.where(wanted(job.mode, q, job.o), far[q], 0.0)
        outs[k][...] = part


def dual_kernel(
    sloc_ref, t_ref, off_ref, off_next_ref, beyond_ref, rim_own_ref, rim_next_ref,
    near, far, group, beyond_buf, rim_src_own, rim_src_next, rim_own_buf, rim_next_buf,
    off_src, off_next_buf, s1, r1, s2, r2, sems,
):
    job = Job("hours", "suffix", 8, lax.axis_size("hours"))
    job.place()
    n_r = lax.axis_size("river")
    n_h = lax.axis_size("hours")
    r = lax.axis_index("river")
    h = lax.axis_index("hours")
    has_up, has_down = r > 0, r < n_r - 1
    has_before, has_after = h > 0, h < n_h - 1

    barrier = pltpu.get_barrier_semaphore()
    for dev in job.peers():
        pl.semaphore_signal(barrier, 1, device_id=dev, device_id_type=MESH)
    for flag, dev in ((has_up, (r - 1, h)), (has_down, (r + 1, h)), (has_before, (r, h - 1)), (has_after, (r, h + 1))):

        @pl.when(flag)
        def _():
            pl.semaphore_signal(barrier, 1, device_id=dev, device_id_type=MESH)

    extra = sum(jnp.where(flag, 1, 0) for flag in (has_up, has_down, has_before, has_after))
    pl.semaphore_wait(barrier, job.inner + job.outer - 2 + extra)

    def link(src, dst, k, dev):
        return pltpu.make_async_remote_copy(
            src_ref=src, dst_ref=dst, send_sem=sems.at[2 * k], recv_sem=sems.at[2 * k + 1],
            device_id=dev, device_id_type=MESH)

    to_up = lambda src, dst, k: link(src, dst, k, (r - 1, h))
    to_before = lambda src, dst, k: link(src, dst, k, (r, h - 1))

    def across(p, landing):
        return pltpu.make_async_remote_copy(
            src_ref=t_ref, dst_ref=near.at[landing], send_sem=s1.at[p], recv_sem=r1.at[landing],
            device_id=job.device(job.o * job.inner + p), device_id_type=MESH)

    for s in range(1, job.inner):
        across(lax.rem(job.i + s, job.inner), job.i).start()

    @pl.when(has_up)
    def _():
        to_up(sloc_ref, beyond_buf, 0).start()

    rim_src_own[...] = sloc_ref[:, 0:DMAX, :] - sloc_ref[:, 0:1, :]

    @pl.when(has_before)
    def _():
        to_before(rim_src_own, rim_own_buf, 1).start()

    for s in range(1, job.inner):
        p = lax.rem(job.i + s, job.inner)
        across(p, job.i).wait_send()
        across(p, p).wait_recv()
    own = t_ref[...]
    total = own
    part = jnp.zeros_like(own)
    for s in range(1, job.inner):
        p = lax.rem(job.i + s, job.inner)
        block = near[p]
        total = total + block
        part = part + jnp.where(p > job.i, block, 0.0)
    group[...] = total

    def up(q, landing):
        return pltpu.make_async_remote_copy(
            src_ref=group, dst_ref=far.at[landing], send_sem=s2.at[q], recv_sem=r2.at[landing],
            device_id=job.device(q * job.inner + job.i), device_id_type=MESH)

    for s in range(1, job.outer):
        q = lax.rem(job.o + s, job.outer)

        @pl.when(job.o > q)
        def _():
            up(q, job.o).start()

    @pl.when(has_down)
    def _():
        to_up(sloc_ref, beyond_buf, 0).wait_recv()
        rim_src_next[...] = beyond_buf[:, 0:DMAX, :] - beyond_buf[:, 0:1, :]

    @pl.when(jnp.logical_and(has_down, has_before))
    def _():
        to_before(rim_src_next, rim_next_buf, 2).start()

    for s in range(1, job.outer):
        q = lax.rem(job.o + s, job.outer)

        @pl.when(job.o > q)
        def _():
            up(q, job.o).wait_send()

        @pl.when(q > job.o)
        def _():
            up(q, q).wait_recv()

    for s in range(1, job.outer):
        q = lax.rem(job.o + s, job.outer)
        part = part + jnp.where(q > job.o, far[q], 0.0)
    off_src[...] = part
    off_ref[...] = part

    @pl.when(has_up)
    def _():
        to_up(off_src, off_next_buf, 3).start()

    @pl.when(has_up)
    def _():
        to_up(sloc_ref, beyond_buf, 0).wait_send()
        to_up(off_src, off_next_buf, 3).wait_send()

    @pl.when(has_before)
    def _():
        to_before(rim_src_own, rim_own_buf, 1).wait_send()

    @pl.when(jnp.logical_and(has_down, has_before))
    def _():
        to_before(rim_src_next, rim_next_buf, 2).wait_send()

    @pl.when(has_after)
    def _():
        to_before(rim_src_own, rim_own_buf, 1).wait_recv()
        rim_own_ref[...] = rim_own_buf[...]

    @pl.when(jnp.logical_not(has_after))
    def _():
        rim_own_ref[...] = jnp.zeros_like(rim_own_ref)

    @pl.when(jnp.logical_and(has_down, has_after))
    def _():
        to_before(rim_src_next, rim_next_buf, 2).wait_recv()
        rim_next_ref[...] = rim_next_buf[...]

    @pl.when(jnp.logical_not(jnp.logical_and(has_down, has_after)))
    def _():
        rim_next_ref[...] = jnp.zeros_like(rim_next_ref)

    @pl.when(has_down)
    def _():
        to_up(off_src, off_next_buf, 3).wait_recv()
        off_next_ref[...] = off_next_buf[...]
        beyond_ref[...] = beyond_buf[...]

    @pl.when(jnp.logical_not(has_down))
    def _():
        off_next_ref[...] = jnp.zeros_like(off_next_ref)
        beyond_ref[...] = jnp.zeros_like(beyond_ref)


def dual_exchange(sloc):
    res, length, width = sloc.shape
    t = sloc[:, 0].reshape(-1, 128)
    inner = 8
    outer = lax.axis_size("hours") // inner
    rim = (res, DMAX, width)
    vmem = pl.BlockSpec(memory_space=pltpu.VMEM)
    off, off_next, beyond, rim_own, rim_next = pl.pallas_call(
        dual_kernel,
        out_shape=[
            jax.ShapeDtypeStruct(t.shape, t.dtype),
            jax.ShapeDtypeStruct(t.shape, t.dtype),
            jax.ShapeDtypeStruct(sloc.shape, sloc.dtype),
            jax.ShapeDtypeStruct(rim, sloc.dtype),
            jax.ShapeDtypeStruct(rim, sloc.dtype),
        ],
        in_specs=[vmem, vmem],
        out_specs=[vmem] * 5,
        scratch_shapes=[
            pltpu.VMEM((inner,) + t.shape, t.dtype),
            pltpu.VMEM((outer,) + t.shape, t.dtype),
            pltpu.VMEM(t.shape, t.dtype),
            pltpu.VMEM(sloc.shape, sloc.dtype),
            pltpu.VMEM(rim, sloc.dtype),
            pltpu.VMEM(rim, sloc.dtype),
            pltpu.VMEM(rim, sloc.dtype),
            pltpu.VMEM(rim, sloc.dtype),
            pltpu.VMEM(t.shape, t.dtype),
            pltpu.VMEM(t.shape, t.dtype),
            pltpu.SemaphoreType.DMA((inner,)),
            pltpu.SemaphoreType.DMA((inner,)),
            pltpu.SemaphoreType.DMA((outer,)),
            pltpu.SemaphoreType.DMA((outer,)),
            pltpu.SemaphoreType.DMA((8,)),
        ],
        compiler_params=pltpu.CompilerParams(collective_id=0, has_side_effects=True, vmem_limit_bytes=48 * 1024 * 1024),
    )(sloc, t)
    return off.reshape(res, width), off_next.reshape(res, width), beyond, rim_own, rim_next


def flow_kernel(
    main_ref, rim_own_ref, rim_next_ref, a_ref, b_ref, power_ref,
    incoming_ref, rim_own_in_ref, rim_next_in_ref, pa_ref, supplied_ref,
    near_h, far_h, group_h, near_r, far_r, group_r, incoming_buf, rim_own_buf, rim_next_buf,
    a_src, b_buf, s1h, r1h, s2h, r2h, s1r, r1r, s2r, r2r, sems,
):
    jobs = [Job("hours", "prefix", 8, lax.axis_size("hours")), Job("river", "sum", 8, lax.axis_size("river"))]
    for job in jobs:
        job.place()
    n_r = lax.axis_size("river")
    n_h = lax.axis_size("hours")
    r = lax.axis_index("river")
    h = lax.axis_index("hours")
    has_up, has_down = r > 0, r < n_r - 1
    has_before, has_after = h > 0, h < n_h - 1
    diag_down = jnp.logical_and(has_down, has_after)
    diag_up = jnp.logical_and(has_up, has_before)

    barrier = pltpu.get_barrier_semaphore()
    fixed = 0
    for job in jobs:
        for dev in job.peers():
            pl.semaphore_signal(barrier, 1, device_id=dev, device_id_type=MESH)
            fixed += 1
    links = (
        (has_up, (r - 1, h)), (has_down, (r + 1, h)), (has_before, (r, h - 1)), (has_after, (r, h + 1)),
        (diag_down, (r + 1, h + 1)), (diag_up, (r - 1, h - 1)),
    )
    for flag, dev in links:

        @pl.when(flag)
        def _():
            pl.semaphore_signal(barrier, 1, device_id=dev, device_id_type=MESH)

    extra = sum(jnp.where(flag, 1, 0) for flag, _ in links)
    pl.semaphore_wait(barrier, fixed + extra)

    def link(src, dst, k, dev):
        return pltpu.make_async_remote_copy(
            src_ref=src, dst_ref=dst, send_sem=sems.at[2 * k], recv_sem=sems.at[2 * k + 1],
            device_id=dev, device_id_type=MESH)

    main_copy = link(main_ref, incoming_buf, 0, (r + 1, h))
    rim_own_copy = link(rim_own_ref, rim_own_buf, 1, (r, h + 1))
    rim_next_copy = link(rim_next_ref, rim_next_buf, 2, (r + 1, h + 1))
    b_copy = link(b_ref, b_buf, 3, (r + 1, h))

    @pl.when(has_down)
    def _():
        b_copy.start()
        main_copy.start()

    @pl.when(has_after)
    def _():
        rim_own_copy.start()

    @pl.when(diag_down)
    def _():
        rim_next_copy.start()

    bufs = [(a_src, near_h, far_h, group_h, s1h, r1h, s2h, r2h), (power_ref, near_r, far_r, group_r, s1r, r1r, s2r, r2r)]

    def across(job, x_ref, near, s1, r1, p, landing):
        return pltpu.make_async_remote_copy(
            src_ref=x_ref, dst_ref=near.at[landing], send_sem=s1.at[p], recv_sem=r1.at[landing],
            device_id=job.device(job.o * job.inner + p), device_id_type=MESH)

    for job, (x_ref, near, far, group, s1, r1, s2, r2) in zip(jobs[::-1], bufs[::-1]):
        if job.axis == "hours":

            @pl.when(has_up)
            def _():
                b_copy.wait_recv()
                a_src[...] = a_ref[...] + b_buf[...]

            @pl.when(jnp.logical_not(has_up))
            def _():
                a_src[...] = a_ref[...]

        for s in range(1, job.inner):
            across(job, x_ref, near, s1, r1, lax.rem(job.i + s, job.inner), job.i).start()
    parts = []
    for job, (x_ref, near, far, group, s1, r1, s2, r2) in zip(jobs, bufs):
        for s in range(1, job.inner):
            p = lax.rem(job.i + s, job.inner)
            across(job, x_ref, near, s1, r1, p, job.i).wait_send()
            across(job, x_ref, near, s1, r1, p, p).wait_recv()
        own = x_ref[...]
        total = own
        part = own if job.mode == "sum" else jnp.zeros_like(own)
        for s in range(1, job.inner):
            p = lax.rem(job.i + s, job.inner)
            block = near[p]
            total = total + block
            if job.mode == "sum":
                part = part + block
            else:
                part = part + jnp.where(wanted(job.mode, p, job.i), block, 0.0)
        group[...] = total
        parts.append(part)

    def up(job, group, far, s2, r2, q, landing):
        return pltpu.make_async_remote_copy(
            src_ref=group, dst_ref=far.at[landing], send_sem=s2.at[q], recv_sem=r2.at[landing],
            device_id=job.device(q * job.inner + job.i), device_id_type=MESH)

    for job, (x_ref, near, far, group, s1, r1, s2, r2) in zip(jobs, bufs):
        for s in range(1, job.outer):
            q = lax.rem(job.o + s, job.outer)

            @pl.when(wanted(job.mode, job.o, q))
            def _():
                up(job, group, far, s2, r2, q, job.o).start()

    results = []
    for job, part, (x_ref, near, far, group, s1, r1, s2, r2) in zip(jobs, parts, bufs):
        for s in range(1, job.outer):
            q = lax.rem(job.o + s, job.outer)

            @pl.when(wanted(job.mode, job.o, q))
            def _():
                up(job, group, far, s2, r2, q, job.o).wait_send()

            @pl.when(wanted(job.mode, q, job.o))
            def _():
                up(job, group, far, s2, r2, q, q).wait_recv()

        for s in range(1, job.outer):
            q = lax.rem(job.o + s, job.outer)
            part = part + jnp.where(wanted(job.mode, q, job.o), far[q], 0.0)
        results.append(part)
    scanned, supplied = results
    pa_ref[...] = scanned
    supplied_ref[...] = supplied

    @pl.when(has_down)
    def _():
        main_copy.wait_send()
        b_copy.wait_send()

    @pl.when(has_after)
    def _():
        rim_own_copy.wait_send()

    @pl.when(diag_down)
    def _():
        rim_next_copy.wait_send()

    @pl.when(has_up)
    def _():
        main_copy.wait_recv()
        incoming_ref[...] = incoming_buf[...]

    @pl.when(jnp.logical_not(has_up))
    def _():
        incoming_ref[...] = jnp.zeros_like(incoming_ref)

    @pl.when(has_before)
    def _():
        rim_own_copy.wait_recv()
        rim_own_in_ref[...] = rim_own_buf[...]

    @pl.when(jnp.logical_not(has_before))
    def _():
        rim_own_in_ref[...] = jnp.zeros_like(rim_own_in_ref)

    @pl.when(diag_up)
    def _():
        rim_next_copy.wait_recv()
        rim_next_in_ref[...] = rim_next_buf[...]

    @pl.when(jnp.logical_not(diag_up))
    def _():
        rim_next_in_ref[...] = jnp.zeros_like(rim_next_in_ref)


def flow_exchange(main_next, rim_own, rim_next, own_totals, next_totals, power):
    res, width = own_totals.shape
    a = own_totals.reshape(-1, 128)
    b = next_totals.reshape(-1, 128)
    flat_power = power.reshape(-1, 128)
    inner = 8
    outer_h = lax.axis_size("hours") // inner
    outer_r = lax.axis_size("river") // inner
    vmem = pl.BlockSpec(memory_space=pltpu.VMEM)
    shape = lambda x: jax.ShapeDtypeStruct(x.shape, x.dtype)
    incoming, rim_own_in, rim_next_in, pa, supplied = pl.pallas_call(
        flow_kernel,
        out_shape=[shape(main_next), shape(rim_own), shape(rim_next), shape(a), shape(flat_power)],
        in_specs=[vmem] * 6,
        out_specs=[vmem] * 5,
        scratch_shapes=[
            pltpu.VMEM((inner,) + a.shape, a.dtype),
            pltpu.VMEM((outer_h,) + a.shape, a.dtype),
            pltpu.VMEM(a.shape, a.dtype),
            pltpu.VMEM((inner,) + flat_power.shape, a.dtype),
            pltpu.VMEM((outer_r,) + flat_power.shape, a.dtype),
            pltpu.VMEM(flat_power.shape, a.dtype),
            pltpu.VMEM(main_next.shape, a.dtype),
            pltpu.VMEM(rim_own.shape, a.dtype),
            pltpu.VMEM(rim_next.shape, a.dtype),
            pltpu.VMEM(a.shape, a.dtype),
            pltpu.VMEM(a.shape, a.dtype),
            pltpu.SemaphoreType.DMA((inner,)),
            pltpu.SemaphoreType.DMA((inner,)),
            pltpu.SemaphoreType.DMA((outer_h,)),
            pltpu.SemaphoreType.DMA((outer_h,)),
            pltpu.SemaphoreType.DMA((inner,)),
            pltpu.SemaphoreType.DMA((inner,)),
            pltpu.SemaphoreType.DMA((outer_r,)),
            pltpu.SemaphoreType.DMA((outer_r,)),
            pltpu.SemaphoreType.DMA((8,)),
        ],
        compiler_params=pltpu.CompilerParams(collective_id=1, has_side_effects=True, vmem_limit_bytes=48 * 1024 * 1024),
    )(main_next, rim_own, rim_next, a, b, flat_power)
    return incoming, rim_own_in, rim_next_in, pa.reshape(res, width), supplied.reshape(power.shape)


def combine(parts, specs, collective):
    shapes = [part.shape for part in parts]
    parts = [part.reshape(-1, 128) for part in parts]
    jobs = [Job(axis, mode, inner, lax.axis_size(axis)) for axis, mode, inner in specs]
    scratch = []
    for part, job in zip(parts, jobs):
        scratch += [
            pltpu.VMEM((job.inner,) + part.shape, part.dtype),
            pltpu.VMEM((job.outer,) + part.shape, part.dtype),
            pltpu.VMEM(part.shape, part.dtype),
            pltpu.SemaphoreType.DMA((job.inner,)),
            pltpu.SemaphoreType.DMA((job.inner,)),
            pltpu.SemaphoreType.DMA((job.outer,)),
            pltpu.SemaphoreType.DMA((job.outer,)),
        ]
    results = pl.pallas_call(
        functools.partial(multi_kernel, jobs),
        out_shape=[jax.ShapeDtypeStruct(part.shape, part.dtype) for part in parts],
        in_specs=[pl.BlockSpec(memory_space=pltpu.VMEM)] * len(parts),
        out_specs=[pl.BlockSpec(memory_space=pltpu.VMEM)] * len(parts),
        scratch_shapes=scratch,
        compiler_params=pltpu.CompilerParams(collective_id=collective, has_side_effects=True),
    )(*parts)
    return [result.reshape(shape) for result, shape in zip(results, shapes)]


def add_pair(earlier_part, later_part):
    return earlier_part + later_part


def hold_back(field, travel_delay, earlier_rim):
    length = field.shape[1]
    extended = jnp.concatenate([earlier_rim, field], 1)
    result = jnp.zeros_like(field)
    for lag_hours in range(1, DMAX + 1):
        window = extended[:, DMAX - lag_hours : DMAX - lag_hours + length]
        result = result + jnp.where((travel_delay == lag_hours)[:, None, None], window, 0.0)
    return result


def bring_forward(field, travel_delay, later_rim):
    length = field.shape[1]
    extended = jnp.concatenate([field, later_rim], 1)
    result = jnp.zeros_like(field)
    for lag_hours in range(1, DMAX + 1):
        window = extended[:, lag_hours : lag_hours + length]
        result = result + jnp.where((travel_delay == lag_hours)[:, None, None], window, 0.0)
    return result


def route_down(matrix, field):
    return jnp.einsum("ij,jtw->itw", matrix, field, precision=lax.Precision.HIGHEST)


def route_up(matrix, field):
    return jnp.einsum("ij,itw->jtw", matrix, field, precision=lax.Precision.HIGHEST)


def iterate(fields, statics, scales, suffix_sum, from_earlier, from_later):
    release, storage_dual, demand_dual, cost, inflow, demand = fields
    (
        storage_start,
        storage_low,
        storage_high,
        release_cap,
        efficiency,
        travel_delay,
        to_own,
        to_next,
    ) = statics
    scale_time, scale_sum = scales
    local = suffix_local(storage_dual)
    off, off_next, beyond, rim_own, rim_next = dual_exchange(local)
    suffix = local + off[:, None]
    both = jnp.concatenate([to_own, to_next], 0)
    length = suffix.shape[1]
    sinks = route_up(
        both,
        jnp.concatenate(
            [
                jnp.concatenate([suffix, rim_own + off[:, None]], 1),
                jnp.concatenate([beyond + off_next[:, None], rim_next + off_next[:, None]], 1),
            ],
            0,
        ),
    )
    at_sink, rim_sink = sinks[:, :length], sinks[:, length:]
    last = lax.axis_index("hours") == lax.axis_size("hours") - 1
    later_duals = bring_forward(at_sink, travel_delay, jnp.where(last, 0.0, rim_sink))
    gradient = (
        cost
        + scale_time * (later_duals - suffix)
        + scale_sum * efficiency[:, None, None] * demand_dual[None]
    )
    release_new = jnp.clip(release - primal_step * gradient, 0.0, release_cap[:, None, None])
    extrapolated = 2.0 * release_new - release
    length = extrapolated.shape[1]
    tail = extrapolated[:, length - DMAX :]
    settled = hold_back(extrapolated, travel_delay, jnp.zeros_like(tail))
    rim_delayed = hold_back(jnp.zeros_like(extrapolated), travel_delay, tail)[:, :DMAX]
    res = settled.shape[0]
    routed_all = route_down(both, jnp.concatenate([settled, rim_delayed], 1))
    main_own, main_next = routed_all[:res, :length], routed_all[res:, :length]
    rim_own, rim_next = routed_all[:res, length:], routed_all[res:, length:]
    base = inflow + main_own - extrapolated
    own_totals = jnp.sum(base, 1) + jnp.sum(rim_own, 1)
    next_totals = jnp.sum(main_next, 1) + jnp.sum(rim_next, 1)
    partial_power = jnp.sum(scale_sum * efficiency[:, None, None] * extrapolated, 0)
    incoming, rim_own_in, rim_next_in, offset, supplied = flow_exchange(
        main_next, rim_own, rim_next, own_totals, next_totals, partial_power
    )
    arrived = jnp.concatenate([rim_own_in + rim_next_in, jnp.zeros_like(base[:, DMAX:])], 1)
    local_sum = jnp.cumsum(base + incoming + arrived, 1)
    offset = offset - jnp.sum(rim_own_in, 1) - jnp.sum(rim_next_in, 1)
    storage = storage_start[:, None, None] + scale_time * (local_sum + offset[:, None])
    lower_bound = storage_low[:, None, None]
    upper_bound = storage_high[:, None, None]
    storage_dual_new = (
        storage_dual
        + dual_step * storage
        - dual_step * jnp.clip(storage_dual / dual_step + storage, lower_bound, upper_bound)
    )
    storage_excess = storage - jnp.clip(storage, lower_bound, upper_bound)
    demand_dual_new = jnp.minimum(demand_dual + dual_step * (supplied - demand), 0.0)
    return (release_new, storage_dual_new, demand_dual_new, storage_excess)


def suffix_local(field):
    return lax.cumsum(field, 1, reverse=True)


def shards(
    release,
    storage_dual,
    demand_dual,
    cost,
    inflow,
    demand,
    storage_start,
    storage_low,
    storage_high,
    release_cap,
    efficiency,
    downstream,
    travel_delay,
):
    res_dev = release.shape[0]
    scale_time = 1.0 / (release.shape[1] * lax.axis_size("hours"))
    scale_sum = 1.0 / math.sqrt(res_dev * lax.axis_size("river"))
    base_index = lax.axis_index("river") * res_dev
    target = downstream - base_index
    indices = jnp.arange(res_dev, dtype=jnp.int32)
    to_own = (target[None, :] == indices[:, None]).astype(jnp.float32)
    to_next = (target[None, :] == indices[:, None] + res_dev).astype(jnp.float32)
    statics = (
        storage_start,
        storage_low,
        storage_high,
        release_cap,
        efficiency,
        travel_delay,
        to_own,
        to_next,
    )
    scales = (scale_time, scale_sum)

    def suffix_blocks(field):
        local_sum = suffix_local(field)
        totals = local_sum[:, 0]
        (offset,) = combine([totals], [("hours", "suffix", 8)], 0)
        return local_sum + offset[:, None]

    def earlier_block(part):
        return passed_along(part, "hours", 1)

    def later_block(part):
        return passed_along(part, "hours", -1)

    fields = (release, storage_dual, demand_dual, cost, inflow, demand)
    return iterate(
        fields, statics, scales, suffix_blocks, earlier_block, later_block
    )


def solution(mesh):
    return jax.shard_map(
        shards,
        mesh=mesh,
        in_specs=(
            P("river", "hours", None),
            P("river", "hours", None),
            P("hours", None),
            P("river", "hours", None),
            P("river", "hours", None),
            P("hours", None),
            P("river"),
            P("river"),
            P("river"),
            P("river"),
            P("river"),
            P("river"),
            P("river"),
        ),
        out_specs=(
            P("river", "hours", None),
            P("river", "hours", None),
            P("hours", None),
            P("river", "hours", None),
        ),
        check_vma=False,
    )
```

```python
import functools
import math

import jax
import jax.numpy as jnp
from jax import lax
from jax.experimental import pallas as pl
from jax.experimental.pallas import tpu as pltpu
from jax.sharding import PartitionSpec as P

DMAX = 6


primal_step = 1.0
dual_step = 0.1


def passed_along(block, axis, distance):
    devices = range(lax.axis_size(axis))
    route = [(i - distance, i) for i in devices if i - distance in devices]
    return lax.ppermute(block, axis, route)


MESH = pl.DeviceIdType.MESH


def wanted(mode, src, dst):
    if mode == "prefix":
        return src < dst
    if mode == "suffix":
        return src > dst
    return src != dst


class Job:
    def __init__(self, axis, mode, inner, n):
        self.axis, self.mode, self.inner = axis, mode, inner
        self.outer = n // inner
        self.other = "river" if axis == "hours" else "hours"

    def place(self):
        me = lax.axis_index(self.axis)
        self.fixed = lax.axis_index(self.other)
        self.o = me // self.inner
        self.i = me % self.inner

    def device(self, p):
        return (self.fixed, p) if self.axis == "hours" else (p, self.fixed)

    def peers(self):
        inner, outer, o, i = self.inner, self.outer, self.o, self.i
        near = [self.device(o * inner + lax.rem(i + s, inner)) for s in range(1, inner)]
        far = [self.device(lax.rem(o + s, outer) * inner + i) for s in range(1, outer)]
        return near + far


def multi_kernel(jobs, *refs):
    count = len(jobs)
    ins, outs, rest = refs[:count], refs[count:2 * count], refs[2 * count:]
    for job in jobs:
        job.place()
    barrier = pltpu.get_barrier_semaphore()
    partners = 0
    for job in jobs:
        for dev in job.peers():
            pl.semaphore_signal(barrier, 1, device_id=dev, device_id_type=MESH)
            partners += 1
    pl.semaphore_wait(barrier, partners)

    def across(job, x_ref, near, s1, r1, p, landing):
        return pltpu.make_async_remote_copy(
            src_ref=x_ref, dst_ref=near.at[landing], send_sem=s1.at[p], recv_sem=r1.at[landing],
            device_id=job.device(job.o * job.inner + p), device_id_type=MESH)

    for k, job in enumerate(jobs):
        near, far, group, s1, r1, s2, r2 = rest[7 * k:7 * k + 7]
        for s in range(1, job.inner):
            p = lax.rem(job.i + s, job.inner)
            across(job, ins[k], near, s1, r1, p, job.i).start()
    parts = []
    for k, job in enumerate(jobs):
        near, far, group, s1, r1, s2, r2 = rest[7 * k:7 * k + 7]
        for s in range(1, job.inner):
            p = lax.rem(job.i + s, job.inner)
            across(job, ins[k], near, s1, r1, p, job.i).wait_send()
            across(job, ins[k], near, s1, r1, p, p).wait_recv()
        own = ins[k][...]
        total = own
        part = own if job.mode == "sum" else jnp.zeros_like(own)
        for s in range(1, job.inner):
            p = lax.rem(job.i + s, job.inner)
            block = near[p]
            total = total + block
            if job.mode == "sum":
                part = part + block
            else:
                part = part + jnp.where(wanted(job.mode, p, job.i), block, 0.0)
        group[...] = total
        parts.append(part)

    def up(job, group, far, s2, r2, q, landing):
        return pltpu.make_async_remote_copy(
            src_ref=group, dst_ref=far.at[landing], send_sem=s2.at[q], recv_sem=r2.at[landing],
            device_id=job.device(q * job.inner + job.i), device_id_type=MESH)

    for k, job in enumerate(jobs):
        near, far, group, s1, r1, s2, r2 = rest[7 * k:7 * k + 7]
        for s in range(1, job.outer):
            q = lax.rem(job.o + s, job.outer)

            @pl.when(wanted(job.mode, job.o, q))
            def _():
                up(job, group, far, s2, r2, q, job.o).start()

    for k, job in enumerate(jobs):
        near, far, group, s1, r1, s2, r2 = rest[7 * k:7 * k + 7]
        part = parts[k]
        for s in range(1, job.outer):
            q = lax.rem(job.o + s, job.outer)

            @pl.when(wanted(job.mode, job.o, q))
            def _():
                up(job, group, far, s2, r2, q, job.o).wait_send()

            @pl.when(wanted(job.mode, q, job.o))
            def _():
                up(job, group, far, s2, r2, q, q).wait_recv()

        for s in range(1, job.outer):
            q = lax.rem(job.o + s, job.outer)
            part = part + jnp.where(wanted(job.mode, q, job.o), far[q], 0.0)
        outs[k][...] = part


def dual_kernel(
    sloc_ref, t_ref, off_ref, off_next_ref, beyond_ref, rim_own_ref, rim_next_ref,
    near, far, group, beyond_buf, rim_src_own, rim_src_next, rim_own_buf, rim_next_buf,
    off_src, off_next_buf, s1, r1, s2, r2, sems,
):
    job = Job("hours", "suffix", 8, lax.axis_size("hours"))
    job.place()
    n_r = lax.axis_size("river")
    n_h = lax.axis_size("hours")
    r = lax.axis_index("river")
    h = lax.axis_index("hours")
    has_up, has_down = r > 0, r < n_r - 1
    has_before, has_after = h > 0, h < n_h - 1

    barrier = pltpu.get_barrier_semaphore()
    for dev in job.peers():
        pl.semaphore_signal(barrier, 1, device_id=dev, device_id_type=MESH)
    for flag, dev in ((has_up, (r - 1, h)), (has_down, (r + 1, h)), (has_before, (r, h - 1)), (has_after, (r, h + 1))):

        @pl.when(flag)
        def _():
            pl.semaphore_signal(barrier, 1, device_id=dev, device_id_type=MESH)

    extra = sum(jnp.where(flag, 1, 0) for flag in (has_up, has_down, has_before, has_after))
    pl.semaphore_wait(barrier, job.inner + job.outer - 2 + extra)

    def link(src, dst, k, dev):
        return pltpu.make_async_remote_copy(
            src_ref=src, dst_ref=dst, send_sem=sems.at[2 * k], recv_sem=sems.at[2 * k + 1],
            device_id=dev, device_id_type=MESH)

    to_up = lambda src, dst, k: link(src, dst, k, (r - 1, h))
    to_before = lambda src, dst, k: link(src, dst, k, (r, h - 1))

    def across(p, landing):
        return pltpu.make_async_remote_copy(
            src_ref=t_ref, dst_ref=near.at[landing], send_sem=s1.at[p], recv_sem=r1.at[landing],
            device_id=job.device(job.o * job.inner + p), device_id_type=MESH)

    for s in range(1, job.inner):
        across(lax.rem(job.i + s, job.inner), job.i).start()

    @pl.when(has_up)
    def _():
        to_up(sloc_ref, beyond_buf, 0).start()

    rim_src_own[...] = sloc_ref[:, 0:DMAX, :] - sloc_ref[:, 0:1, :]

    @pl.when(has_before)
    def _():
        to_before(rim_src_own, rim_own_buf, 1).start()

    for s in range(1, job.inner):
        p = lax.rem(job.i + s, job.inner)
        across(p, job.i).wait_send()
        across(p, p).wait_recv()
    own = t_ref[...]
    total = own
    part = jnp.zeros_like(own)
    for s in range(1, job.inner):
        p = lax.rem(job.i + s, job.inner)
        block = near[p]
        total = total + block
        part = part + jnp.where(p > job.i, block, 0.0)
    group[...] = total

    def up(q, landing):
        return pltpu.make_async_remote_copy(
            src_ref=group, dst_ref=far.at[landing], send_sem=s2.at[q], recv_sem=r2.at[landing],
            device_id=job.device(q * job.inner + job.i), device_id_type=MESH)

    for s in range(1, job.outer):
        q = lax.rem(job.o + s, job.outer)

        @pl.when(job.o > q)
        def _():
            up(q, job.o).start()

    @pl.when(has_down)
    def _():
        to_up(sloc_ref, beyond_buf, 0).wait_recv()
        rim_src_next[...] = beyond_buf[:, 0:DMAX, :] - beyond_buf[:, 0:1, :]

    @pl.when(jnp.logical_and(has_down, has_before))
    def _():
        to_before(rim_src_next, rim_next_buf, 2).start()

    for s in range(1, job.outer):
        q = lax.rem(job.o + s, job.outer)

        @pl.when(job.o > q)
        def _():
            up(q, job.o).wait_send()

        @pl.when(q > job.o)
        def _():
            up(q, q).wait_recv()

    for s in range(1, job.outer):
        q = lax.rem(job.o + s, job.outer)
        part = part + jnp.where(q > job.o, far[q], 0.0)
    off_src[...] = part
    off_ref[...] = part

    @pl.when(has_up)
    def _():
        to_up(off_src, off_next_buf, 3).start()

    @pl.when(has_up)
    def _():
        to_up(sloc_ref, beyond_buf, 0).wait_send()
        to_up(off_src, off_next_buf, 3).wait_send()

    @pl.when(has_before)
    def _():
        to_before(rim_src_own, rim_own_buf, 1).wait_send()

    @pl.when(jnp.logical_and(has_down, has_before))
    def _():
        to_before(rim_src_next, rim_next_buf, 2).wait_send()

    @pl.when(has_after)
    def _():
        to_before(rim_src_own, rim_own_buf, 1).wait_recv()
        rim_own_ref[...] = rim_own_buf[...]

    @pl.when(jnp.logical_not(has_after))
    def _():
        rim_own_ref[...] = jnp.zeros_like(rim_own_ref)

    @pl.when(jnp.logical_and(has_down, has_after))
    def _():
        to_before(rim_src_next, rim_next_buf, 2).wait_recv()
        rim_next_ref[...] = rim_next_buf[...]

    @pl.when(jnp.logical_not(jnp.logical_and(has_down, has_after)))
    def _():
        rim_next_ref[...] = jnp.zeros_like(rim_next_ref)

    @pl.when(has_down)
    def _():
        to_up(off_src, off_next_buf, 3).wait_recv()
        off_next_ref[...] = off_next_buf[...]
        beyond_ref[...] = beyond_buf[...]

    @pl.when(jnp.logical_not(has_down))
    def _():
        off_next_ref[...] = jnp.zeros_like(off_next_ref)
        beyond_ref[...] = jnp.zeros_like(beyond_ref)


def dual_exchange(sloc):
    res, length, width = sloc.shape
    t = sloc[:, 0].reshape(-1, 128)
    inner = 8
    outer = lax.axis_size("hours") // inner
    rim = (res, DMAX, width)
    vmem = pl.BlockSpec(memory_space=pltpu.VMEM)
    off, off_next, beyond, rim_own, rim_next = pl.pallas_call(
        dual_kernel,
        out_shape=[
            jax.ShapeDtypeStruct(t.shape, t.dtype),
            jax.ShapeDtypeStruct(t.shape, t.dtype),
            jax.ShapeDtypeStruct(sloc.shape, sloc.dtype),
            jax.ShapeDtypeStruct(rim, sloc.dtype),
            jax.ShapeDtypeStruct(rim, sloc.dtype),
        ],
        in_specs=[vmem, vmem],
        out_specs=[vmem] * 5,
        scratch_shapes=[
            pltpu.VMEM((inner,) + t.shape, t.dtype),
            pltpu.VMEM((outer,) + t.shape, t.dtype),
            pltpu.VMEM(t.shape, t.dtype),
            pltpu.VMEM(sloc.shape, sloc.dtype),
            pltpu.VMEM(rim, sloc.dtype),
            pltpu.VMEM(rim, sloc.dtype),
            pltpu.VMEM(rim, sloc.dtype),
            pltpu.VMEM(rim, sloc.dtype),
            pltpu.VMEM(t.shape, t.dtype),
            pltpu.VMEM(t.shape, t.dtype),
            pltpu.SemaphoreType.DMA((inner,)),
            pltpu.SemaphoreType.DMA((inner,)),
            pltpu.SemaphoreType.DMA((outer,)),
            pltpu.SemaphoreType.DMA((outer,)),
            pltpu.SemaphoreType.DMA((8,)),
        ],
        compiler_params=pltpu.CompilerParams(collective_id=0, has_side_effects=True, vmem_limit_bytes=48 * 1024 * 1024),
    )(sloc, t)
    return off.reshape(res, width), off_next.reshape(res, width), beyond, rim_own, rim_next


def flow_kernel(
    main_ref, rim_own_ref, rim_next_ref, a_ref, b_ref, power_ref,
    incoming_ref, rim_own_in_ref, rim_next_in_ref, pa_ref, supplied_ref,
    near_h, far_h, group_h, near_r, far_r, group_r, incoming_buf, rim_own_buf, rim_next_buf,
    a_src, b_buf, s1h, r1h, s2h, r2h, s1r, r1r, s2r, r2r, sems,
):
    jobs = [Job("hours", "prefix", 8, lax.axis_size("hours")), Job("river", "sum", 8, lax.axis_size("river"))]
    for job in jobs:
        job.place()
    n_r = lax.axis_size("river")
    n_h = lax.axis_size("hours")
    r = lax.axis_index("river")
    h = lax.axis_index("hours")
    has_up, has_down = r > 0, r < n_r - 1
    has_before, has_after = h > 0, h < n_h - 1
    diag_down = jnp.logical_and(has_down, has_after)
    diag_up = jnp.logical_and(has_up, has_before)

    barrier = pltpu.get_barrier_semaphore()
    fixed = 0
    for job in jobs:
        for dev in job.peers():
            pl.semaphore_signal(barrier, 1, device_id=dev, device_id_type=MESH)
            fixed += 1
    links = (
        (has_up, (r - 1, h)), (has_down, (r + 1, h)), (has_before, (r, h - 1)), (has_after, (r, h + 1)),
        (diag_down, (r + 1, h + 1)), (diag_up, (r - 1, h - 1)),
    )
    for flag, dev in links:

        @pl.when(flag)
        def _():
            pl.semaphore_signal(barrier, 1, device_id=dev, device_id_type=MESH)

    extra = sum(jnp.where(flag, 1, 0) for flag, _ in links)
    pl.semaphore_wait(barrier, fixed + extra)

    def link(src, dst, k, dev):
        return pltpu.make_async_remote_copy(
            src_ref=src, dst_ref=dst, send_sem=sems.at[2 * k], recv_sem=sems.at[2 * k + 1],
            device_id=dev, device_id_type=MESH)

    main_copy = link(main_ref, incoming_buf, 0, (r + 1, h))
    rim_own_copy = link(rim_own_ref, rim_own_buf, 1, (r, h + 1))
    rim_next_copy = link(rim_next_ref, rim_next_buf, 2, (r + 1, h + 1))
    b_copy = link(b_ref, b_buf, 3, (r + 1, h))

    @pl.when(has_down)
    def _():
        b_copy.start()
        main_copy.start()

    @pl.when(has_after)
    def _():
        rim_own_copy.start()

    @pl.when(diag_down)
    def _():
        rim_next_copy.start()

    bufs = [(a_src, near_h, far_h, group_h, s1h, r1h, s2h, r2h), (power_ref, near_r, far_r, group_r, s1r, r1r, s2r, r2r)]

    def across(job, x_ref, near, s1, r1, p, landing):
        return pltpu.make_async_remote_copy(
            src_ref=x_ref, dst_ref=near.at[landing], send_sem=s1.at[p], recv_sem=r1.at[landing],
            device_id=job.device(job.o * job.inner + p), device_id_type=MESH)

    for job, (x_ref, near, far, group, s1, r1, s2, r2) in zip(jobs[::-1], bufs[::-1]):
        if job.axis == "hours":

            @pl.when(has_up)
            def _():
                b_copy.wait_recv()
                a_src[...] = a_ref[...] + b_buf[...]

            @pl.when(jnp.logical_not(has_up))
            def _():
                a_src[...] = a_ref[...]

        for s in range(1, job.inner):
            across(job, x_ref, near, s1, r1, lax.rem(job.i + s, job.inner), job.i).start()
    parts = []
    for job, (x_ref, near, far, group, s1, r1, s2, r2) in zip(jobs, bufs):
        for s in range(1, job.inner):
            p = lax.rem(job.i + s, job.inner)
            across(job, x_ref, near, s1, r1, p, job.i).wait_send()
            across(job, x_ref, near, s1, r1, p, p).wait_recv()
        own = x_ref[...]
        total = own
        part = own if job.mode == "sum" else jnp.zeros_like(own)
        for s in range(1, job.inner):
            p = lax.rem(job.i + s, job.inner)
            block = near[p]
            total = total + block
            if job.mode == "sum":
                part = part + block
            else:
                part = part + jnp.where(wanted(job.mode, p, job.i), block, 0.0)
        group[...] = total
        parts.append(part)

    def up(job, group, far, s2, r2, q, landing):
        return pltpu.make_async_remote_copy(
            src_ref=group, dst_ref=far.at[landing], send_sem=s2.at[q], recv_sem=r2.at[landing],
            device_id=job.device(q * job.inner + job.i), device_id_type=MESH)

    for job, (x_ref, near, far, group, s1, r1, s2, r2) in zip(jobs, bufs):
        for s in range(1, job.outer):
            q = lax.rem(job.o + s, job.outer)

            @pl.when(wanted(job.mode, job.o, q))
            def _():
                up(job, group, far, s2, r2, q, job.o).start()

    results = []
    for job, part, (x_ref, near, far, group, s1, r1, s2, r2) in zip(jobs, parts, bufs):
        for s in range(1, job.outer):
            q = lax.rem(job.o + s, job.outer)

            @pl.when(wanted(job.mode, job.o, q))
            def _():
                up(job, group, far, s2, r2, q, job.o).wait_send()

            @pl.when(wanted(job.mode, q, job.o))
            def _():
                up(job, group, far, s2, r2, q, q).wait_recv()

        for s in range(1, job.outer):
            q = lax.rem(job.o + s, job.outer)
            part = part + jnp.where(wanted(job.mode, q, job.o), far[q], 0.0)
        results.append(part)
    scanned, supplied = results
    pa_ref[...] = scanned
    supplied_ref[...] = supplied

    @pl.when(has_down)
    def _():
        main_copy.wait_send()
        b_copy.wait_send()

    @pl.when(has_after)
    def _():
        rim_own_copy.wait_send()

    @pl.when(diag_down)
    def _():
        rim_next_copy.wait_send()

    @pl.when(has_up)
    def _():
        main_copy.wait_recv()
        incoming_ref[...] = incoming_buf[...]

    @pl.when(jnp.logical_not(has_up))
    def _():
        incoming_ref[...] = jnp.zeros_like(incoming_ref)

    @pl.when(has_before)
    def _():
        rim_own_copy.wait_recv()
        rim_own_in_ref[...] = rim_own_buf[...]

    @pl.when(jnp.logical_not(has_before))
    def _():
        rim_own_in_ref[...] = jnp.zeros_like(rim_own_in_ref)

    @pl.when(diag_up)
    def _():
        rim_next_copy.wait_recv()
        rim_next_in_ref[...] = rim_next_buf[...]

    @pl.when(jnp.logical_not(diag_up))
    def _():
        rim_next_in_ref[...] = jnp.zeros_like(rim_next_in_ref)


def flow_exchange(main_next, rim_own, rim_next, own_totals, next_totals, power):
    res, width = own_totals.shape
    a = own_totals.reshape(-1, 128)
    b = next_totals.reshape(-1, 128)
    flat_power = power.reshape(-1, 128)
    inner = 8
    outer_h = lax.axis_size("hours") // inner
    outer_r = lax.axis_size("river") // inner
    vmem = pl.BlockSpec(memory_space=pltpu.VMEM)
    shape = lambda x: jax.ShapeDtypeStruct(x.shape, x.dtype)
    incoming, rim_own_in, rim_next_in, pa, supplied = pl.pallas_call(
        flow_kernel,
        out_shape=[shape(main_next), shape(rim_own), shape(rim_next), shape(a), shape(flat_power)],
        in_specs=[vmem] * 6,
        out_specs=[vmem] * 5,
        scratch_shapes=[
            pltpu.VMEM((inner,) + a.shape, a.dtype),
            pltpu.VMEM((outer_h,) + a.shape, a.dtype),
            pltpu.VMEM(a.shape, a.dtype),
            pltpu.VMEM((inner,) + flat_power.shape, a.dtype),
            pltpu.VMEM((outer_r,) + flat_power.shape, a.dtype),
            pltpu.VMEM(flat_power.shape, a.dtype),
            pltpu.VMEM(main_next.shape, a.dtype),
            pltpu.VMEM(rim_own.shape, a.dtype),
            pltpu.VMEM(rim_next.shape, a.dtype),
            pltpu.VMEM(a.shape, a.dtype),
            pltpu.VMEM(a.shape, a.dtype),
            pltpu.SemaphoreType.DMA((inner,)),
            pltpu.SemaphoreType.DMA((inner,)),
            pltpu.SemaphoreType.DMA((outer_h,)),
            pltpu.SemaphoreType.DMA((outer_h,)),
            pltpu.SemaphoreType.DMA((inner,)),
            pltpu.SemaphoreType.DMA((inner,)),
            pltpu.SemaphoreType.DMA((outer_r,)),
            pltpu.SemaphoreType.DMA((outer_r,)),
            pltpu.SemaphoreType.DMA((8,)),
        ],
        compiler_params=pltpu.CompilerParams(collective_id=1, has_side_effects=True, vmem_limit_bytes=48 * 1024 * 1024),
    )(main_next, rim_own, rim_next, a, b, flat_power)
    return incoming, rim_own_in, rim_next_in, pa.reshape(res, width), supplied.reshape(power.shape)


def combine(parts, specs, collective):
    shapes = [part.shape for part in parts]
    parts = [part.reshape(-1, 128) for part in parts]
    jobs = [Job(axis, mode, inner, lax.axis_size(axis)) for axis, mode, inner in specs]
    scratch = []
    for part, job in zip(parts, jobs):
        scratch += [
            pltpu.VMEM((job.inner,) + part.shape, part.dtype),
            pltpu.VMEM((job.outer,) + part.shape, part.dtype),
            pltpu.VMEM(part.shape, part.dtype),
            pltpu.SemaphoreType.DMA((job.inner,)),
            pltpu.SemaphoreType.DMA((job.inner,)),
            pltpu.SemaphoreType.DMA((job.outer,)),
            pltpu.SemaphoreType.DMA((job.outer,)),
        ]
    results = pl.pallas_call(
        functools.partial(multi_kernel, jobs),
        out_shape=[jax.ShapeDtypeStruct(part.shape, part.dtype) for part in parts],
        in_specs=[pl.BlockSpec(memory_space=pltpu.VMEM)] * len(parts),
        out_specs=[pl.BlockSpec(memory_space=pltpu.VMEM)] * len(parts),
        scratch_shapes=scratch,
        compiler_params=pltpu.CompilerParams(collective_id=collective, has_side_effects=True),
    )(*parts)
    return [result.reshape(shape) for result, shape in zip(results, shapes)]


def add_pair(earlier_part, later_part):
    return earlier_part + later_part


def hold_back(field, travel_delay, earlier_rim):
    length = field.shape[1]
    extended = jnp.concatenate([earlier_rim, field], 1)
    result = jnp.zeros_like(field)
    for lag_hours in range(1, DMAX + 1):
        window = extended[:, DMAX - lag_hours : DMAX - lag_hours + length]
        result = result + jnp.where((travel_delay == lag_hours)[:, None, None], window, 0.0)
    return result


def bring_forward(field, travel_delay, later_rim):
    length = field.shape[1]
    extended = jnp.concatenate([field, later_rim], 1)
    result = jnp.zeros_like(field)
    for lag_hours in range(1, DMAX + 1):
        window = extended[:, lag_hours : lag_hours + length]
        result = result + jnp.where((travel_delay == lag_hours)[:, None, None], window, 0.0)
    return result


def route_down(matrix, field):
    return jnp.einsum("ij,jtw->itw", matrix, field, precision=lax.Precision.HIGHEST)


def route_up(matrix, field):
    return jnp.einsum("ij,itw->jtw", matrix, field, precision=lax.Precision.HIGHEST)


def iterate(fields, statics, scales, suffix_sum, from_earlier, from_later):
    release, storage_dual, demand_dual, cost, inflow, demand = fields
    (
        storage_start,
        storage_low,
        storage_high,
        release_cap,
        efficiency,
        travel_delay,
        to_own,
        to_next,
    ) = statics
    scale_time, scale_sum = scales
    local = suffix_local(storage_dual)
    off, off_next, beyond, rim_own, rim_next = dual_exchange(local)
    suffix = local + off[:, None]
    both = jnp.concatenate([to_own, to_next], 0)
    length = suffix.shape[1]
    sinks = route_up(
        both,
        jnp.concatenate(
            [
                jnp.concatenate([suffix, rim_own + off[:, None]], 1),
                jnp.concatenate([beyond + off_next[:, None], rim_next + off_next[:, None]], 1),
            ],
            0,
        ),
    )
    at_sink, rim_sink = sinks[:, :length], sinks[:, length:]
    last = lax.axis_index("hours") == lax.axis_size("hours") - 1
    later_duals = bring_forward(at_sink, travel_delay, jnp.where(last, 0.0, rim_sink))
    gradient = (
        cost
        + scale_time * (later_duals - suffix)
        + scale_sum * efficiency[:, None, None] * demand_dual[None]
    )
    release_new = jnp.clip(release - primal_step * gradient, 0.0, release_cap[:, None, None])
    extrapolated = 2.0 * release_new - release
    length = extrapolated.shape[1]
    tail = extrapolated[:, length - DMAX :]
    settled = hold_back(extrapolated, travel_delay, jnp.zeros_like(tail))
    rim_delayed = hold_back(jnp.zeros_like(extrapolated), travel_delay, tail)[:, :DMAX]
    res = settled.shape[0]
    routed_all = route_down(both, jnp.concatenate([settled, rim_delayed], 1))
    main_own, main_next = routed_all[:res, :length], routed_all[res:, :length]
    rim_own, rim_next = routed_all[:res, length:], routed_all[res:, length:]
    base = inflow + main_own - extrapolated
    own_totals = jnp.sum(inflow - extrapolated, 1) + jnp.sum(routed_all[:res], 1)
    next_totals = jnp.sum(routed_all[res:], 1)
    partial_power = jnp.sum(scale_sum * efficiency[:, None, None] * extrapolated, 0)
    incoming, rim_own_in, rim_next_in, offset, supplied = flow_exchange(
        main_next, rim_own, rim_next, own_totals, next_totals, partial_power
    )
    landed = rim_own_in + rim_next_in
    arrived = jnp.concatenate([landed, jnp.zeros_like(base[:, DMAX:])], 1)
    local_sum = jnp.cumsum(base + incoming + arrived, 1)
    offset = offset - jnp.sum(landed, 1)
    storage = storage_start[:, None, None] + scale_time * (local_sum + offset[:, None])
    lower_bound = storage_low[:, None, None]
    upper_bound = storage_high[:, None, None]
    storage_dual_new = (
        storage_dual
        + dual_step * storage
        - dual_step * jnp.clip(storage_dual / dual_step + storage, lower_bound, upper_bound)
    )
    storage_excess = storage - jnp.clip(storage, lower_bound, upper_bound)
    demand_dual_new = jnp.minimum(demand_dual + dual_step * (supplied - demand), 0.0)
    return (release_new, storage_dual_new, demand_dual_new, storage_excess)


def suffix_local(field):
    return lax.cumsum(field, 1, reverse=True)


def shards(
    release,
    storage_dual,
    demand_dual,
    cost,
    inflow,
    demand,
    storage_start,
    storage_low,
    storage_high,
    release_cap,
    efficiency,
    downstream,
    travel_delay,
):
    res_dev = release.shape[0]
    scale_time = 1.0 / (release.shape[1] * lax.axis_size("hours"))
    scale_sum = 1.0 / math.sqrt(res_dev * lax.axis_size("river"))
    base_index = lax.axis_index("river") * res_dev
    target = downstream - base_index
    indices = jnp.arange(res_dev, dtype=jnp.int32)
    to_own = (target[None, :] == indices[:, None]).astype(jnp.float32)
    to_next = (target[None, :] == indices[:, None] + res_dev).astype(jnp.float32)
    statics = (
        storage_start,
        storage_low,
        storage_high,
        release_cap,
        efficiency,
        travel_delay,
        to_own,
        to_next,
    )
    scales = (scale_time, scale_sum)

    def suffix_blocks(field):
        local_sum = suffix_local(field)
        totals = local_sum[:, 0]
        (offset,) = combine([totals], [("hours", "suffix", 8)], 0)
        return local_sum + offset[:, None]

    def earlier_block(part):
        return passed_along(part, "hours", 1)

    def later_block(part):
        return passed_along(part, "hours", -1)

    fields = (release, storage_dual, demand_dual, cost, inflow, demand)
    return iterate(
        fields, statics, scales, suffix_blocks, earlier_block, later_block
    )


def solution(mesh):
    return jax.shard_map(
        shards,
        mesh=mesh,
        in_specs=(
            P("river", "hours", None),
            P("river", "hours", None),
            P("hours", None),
            P("river", "hours", None),
            P("river", "hours", None),
            P("hours", None),
            P("river"),
            P("river"),
            P("river"),
            P("river"),
            P("river"),
            P("river"),
            P("river"),
        ),
        out_specs=(
            P("river", "hours", None),
            P("river", "hours", None),
            P("hours", None),
            P("river", "hours", None),
        ),
        check_vma=False,
    )
```

```python
import functools
import math

import jax
import jax.numpy as jnp
from jax import lax
from jax.experimental import pallas as pl
from jax.experimental.pallas import tpu as pltpu
from jax.sharding import PartitionSpec as P

DMAX = 6


primal_step = 1.0
dual_step = 0.1


def passed_along(block, axis, distance):
    devices = range(lax.axis_size(axis))
    route = [(i - distance, i) for i in devices if i - distance in devices]
    return lax.ppermute(block, axis, route)


MESH = pl.DeviceIdType.MESH


def wanted(mode, src, dst):
    if mode == "prefix":
        return src < dst
    if mode == "suffix":
        return src > dst
    return src != dst


class Job:
    def __init__(self, axis, mode, inner, n):
        self.axis, self.mode, self.inner = axis, mode, inner
        self.outer = n // inner
        self.other = "river" if axis == "hours" else "hours"

    def place(self):
        me = lax.axis_index(self.axis)
        self.fixed = lax.axis_index(self.other)
        self.o = me // self.inner
        self.i = me % self.inner

    def device(self, p):
        return (self.fixed, p) if self.axis == "hours" else (p, self.fixed)

    def peers(self):
        inner, outer, o, i = self.inner, self.outer, self.o, self.i
        near = [self.device(o * inner + lax.rem(i + s, inner)) for s in range(1, inner)]
        far = [self.device(lax.rem(o + s, outer) * inner + i) for s in range(1, outer)]
        return near + far


def multi_kernel(jobs, *refs):
    count = len(jobs)
    ins, outs, rest = refs[:count], refs[count:2 * count], refs[2 * count:]
    for job in jobs:
        job.place()
    barrier = pltpu.get_barrier_semaphore()
    partners = 0
    for job in jobs:
        for dev in job.peers():
            pl.semaphore_signal(barrier, 1, device_id=dev, device_id_type=MESH)
            partners += 1
    pl.semaphore_wait(barrier, partners)

    def across(job, x_ref, near, s1, r1, p, landing):
        return pltpu.make_async_remote_copy(
            src_ref=x_ref, dst_ref=near.at[landing], send_sem=s1.at[p], recv_sem=r1.at[landing],
            device_id=job.device(job.o * job.inner + p), device_id_type=MESH)

    for k, job in enumerate(jobs):
        near, far, group, s1, r1, s2, r2 = rest[7 * k:7 * k + 7]
        for s in range(1, job.inner):
            p = lax.rem(job.i + s, job.inner)
            across(job, ins[k], near, s1, r1, p, job.i).start()
    parts = []
    for k, job in enumerate(jobs):
        near, far, group, s1, r1, s2, r2 = rest[7 * k:7 * k + 7]
        for s in range(1, job.inner):
            p = lax.rem(job.i + s, job.inner)
            across(job, ins[k], near, s1, r1, p, job.i).wait_send()
            across(job, ins[k], near, s1, r1, p, p).wait_recv()
        own = ins[k][...]
        total = own
        part = own if job.mode == "sum" else jnp.zeros_like(own)
        for s in range(1, job.inner):
            p = lax.rem(job.i + s, job.inner)
            block = near[p]
            total = total + block
            if job.mode == "sum":
                part = part + block
            else:
                part = part + jnp.where(wanted(job.mode, p, job.i), block, 0.0)
        group[...] = total
        parts.append(part)

    def up(job, group, far, s2, r2, q, landing):
        return pltpu.make_async_remote_copy(
            src_ref=group, dst_ref=far.at[landing], send_sem=s2.at[q], recv_sem=r2.at[landing],
            device_id=job.device(q * job.inner + job.i), device_id_type=MESH)

    for k, job in enumerate(jobs):
        near, far, group, s1, r1, s2, r2 = rest[7 * k:7 * k + 7]
        for s in range(1, job.outer):
            q = lax.rem(job.o + s, job.outer)

            @pl.when(wanted(job.mode, job.o, q))
            def _():
                up(job, group, far, s2, r2, q, job.o).start()

    for k, job in enumerate(jobs):
        near, far, group, s1, r1, s2, r2 = rest[7 * k:7 * k + 7]
        part = parts[k]
        for s in range(1, job.outer):
            q = lax.rem(job.o + s, job.outer)

            @pl.when(wanted(job.mode, job.o, q))
            def _():
                up(job, group, far, s2, r2, q, job.o).wait_send()

            @pl.when(wanted(job.mode, q, job.o))
            def _():
                up(job, group, far, s2, r2, q, q).wait_recv()

        for s in range(1, job.outer):
            q = lax.rem(job.o + s, job.outer)
            part = part + jnp.where(wanted(job.mode, q, job.o), far[q], 0.0)
        outs[k][...] = part


def dual_kernel(
    sloc_ref, t_ref, off_ref, off_next_ref, beyond_ref, rim_own_ref, rim_next_ref,
    near, far, group, beyond_buf, rim_src_own, rim_src_next, rim_own_buf, rim_next_buf,
    off_src, off_next_buf, s1, r1, s2, r2, sems,
):
    job = Job("hours", "suffix", 8, lax.axis_size("hours"))
    job.place()
    n_r = lax.axis_size("river")
    n_h = lax.axis_size("hours")
    r = lax.axis_index("river")
    h = lax.axis_index("hours")
    has_up, has_down = r > 0, r < n_r - 1
    has_before, has_after = h > 0, h < n_h - 1

    barrier = pltpu.get_barrier_semaphore()
    for dev in job.peers():
        pl.semaphore_signal(barrier, 1, device_id=dev, device_id_type=MESH)
    for flag, dev in ((has_up, (r - 1, h)), (has_down, (r + 1, h)), (has_before, (r, h - 1)), (has_after, (r, h + 1))):

        @pl.when(flag)
        def _():
            pl.semaphore_signal(barrier, 1, device_id=dev, device_id_type=MESH)

    extra = sum(jnp.where(flag, 1, 0) for flag in (has_up, has_down, has_before, has_after))
    pl.semaphore_wait(barrier, job.inner + job.outer - 2 + extra)

    def link(src, dst, k, dev):
        return pltpu.make_async_remote_copy(
            src_ref=src, dst_ref=dst, send_sem=sems.at[2 * k], recv_sem=sems.at[2 * k + 1],
            device_id=dev, device_id_type=MESH)

    to_up = lambda src, dst, k: link(src, dst, k, (r - 1, h))
    to_before = lambda src, dst, k: link(src, dst, k, (r, h - 1))

    def across(p, landing):
        return pltpu.make_async_remote_copy(
            src_ref=t_ref, dst_ref=near.at[landing], send_sem=s1.at[p], recv_sem=r1.at[landing],
            device_id=job.device(job.o * job.inner + p), device_id_type=MESH)

    for s in range(1, job.inner):
        across(lax.rem(job.i + s, job.inner), job.i).start()

    @pl.when(has_up)
    def _():
        to_up(sloc_ref, beyond_buf, 0).start()

    rim_src_own[...] = sloc_ref[:, 0:DMAX, :] - sloc_ref[:, 0:1, :]

    @pl.when(has_before)
    def _():
        to_before(rim_src_own, rim_own_buf, 1).start()

    for s in range(1, job.inner):
        p = lax.rem(job.i + s, job.inner)
        across(p, job.i).wait_send()
        across(p, p).wait_recv()
    own = t_ref[...]
    total = own
    part = jnp.zeros_like(own)
    for s in range(1, job.inner):
        p = lax.rem(job.i + s, job.inner)
        block = near[p]
        total = total + block
        part = part + jnp.where(p > job.i, block, 0.0)
    group[...] = total

    def up(q, landing):
        return pltpu.make_async_remote_copy(
            src_ref=group, dst_ref=far.at[landing], send_sem=s2.at[q], recv_sem=r2.at[landing],
            device_id=job.device(q * job.inner + job.i), device_id_type=MESH)

    for s in range(1, job.outer):
        q = lax.rem(job.o + s, job.outer)

        @pl.when(job.o > q)
        def _():
            up(q, job.o).start()

    @pl.when(has_down)
    def _():
        to_up(sloc_ref, beyond_buf, 0).wait_recv()
        rim_src_next[...] = beyond_buf[:, 0:DMAX, :] - beyond_buf[:, 0:1, :]

    @pl.when(jnp.logical_and(has_down, has_before))
    def _():
        to_before(rim_src_next, rim_next_buf, 2).start()

    for s in range(1, job.outer):
        q = lax.rem(job.o + s, job.outer)

        @pl.when(job.o > q)
        def _():
            up(q, job.o).wait_send()

        @pl.when(q > job.o)
        def _():
            up(q, q).wait_recv()

    for s in range(1, job.outer):
        q = lax.rem(job.o + s, job.outer)
        part = part + jnp.where(q > job.o, far[q], 0.0)
    off_src[...] = part
    off_ref[...] = part

    @pl.when(has_up)
    def _():
        to_up(off_src, off_next_buf, 3).start()

    @pl.when(has_up)
    def _():
        to_up(sloc_ref, beyond_buf, 0).wait_send()
        to_up(off_src, off_next_buf, 3).wait_send()

    @pl.when(has_before)
    def _():
        to_before(rim_src_own, rim_own_buf, 1).wait_send()

    @pl.when(jnp.logical_and(has_down, has_before))
    def _():
        to_before(rim_src_next, rim_next_buf, 2).wait_send()

    @pl.when(has_after)
    def _():
        to_before(rim_src_own, rim_own_buf, 1).wait_recv()
        rim_own_ref[...] = rim_own_buf[...]

    @pl.when(jnp.logical_not(has_after))
    def _():
        rim_own_ref[...] = jnp.zeros_like(rim_own_ref)

    @pl.when(jnp.logical_and(has_down, has_after))
    def _():
        to_before(rim_src_next, rim_next_buf, 2).wait_recv()
        rim_next_ref[...] = rim_next_buf[...]

    @pl.when(jnp.logical_not(jnp.logical_and(has_down, has_after)))
    def _():
        rim_next_ref[...] = jnp.zeros_like(rim_next_ref)

    @pl.when(has_down)
    def _():
        to_up(off_src, off_next_buf, 3).wait_recv()
        off_next_ref[...] = off_next_buf[...]
        beyond_ref[...] = beyond_buf[...]

    @pl.when(jnp.logical_not(has_down))
    def _():
        off_next_ref[...] = jnp.zeros_like(off_next_ref)
        beyond_ref[...] = jnp.zeros_like(beyond_ref)


def dual_exchange(sloc):
    res, length, width = sloc.shape
    t = sloc[:, 0].reshape(-1, 128)
    inner = 8
    outer = lax.axis_size("hours") // inner
    rim = (res, DMAX, width)
    vmem = pl.BlockSpec(memory_space=pltpu.VMEM)
    off, off_next, beyond, rim_own, rim_next = pl.pallas_call(
        dual_kernel,
        out_shape=[
            jax.ShapeDtypeStruct(t.shape, t.dtype),
            jax.ShapeDtypeStruct(t.shape, t.dtype),
            jax.ShapeDtypeStruct(sloc.shape, sloc.dtype),
            jax.ShapeDtypeStruct(rim, sloc.dtype),
            jax.ShapeDtypeStruct(rim, sloc.dtype),
        ],
        in_specs=[vmem, vmem],
        out_specs=[vmem] * 5,
        scratch_shapes=[
            pltpu.VMEM((inner,) + t.shape, t.dtype),
            pltpu.VMEM((outer,) + t.shape, t.dtype),
            pltpu.VMEM(t.shape, t.dtype),
            pltpu.VMEM(sloc.shape, sloc.dtype),
            pltpu.VMEM(rim, sloc.dtype),
            pltpu.VMEM(rim, sloc.dtype),
            pltpu.VMEM(rim, sloc.dtype),
            pltpu.VMEM(rim, sloc.dtype),
            pltpu.VMEM(t.shape, t.dtype),
            pltpu.VMEM(t.shape, t.dtype),
            pltpu.SemaphoreType.DMA((inner,)),
            pltpu.SemaphoreType.DMA((inner,)),
            pltpu.SemaphoreType.DMA((outer,)),
            pltpu.SemaphoreType.DMA((outer,)),
            pltpu.SemaphoreType.DMA((8,)),
        ],
        compiler_params=pltpu.CompilerParams(collective_id=0, has_side_effects=True, vmem_limit_bytes=48 * 1024 * 1024),
    )(sloc, t)
    return off.reshape(res, width), off_next.reshape(res, width), beyond, rim_own, rim_next


def flow_kernel(
    main_ref, rim_own_ref, rim_next_ref, a_ref, b_ref, power_ref,
    incoming_ref, rim_own_in_ref, rim_next_in_ref, pa_ref, supplied_ref,
    near_h, far_h, group_h, near_r, far_r, group_r, incoming_buf, rim_own_buf, rim_next_buf,
    a_src, b_buf, s1h, r1h, s2h, r2h, s1r, r1r, s2r, r2r, sems,
):
    jobs = [Job("hours", "prefix", 8, lax.axis_size("hours")), Job("river", "sum", 8, lax.axis_size("river"))]
    for job in jobs:
        job.place()
    n_r = lax.axis_size("river")
    n_h = lax.axis_size("hours")
    r = lax.axis_index("river")
    h = lax.axis_index("hours")
    has_up, has_down = r > 0, r < n_r - 1
    has_before, has_after = h > 0, h < n_h - 1
    diag_down = jnp.logical_and(has_down, has_after)
    diag_up = jnp.logical_and(has_up, has_before)

    barrier = pltpu.get_barrier_semaphore()
    fixed = 0
    for job in jobs:
        for dev in job.peers():
            pl.semaphore_signal(barrier, 1, device_id=dev, device_id_type=MESH)
            fixed += 1
    links = (
        (has_up, (r - 1, h)), (has_down, (r + 1, h)), (has_before, (r, h - 1)), (has_after, (r, h + 1)),
        (diag_down, (r + 1, h + 1)), (diag_up, (r - 1, h - 1)),
    )
    for flag, dev in links:

        @pl.when(flag)
        def _():
            pl.semaphore_signal(barrier, 1, device_id=dev, device_id_type=MESH)

    extra = sum(jnp.where(flag, 1, 0) for flag, _ in links)
    pl.semaphore_wait(barrier, fixed + extra)

    def link(src, dst, k, dev):
        return pltpu.make_async_remote_copy(
            src_ref=src, dst_ref=dst, send_sem=sems.at[2 * k], recv_sem=sems.at[2 * k + 1],
            device_id=dev, device_id_type=MESH)

    main_copy = link(main_ref, incoming_buf, 0, (r + 1, h))
    rim_own_copy = link(rim_own_ref, rim_own_buf, 1, (r, h + 1))
    rim_next_copy = link(rim_next_ref, rim_next_buf, 2, (r + 1, h + 1))
    b_copy = link(b_ref, b_buf, 3, (r + 1, h))

    @pl.when(has_down)
    def _():
        b_copy.start()
        main_copy.start()

    @pl.when(has_after)
    def _():
        rim_own_copy.start()

    @pl.when(diag_down)
    def _():
        rim_next_copy.start()

    bufs = [(a_src, near_h, far_h, group_h, s1h, r1h, s2h, r2h), (power_ref, near_r, far_r, group_r, s1r, r1r, s2r, r2r)]

    def across(job, x_ref, near, s1, r1, p, landing):
        return pltpu.make_async_remote_copy(
            src_ref=x_ref, dst_ref=near.at[landing], send_sem=s1.at[p], recv_sem=r1.at[landing],
            device_id=job.device(job.o * job.inner + p), device_id_type=MESH)

    for job, (x_ref, near, far, group, s1, r1, s2, r2) in zip(jobs[::-1], bufs[::-1]):
        if job.axis == "hours":

            @pl.when(has_up)
            def _():
                b_copy.wait_recv()
                a_src[...] = a_ref[...] + b_buf[...]

            @pl.when(jnp.logical_not(has_up))
            def _():
                a_src[...] = a_ref[...]

        for s in range(1, job.inner):
            across(job, x_ref, near, s1, r1, lax.rem(job.i + s, job.inner), job.i).start()
    parts = []
    for job, (x_ref, near, far, group, s1, r1, s2, r2) in zip(jobs, bufs):
        for s in range(1, job.inner):
            p = lax.rem(job.i + s, job.inner)
            across(job, x_ref, near, s1, r1, p, job.i).wait_send()
            across(job, x_ref, near, s1, r1, p, p).wait_recv()
        own = x_ref[...]
        total = own
        part = own if job.mode == "sum" else jnp.zeros_like(own)
        for s in range(1, job.inner):
            p = lax.rem(job.i + s, job.inner)
            block = near[p]
            total = total + block
            if job.mode == "sum":
                part = part + block
            else:
                part = part + jnp.where(wanted(job.mode, p, job.i), block, 0.0)
        group[...] = total
        parts.append(part)

    def up(job, group, far, s2, r2, q, landing):
        return pltpu.make_async_remote_copy(
            src_ref=group, dst_ref=far.at[landing], send_sem=s2.at[q], recv_sem=r2.at[landing],
            device_id=job.device(q * job.inner + job.i), device_id_type=MESH)

    for job, (x_ref, near, far, group, s1, r1, s2, r2) in zip(jobs, bufs):
        for s in range(1, job.outer):
            q = lax.rem(job.o + s, job.outer)

            @pl.when(wanted(job.mode, job.o, q))
            def _():
                up(job, group, far, s2, r2, q, job.o).start()

    results = []
    for job, part, (x_ref, near, far, group, s1, r1, s2, r2) in zip(jobs, parts, bufs):
        for s in range(1, job.outer):
            q = lax.rem(job.o + s, job.outer)

            @pl.when(wanted(job.mode, job.o, q))
            def _():
                up(job, group, far, s2, r2, q, job.o).wait_send()

            @pl.when(wanted(job.mode, q, job.o))
            def _():
                up(job, group, far, s2, r2, q, q).wait_recv()

        for s in range(1, job.outer):
            q = lax.rem(job.o + s, job.outer)
            part = part + jnp.where(wanted(job.mode, q, job.o), far[q], 0.0)
        results.append(part)
    scanned, supplied = results
    pa_ref[...] = scanned
    supplied_ref[...] = supplied

    @pl.when(has_down)
    def _():
        main_copy.wait_send()
        b_copy.wait_send()

    @pl.when(has_after)
    def _():
        rim_own_copy.wait_send()

    @pl.when(diag_down)
    def _():
        rim_next_copy.wait_send()

    @pl.when(has_up)
    def _():
        main_copy.wait_recv()
        incoming_ref[...] = incoming_buf[...]

    @pl.when(jnp.logical_not(has_up))
    def _():
        incoming_ref[...] = jnp.zeros_like(incoming_ref)

    @pl.when(has_before)
    def _():
        rim_own_copy.wait_recv()
        rim_own_in_ref[...] = rim_own_buf[...]

    @pl.when(jnp.logical_not(has_before))
    def _():
        rim_own_in_ref[...] = jnp.zeros_like(rim_own_in_ref)

    @pl.when(diag_up)
    def _():
        rim_next_copy.wait_recv()
        rim_next_in_ref[...] = rim_next_buf[...]

    @pl.when(jnp.logical_not(diag_up))
    def _():
        rim_next_in_ref[...] = jnp.zeros_like(rim_next_in_ref)


def flow_exchange(main_next, rim_own, rim_next, own_totals, next_totals, power):
    res, width = own_totals.shape
    a = own_totals.reshape(-1, 128)
    b = next_totals.reshape(-1, 128)
    flat_power = power.reshape(-1, 128)
    inner = 8
    outer_h = lax.axis_size("hours") // inner
    outer_r = lax.axis_size("river") // inner
    vmem = pl.BlockSpec(memory_space=pltpu.VMEM)
    shape = lambda x: jax.ShapeDtypeStruct(x.shape, x.dtype)
    incoming, rim_own_in, rim_next_in, pa, supplied = pl.pallas_call(
        flow_kernel,
        out_shape=[shape(main_next), shape(rim_own), shape(rim_next), shape(a), shape(flat_power)],
        in_specs=[vmem] * 6,
        out_specs=[vmem] * 5,
        scratch_shapes=[
            pltpu.VMEM((inner,) + a.shape, a.dtype),
            pltpu.VMEM((outer_h,) + a.shape, a.dtype),
            pltpu.VMEM(a.shape, a.dtype),
            pltpu.VMEM((inner,) + flat_power.shape, a.dtype),
            pltpu.VMEM((outer_r,) + flat_power.shape, a.dtype),
            pltpu.VMEM(flat_power.shape, a.dtype),
            pltpu.VMEM(main_next.shape, a.dtype),
            pltpu.VMEM(rim_own.shape, a.dtype),
            pltpu.VMEM(rim_next.shape, a.dtype),
            pltpu.VMEM(a.shape, a.dtype),
            pltpu.VMEM(a.shape, a.dtype),
            pltpu.SemaphoreType.DMA((inner,)),
            pltpu.SemaphoreType.DMA((inner,)),
            pltpu.SemaphoreType.DMA((outer_h,)),
            pltpu.SemaphoreType.DMA((outer_h,)),
            pltpu.SemaphoreType.DMA((inner,)),
            pltpu.SemaphoreType.DMA((inner,)),
            pltpu.SemaphoreType.DMA((outer_r,)),
            pltpu.SemaphoreType.DMA((outer_r,)),
            pltpu.SemaphoreType.DMA((8,)),
        ],
        compiler_params=pltpu.CompilerParams(collective_id=1, has_side_effects=True, vmem_limit_bytes=48 * 1024 * 1024),
    )(main_next, rim_own, rim_next, a, b, flat_power)
    return incoming, rim_own_in, rim_next_in, pa.reshape(res, width), supplied.reshape(power.shape)


def combine(parts, specs, collective):
    shapes = [part.shape for part in parts]
    parts = [part.reshape(-1, 128) for part in parts]
    jobs = [Job(axis, mode, inner, lax.axis_size(axis)) for axis, mode, inner in specs]
    scratch = []
    for part, job in zip(parts, jobs):
        scratch += [
            pltpu.VMEM((job.inner,) + part.shape, part.dtype),
            pltpu.VMEM((job.outer,) + part.shape, part.dtype),
            pltpu.VMEM(part.shape, part.dtype),
            pltpu.SemaphoreType.DMA((job.inner,)),
            pltpu.SemaphoreType.DMA((job.inner,)),
            pltpu.SemaphoreType.DMA((job.outer,)),
            pltpu.SemaphoreType.DMA((job.outer,)),
        ]
    results = pl.pallas_call(
        functools.partial(multi_kernel, jobs),
        out_shape=[jax.ShapeDtypeStruct(part.shape, part.dtype) for part in parts],
        in_specs=[pl.BlockSpec(memory_space=pltpu.VMEM)] * len(parts),
        out_specs=[pl.BlockSpec(memory_space=pltpu.VMEM)] * len(parts),
        scratch_shapes=scratch,
        compiler_params=pltpu.CompilerParams(collective_id=collective, has_side_effects=True),
    )(*parts)
    return [result.reshape(shape) for result, shape in zip(results, shapes)]


def add_pair(earlier_part, later_part):
    return earlier_part + later_part


def hold_back(field, travel_delay, earlier_rim):
    length = field.shape[1]
    extended = jnp.concatenate([earlier_rim, field], 1)
    result = jnp.zeros_like(field)
    for lag_hours in range(1, DMAX + 1):
        window = extended[:, DMAX - lag_hours : DMAX - lag_hours + length]
        result = result + jnp.where((travel_delay == lag_hours)[:, None, None], window, 0.0)
    return result


def bring_forward(field, travel_delay, later_rim):
    length = field.shape[1]
    extended = jnp.concatenate([field, later_rim], 1)
    result = jnp.zeros_like(field)
    for lag_hours in range(1, DMAX + 1):
        window = extended[:, lag_hours : lag_hours + length]
        result = result + jnp.where((travel_delay == lag_hours)[:, None, None], window, 0.0)
    return result


def route_down(matrix, field):
    return jnp.einsum("ij,jtw->itw", matrix, field, precision=lax.Precision.HIGHEST)


def route_up(matrix, field):
    return jnp.einsum("ij,itw->jtw", matrix, field, precision=lax.Precision.HIGHEST)


def iterate(fields, statics, scales, suffix_sum, from_earlier, from_later):
    release, storage_dual, demand_dual, cost, inflow, demand = fields
    (
        storage_start,
        storage_low,
        storage_high,
        release_cap,
        efficiency,
        travel_delay,
        to_own,
        to_next,
    ) = statics
    scale_time, scale_sum = scales
    local = suffix_local(storage_dual)
    off, off_next, beyond, rim_own, rim_next = dual_exchange(local)
    suffix = local + off[:, None]
    both = jnp.concatenate([to_own, to_next], 0)
    length = suffix.shape[1]
    sinks = route_up(
        both,
        jnp.concatenate(
            [
                jnp.concatenate([local, rim_own], 1),
                jnp.concatenate([beyond, rim_next], 1),
            ],
            0,
        ),
    ) + route_up(both, jnp.concatenate([off, off_next], 0)[:, None])
    at_sink, rim_sink = sinks[:, :length], sinks[:, length:]
    last = lax.axis_index("hours") == lax.axis_size("hours") - 1
    later_duals = bring_forward(at_sink, travel_delay, jnp.where(last, 0.0, rim_sink))
    gradient = (
        cost
        + scale_time * (later_duals - suffix)
        + scale_sum * efficiency[:, None, None] * demand_dual[None]
    )
    release_new = jnp.clip(release - primal_step * gradient, 0.0, release_cap[:, None, None])
    extrapolated = 2.0 * release_new - release
    length = extrapolated.shape[1]
    tail = extrapolated[:, length - DMAX :]
    settled = hold_back(extrapolated, travel_delay, jnp.zeros_like(tail))
    rim_delayed = hold_back(jnp.zeros_like(extrapolated), travel_delay, tail)[:, :DMAX]
    res = settled.shape[0]
    routed_all = route_down(both, jnp.concatenate([settled, rim_delayed], 1))
    main_own, main_next = routed_all[:res, :length], routed_all[res:, :length]
    rim_own, rim_next = routed_all[:res, length:], routed_all[res:, length:]
    base = inflow + main_own - extrapolated
    own_totals = jnp.sum(inflow - extrapolated, 1) + jnp.sum(routed_all[:res], 1)
    next_totals = jnp.sum(routed_all[res:], 1)
    partial_power = jnp.sum(scale_sum * efficiency[:, None, None] * extrapolated, 0)
    incoming, rim_own_in, rim_next_in, offset, supplied = flow_exchange(
        main_next, rim_own, rim_next, own_totals, next_totals, partial_power
    )
    landed = rim_own_in + rim_next_in
    arrived = jnp.concatenate([landed, jnp.zeros_like(base[:, DMAX:])], 1)
    local_sum = jnp.cumsum(base + incoming + arrived, 1)
    offset = offset - jnp.sum(landed, 1)
    storage = storage_start[:, None, None] + scale_time * (local_sum + offset[:, None])
    lower_bound = storage_low[:, None, None]
    upper_bound = storage_high[:, None, None]
    storage_dual_new = (
        storage_dual
        + dual_step * storage
        - dual_step * jnp.clip(storage_dual / dual_step + storage, lower_bound, upper_bound)
    )
    storage_excess = storage - jnp.clip(storage, lower_bound, upper_bound)
    demand_dual_new = jnp.minimum(demand_dual + dual_step * (supplied - demand), 0.0)
    return (release_new, storage_dual_new, demand_dual_new, storage_excess)


def suffix_local(field):
    return lax.cumsum(field, 1, reverse=True)


def shards(
    release,
    storage_dual,
    demand_dual,
    cost,
    inflow,
    demand,
    storage_start,
    storage_low,
    storage_high,
    release_cap,
    efficiency,
    downstream,
    travel_delay,
):
    res_dev = release.shape[0]
    scale_time = 1.0 / (release.shape[1] * lax.axis_size("hours"))
    scale_sum = 1.0 / math.sqrt(res_dev * lax.axis_size("river"))
    base_index = lax.axis_index("river") * res_dev
    target = downstream - base_index
    indices = jnp.arange(res_dev, dtype=jnp.int32)
    to_own = (target[None, :] == indices[:, None]).astype(jnp.float32)
    to_next = (target[None, :] == indices[:, None] + res_dev).astype(jnp.float32)
    statics = (
        storage_start,
        storage_low,
        storage_high,
        release_cap,
        efficiency,
        travel_delay,
        to_own,
        to_next,
    )
    scales = (scale_time, scale_sum)

    def suffix_blocks(field):
        local_sum = suffix_local(field)
        totals = local_sum[:, 0]
        (offset,) = combine([totals], [("hours", "suffix", 8)], 0)
        return local_sum + offset[:, None]

    def earlier_block(part):
        return passed_along(part, "hours", 1)

    def later_block(part):
        return passed_along(part, "hours", -1)

    fields = (release, storage_dual, demand_dual, cost, inflow, demand)
    return iterate(
        fields, statics, scales, suffix_blocks, earlier_block, later_block
    )


def solution(mesh):
    return jax.shard_map(
        shards,
        mesh=mesh,
        in_specs=(
            P("river", "hours", None),
            P("river", "hours", None),
            P("hours", None),
            P("river", "hours", None),
            P("river", "hours", None),
            P("hours", None),
            P("river"),
            P("river"),
            P("river"),
            P("river"),
            P("river"),
            P("river"),
            P("river"),
        ),
        out_specs=(
            P("river", "hours", None),
            P("river", "hours", None),
            P("hours", None),
            P("river", "hours", None),
        ),
        check_vma=False,
    )
```
